32 devices in a mesh: wide: 8 (over z, y), narrow: 4 (over x, core).
Axes of the slice: x: 2, y: 2, z: 4, core: 2. Of those that a mesh axis runs over, the one named last changes fastest.
Arguments:
- passages: bfloat16 [24, 512, 768], P('wide', 'narrow'), may hold values from -6 to 6
- queries: bfloat16 [8, 512, 768], P('wide', 'narrow'), may hold values from -6 to 6
- passage_cot: bfloat16 [24, 512, 768], P('wide', 'narrow'), may hold values from -3 to 3
- query_cot: bfloat16 [8, 512, 768], P('wide', 'narrow'), may hold values from -3 to 3
- passage_lengths: int32 [24, 5], P('wide'), may hold values from 1 to 400, as said below
- query_lengths: int32 [8, 17], P('wide'), may hold values from 1 to 40, 512 in all within a row
- labels: int32 [128], P('wide'), may hold values from 0 to 95
- w_qkv: bfloat16 [2, 768, 2304], P(None, ('wide', 'narrow')), may hold values from -0.3125 to 0.3125
- w_out: bfloat16 [2, 768, 768], P(None, ('wide', 'narrow')), may hold values from -0.875 to 0.875
- w_in: bfloat16 [2, 768, 3072], P(None, ('wide', 'narrow')), may hold values from -0.21875 to 0.21875
- w_back: bfloat16 [2, 3072, 768], P(None, ('wide', 'narrow')), may hold values from -0.15625 to 0.15625
- biases: bfloat16 [2, 6, 768], P(None, None, ('wide', 'narrow')), may hold values from -1 to 1
- norm_gains: bfloat16 [2, 2, 768], P(None, None, ('wide', 'narrow')), may hold values from 0.5 to 1.5
- in_bias: bfloat16 [2, 3072], P(None, ('wide', 'narrow')), may hold values from -1 to 1
Outputs:
- passage_out: bfloat16 [24, 512, 768], P('wide', 'narrow')
- query_out: bfloat16 [8, 512, 768], P('wide', 'narrow')
- passage_grad: bfloat16 [24, 512, 768], P('wide', 'narrow')
- query_grad: bfloat16 [8, 512, 768], P('wide', 'narrow')
- grad_w_qkv: float32 [2, 768, 2304], P(None, 'wide', 'narrow')
- grad_w_out: float32 [2, 768, 768], P(None, 'wide', 'narrow')
- grad_w_in: float32 [2, 768, 3072], P(None, 'wide', 'narrow')
- grad_w_back: float32 [2, 3072, 768], P(None, 'wide', 'narrow')
- grad_biases: float32 [2, 6, 768], P(None, None, ('wide', 'narrow'))
- grad_gains: float32 [2, 2, 768], P(None, None, ('wide', 'narrow'))
- grad_in_bias: float32 [2, 3072], P(None, ('wide', 'narrow'))
- rms_stats: float32 [2, 4], replicated
The draws below stay inside these ranges and needn't reach their ends.
Inputs may be any that keep to these rules, and one draw needn't show every extreme that they name: `passage_lengths`: entries s < 4 of a row are its passages' lengths, the last entry its padding's; each row sums to 512. Among the 3 rows of each index of wide, one row, drawn from the seed, begins with a passage of exactly 400 tokens. `query_lengths`: entries s < 16 of a row are its queries' lengths, the last entry its padding's; each row sums to 512, and some row of every draw has an entry of exactly 40. `labels`: query r * 16 + s is segment s of query row r; passage r * 4 + s is segment s of passage row r.
All inputs are finite; a program needn't handle non-finite values.
Results may differ from the reference program's by a relative error of at most 0.015.
Values may be sent and summed in bfloat16 or wider, within the bound.
No kernel may reach another device: no remote copies, remote signals or barrier semaphores. Data moves between devices by JAX's collectives and lax.ppermute only.
A program may use at most 256 MiB of HBM per device.

```python
import math
import jax
import jax.numpy as jnp
import numpy as np
from jax import lax

D = 768
HEADS = 12
HEAD_DIM = 64
FF = 3072
L = 512
SEGS = 4
QSEGS = 16
P_MOST = 400
Q_MOST = 40
P_DEV = 3
Q_DEV = 1
NPR = 24
NQR = 8
NP = 96
NQ = 128


def split_total(weights, total):
    count = weights.shape[-1]
    spare = total - count
    weight_sum = jnp.sum(weights, axis=-1, keepdims=True, dtype=jnp.int32)
    shares = spare * weights // weight_sum
    leftover = spare - jnp.sum(shares, axis=-1, keepdims=True, dtype=jnp.int32)
    first_col = (jnp.arange(count, dtype=jnp.int32) == 0).astype(jnp.int32)[None, :]
    return shares + leftover * first_col + 1


def draw_passage_lengths(key, part):
    key_drawn = jax.random.fold_in(key, 11)
    key_long = jax.random.fold_in(key, 12)
    key_pick = jax.random.fold_in(key, 13)
    drawn_weights = jax.random.randint(key_drawn, (NPR, SEGS + 1), 10, 101, dtype=jnp.int32)
    drawn_rows = split_total(drawn_weights, L)
    long_weights = jax.random.randint(key_long, (NPR, SEGS), 10, 101, dtype=jnp.int32)
    long_rest = split_total(long_weights, L - P_MOST)
    long_rows = jnp.concatenate([jnp.full((NPR, 1), P_MOST, jnp.int32), long_rest], axis=1)
    groups = NPR // P_DEV
    picked = jax.random.randint(key_pick, (groups,), 0, P_DEV, dtype=jnp.int32)
    row_ids = jnp.arange(NPR, dtype=jnp.int32)
    chosen = row_ids % P_DEV == jnp.repeat(picked, P_DEV)
    return jnp.where(chosen[:, None], long_rows, drawn_rows).astype(jnp.int32)


def set_ends(drawn, key, least, high):
    longest = drawn.shape.index(max(drawn.shape))
    spots = []
    for shift in (0, 1):
        where = [jax.random.randint(jax.random.fold_in(key, axis), (), 0, length) for axis, length in enumerate(drawn.shape)]
        where[longest] = (where[longest] + shift) % drawn.shape[longest]
        spots.append(tuple(where))
    return drawn.at[spots[0]].set(least).at[spots[1]].set(high)


def steps_of(own_key, extent, split, least, high):
    level = 1.0
    for axis_at, shards_of in split:
        heights = jax.random.uniform(jax.random.fold_in(jax.random.fold_in(own_key, 6), axis_at), (shards_of,), jnp.float32, least / len(split), high / len(split))
        level = level * jnp.repeat(jnp.exp(heights), extent[axis_at] // shards_of).reshape((-1,) + (1,) * (len(extent) - 1 - axis_at))
    return level


def length_profile(amount, total, bound, slope):
    loads = [(1 << 20) // math.isqrt(grade ** slope) + 1 for grade in range(2, amount + 1)]
    rest, counts = total - bound - (amount - 1), [1] * (amount - 1)
    while rest > 0:
        movable = [i for i in range(amount - 1) if counts[i] < bound]
        mass, budget = sum([loads[i] for i in movable]), rest
        for i in movable:
            more = min(bound - counts[i], max(1, budget * loads[i] // mass), rest)
            counts[i] = counts[i] + more
            rest = rest - more
    return np.array([bound] + counts)


def uneven_parts(key, amount, total, most, skew):
    if amount == 2:
        one = jax.random.randint(key, (), max(1, total - most), min(most, total - 1) + 1)
        return jnp.stack([one, total - one])
    sizes = jnp.asarray(length_profile(amount, total, most, skew), jnp.int32)
    pairs = (amount - 1) // 2
    giver, receiver = sizes[1:1 + 2 * pairs:2], sizes[2:2 + 2 * pairs:2]
    margin = jnp.minimum(giver - 1, most - receiver)
    shifted = jax.random.randint(jax.random.fold_in(key, 1), (pairs,), 0, 1 << 20) % (margin + 1)
    sizes = sizes.at[1:1 + 2 * pairs:2].set(giver - shifted).at[2:2 + 2 * pairs:2].set(receiver + shifted)
    return sizes[jax.random.permutation(jax.random.fold_in(key, 2), amount)]


def bell_draw(stream_key, shape, spread, most, shards=(), kind=jnp.bfloat16):
    level = steps_of(stream_key, shape, shards, -0.22, 0.18) if shards else 1.0
    values = jax.random.normal(stream_key, shape, jnp.float32) * spread * level
    return jnp.minimum(jnp.maximum(values, -most), most).astype(kind)


def setup_inputs(seed: int = 0) -> dict:
    key_list = jax.random.split(jax.random.key(seed), 15)
    passages = bell_draw(key_list[0], (NPR, L, D), 1.0, 6.0, ((0, 8), (1, 4)))
    queries = bell_draw(key_list[1], (NQR, L, D), 1.0, 6.0, ((0, 8), (1, 4)))
    passage_cot = bell_draw(key_list[2], (NPR, L, D), 0.5, 3.0, ((0, 8), (1, 4)))
    query_cot = bell_draw(key_list[3], (NQR, L, D), 0.5, 3.0, ((0, 8), (1, 4)))
    passage_lengths = draw_passage_lengths(jax.random.fold_in(key_list[14], 71), 0)
    query_lengths = jax.vmap(lambda own: uneven_parts(own, QSEGS + 1, L, Q_MOST, 2))(jax.random.split(key_list[5], NQR)).reshape((NQR, QSEGS + 1)).astype(jnp.int32)
    labels = set_ends(jax.random.randint(key_list[6], (NQ,), 0, NP), jax.random.fold_in(key_list[6], 1), 0, NP - 1).astype(jnp.int32)
    w_qkv = bell_draw(key_list[7], (2, D, 3 * D), (D // 2) ** -0.5, 0.3125, ((1, 32),))
    w_out = bell_draw(key_list[8], (2, D, D), (D // 16) ** -0.5, 0.875, ((1, 32),))
    w_in = bell_draw(key_list[9], (2, D, FF), D ** -0.5, 0.21875, ((1, 32),))
    w_back = bell_draw(key_list[10], (2, FF, D), (FF // 2) ** -0.5, 0.15625, ((1, 32),))
    biases = bell_draw(key_list[11], (2, 6, D), 0.2, 1.0, ((2, 32),))
    norm_gains = jnp.clip(1.0 + 0.1 * jax.random.normal(key_list[12], (2, 2, D), jnp.float32), 0.5, 1.5).astype(jnp.bfloat16)
    in_bias = bell_draw(key_list[13], (2, FF), 0.2, 1.0, ((1, 32),))
    return {"passages": passages, "queries": queries, "passage_cot": passage_cot, "query_cot": query_cot, "passage_lengths": passage_lengths, "query_lengths": query_lengths, "labels": labels, "w_qkv": w_qkv, "w_out": w_out, "w_in": w_in, "w_back": w_back, "biases": biases, "norm_gains": norm_gains, "in_bias": in_bias}


PRECISE = lax.Precision.HIGHEST
EPSILON = 1e-05
SCORE_DIV = 12.0
MASKED = -1e+30

@jax.custom_vjp
def low(v):
    return lax.optimization_barrier(v.astype(jnp.bfloat16)).astype(jnp.float32)

@jax.custom_vjp
def low_back(v):
    return v

def low_keep(v):
    return (low(v), None)

def low_pass(kept, grad):
    return (grad,)

def back_keep(v):
    return (v, None)

def back_low(kept, grad):
    return (low(grad),)
low.defvjp(low_keep, low_pass)
low_back.defvjp(back_keep, back_low)

def layer_norm(inputs, gain_row, shift_row):
    row_mean = lax.optimization_barrier(jnp.mean(inputs, axis=-1, keepdims=True))
    centered = inputs - row_mean
    row_var = lax.optimization_barrier(jnp.mean(centered * centered, axis=-1, keepdims=True))
    return centered * lax.rsqrt(row_var + EPSILON) * gain_row + shift_row

def segment_table(lengths, positions):
    row_ends = jnp.cumsum(lengths, axis=1, dtype=jnp.int32)
    starts = row_ends - lengths
    boundary = row_ends[:, :-1]
    segment = lax.optimization_barrier(jnp.sum((positions[None, :, None] >= boundary[:, None, :]).astype(jnp.int32), axis=2, dtype=jnp.int32))
    return (segment, starts[:, :-1])

def layer_block(inputs, segment, seg_count, params):
    w_qkv, w_out, w_in, w_back, biases, norm_gains, in_bias = params
    row_count, length, model_width = inputs.shape
    flat_rows = inputs.reshape(row_count * length, model_width)
    projected = jnp.dot(flat_rows, w_qkv, precision=PRECISE)
    query_vec = low_back(low(projected[:, :model_width] + biases[0]))
    key_vec = low_back(low(projected[:, model_width:2 * model_width]))
    value_vec = low_back(low(projected[:, 2 * model_width:] + biases[1]))
    head_shape = (row_count, length, HEADS, HEAD_DIM)
    raw_scores = jnp.einsum('rqhd,rkhd->rhqk', query_vec.reshape(head_shape), key_vec.reshape(head_shape), precision=PRECISE)
    scores = low_back(raw_scores * HEAD_DIM ** (-0.5))
    same_seg = segment[:, :, None] == segment[:, None, :]
    scores = jnp.where(same_seg[:, None], scores, MASKED)
    weights = jax.nn.softmax(scores, axis=-1)
    context = jnp.einsum('rhqk,rkhd->rqhd', low(weights), value_vec.reshape(head_shape), precision=PRECISE)
    context = low_back(low(context.reshape(row_count * length, model_width)))
    branch = low_back(jnp.dot(context, w_out, precision=PRECISE) + biases[2])
    residual = flat_rows + branch
    normed = layer_norm(residual, norm_gains[0], biases[3])
    hidden_pre = low_back(jnp.dot(low(normed), w_in, precision=PRECISE) + in_bias)
    active = low(jax.nn.gelu(hidden_pre, approximate=False))
    ffn_out = low_back(jnp.dot(active, w_back, precision=PRECISE) + biases[4])
    residual_two = normed + ffn_out
    output = layer_norm(residual_two, norm_gains[1], biases[5])
    valid_col = (segment < seg_count).reshape(row_count * length, 1).astype(jnp.float32)
    sums = jnp.stack([jnp.sum(valid_col * residual * residual), jnp.sum(valid_col * branch * branch), jnp.sum(valid_col * residual_two * residual_two), jnp.sum(valid_col * ffn_out * ffn_out)])
    return (output.reshape(row_count, length, model_width), sums)

def tower_run(inputs, segment, seg_count, params, group_rows):
    row_count = inputs.shape[0]
    grouped = inputs.reshape(row_count // group_rows, group_rows, inputs.shape[1], inputs.shape[2])
    seg_groups = segment.reshape(row_count // group_rows, group_rows, segment.shape[1])

    def step_fn(carried, group_item):
        output, sums = layer_block(group_item[0], group_item[1], seg_count, params)
        return (carried + sums, output)
    totals, outputs = lax.scan(jax.checkpoint(step_fn), jnp.zeros((4,), jnp.float32), (grouped, seg_groups))
    return (outputs.reshape(inputs.shape), totals)

def reference(passages, queries, passage_cot, query_cot, passage_lengths, query_lengths, labels, w_qkv, w_out, w_in, w_back, biases, norm_gains, in_bias):
    positions = jnp.arange(L, dtype=jnp.int32)
    pass_seg, pass_starts = segment_table(passage_lengths, positions)
    query_seg, query_starts = segment_table(query_lengths, positions)
    params = tuple((array.astype(jnp.float32) for array in (w_qkv, w_out, w_in, w_back, biases, norm_gains, in_bias)))
    pass_input = passages.astype(jnp.float32)
    query_input = queries.astype(jnp.float32)

    def forward(params, pass_input, query_input):
        pass_params = tuple((array[0] for array in params))
        query_params = tuple((array[1] for array in params))
        pass_output, pass_sums = tower_run(pass_input, pass_seg, SEGS, pass_params, P_DEV)
        query_output, query_sums = tower_run(query_input, query_seg, QSEGS, query_params, 8 * Q_DEV)
        pooled_pass = low(jnp.take_along_axis(pass_output, pass_starts[:, :, None], axis=1).reshape(NP, D))
        pooled_query = low(jnp.take_along_axis(query_output, query_starts[:, :, None], axis=1).reshape(NQ, D))
        match = low_back(jnp.dot(pooled_query, pooled_pass.T, precision=PRECISE)) / SCORE_DIV
        log_total = jax.nn.logsumexp(match, axis=1)
        picked = jnp.take_along_axis(match, labels[:, None], axis=1)[:, 0]
        loss = jnp.sum(log_total - picked)
        return (pass_output, query_output, loss, pass_sums, query_sums)
    results, pullback = jax.vjp(forward, params, pass_input, query_input)
    pass_output, query_output, loss, pass_sums, query_sums = results
    valid_pass = (pass_seg < SEGS).astype(jnp.float32)[:, :, None]
    valid_query = (query_seg < QSEGS).astype(jnp.float32)[:, :, None]
    cotangents = (passage_cot.astype(jnp.float32) * valid_pass, query_cot.astype(jnp.float32) * valid_query, jnp.ones_like(loss), jnp.zeros_like(pass_sums), jnp.zeros_like(query_sums))
    gradients, pass_grad, query_grad = pullback(cotangents)
    rms_stats = jnp.sqrt(jnp.stack([pass_sums / (jnp.sum(valid_pass) * D), query_sums / (jnp.sum(valid_query) * D)]))
    return (pass_output.astype(jnp.bfloat16), query_output.astype(jnp.bfloat16), pass_grad.astype(jnp.bfloat16), query_grad.astype(jnp.bfloat16), gradients[0], gradients[1], gradients[2], gradients[3], gradients[4], gradients[5], gradients[6], rms_stats)
```

```python
import functools

import jax
import jax.numpy as jnp
from jax import lax
from jax.experimental import pallas as pl
from jax.experimental.pallas import tpu as pltpu
from jax.sharding import PartitionSpec as P

HEAD_DIM = 64
LEVELS = 4
EPSILON = 1e-05
SCORE_DIV = 12.0
MASKED = -1e30
BF = jnp.bfloat16
F32 = jnp.float32
BOTH = ("wide", "narrow")


def matmul(left, right):
    return jnp.dot(left, right, preferred_element_type=F32)


def inner_rows(left, right):
    return lax.dot_general(left, right, (((0,), (0,)), ((), ())), preferred_element_type=F32)


def inner_cols(left, right):
    return lax.dot_general(left, right, (((1,), (1,)), ((), ())), preferred_element_type=F32)


def layer_norm(inputs, gain_row, shift_row):
    row_mean = jnp.mean(inputs, axis=-1, keepdims=True)
    centered = inputs - row_mean
    row_var = jnp.mean(centered * centered, axis=-1, keepdims=True)
    return centered * lax.rsqrt(row_var + EPSILON) * gain_row + shift_row


def gelu_exact(inputs):
    return jax.nn.gelu(inputs, approximate=False)


def split_heads(matrix):
    return matrix.reshape(matrix.shape[0], matrix.shape[1] // HEAD_DIM, HEAD_DIM)


def flip(x, axis, mask):
    size = lax.axis_size(axis)
    return lax.ppermute(x, axis, [(i, i ^ mask) for i in range(size)])


def swap_levels(x, k, stride):
    pairs = []
    for i in range(stride):
        pairs += [(i, k * stride + i), (k * stride + i, i)]
    return lax.ppermute(x, "wide", pairs)


def bits_of(size):
    return [1 << b for b in range(size.bit_length() - 1)]


class Place:
    def __init__(self):
        self.wide = lax.axis_size("wide")
        self.narrow = lax.axis_size("narrow")
        self.stride = self.wide // LEVELS
        self.w = lax.axis_index("wide")
        self.n = lax.axis_index("narrow")
        self.z = self.w // self.stride
        self.y = self.w % self.stride
        self.me = self.w * self.narrow + self.n


def to_rows(place, pass_part, query_part):
    s = place.stride
    got = []
    for k in range(1, LEVELS):
        got.append(swap_levels(jnp.where(place.z == 0, pass_part[k - 1], query_part[0]), k, s))
    spare = got[0] + got[1] + got[2]
    four = [
        jnp.where(place.z == 0, query_part[0], pass_part[0]),
        jnp.where(place.z == 0, got[0], pass_part[1]),
        jnp.where(place.z == 0, got[1], pass_part[2]),
        jnp.where(place.z == 0, got[2], spare),
    ]
    mine = lax.all_to_all(jnp.stack(four), "narrow", 0, 0, tiled=True)
    return mine.reshape(-1, mine.shape[-1])


def from_rows(place, row):
    s = place.stride
    four = lax.all_to_all(
        row.reshape(place.narrow, -1, row.shape[-1]), "narrow", 0, 0, tiled=True
    )
    got = []
    for k in range(1, LEVELS):
        got.append(swap_levels(jnp.where(place.z == 0, four[k], four[3]), k, s))
    spare = got[0] + got[1] + got[2]
    pass_part = jnp.where(place.z == 0, jnp.stack(got), four[:3])
    query_part = jnp.where(place.z == 0, four[0], spare)[None]
    return pass_part, query_part


def assemble_kernel(plan, widths, me_ref, *refs):
    pieces, outs = refs[: len(plan)], refs[len(plan) :]
    me = me_ref[0]
    for piece, masks in zip(pieces, plan):
        for slot, mask in enumerate(masks):
            column = 0
            for out, width in zip(outs, widths):
                out[me ^ mask] = piece[slot, :, column : column + width]
                column += width


def assemble(place, pieces, plan, widths):
    total = place.wide * place.narrow
    rows = pieces[0].shape[1]
    vmem = pl.BlockSpec(memory_space=pltpu.VMEM)
    outs = pl.pallas_call(
        functools.partial(assemble_kernel, plan, widths),
        out_shape=[jax.ShapeDtypeStruct((total, rows, width), BF) for width in widths],
        in_specs=[pl.BlockSpec(memory_space=pltpu.SMEM)] + [vmem] * len(pieces),
        out_specs=[vmem] * len(widths),
        compiler_params=pltpu.CompilerParams(vmem_limit_bytes=32 << 20),
    )(place.me.reshape(1), *pieces)
    return [out.reshape(total * rows, out.shape[-1]) for out in outs]


def gather_tower(place, pair, widths):
    s, narrow = place.stride, place.narrow
    level = s * narrow
    slots = [jnp.where(place.z == 0, pair[1], pair[0])]
    for k in range(1, LEVELS):
        send = jnp.where((place.z ^ k) == 0, pair[1], pair[0])
        slots.append(flip(send, "wide", k * s))
    first, first_masks = jnp.stack(slots[:2]), [0, level]
    second, second_masks = jnp.stack(slots[2:]), [2 * level, 3 * level]
    pieces, plan = [], []

    def keep(piece, masks):
        pieces.append(piece)
        plan.append(tuple(masks))
        pieces.append(flip(piece, "narrow", 1))
        plan.append(tuple(m ^ 1 for m in masks))

    for b in bits_of(s):
        other = flip(first, "wide", b)
        first = jnp.concatenate([first, other])
        first_masks = first_masks + [m ^ (b * narrow) for m in first_masks]
    keep(first, first_masks)
    keep(flip(first, "narrow", 2), [m ^ 2 for m in first_masks])
    keep(second, second_masks)
    other = flip(second, "narrow", 2)
    keep(other, [m ^ 2 for m in second_masks])
    second = jnp.concatenate([second, other])
    second_masks = second_masks + [m ^ 2 for m in second_masks]
    for b in bits_of(s):
        other = flip(second, "wide", b)
        other_masks = [m ^ (b * narrow) for m in second_masks]
        keep(other, other_masks)
        second = jnp.concatenate([second, other])
        second_masks = second_masks + other_masks
    return assemble(place, pieces, plan, widths)


def pick(x, index, dim):
    return lax.dynamic_index_in_dim(x, index, dim, keepdims=False)


def halve(x, place, axis, mask, dim):
    index = place.n if axis == "narrow" else place.w
    bit = jnp.where((index & mask) != 0, 1, 0)
    got = flip(pick(x, 1 - bit, dim).astype(BF), axis, mask)
    return pick(x, bit, dim) + got.astype(F32)


def scatter_tower(place, partial):
    s = place.stride
    rows, narrow, cols = partial.shape
    per = rows // place.wide
    x = partial.reshape(rows, 2, 2, cols)
    x = halve(x, place, "narrow", 1, 2)
    x = x.reshape(LEVELS, s, per, 2, cols)
    first, second = x[:2], x[2:]

    def over_columns(part):
        for b in reversed(bits_of(s)):
            shape = part.shape
            part = part.reshape(shape[0], 2, shape[1] // 2, *shape[2:])
            part = halve(part, place, "wide", b, 1)
        return part[:, 0]

    first = over_columns(halve(first, place, "narrow", 2, 3))
    second = halve(over_columns(second), place, "narrow", 2, 2)
    levels = jnp.concatenate([first, second])
    slots = [pick(levels, place.z, 0)]
    for k in range(1, LEVELS):
        got = flip(pick(levels, place.z ^ k, 0).astype(BF), "wide", k * s)
        slots.append(got.astype(F32))
    tower0 = sum(jnp.where(place.z == k, 0.0, slots[k]) for k in range(LEVELS))
    tower1 = sum(jnp.where(place.z == k, slots[k], 0.0) for k in range(LEVELS))
    return jnp.stack([tower0, tower1])


def column_blocks(right, narrow):
    return right.reshape(right.shape[0], narrow, -1)


def grad_blocks(left, right, narrow):
    out = inner_rows(left, right)
    return out.reshape(out.shape[0], narrow, -1)


def masked_scores(query_heads, key_heads, segment):
    scores = jnp.einsum(
        "qhd,khd->hqk", query_heads, key_heads, preferred_element_type=F32
    ) * HEAD_DIM ** (-0.5)
    same_seg = segment[:, None] == segment[None, :]
    return jnp.where(same_seg[None], scores, MASKED)


def attend(query, key, value, segment):
    scores = masked_scores(split_heads(query), split_heads(key), segment)
    row_max = jnp.max(scores, axis=-1, keepdims=True)
    shifted = jnp.exp(scores - row_max)
    row_total = jnp.sum(shifted, axis=-1, keepdims=True)
    row_probs = (shifted / row_total).astype(BF)
    context = jnp.einsum("hqk,khd->qhd", row_probs, split_heads(value), preferred_element_type=F32)
    log_sum = (row_max + jnp.log(row_total))[:, :, 0]
    return context.reshape(query.shape).astype(BF), log_sum


def attend_back(query, key, value, segment, log_sum, grad):
    q, k, v, g = split_heads(query), split_heads(key), split_heads(value), split_heads(grad)
    row_probs = jnp.exp(masked_scores(q, k, segment) - log_sum[:, :, None])
    grad_probs = jnp.einsum("qhd,khd->hqk", g, v, preferred_element_type=F32)
    row_delta = jnp.sum(row_probs * grad_probs, axis=-1, keepdims=True)
    grad_scores = (row_probs * (grad_probs - row_delta)).astype(BF)
    scale = HEAD_DIM ** (-0.5)
    grad_q = jnp.einsum("hqk,khd->qhd", grad_scores, k, preferred_element_type=F32) * scale
    grad_k = jnp.einsum("hqk,qhd->khd", grad_scores, q, preferred_element_type=F32) * scale
    grad_v = jnp.einsum("hqk,qhd->khd", row_probs.astype(BF), g, preferred_element_type=F32)
    shape = query.shape
    return (
        grad_q.reshape(shape).astype(BF),
        grad_k.reshape(shape).astype(BF),
        grad_v.reshape(shape).astype(BF),
    )


def row_of(z, y, n, s):
    own = (z * s + y) * 3 + n
    spare = y * 3 + (z - 1)
    return jnp.where(z == 0, n * s + y, jnp.where(n < 3, own, spare))


def body(
    passages,
    queries,
    passage_cot,
    query_cot,
    passage_lengths,
    query_lengths,
    labels,
    w_qkv,
    w_out,
    w_in,
    w_back,
    biases,
    norm_gains,
    in_bias,
):
    place = Place()
    s, narrow, devices = place.stride, place.narrow, place.wide * place.narrow
    model_width = passages.shape[2]
    length = passages.shape[1] * narrow
    segs, qsegs = passage_lengths.shape[1] - 1, query_lengths.shape[1] - 1
    on_query = place.z == 0

    piece = model_width // devices
    small = jnp.concatenate(
        [biases.reshape(2, -1), norm_gains.reshape(2, -1), in_bias.reshape(2, -1)], axis=1
    )
    whole = jnp.concatenate(
        [passage_lengths.reshape(-1), query_lengths.reshape(-1), labels.reshape(-1)]
    )
    whole = jnp.concatenate([whole // 32, whole % 32]).astype(BF)
    to_query = (jnp.arange(devices) < s * narrow)[:, None]
    small = jnp.where(to_query, small[1][None], small[0][None])
    small = jnp.concatenate(
        [small, jnp.broadcast_to(whole[None], (devices, whole.shape[0]))], axis=1
    )
    small_count = small.shape[1] - whole.shape[0]
    small = lax.all_to_all(small, BOTH, 0, 0, tiled=True)

    inputs = to_rows(place, passages, queries)
    (w_qkv_all,) = gather_tower(place, w_qkv, (w_qkv.shape[2],))
    out_in = jnp.concatenate([w_out, w_in], axis=2)
    w_out_all, w_in_all = gather_tower(place, out_in, (w_out.shape[2], w_in.shape[2]))
    (w_back_all,) = gather_tower(place, w_back, (w_back.shape[2],))
    cot = to_rows(place, passage_cot, query_cot)

    params, ints = small[:, :small_count].astype(F32), small[:, small_count:].astype(F32)
    n_bias, n_gain = biases.shape[1], norm_gains.shape[1]

    def unpack(part, count):
        return part.reshape(devices, count, -1).transpose(1, 0, 2).reshape(count, -1)

    tower_bias = unpack(params[:, : n_bias * piece], n_bias)
    tower_gain = unpack(params[:, n_bias * piece : (n_bias + n_gain) * piece], n_gain)
    tower_in_bias = unpack(params[:, (n_bias + n_gain) * piece :], 1)
    half = ints.shape[1] // 2
    ints = (ints[::narrow, :half] * 32 + ints[::narrow, half:]).astype(jnp.int32)
    n_pass = passage_lengths.size
    n_query = query_lengths.size
    pass_lens = ints[:, :n_pass].reshape(-1, segs + 1)
    query_lens = ints[:, n_pass : n_pass + n_query].reshape(-1, qsegs + 1)
    label_all = ints[:, n_pass + n_query :].reshape(-1, qsegs)
    my_row = row_of(place.z, place.y, place.n, s)
    pass_row = pick(pass_lens, jnp.where(on_query, 0, my_row), 0)
    query_row = pick(query_lens, jnp.where(on_query, my_row, 0), 0)
    ends_p = jnp.cumsum(pass_row)[:-1]
    ends_q = jnp.cumsum(query_row)[:-1]
    ends_p = jnp.concatenate([ends_p, jnp.full((qsegs - segs,), length + 1, jnp.int32)])
    starts_p = jnp.concatenate([jnp.zeros((1,), jnp.int32), ends_p[:-1]])
    starts_p = jnp.where(jnp.arange(qsegs) < segs, starts_p, length + 1)
    starts_q = jnp.concatenate([jnp.zeros((1,), jnp.int32), ends_q[:-1]])
    ends = jnp.where(on_query, ends_q, ends_p)
    starts = jnp.where(on_query, starts_q, starts_p)
    seg_count = jnp.where(on_query, qsegs, segs)
    position = jnp.arange(length, dtype=jnp.int32)
    segment = jnp.sum((position[:, None] >= ends[None, :]).astype(jnp.int32), axis=1)
    valid = (segment < seg_count).astype(F32)[:, None]
    first_hot = starts[:, None] == position[None, :]

    projected = matmul(inputs, w_qkv_all)
    query = (projected[:, :model_width] + tower_bias[0]).astype(BF)
    key = projected[:, model_width : 2 * model_width].astype(BF)
    value = (projected[:, 2 * model_width :] + tower_bias[1]).astype(BF)
    context, log_sum = attend(query, key, value, segment)
    branch = matmul(context, w_out_all) + tower_bias[2]
    residual = inputs.astype(F32) + branch
    normed = layer_norm(residual, tower_gain[0], tower_bias[3])
    normed_low = normed.astype(BF)
    hidden_pre = matmul(normed_low, w_in_all) + tower_in_bias[0]
    active = gelu_exact(hidden_pre).astype(BF)
    ffn_out = matmul(active, w_back_all) + tower_bias[4]
    residual_two = normed + ffn_out
    output_low = layer_norm(residual_two, tower_gain[1], tower_bias[5]).astype(BF)
    stats = jnp.stack(
        [
            jnp.sum(valid * residual * residual),
            jnp.sum(valid * branch * branch),
            jnp.sum(valid * residual_two * residual_two),
            jnp.sum(valid * ffn_out * ffn_out),
            jnp.sum(valid),
        ]
    )
    passage_out, query_out = from_rows(place, output_low)

    pooled = matmul(first_hot.astype(BF), output_low).astype(BF)
    seen = [pooled]
    for k in range(1, LEVELS):
        seen.append(flip(pooled, "wide", k * s))
    column = []
    for level in range(LEVELS):
        rows = qsegs if level == 0 else segs
        part = jnp.zeros((rows, model_width), BF)
        for k in range(LEVELS):
            part = jnp.where((place.z ^ k) == level, seen[k][:rows], part)
        column.append(part)
    columns = jnp.concatenate(column)[None]
    masks = [0]
    for axis, step, mask in (
        [("wide", b, b * narrow) for b in bits_of(s)]
        + [("narrow", b, b) for b in reversed(bits_of(narrow))]
    ):
        columns = jnp.concatenate([columns, flip(columns, axis, step)])
        masks = masks + [m ^ mask for m in masks]
    here = place.y * narrow + place.n
    there = here ^ jnp.array(masks, jnp.int32)
    their_y, their_n = there // narrow, there % narrow
    every_query = columns[:, :qsegs].reshape(-1, model_width)
    every_pass = columns[:, qsegs:].reshape(-1, model_width)
    label_rows = label_all[row_of(jnp.int32(0), their_y, their_n, s)].reshape(-1)
    levels = jnp.arange(1, LEVELS)
    pass_rows = row_of(levels[None, :], their_y[:, None], their_n[:, None], s)
    pass_ids = (pass_rows[:, :, None] * segs + jnp.arange(segs)).reshape(-1)
    match = inner_cols(every_query, every_pass) / SCORE_DIV
    match_max = jnp.max(match, axis=1, keepdims=True)
    match_exp = jnp.exp(match - match_max)
    match_probs = match_exp / jnp.sum(match_exp, axis=1, keepdims=True)
    label_hot = (label_rows[:, None] == pass_ids[None, :]).astype(F32)
    grad_match = ((match_probs - label_hot) / SCORE_DIV).astype(BF)
    grad_query_pool = matmul(grad_match[:qsegs], every_pass)
    my_cols = lax.dynamic_slice_in_dim(
        grad_match, jnp.maximum(place.z - 1, 0) * segs, segs, axis=1
    )
    grad_pass_pool = inner_rows(my_cols, every_query)
    grad_pool = jnp.where(
        on_query,
        grad_query_pool,
        jnp.concatenate([grad_pass_pool, jnp.zeros((qsegs - segs, model_width), F32)]),
    )

    grad_output = cot.astype(F32) * valid
    grad_output = grad_output + lax.dot_general(
        first_hot.astype(F32),
        grad_pool,
        (((0,), (0,)), ((), ())),
        precision=lax.Precision.HIGHEST,
    )
    norm_two_back = jax.vjp(layer_norm, residual_two, tower_gain[1], tower_bias[5])[1]
    grad_resid_two, grad_gain_two, grad_shift_two = norm_two_back(grad_output)
    grad_ffn = grad_resid_two.astype(BF)
    grad_ffn_bias = jnp.sum(grad_ffn.astype(F32), axis=0)
    grad_w_back = scatter_tower(place, grad_blocks(active, grad_ffn, narrow))
    grad_active = inner_cols(grad_ffn, w_back_all)
    gelu_back = jax.vjp(gelu_exact, hidden_pre)[1]
    grad_hidden = gelu_back(grad_active)[0].astype(BF)
    grad_in_bias = jnp.sum(grad_hidden.astype(F32), axis=0)
    grad_normed = grad_resid_two + inner_cols(grad_hidden, w_in_all)
    norm_one_back = jax.vjp(layer_norm, residual, tower_gain[0], tower_bias[3])[1]
    grad_residual, grad_gain_one, grad_shift_one = norm_one_back(grad_normed)
    grad_branch = grad_residual.astype(BF)
    grad_out_bias = jnp.sum(grad_branch.astype(F32), axis=0)
    grad_out_in = scatter_tower(
        place,
        jnp.concatenate(
            [
                grad_blocks(context, grad_branch, narrow),
                grad_blocks(normed_low, grad_hidden, narrow),
            ],
            axis=2,
        ),
    )
    grad_context = inner_cols(grad_branch, w_out_all).astype(BF)
    grad_q, grad_k, grad_v = attend_back(query, key, value, segment, log_sum, grad_context)
    grad_qkv = jnp.concatenate([grad_q, grad_k, grad_v], axis=-1)
    grad_w_qkv = scatter_tower(place, grad_blocks(inputs, grad_qkv, narrow))
    input_grad = (grad_residual + inner_cols(grad_qkv, w_qkv_all)).astype(BF)
    passage_grad, query_grad = from_rows(place, input_grad)
    out_cols = w_out.shape[2] // narrow
    grad_w_out, grad_w_in = grad_out_in[:, :, :out_cols], grad_out_in[:, :, out_cols:]

    def share(rows):
        count = rows.shape[0]
        return rows.reshape(count, devices, -1).transpose(1, 0, 2).reshape(devices, -1)

    bias_rows = jnp.stack(
        [
            jnp.sum(grad_q.astype(F32), axis=0),
            jnp.sum(grad_v.astype(F32), axis=0),
            grad_out_bias,
            grad_shift_one,
            grad_ffn_bias,
            grad_shift_two,
            grad_gain_one,
            grad_gain_two,
        ]
    )
    shares = jnp.concatenate(
        [
            share(bias_rows),
            share(grad_in_bias[None]),
            jnp.broadcast_to(stats[None], (devices, stats.shape[0])),
        ],
        axis=1,
    )
    shares = lax.all_to_all(shares, BOTH, 0, 0, tiled=True)
    shares = shares.reshape(LEVELS, -1, shares.shape[1]).sum(axis=1)
    shares = jnp.stack([shares[1] + shares[2] + shares[3], shares[0]])
    grad_biases = shares[:, : n_bias * piece].reshape(2, n_bias, piece)
    grad_gains = shares[:, n_bias * piece : (n_bias + n_gain) * piece].reshape(2, n_gain, piece)
    grad_inb = shares[:, (n_bias + n_gain) * piece : -stats.shape[0]]
    totals = shares[:, -stats.shape[0] :]
    rms_stats = jnp.sqrt(totals[:, :4] / (totals[:, 4:] * model_width))
    return (
        passage_out,
        query_out,
        passage_grad,
        query_grad,
        grad_w_qkv,
        grad_w_out,
        grad_w_in,
        grad_w_back,
        grad_biases,
        grad_gains,
        grad_inb,
        rms_stats,
    )


def solution(mesh):
    return jax.shard_map(
        body,
        mesh=mesh,
        in_specs=(
            P("wide", "narrow", None),
            P("wide", "narrow", None),
            P("wide", "narrow", None),
            P("wide", "narrow", None),
            P("wide", None),
            P("wide", None),
            P("wide"),
            P(None, ("wide", "narrow"), None),
            P(None, ("wide", "narrow"), None),
            P(None, ("wide", "narrow"), None),
            P(None, ("wide", "narrow"), None),
            P(None, None, ("wide", "narrow")),
            P(None, None, ("wide", "narrow")),
            P(None, ("wide", "narrow")),
        ),
        out_specs=(
            P("wide", "narrow", None),
            P("wide", "narrow", None),
            P("wide", "narrow", None),
            P("wide", "narrow", None),
            P(None, "wide", "narrow"),
            P(None, "wide", "narrow"),
            P(None, "wide", "narrow"),
            P(None, "wide", "narrow"),
            P(None, None, ("wide", "narrow")),
            P(None, None, ("wide", "narrow")),
            P(None, ("wide", "narrow")),
            P(),
        ),
        check_vma=False,
    )
```

```python
import functools
import math

import jax
import jax.numpy as jnp
from jax import lax
from jax.experimental import pallas as pl
from jax.experimental.pallas import tpu as pltpu
from jax.sharding import PartitionSpec as P

HEAD_DIM = 64
LEVELS = 4
GROUP = 4
POOL = 32
VMEM = 58 << 20
OTHERS = ((1, 1), (1, 0), (0, 1))


def cost(us):
    return pl.CostEstimate(flops=int(us * 1.15e9), bytes_accessed=1024, transcendentals=0)


EPSILON = 1e-05
SCORE_DIV = 12.0
MASKED = -1e30
BF = jnp.bfloat16
F32 = jnp.float32
BOTH = ("wide", "narrow")


def matmul(left, right):
    return jnp.dot(left, right, preferred_element_type=F32)


def inner_rows(left, right):
    return lax.dot_general(left, right, (((0,), (0,)), ((), ())), preferred_element_type=F32)


def inner_cols(left, right):
    return lax.dot_general(left, right, (((1,), (1,)), ((), ())), preferred_element_type=F32)


def flip(x, axis, mask):
    size = lax.axis_size(axis)
    return lax.ppermute(x, axis, [(i, i ^ mask) for i in range(size)])


def flip_both(x, wide_mask, narrow_mask):
    wide, narrow = lax.axis_size("wide"), lax.axis_size("narrow")
    mask = wide_mask * narrow + narrow_mask
    return lax.ppermute(x, BOTH, [(i, i ^ mask) for i in range(wide * narrow)])


def phase(*values):
    return lax.optimization_barrier(values)


def across_levels(x, stride):
    groups = [[k * stride + i for k in range(LEVELS)] for i in range(stride)]
    return lax.all_to_all(x, "wide", 0, 0, axis_index_groups=groups, tiled=True)


def swap_levels(x, k, stride):
    pairs = []
    for i in range(stride):
        pairs += [(i, k * stride + i), (k * stride + i, i)]
    return lax.ppermute(x, "wide", pairs)


def bits_of(size):
    return [1 << b for b in range(size.bit_length() - 1)]


class Place:
    def __init__(self):
        self.wide = lax.axis_size("wide")
        self.narrow = lax.axis_size("narrow")
        self.stride = self.wide // LEVELS
        self.w = lax.axis_index("wide")
        self.n = lax.axis_index("narrow")
        self.z = self.w // self.stride
        self.y = self.w % self.stride
        self.me = self.w * self.narrow + self.n


def swap_in(place, pass_part, query_part):
    query = jnp.broadcast_to(query_part, (LEVELS, *query_part.shape[1:]))
    first = jnp.concatenate([query_part, pass_part])
    return across_levels(jnp.where(place.z == 0, first, query), place.stride)


def swap_in_directly(place, pass_part, query_part):
    got = [
        swap_levels(jnp.where(place.z == 0, pass_part[k - 1], query_part[0]), k, place.stride)
        for k in range(1, LEVELS)
    ]
    first = jnp.where(place.z == 0, query_part[0], got[0] + got[1] + got[2])
    return jnp.stack([first] + got)


def to_row(place, pass_part, query_part, got):
    four = jnp.where(place.z == 0, got, jnp.concatenate([pass_part, got[:1]]))
    mine = lax.all_to_all(four, "narrow", 0, 0, tiled=True)
    return mine.reshape(-1, mine.shape[-1])


def row_pieces(place, row):
    return lax.all_to_all(
        row.reshape(place.narrow, -1, row.shape[-1]), "narrow", 0, 0, tiled=True
    )


def swap_out(place, four):
    last = jnp.broadcast_to(four[3:], four.shape)
    return across_levels(jnp.where(place.z == 0, four, last), place.stride)


def from_row(place, four, got):
    pass_part = jnp.where(place.z == 0, got[1:], four[:3])
    query_part = jnp.where(place.z == 0, four[:1], got[:1])
    return pass_part, query_part


def assemble_kernel(plan, parts, me_ref, *refs):
    pieces, outs, sems = refs[: len(plan)], refs[len(plan) : -1], refs[-1]
    me = me_ref[0]
    copies = []
    for piece, masks in zip(pieces, plan):
        width = piece.shape[2] // sum(parts)
        for slot, mask in enumerate(masks):
            column = 0
            for out, count in zip(outs, parts):
                for part in range(count):
                    source = piece.at[slot, :, pl.ds(column, width)]
                    target = out.at[part, me ^ mask]
                    copies.append(pltpu.make_async_copy(source, target, sems.at[len(copies)]))
                    column += width
    for copy in copies:
        copy.start()
    for copy in copies:
        copy.wait()


def assemble(place, pieces, plan, parts):
    total = place.wide * place.narrow
    rows = pieces[0].shape[1]
    width = pieces[0].shape[2] // sum(parts)
    outs = pl.pallas_call(
        functools.partial(assemble_kernel, plan, parts),
        out_shape=[jax.ShapeDtypeStruct((count, total, rows, width), BF) for count in parts],
        in_specs=[pl.BlockSpec(memory_space=pltpu.SMEM)]
        + [pl.BlockSpec(memory_space=pl.ANY)] * len(pieces),
        out_specs=[pl.BlockSpec(memory_space=pltpu.VMEM)] * len(parts),
        scratch_shapes=[pltpu.SemaphoreType.DMA((total * sum(parts),))],
        cost_estimate=cost(5),
        compiler_params=pltpu.CompilerParams(vmem_limit_bytes=VMEM),
    )(place.me.reshape(1), *pieces)
    return [out.reshape(out.shape[0], total * rows, width) for out in outs]


def gather_levels(place, pair):
    slots = {0: jnp.where(place.z == 0, pair[1], pair[0])}
    for k in (3, 2, 1):
        send = jnp.where((place.z ^ k) == 0, pair[1], pair[0])
        slots[k] = flip(send, "wide", k * place.stride)
    return jnp.stack([slots[k] for k in range(LEVELS)])


def gather_columns(place, levels):
    s, narrow = place.stride, place.narrow
    own = [k * s * narrow for k in range(LEVELS)]
    pieces, plan = [levels], [own]
    if s == 2:
        for wide_mask, narrow_mask in ((1, 2), (0, 2), (1, 0)):
            pieces.append(flip_both(levels, wide_mask, narrow_mask))
            plan.append([m ^ (wide_mask * narrow + narrow_mask) for m in own])
    else:
        for b in bits_of(s):
            for i in range(len(pieces)):
                pieces.append(flip(pieces[i], "wide", b))
                plan.append([m ^ (b * narrow) for m in plan[i]])
        for i in range(len(pieces)):
            pieces.append(flip(pieces[i], "narrow", 2))
            plan.append([m ^ 2 for m in plan[i]])
    return pieces, plan


def gather_cores(pieces, plan):
    others = [flip(piece, "narrow", 1) for piece in pieces]
    return list(pieces) + others, plan + [[m ^ 1 for m in masks] for masks in plan]


def pick(x, index, dim):
    return lax.dynamic_index_in_dim(x, index, dim, keepdims=False)


def halve(x, place, axis, mask, dim):
    index = place.n if axis == "narrow" else place.w
    bit = jnp.where((index & mask) != 0, 1, 0)
    got = flip(pick(x, 1 - bit, dim).astype(BF), axis, mask)
    return pick(x, bit, dim) + got.astype(F32)


def scatter_tower(place, partial):
    s = place.stride
    rows, narrow, cols = partial.shape
    per = rows // place.wide
    x = partial.reshape(rows, 2, 2, cols)
    x = halve(x, place, "narrow", 1, 2)
    x = x.reshape(LEVELS, s, per, 2, cols)
    first, second = x[:2], x[2:]

    def over_columns(part):
        for b in reversed(bits_of(s)):
            shape = part.shape
            part = part.reshape(shape[0], 2, shape[1] // 2, *shape[2:])
            part = halve(part, place, "wide", b, 1)
        return part[:, 0]

    first = over_columns(halve(first, place, "narrow", 2, 3))
    second = halve(over_columns(second), place, "narrow", 2, 2)
    return jnp.stack(sum_levels(place, send_levels(place, jnp.concatenate([first, second]))))


def send_levels(place, levels):
    slots = [None] * LEVELS
    slots[0] = pick(levels, place.z, 0)
    for k in (3, 2, 1):
        slots[k] = flip(pick(levels, place.z ^ k, 0).astype(BF), "wide", k * place.stride)
    return slots


def sum_levels(place, slots):
    tower0 = sum(jnp.where(place.z == k, 0.0, slots[k].astype(F32)) for k in range(LEVELS))
    tower1 = sum(jnp.where(place.z == k, slots[k].astype(F32), 0.0) for k in range(LEVELS))
    return tower0, tower1


def share_kernel(at_ref, keep_ref, got_ref, own_ref, *sent_refs):
    x, y = at_ref[0], at_ref[1]

    def share(dx, dy):
        at = (x ^ dx, 0, y ^ dy)
        return keep_ref[at].astype(F32) + got_ref[at].astype(F32)

    own_ref[0] = share(0, 0)
    for ref, (dx, dy) in zip(sent_refs, OTHERS):
        ref[0] = share(dx, dy).astype(BF)


def column_shares(place, keep, got):
    r, c = got.shape[2:]
    block = pl.BlockSpec((2, 1, place.stride, r, c), lambda i, at: (0, i, 0, 0, 0))
    out = pl.BlockSpec((1, r, c), lambda i, at: (i, 0, 0))
    shape = (2, LEVELS, place.stride, r, c)
    return pl.pallas_call(
        share_kernel,
        grid_spec=pltpu.PrefetchScalarGridSpec(
            num_scalar_prefetch=1, grid=(LEVELS,), in_specs=[block] * 2, out_specs=[out] * 4
        ),
        out_shape=[jax.ShapeDtypeStruct((LEVELS, r, c), F32)]
        + [jax.ShapeDtypeStruct((LEVELS, r, c), BF)] * 3,
        compiler_params=pltpu.CompilerParams(vmem_limit_bytes=VMEM),
        cost_estimate=cost(6),
    )(jnp.stack([place.n // 2, place.y]), keep.reshape(shape), got.reshape(shape))


def send_columns(shares):
    return [shares[0]] + [
        flip_both(sent, dy, 2 * dx) for sent, (dx, dy) in zip(shares[1:], OTHERS)
    ]


def level_kernel(z_ref, own_ref, *refs):
    got_refs, (sum_ref, *sent_refs) = refs[:3], refs[3:]
    for k in range(LEVELS):
        at = z_ref[0] ^ k
        total = own_ref[at]
        for ref in got_refs:
            total = total + ref[at].astype(F32)
        if k == 0:
            sum_ref[...] = total
        else:
            sent_refs[k - 1][...] = total.astype(BF)


def level_shares(place, columns):
    r, c = columns[0].shape[1:]
    vmem = pl.BlockSpec(memory_space=pltpu.VMEM)
    return pl.pallas_call(
        level_kernel,
        in_specs=[pl.BlockSpec(memory_space=pltpu.SMEM)] + [vmem] * 4,
        out_specs=[vmem] * 4,
        out_shape=[jax.ShapeDtypeStruct((r, c), F32)] + [jax.ShapeDtypeStruct((r, c), BF)] * 3,
        compiler_params=pltpu.CompilerParams(vmem_limit_bytes=VMEM),
        cost_estimate=cost(3),
    )(place.z.reshape(1), *columns)


def swap_shares(place, shares):
    slots = [shares[0], None, None, None]
    for k in (3, 2, 1):
        slots[k] = flip(shares[k], "wide", k * place.stride)
    return slots


def product_kernel(step, me_ref, *refs):
    send_ref, keep_ref = refs[-2:]
    left_refs = refs[:-2]
    to_send = pl.program_id(0) < 2

    @pl.when(to_send)
    def _():
        step(left_refs, lambda at, v: send_ref.__setitem__((0, *at), v.astype(BF)))

    @pl.when(jnp.logical_not(to_send))
    def _():
        step(left_refs, lambda at, v: keep_ref.__setitem__((0, *at), v.astype(BF)))


def products(place, step, operands, specs, block):
    def target(j, me):
        return (j % 2) * 2 + jnp.where(j < 2, 1 - me[0] % 2, me[0] % 2)

    wide = place.wide
    grid_spec = pltpu.PrefetchScalarGridSpec(
        num_scalar_prefetch=1,
        grid=(4,),
        in_specs=specs(target),
        out_specs=[
            pl.BlockSpec((1, wide, *block), lambda j, me: (jnp.minimum(j, 1), 0, 0, 0)),
            pl.BlockSpec((1, wide, *block), lambda j, me: (jnp.maximum(j - 2, 0), 0, 0, 0)),
        ],
    )
    return pl.pallas_call(
        functools.partial(product_kernel, step),
        grid_spec=grid_spec,
        out_shape=[
            jax.ShapeDtypeStruct((2, wide, *block), BF),
            jax.ShapeDtypeStruct((2, wide, *block), BF),
        ],
        compiler_params=pltpu.CompilerParams(vmem_limit_bytes=VMEM),
        cost_estimate=cost(8),
    )(place.n.reshape(1), *operands)


def whole(shape):
    return pl.BlockSpec(shape, lambda j, me: (0,) * len(shape))


def grad_blocks(left, right, narrow):
    out = inner_rows(left, right)
    return out.reshape(out.shape[0], narrow, -1)


def products_back(place, active, blocks):
    t, ff = active.shape
    cols, rows = blocks.shape[2], ff // place.wide

    def step(refs, store):
        left, right = refs
        value = inner_rows(right[0], left[...])
        for w in range(place.wide):
            store((w,), value[:, w * rows : (w + 1) * rows])

    return products(
        place,
        step,
        (active, blocks),
        lambda target: [
            whole((t, ff)),
            pl.BlockSpec((1, t, cols), lambda j, me: (target(j, me), 0, 0)),
        ],
        (cols, rows),
    )


def finish_back(place, slots):
    return jnp.stack([part.T for part in sum_levels(place, slots)])


def products_out_in(place, context, blocks, normed, grad_hidden):
    narrow = place.narrow
    t, d = context.shape
    rows = d // place.wide
    cols_out, cols_in = blocks.shape[2], grad_hidden.shape[1] // narrow
    fold = cols_in // cols_out
    low = rows // fold

    def step(refs, store):
        context_ref, branch_ref, normed_ref, hidden_ref = refs
        value = inner_rows(normed_ref[...], hidden_ref[...])
        for w in range(place.wide):
            store((w, slice(0, rows)), value[w * rows : (w + 1) * rows])
        value = inner_rows(context_ref[...], branch_ref[0])
        for w in range(place.wide):
            for g in range(fold):
                store(
                    (w, slice(rows, rows + low), slice(g * cols_out, (g + 1) * cols_out)),
                    value[w * rows + g * low : w * rows + (g + 1) * low],
                )

    return products(
        place,
        step,
        (context, blocks, normed, grad_hidden),
        lambda target: [
            whole((t, d)),
            pl.BlockSpec((1, t, cols_out), lambda j, me: (target(j, me), 0, 0)),
            whole((t, d)),
            pl.BlockSpec((t, cols_in), lambda j, me: (0, target(j, me))),
        ],
        (rows + low, cols_in),
    )


def finish_out_in(place, slots, rows):
    parts = sum_levels(place, slots)
    low, cols = parts[0].shape[0] - rows, parts[0].shape[1]
    fold = rows // low
    grad_in = jnp.stack([part[:rows] for part in parts])
    grad_out = [
        jnp.moveaxis(part[rows:].reshape(low, fold, -1), 1, 0).reshape(rows, -1) for part in parts
    ]
    return jnp.stack(grad_out), grad_in


def products_qkv(place, inputs, blocks):
    t, d = inputs.shape
    rows, cols = d // place.wide, blocks.shape[2]
    half = rows // 2

    def step(refs, store):
        left, right = refs
        value = inner_rows(left[...], right[0])
        for w in range(place.wide):
            for g in range(2):
                store(
                    (w, slice(None), slice(g * cols, (g + 1) * cols)),
                    value[w * rows + g * half : w * rows + (g + 1) * half],
                )

    return products(
        place,
        step,
        (inputs, blocks),
        lambda target: [
            whole((t, d)),
            pl.BlockSpec((1, t, cols), lambda j, me: (target(j, me), 0, 0)),
        ],
        (half, 2 * cols),
    )


def finish_qkv(place, slots):
    parts = sum_levels(place, slots)
    cols = parts[0].shape[1] // 2
    return jnp.stack([jnp.concatenate([p[:, :cols], p[:, cols:]]) for p in parts])


def attend_kernel(x_ref, w_ref, rows_ref, seg_row_ref, seg_col_ref, qkv_ref, ctx_ref, lse_ref):
    x = x_ref[...]
    same = seg_col_ref[...] == seg_row_ref[...]
    qkv_ref[0] = (matmul(x, w_ref[0]) + rows_ref[0:1]).astype(BF)
    qkv_ref[1] = matmul(x, w_ref[1]).astype(BF)
    qkv_ref[2] = (matmul(x, w_ref[2]) + rows_ref[1:2]).astype(BF)
    for h in range(GROUP):
        lanes = slice(h * HEAD_DIM, (h + 1) * HEAD_DIM)
        q, k, v = qkv_ref[0, :, lanes], qkv_ref[1, :, lanes], qkv_ref[2, :, lanes]
        scores = jnp.where(same, inner_cols(k, q) * HEAD_DIM ** (-0.5), MASKED)
        top = jnp.max(scores, axis=0, keepdims=True)
        shifted = jnp.exp(scores - top)
        total = jnp.sum(shifted, axis=0, keepdims=True)
        probs = (shifted * (1.0 / total)).astype(BF)
        ctx_ref[:, lanes] = inner_rows(probs, v).astype(BF)
        lse_ref[0, h : h + 1, :] = top + jnp.log(total)


def attend(x, w_qkv, rows, segment):
    t, d = x.shape
    width = GROUP * HEAD_DIM
    steps = d // width
    return pl.pallas_call(
        attend_kernel,
        grid=(steps,),
        in_specs=[
            pl.BlockSpec((t, d), lambda j: (0, 0)),
            pl.BlockSpec((3, d, width), lambda j: (0, 0, j)),
            pl.BlockSpec((8, width), lambda j: (0, j)),
            pl.BlockSpec((1, t), lambda j: (0, 0)),
            pl.BlockSpec((t, 1), lambda j: (0, 0)),
        ],
        out_specs=[
            pl.BlockSpec((3, t, width), lambda j: (0, 0, j)),
            pl.BlockSpec((t, width), lambda j: (0, j)),
            pl.BlockSpec((1, GROUP, t), lambda j: (j, 0, 0)),
        ],
        out_shape=[
            jax.ShapeDtypeStruct((3, t, d), BF),
            jax.ShapeDtypeStruct((t, d), BF),
            jax.ShapeDtypeStruct((steps, GROUP, t), F32),
        ],
        compiler_params=pltpu.CompilerParams(vmem_limit_bytes=VMEM),
        cost_estimate=cost(11),
    )(x, w_qkv, rows, segment.reshape(1, t), segment.reshape(t, 1))


def attend_back_kernel(
    gb_ref, w_ref, qkv_ref, lse_ref, seg_row_ref, seg_col_ref, out_ref, blocks_ref, sums_ref
):
    scale = HEAD_DIM ** (-0.5)
    same = seg_col_ref[...] == seg_row_ref[...]
    grad = inner_cols(gb_ref[...], w_ref[...]).astype(BF)
    for h in range(GROUP):
        lanes = slice(h * HEAD_DIM, (h + 1) * HEAD_DIM)
        q, k, v = qkv_ref[0, :, lanes], qkv_ref[1, :, lanes], qkv_ref[2, :, lanes]
        g = grad[:, lanes]
        scores = jnp.where(same, inner_cols(k, q) * scale, MASKED)
        probs = jnp.exp(scores - lse_ref[0, h : h + 1, :])
        grad_probs = inner_cols(v, g)
        delta = jnp.sum(probs * grad_probs, axis=0, keepdims=True)
        grad_scores = (probs * (grad_probs - delta)).astype(BF)
        out_ref[0, :, lanes] = (inner_rows(grad_scores, k) * scale).astype(BF)
        out_ref[1, :, lanes] = (matmul(grad_scores, q) * scale).astype(BF)
        out_ref[2, :, lanes] = matmul(probs.astype(BF), g).astype(BF)
    sums_ref[0:1] = jnp.sum(out_ref[0].astype(F32), axis=0, keepdims=True)
    sums_ref[1:2] = jnp.sum(out_ref[2].astype(F32), axis=0, keepdims=True)
    per_block = blocks_ref.shape[2] // HEAD_DIM
    heads = blocks_ref.shape[0] * per_block // 3
    for step in range(heads // GROUP):

        @pl.when(pl.program_id(0) == step)
        def _(step=step):
            for part in range(3):
                for h in range(GROUP):
                    block, at = divmod(part * heads + step * GROUP + h, per_block)
                    blocks_ref[block, :, at * HEAD_DIM : (at + 1) * HEAD_DIM] = out_ref[
                        part, :, h * HEAD_DIM : (h + 1) * HEAD_DIM
                    ]


def attend_back(grad_branch, w_out, qkv, lse, segment, narrow):
    t, d = grad_branch.shape
    width = GROUP * HEAD_DIM
    return pl.pallas_call(
        attend_back_kernel,
        grid=(d // width,),
        in_specs=[
            pl.BlockSpec((t, d), lambda j: (0, 0)),
            pl.BlockSpec((width, d), lambda j: (j, 0)),
            pl.BlockSpec((3, t, width), lambda j: (0, 0, j)),
            pl.BlockSpec((1, GROUP, t), lambda j: (j, 0, 0)),
            pl.BlockSpec((1, t), lambda j: (0, 0)),
            pl.BlockSpec((t, 1), lambda j: (0, 0)),
        ],
        out_specs=[
            pl.BlockSpec((3, t, width), lambda j: (0, 0, j)),
            pl.BlockSpec((narrow, t, 3 * d // narrow), lambda j: (0, 0, 0)),
            pl.BlockSpec((2, width), lambda j: (0, j)),
        ],
        out_shape=[
            jax.ShapeDtypeStruct((3, t, d), BF),
            jax.ShapeDtypeStruct((narrow, t, 3 * d // narrow), BF),
            jax.ShapeDtypeStruct((2, d), F32),
        ],
        compiler_params=pltpu.CompilerParams(vmem_limit_bytes=VMEM),
        cost_estimate=cost(20),
    )(grad_branch, w_out, qkv, lse, segment.reshape(1, t), segment.reshape(t, 1))


def hidden_kernel(x_ref, w_ref, bias_ref, active_ref, slope_ref):
    pre = matmul(x_ref[...], w_ref[0]) + bias_ref[...]
    below = 0.5 + 0.5 * lax.erf(pre * 0.5**0.5)
    active_ref[...] = (pre * below).astype(BF)
    density = jnp.exp(-0.5 * pre * pre) * (2.0 * math.pi) ** (-0.5)
    slope_ref[...] = (below + pre * density).astype(BF)


def hidden_layer(x, w_in, in_bias):
    t, d = x.shape
    parts, _, width = w_in.shape
    block = pl.BlockSpec((t, width), lambda j: (0, j))
    shape = jax.ShapeDtypeStruct((t, parts * width), BF)
    return pl.pallas_call(
        hidden_kernel,
        grid=(parts,),
        in_specs=[
            pl.BlockSpec((t, d), lambda j: (0, 0)),
            pl.BlockSpec((1, d, width), lambda j: (j, 0, 0)),
            pl.BlockSpec((1, width), lambda j: (0, j)),
        ],
        out_specs=[block, block],
        out_shape=[shape, shape],
        compiler_params=pltpu.CompilerParams(vmem_limit_bytes=VMEM),
        cost_estimate=cost(8),
    )(x, w_in, in_bias)


def norm_parts(value):
    mean = jnp.mean(value, axis=-1, keepdims=True)
    centered = value - mean
    scale = lax.rsqrt(jnp.mean(centered * centered, axis=-1, keepdims=True) + EPSILON)
    return centered * scale, scale


def norm_back(grad, unit, scale, gain):
    e = grad * gain
    part = jnp.mean(e * unit, axis=-1, keepdims=True)
    return (e - jnp.mean(e, axis=-1, keepdims=True) - unit * part) * scale


def total(value):
    return jnp.sum(jnp.sum(value, axis=0, keepdims=True), axis=1, keepdims=True)


def column_sum(value):
    return jnp.sum(value, axis=0, keepdims=True)


def store_blocks(ref, value):
    count, _, width = ref.shape
    for i in range(count):
        ref[i] = value[:, i * width : (i + 1) * width]


def calls(kernel, outs, us, **kwargs):
    return pl.pallas_call(
        kernel,
        out_shape=[jax.ShapeDtypeStruct(shape, dtype) for shape, dtype in outs],
        compiler_params=pltpu.CompilerParams(vmem_limit_bytes=VMEM),
        cost_estimate=cost(us),
        **kwargs,
    )


def branch_kernel(ctx, w, x, rows, valid, normed, low, unit, scale, stats):
    branch = matmul(ctx[...], w[0]) + rows[2:3]
    residual = x[...].astype(F32) + branch
    unit[...], scale[...] = norm_parts(residual)
    normed[...] = unit[...] * rows[6:7] + rows[3:4]
    low[...] = normed[...].astype(BF)
    for i, value in enumerate((residual, branch)):
        stats[i : i + 1] = jnp.broadcast_to(total(valid[...] * value * value), (1, 128))


def branch_layer(context, w_out, inputs, rows, valid):
    t, d = inputs.shape
    outs = [((t, d), F32), ((t, d), BF), ((t, d), F32), ((t, 1), F32), ((2, 128), F32)]
    return calls(branch_kernel, outs, 5)(context, w_out, inputs, rows, valid)


def output_kernel(active, w, normed, rows, valid, hot, low, unit, scale, pooled, stats, acc):
    step = pl.program_id(0)
    product = matmul(active[...], w[...])

    @pl.when(step == 0)
    def _():
        acc[...] = product

    @pl.when(step > 0)
    def _():
        acc[...] += product

    @pl.when(step == pl.num_programs(0) - 1)
    def _():
        ffn_out = acc[...] + rows[4:5]
        residual = normed[...] + ffn_out
        unit[...], scale[...] = norm_parts(residual)
        low[...] = (unit[...] * rows[7:8] + rows[5:6]).astype(BF)
        pooled[...] = matmul(hot[...].astype(BF), low[...]).astype(BF)
        sums = (valid[...] * residual * residual, valid[...] * ffn_out * ffn_out, valid[...])
        for i, value in enumerate(sums):
            stats[i : i + 1] = jnp.broadcast_to(total(value), (1, 128))


def all_of(shape):
    return pl.BlockSpec(shape, lambda j: (0,) * len(shape))


def output_layer(active, w_back, normed, rows, valid, hot):
    t, ff = active.shape
    d = w_back.shape[1]
    steps = ff // d
    outs = [((t, d), BF), ((t, d), F32), ((t, 1), F32), ((hot.shape[0], d), BF), ((3, 128), F32)]
    return calls(
        output_kernel,
        outs,
        9,
        grid=(steps,),
        in_specs=[
            pl.BlockSpec((t, d), lambda j: (0, j)),
            pl.BlockSpec((d, d), lambda j: (j, 0)),
        ]
        + [all_of(a.shape) for a in (normed, rows, valid, hot)],
        out_specs=[all_of(shape) for shape, _ in outs],
        scratch_shapes=[pltpu.VMEM((t, d), F32)],
    )(active, w_back, normed, rows, valid, hot)


def output_back_kernel(cot, valid, hot, pool, unit, scale, rows, grad, low, blocks, sums):
    grad_out = cot[...].astype(F32) * valid[...] + lax.dot_general(
        hot[...],
        pool[...],
        (((0,), (0,)), ((), ())),
        precision=lax.Precision.HIGHEST,
        preferred_element_type=F32,
    )
    sums[0:1] = column_sum(grad_out * unit[...])
    sums[1:2] = column_sum(grad_out)
    grad[...] = norm_back(grad_out, unit[...], scale[...], rows[7:8])
    low[...] = grad[...].astype(BF)
    sums[2:3] = column_sum(low[...].astype(F32))
    store_blocks(blocks, low[...])


def output_back(cot, valid, hot, pool, unit, scale, rows, narrow):
    t, d = cot.shape
    outs = [((t, d), F32), ((t, d), BF), ((narrow, t, d // narrow), BF), ((3, d), F32)]
    return calls(output_back_kernel, outs, 6)(cot, valid, hot, pool, unit, scale, rows)


def hidden_back_kernel(
    low, w_back, slope, w_in, grad, unit, scale, rows, hidden, inb, residual, branch, blocks, sums, acc
):
    step = pl.program_id(0)
    hidden[...] = (inner_cols(low[...], w_back[...]) * slope[...].astype(F32)).astype(BF)
    inb[...] = column_sum(hidden[...].astype(F32))
    product = inner_cols(hidden[...], w_in[0])

    @pl.when(step == 0)
    def _():
        acc[...] = grad[...] + product

    @pl.when(step > 0)
    def _():
        acc[...] += product

    @pl.when(step == pl.num_programs(0) - 1)
    def _():
        value = acc[...]
        sums[0:1] = column_sum(value * unit[...])
        sums[1:2] = column_sum(value)
        residual[...] = norm_back(value, unit[...], scale[...], rows[6:7])
        branch[...] = residual[...].astype(BF)
        sums[2:3] = column_sum(branch[...].astype(F32))
        store_blocks(blocks, branch[...])


def hidden_back(low, w_back, slope, w_in, grad, unit, scale, rows, narrow):
    t, d = low.shape
    ff = slope.shape[1]
    tile = pl.BlockSpec((t, d), lambda j: (0, j))
    outs = [
        ((t, ff), BF),
        ((1, ff), F32),
        ((t, d), F32),
        ((t, d), BF),
        ((narrow, t, d // narrow), BF),
        ((3, d), F32),
    ]
    return calls(
        hidden_back_kernel,
        outs,
        14,
        grid=(ff // d,),
        in_specs=[
            all_of(low.shape),
            pl.BlockSpec((d, d), lambda j: (j, 0)),
            tile,
            pl.BlockSpec((1, d, d), lambda j: (j, 0, 0)),
        ]
        + [all_of(a.shape) for a in (grad, unit, scale, rows)],
        out_specs=[tile, pl.BlockSpec((1, d), lambda j: (0, j))]
        + [all_of(shape) for shape, _ in outs[2:]],
        scratch_shapes=[pltpu.VMEM((t, d), F32)],
    )(low, w_back, slope, w_in, grad, unit, scale, rows)


def input_back_kernel(grad, w, residual, out, acc):
    step = pl.program_id(0)
    product = inner_cols(grad[0], w[0])

    @pl.when(step == 0)
    def _():
        acc[...] = residual[...] + product

    @pl.when(step == 1)
    def _():
        acc[...] += product

    @pl.when(step == 2)
    def _():
        out[...] = (acc[...] + product).astype(BF)


def input_back(grad_qkv, w_qkv, residual):
    _, t, d = grad_qkv.shape
    return calls(
        input_back_kernel,
        [((t, d), BF)],
        6,
        grid=(3,),
        in_specs=[
            pl.BlockSpec((1, t, d), lambda j: (j, 0, 0)),
            pl.BlockSpec((1, d, d), lambda j: (j, 0, 0)),
            all_of((t, d)),
        ],
        out_specs=[all_of((t, d))],
        scratch_shapes=[pltpu.VMEM((t, d), F32)],
    )(grad_qkv, w_qkv, residual)[0]


def spread_masks(count, width):
    total_cols = count * width
    column = lax.broadcasted_iota(jnp.int32, (count, total_cols), 1)
    first = lax.broadcasted_iota(jnp.int32, (count, total_cols), 0) * width
    own = (column >= first) & (column < first + width)
    owner = jnp.sum(jnp.where(own, first, 0), axis=0, keepdims=True)
    within = lax.broadcasted_iota(jnp.int32, (width, total_cols), 1) - owner
    spread = within == lax.broadcasted_iota(jnp.int32, (width, total_cols), 0)
    return own, spread.astype(F32)


def unpack_kernel(small, rows, inb):
    count = small.shape[0]
    width = rows.shape[1] // count
    value = small[...].astype(F32)

    def unpack(part, own, spread):
        placed = matmul(part.astype(BF), spread.astype(BF))
        return column_sum(jnp.where(own, placed, 0.0))

    masks = spread_masks(count, width)
    for r in range(8):
        rows[r : r + 1] = unpack(value[:, r * width : (r + 1) * width], *masks)
    masks = spread_masks(count, inb.shape[1] // count)
    inb[...] = unpack(value[:, 8 * width : 8 * width + inb.shape[1] // count], *masks)


def unpack_params(small, d, ff):
    return calls(unpack_kernel, [((8, d), F32), ((1, ff), F32)], 2)(small)


def pack_kernel(attn, out, ffn, inb, stats_a, stats_b, packed):
    count = packed.shape[0]
    width = out.shape[1] // count
    vectors = (
        attn[0:1], attn[1:2], out[2:3], out[1:2], ffn[2:3], ffn[1:2], out[0:1], ffn[0:1], inb[...]
    )
    packed[...] = jnp.zeros(packed.shape, F32)
    at = 0
    for i, vector in enumerate(vectors):
        if i in (0, 8):
            width = vector.shape[1] // count
            own, spread = spread_masks(count, width)
        packed[:, at : at + width] = lax.dot_general(
            jnp.where(own, vector, 0.0),
            spread,
            (((1,), (1,)), ((), ())),
            precision=lax.Precision.HIGHEST,
            preferred_element_type=F32,
        )
        at += width
    for i, row in enumerate((stats_a[0:1], stats_a[1:2], stats_b[0:1], stats_b[1:2], stats_b[2:3])):
        packed[:, at + i : at + i + 1] = jnp.broadcast_to(row[:, :1], (count, 1))


def pack_sums(count, attn, out, ffn, inb, stats_a, stats_b):
    return calls(pack_kernel, [((count, 384), F32)], 4)(attn, out, ffn, inb, stats_a, stats_b)[0]


def match_grads(rows, label_rows, label_cols):
    is_query, is_pass = label_rows >= 0, label_cols >= 0
    match = jnp.where(is_pass, inner_cols(rows, rows) / SCORE_DIV, MASKED)
    shifted = jnp.exp(match - jnp.max(match, axis=1, keepdims=True))
    probs = shifted / jnp.sum(shifted, axis=1, keepdims=True)
    hot = (label_rows == label_cols).astype(F32)
    grad = jnp.where(is_query & is_pass, (probs - hot) / SCORE_DIV, 0.0).astype(BF)
    return matmul(grad[:POOL], rows) + inner_rows(grad[:, :POOL], rows)


def match_kernel(rows, label_rows, label_cols, out):
    out[...] = match_grads(rows[...], label_rows[...], label_cols[...])


def row_of(z, y, n, s):
    own = (z * s + y) * 3 + n
    spare = y * 3 + (z - 1)
    return jnp.where(z == 0, n * s + y, jnp.where(n < 3, own, spare))


def body(
    passages,
    queries,
    passage_cot,
    query_cot,
    passage_lengths,
    query_lengths,
    labels,
    w_qkv,
    w_out,
    w_in,
    w_back,
    biases,
    norm_gains,
    in_bias,
):
    place = Place()
    s, narrow, devices = place.stride, place.narrow, place.wide * place.narrow
    model_width = passages.shape[2]
    length = passages.shape[1] * narrow
    segs, qsegs = passage_lengths.shape[1] - 1, query_lengths.shape[1] - 1
    on_query = place.z == 0

    piece = model_width // devices
    small = jnp.concatenate(
        [biases.reshape(2, -1), norm_gains.reshape(2, -1), in_bias.reshape(2, -1)], axis=1
    )
    whole = jnp.concatenate(
        [passage_lengths.reshape(-1), query_lengths.reshape(-1), labels.reshape(-1)]
    )
    whole = jnp.concatenate([whole // 32, whole % 32]).astype(BF)
    small_count = small.shape[1]
    to_query = (jnp.arange(devices) < s * narrow)[:, None]
    small = jnp.where(to_query, small[1][None], small[0][None])
    small = jnp.concatenate([small, jnp.broadcast_to(whole, (devices, whole.shape[0]))], axis=1)

    in_parts = w_in.shape[2] // w_out.shape[2]
    levels_qkv = gather_levels(place, w_qkv)
    swapped = swap_in_directly(place, passages, queries)
    out_in = jnp.concatenate([w_out, w_in], axis=2)
    levels_qkv, swapped, out_in, small = phase(levels_qkv, swapped, out_in, small)

    pieces_qkv, plan = gather_columns(place, levels_qkv)
    inputs = to_row(place, passages, queries, swapped)
    levels_out_in = gather_levels(place, out_in)
    pieces_qkv, inputs, levels_out_in = phase(pieces_qkv, inputs, levels_out_in)

    cores_qkv, core_plan = gather_cores(pieces_qkv, plan)
    cores_qkv, levels_out_in, w_back, small = phase(cores_qkv, levels_out_in, w_back, small)

    pieces_out_in, _ = gather_columns(place, levels_out_in)
    levels_back = gather_levels(place, w_back)
    (w_qkv_all,) = assemble(place, cores_qkv, core_plan, (3,))
    small = lax.all_to_all(small, BOTH, 0, 0, tiled=True)

    n_bias, n_gain = biases.shape[1], norm_gains.shape[1]
    ff = in_bias.shape[1] * devices
    if s == 2:
        rows, inb_row = unpack_params(small, model_width, ff)
    else:
        params = small[:, :small_count].astype(F32)
        vectors = params[:, : (n_bias + n_gain) * piece].reshape(devices, n_bias + n_gain, piece)
        rows = vectors.transpose(1, 0, 2).reshape(n_bias + n_gain, -1)
        inb_row = params[:, (n_bias + n_gain) * piece :].reshape(1, -1)
    ints = small[:, small_count : small_count + whole.shape[0]].astype(F32)
    half = ints.shape[1] // 2
    ints = (ints[::narrow, :half] * 32 + ints[::narrow, half:]).astype(jnp.int32)
    n_pass = passage_lengths.size
    n_query = query_lengths.size
    pass_lens = ints[:, :n_pass].reshape(-1, segs + 1)
    query_lens = ints[:, n_pass : n_pass + n_query].reshape(-1, qsegs + 1)
    label_all = ints[:, n_pass + n_query :].reshape(-1, qsegs)
    my_row = row_of(place.z, place.y, place.n, s)
    pass_row = pick(pass_lens, jnp.where(on_query, 0, my_row), 0)
    query_row = pick(query_lens, jnp.where(on_query, my_row, 0), 0)
    ends_p = jnp.cumsum(pass_row)[:-1]
    ends_q = jnp.cumsum(query_row)[:-1]
    starts_p, starts_q = ends_p - pass_row[:-1], ends_q - query_row[:-1]
    ends_p = jnp.concatenate([ends_p, jnp.full((qsegs - segs,), length + 1, jnp.int32)])
    ends = jnp.where(on_query, ends_q, ends_p)
    seg_count = jnp.where(on_query, qsegs, segs)
    position = jnp.arange(length, dtype=jnp.int32)
    segment = jnp.sum((position[:, None] >= ends[None, :]).astype(jnp.int32), axis=1)
    valid = (segment < seg_count).astype(F32)[:, None]
    slot = jnp.arange(POOL)
    starts = jnp.where(on_query, jnp.concatenate([starts_q, jnp.full((qsegs,), -1)]), -1)
    for z in range(1, LEVELS):
        here = (place.z == z) & (slot >= qsegs + segs * (z - 1)) & (slot < qsegs + segs * z)
        starts = jnp.where(here, jnp.tile(starts_p, POOL // segs), starts)
    hot = (starts[:, None] == position[None, :]).astype(F32)
    masks = [0]
    if s == 2:
        masks += [dy * narrow + 2 * dx for dx, dy in OTHERS]
        masks += [m ^ 1 for m in masks]
    else:
        for mask in [b * narrow for b in bits_of(s)] + [b for b in reversed(bits_of(narrow))]:
            masks = masks + [m ^ mask for m in masks]
    there = (place.y * narrow + place.n) ^ jnp.array(masks, jnp.int32)
    their_y, their_n = there // narrow, there % narrow
    label_rows = label_all[row_of(jnp.int32(0), their_y, their_n, s)]
    label_rows = jnp.pad(label_rows, ((0, 0), (0, POOL - qsegs)), constant_values=-1)
    levels = jnp.arange(1, LEVELS)
    pass_rows = row_of(levels[None, :], their_y[:, None], their_n[:, None], s)
    pass_ids = (pass_rows[:, :, None] * segs + jnp.arange(segs)).reshape(len(masks), -1)
    spare = POOL - qsegs - pass_ids.shape[1]
    label_cols = jnp.pad(pass_ids, ((0, 0), (qsegs, spare)), constant_values=-1)
    label_rows, label_cols = label_rows.reshape(-1, 1), label_cols.reshape(1, -1)

    qkv, context, log_sum = attend(inputs, w_qkv_all, rows, segment)
    tables = (rows, inb_row, segment, valid, hot, label_rows, label_cols)
    context, pieces_out_in, levels_back, cots, tables = phase(
        context, pieces_out_in, levels_back, (passage_cot, query_cot), tables
    )
    rows, inb_row, segment, valid, hot, label_rows, label_cols = tables

    cores_out_in, _ = gather_cores(pieces_out_in, plan)
    cores_out_in, levels_back, cots = phase(cores_out_in, levels_back, cots)

    pieces_back, _ = gather_columns(place, levels_back)
    swapped = swap_in(place, *cots)
    w_out_all, w_in_all = assemble(place, cores_out_in, core_plan, (1, in_parts))
    normed, normed_low, unit_one, scale_one, stats_one = branch_layer(
        context, w_out_all, inputs, rows, valid
    )
    active, slope = hidden_layer(normed_low, w_in_all, inb_row)
    active, pieces_back, swapped = phase(active, pieces_back, swapped)

    cores_back, _ = gather_cores(pieces_back, plan)
    cot = to_row(place, passage_cot, query_cot, swapped)
    w_back_all = assemble(place, cores_back, core_plan, (1,))[0][0]
    output_low, unit_two, scale_two, pooled, stats_two = output_layer(
        active, w_back_all, normed, rows, valid, hot
    )
    pooled, cot = phase(pooled, cot)

    column = sum([flip(pooled, "wide", k * s).astype(F32) for k in (3, 2, 1)], pooled.astype(F32))
    seen = column.astype(BF)[None]
    if s == 2:
        seen = jnp.concatenate([seen] + [flip_both(seen, dy, 2 * dx) for dx, dy in OTHERS])
        seen = jnp.concatenate([seen, flip(seen, "narrow", 1)])
    else:
        for axis, step in [("wide", b) for b in bits_of(s)] + [
            ("narrow", b) for b in reversed(bits_of(narrow))
        ]:
            seen = jnp.concatenate([seen, flip(seen, axis, step)])
    seen = seen.reshape(-1, model_width)
    if s == 2:
        (grad_pool,) = calls(match_kernel, [((POOL, model_width), F32)], 3)(
            seen, label_rows, label_cols
        )
    else:
        grad_pool = match_grads(seen, label_rows, label_cols)

    grad_resid_two, grad_ffn, blocks_c, sums_two = output_back(
        cot, valid, hot, grad_pool, unit_two, scale_two, rows, narrow
    )
    if s == 2:
        send_c, keep_c = products_back(place, active, blocks_c)
        send_c, output_low = phase(send_c, output_low)
        got_c = flip(send_c, "narrow", 1)
        out_four = row_pieces(place, output_low)
        shares_c = column_shares(place, keep_c, got_c)
        shares_c, grad_ffn = phase(shares_c, grad_ffn)

        columns_c = send_columns(shares_c)
    grad_hidden, inb_sums, grad_residual, grad_branch, blocks_b, sums_one = hidden_back(
        grad_ffn, w_back_all, slope, w_in_all, grad_resid_two, unit_one, scale_one, rows, narrow
    )
    if s == 2:
        send_b, keep_b = products_out_in(place, context, blocks_b, normed_low, grad_hidden)
        send_b, columns_c, out_four = phase(send_b, columns_c, out_four)

        got_b = flip(send_b, "narrow", 1)
        level_c = level_shares(place, columns_c)
        shares_b = column_shares(place, keep_b, got_b)
        shares_b, level_c, grad_branch, out_four = phase(shares_b, level_c, grad_branch, out_four)

        columns_b = send_columns(shares_b)
        levels_c = swap_shares(place, level_c)
        swapped = swap_out(place, out_four)
    grad_qkv, blocks_a, sums_qkv = attend_back(
        grad_branch, w_out_all[0], qkv, log_sum, segment, narrow
    )
    if s == 2:
        send_a, keep_a = products_qkv(place, inputs, blocks_a)
        send_a, grad_qkv, columns_b, levels_c, swapped = phase(
            send_a, grad_qkv, columns_b, levels_c, swapped
        )
        passage_out, query_out = from_row(place, out_four, swapped)

        got_a = flip(send_a, "narrow", 1)
        level_b = level_shares(place, columns_b)
    input_grad = input_back(grad_qkv, w_qkv_all, grad_residual)
    packed = pack_sums(devices, sums_qkv, sums_one, sums_two, inb_sums, stats_one, stats_two)
    if s == 2:
        shares_a = column_shares(place, keep_a, got_a)
        shares_a, level_b, input_grad = phase(shares_a, level_b, input_grad)

        columns_a = send_columns(shares_a)
        levels_b = swap_shares(place, level_b)
        in_four = row_pieces(place, input_grad)
        grad_w_back = finish_back(place, levels_c)
        columns_a, levels_b, in_four, packed = phase(columns_a, levels_b, in_four, packed)

        levels_a = swap_shares(place, level_shares(place, columns_a))
        swapped = swap_out(place, in_four)
        packed = lax.all_to_all(packed, BOTH, 0, 0, tiled=True)
        grad_w_out, grad_w_in = finish_out_in(place, levels_b, model_width // place.wide)
        grad_w_qkv = finish_qkv(place, levels_a)
        passage_grad, query_grad = from_row(place, in_four, swapped)
    else:
        packed = lax.all_to_all(packed, BOTH, 0, 0, tiled=True)
        grad_w_back = scatter_tower(place, grad_blocks(active, grad_ffn, narrow))
        grad_w_out = scatter_tower(place, grad_blocks(context, grad_branch, narrow))
        grad_w_in = scatter_tower(place, grad_blocks(normed_low, grad_hidden, narrow))
        flat = jnp.moveaxis(grad_qkv, 0, 1).reshape(length, -1)
        grad_w_qkv = scatter_tower(place, grad_blocks(inputs, flat, narrow))
        out_four, in_four = row_pieces(place, output_low), row_pieces(place, input_grad)
        passage_out, query_out = from_row(place, out_four, swap_out(place, out_four))
        passage_grad, query_grad = from_row(place, in_four, swap_out(place, in_four))

    packed = packed.reshape(LEVELS, -1, packed.shape[1]).sum(axis=1)
    packed = jnp.stack([packed[1] + packed[2] + packed[3], packed[0]])
    edges = [n_bias * piece, (n_bias + n_gain) * piece]
    edges.append(edges[1] + in_bias.shape[1])
    grad_biases = packed[:, : edges[0]].reshape(2, n_bias, piece)
    grad_gains = packed[:, edges[0] : edges[1]].reshape(2, n_gain, piece)
    grad_inb = packed[:, edges[1] : edges[2]]
    totals = packed[:, edges[2] : edges[2] + 5]
    rms_stats = jnp.sqrt(totals[:, :4] / (totals[:, 4:] * model_width))
    return (
        passage_out,
        query_out,
        passage_grad,
        query_grad,
        grad_w_qkv,
        grad_w_out,
        grad_w_in,
        grad_w_back,
        grad_biases,
        grad_gains,
        grad_inb,
        rms_stats,
    )


def solution(mesh):
    return jax.shard_map(
        body,
        mesh=mesh,
        in_specs=(
            P("wide", "narrow", None),
            P("wide", "narrow", None),
            P("wide", "narrow", None),
            P("wide", "narrow", None),
            P("wide", None),
            P("wide", None),
            P("wide"),
            P(None, ("wide", "narrow"), None),
            P(None, ("wide", "narrow"), None),
            P(None, ("wide", "narrow"), None),
            P(None, ("wide", "narrow"), None),
            P(None, None, ("wide", "narrow")),
            P(None, None, ("wide", "narrow")),
            P(None, ("wide", "narrow")),
        ),
        out_specs=(
            P("wide", "narrow", None),
            P("wide", "narrow", None),
            P("wide", "narrow", None),
            P("wide", "narrow", None),
            P(None, "wide", "narrow"),
            P(None, "wide", "narrow"),
            P(None, "wide", "narrow"),
            P(None, "wide", "narrow"),
            P(None, None, ("wide", "narrow")),
            P(None, None, ("wide", "narrow")),
            P(None, ("wide", "narrow")),
            P(),
        ),
        check_vma=False,
    )
```

```python
import functools
import math

import jax
import jax.numpy as jnp
from jax import lax
from jax.experimental import pallas as pl
from jax.experimental.pallas import tpu as pltpu
from jax.sharding import PartitionSpec as P

HEAD_DIM = 64
LEVELS = 4
GROUP = 4
POOL = 32
VMEM = 58 << 20
OTHERS = ((1, 1), (1, 0), (0, 1))


def cost(us):
    return pl.CostEstimate(flops=int(us * 1.15e9), bytes_accessed=1024, transcendentals=0)


EPSILON = 1e-05
SCORE_DIV = 12.0
MASKED = -1e30
BF = jnp.bfloat16
F32 = jnp.float32
BOTH = ("wide", "narrow")


def matmul(left, right):
    return jnp.dot(left, right, preferred_element_type=F32)


def inner_rows(left, right):
    return lax.dot_general(left, right, (((0,), (0,)), ((), ())), preferred_element_type=F32)


def inner_cols(left, right):
    return lax.dot_general(left, right, (((1,), (1,)), ((), ())), preferred_element_type=F32)


def flip(x, axis, mask):
    size = lax.axis_size(axis)
    return lax.ppermute(x, axis, [(i, i ^ mask) for i in range(size)])


def flip_both(x, wide_mask, narrow_mask):
    wide, narrow = lax.axis_size("wide"), lax.axis_size("narrow")
    mask = wide_mask * narrow + narrow_mask
    return lax.ppermute(x, BOTH, [(i, i ^ mask) for i in range(wide * narrow)])


def phase(*values):
    return lax.optimization_barrier(values)


def across_levels(x, stride):
    groups = [[k * stride + i for k in range(LEVELS)] for i in range(stride)]
    return lax.all_to_all(x, "wide", 0, 0, axis_index_groups=groups, tiled=True)


def swap_levels(x, k, stride):
    pairs = []
    for i in range(stride):
        pairs += [(i, k * stride + i), (k * stride + i, i)]
    return lax.ppermute(x, "wide", pairs)


def bits_of(size):
    return [1 << b for b in range(size.bit_length() - 1)]


class Place:
    def __init__(self):
        self.wide = lax.axis_size("wide")
        self.narrow = lax.axis_size("narrow")
        self.stride = self.wide // LEVELS
        self.w = lax.axis_index("wide")
        self.n = lax.axis_index("narrow")
        self.z = self.w // self.stride
        self.y = self.w % self.stride
        self.me = self.w * self.narrow + self.n


def swap_in(place, pass_part, query_part):
    query = jnp.broadcast_to(query_part, (LEVELS, *query_part.shape[1:]))
    first = jnp.concatenate([query_part, pass_part])
    return across_levels(jnp.where(place.z == 0, first, query), place.stride)


def swap_in_directly(place, pass_part, query_part):
    return [
        swap_levels(jnp.where(place.z == 0, pass_part[k - 1], query_part[0]), k, place.stride)
        for k in range(1, LEVELS)
    ]


def join_swapped(place, query_part, got):
    first = jnp.where(place.z == 0, query_part[0], got[0] + got[1] + got[2])
    return jnp.stack([first] + got)


def to_row(place, pass_part, query_part, got):
    four = jnp.where(place.z == 0, got, jnp.concatenate([pass_part, got[:1]]))
    mine = lax.all_to_all(four, "narrow", 0, 0, tiled=True)
    return mine.reshape(-1, mine.shape[-1])


def row_pieces(place, row):
    return lax.all_to_all(
        row.reshape(place.narrow, -1, row.shape[-1]), "narrow", 0, 0, tiled=True
    )


def swap_out(place, four):
    last = jnp.broadcast_to(four[3:], four.shape)
    return across_levels(jnp.where(place.z == 0, four, last), place.stride)


def from_row(place, four, got):
    pass_part = jnp.where(place.z == 0, got[1:], four[:3])
    query_part = jnp.where(place.z == 0, four[:1], got[:1])
    return pass_part, query_part


def toggle(places, mask):
    return [(p[0], p[1] ^ mask) if isinstance(p, tuple) else p ^ mask for p in places]


def block_of(me, place, level):
    if isinstance(place, tuple):
        return ((me & (level - 1)) ^ place[1]) + place[0] * level
    return me ^ place


def assemble_kernel(plan, layout, level, me_ref, *refs):
    pieces, outs, sems = refs[: len(plan)], refs[len(plan) : -1], refs[-1]
    me = me_ref[0]
    copies = []
    for piece, masks in zip(pieces, plan):
        for slot, mask in enumerate(masks):
            for out, part, row, column in layout:
                target = outs[out].at[part, block_of(me, mask, level)]
                rows, columns = outs[out].shape[2:]
                source = piece.at[slot, pl.ds(row, rows), pl.ds(column, columns)]
                copies.append(pltpu.make_async_copy(source, target, sems.at[len(copies)]))
    for copy in copies:
        copy.start()
    for copy in copies:
        copy.wait()


def assemble(place, pieces, plan, layout, outs):
    total = place.wide * place.narrow
    made = pl.pallas_call(
        functools.partial(assemble_kernel, plan, layout, total // LEVELS),
        out_shape=[jax.ShapeDtypeStruct((out[0], total, *out[1:]), BF) for out in outs],
        in_specs=[pl.BlockSpec(memory_space=pltpu.SMEM)]
        + [pl.BlockSpec(memory_space=pl.ANY)] * len(pieces),
        out_specs=[pl.BlockSpec(memory_space=pltpu.VMEM)] * len(outs),
        scratch_shapes=[pltpu.SemaphoreType.DMA((total * len(layout),))],
        cost_estimate=cost(0.1),
        compiler_params=pltpu.CompilerParams(vmem_limit_bytes=VMEM),
    )(place.me.reshape(1), *pieces)
    return [out.reshape(out.shape[0], -1, out.shape[3]) for out in made]


def pick_kernel(z_ref, w_ref, bias_ref, gain_ref, inb_ref, ints_ref, *refs):
    outs, small = refs[:-1], refs[-1]
    rows, width = w_ref.shape[1], small.shape[1]
    n_bias, n_gain = bias_ref.shape[1], gain_ref.shape[1]
    for k, out in enumerate(outs):
        tower = jnp.where(z_ref[0] == k, 1, 0)
        for part in range(3):
            out[part * rows : (part + 1) * rows] = w_ref[tower, :, part * width : (part + 1) * width]
        small[...] = jnp.zeros(small.shape, F32)
        small[:n_bias, : bias_ref.shape[2]] = bias_ref[tower].astype(F32)
        small[n_bias : n_bias + n_gain, : gain_ref.shape[2]] = gain_ref[tower].astype(F32)
        small[:1, 128 : 128 + inb_ref.shape[2]] = inb_ref[tower].astype(F32)
        small[:1, 256 : 256 + ints_ref.shape[1]] = ints_ref[...].astype(F32)
        out[3 * rows :] = small[...].astype(BF)


def pick_towers(place, w_qkv, biases, norm_gains, in_bias, ints):
    width = w_qkv.shape[2] // 3
    vmem = pl.BlockSpec(memory_space=pltpu.VMEM)
    return calls(
        pick_kernel,
        [((3 * w_qkv.shape[1] + 8, width), BF)] * LEVELS,
        2,
        in_specs=[pl.BlockSpec(memory_space=pltpu.SMEM)] + [vmem] * 5,
        scratch_shapes=[pltpu.VMEM((8, width), F32)],
    )(place.z.reshape(1), w_qkv, biases, norm_gains, in_bias[:, None], ints[None])


def gather_levels(place, pair):
    first = lax.broadcasted_iota(jnp.int32, (LEVELS, 1, 1), 0) == 0
    return across_levels(jnp.where(first, pair[1:], pair[:1]), place.stride)


def gather_columns(place, levels, own=None):
    s, narrow = place.stride, place.narrow
    if own is None:
        own = [(level, 0) for level in range(LEVELS)]
    pieces, plan = [levels], [own]
    if s == 2:
        for dx, dy in OTHERS:
            pieces.append(flip_both(levels, dy, 2 * dx))
            plan.append(toggle(own, dy * narrow + 2 * dx))
    else:
        for b in bits_of(s):
            for i in range(len(pieces)):
                pieces.append(flip(pieces[i], "wide", b))
                plan.append(toggle(plan[i], b * narrow))
        for i in range(len(pieces)):
            pieces.append(flip(pieces[i], "narrow", 2))
            plan.append(toggle(plan[i], 2))
    return pieces, plan


def gather_cores(pieces, plan):
    others = [flip(piece, "narrow", 1) for piece in pieces]
    return list(pieces) + others, plan + [toggle(places, 1) for places in plan]


def pick(x, index, dim):
    return lax.dynamic_index_in_dim(x, index, dim, keepdims=False)


def halve(x, place, axis, mask, dim):
    index = place.n if axis == "narrow" else place.w
    bit = jnp.where((index & mask) != 0, 1, 0)
    got = flip(pick(x, 1 - bit, dim).astype(BF), axis, mask)
    return pick(x, bit, dim) + got.astype(F32)


def scatter_tower(place, partial):
    s = place.stride
    rows, narrow, cols = partial.shape
    per = rows // place.wide
    x = partial.reshape(rows, 2, 2, cols)
    x = halve(x, place, "narrow", 1, 2)
    x = x.reshape(LEVELS, s, per, 2, cols)
    first, second = x[:2], x[2:]

    def over_columns(part):
        for b in reversed(bits_of(s)):
            shape = part.shape
            part = part.reshape(shape[0], 2, shape[1] // 2, *shape[2:])
            part = halve(part, place, "wide", b, 1)
        return part[:, 0]

    first = over_columns(halve(first, place, "narrow", 2, 3))
    second = halve(over_columns(second), place, "narrow", 2, 2)
    return jnp.stack(sum_levels(place, send_levels(place, jnp.concatenate([first, second]))))


def send_levels(place, levels):
    slots = [None] * LEVELS
    slots[0] = pick(levels, place.z, 0)
    for k in (3, 2, 1):
        slots[k] = flip(pick(levels, place.z ^ k, 0).astype(BF), "wide", k * place.stride)
    return slots


def sum_levels(place, slots):
    tower0 = sum(jnp.where(place.z == k, 0.0, slots[k].astype(F32)) for k in range(LEVELS))
    tower1 = sum(jnp.where(place.z == k, slots[k].astype(F32), 0.0) for k in range(LEVELS))
    return tower0, tower1


def share_kernel(at_ref, keep_ref, got_ref, own_ref, *sent_refs):
    x, y = at_ref[0], at_ref[1]

    def share(dx, dy):
        at = (x ^ dx, 0, y ^ dy)
        return keep_ref[at].astype(F32) + got_ref[at].astype(F32)

    own_ref[0] = share(0, 0)
    for ref, (dx, dy) in zip(sent_refs, OTHERS):
        ref[0] = share(dx, dy).astype(BF)


def column_shares(place, keep, got):
    r, c = got.shape[2:]
    block = pl.BlockSpec((2, 1, place.stride, r, c), lambda i, at: (0, i, 0, 0, 0))
    out = pl.BlockSpec((1, r, c), lambda i, at: (i, 0, 0))
    shape = (2, LEVELS, place.stride, r, c)
    return pl.pallas_call(
        share_kernel,
        grid_spec=pltpu.PrefetchScalarGridSpec(
            num_scalar_prefetch=1, grid=(LEVELS,), in_specs=[block] * 2, out_specs=[out] * 4
        ),
        out_shape=[jax.ShapeDtypeStruct((LEVELS, r, c), F32)]
        + [jax.ShapeDtypeStruct((LEVELS, r, c), BF)] * 3,
        compiler_params=pltpu.CompilerParams(vmem_limit_bytes=VMEM),
        cost_estimate=cost(1),
    )(jnp.stack([place.n // 2, place.y]), keep.reshape(shape), got.reshape(shape))


def send_columns(shares):
    return [shares[0]] + [
        flip_both(sent, dy, 2 * dx) for sent, (dx, dy) in zip(shares[1:], OTHERS)
    ]


def level_kernel(z_ref, own_ref, *refs):
    got_refs, (sum_ref, *sent_refs) = refs[:3], refs[3:]
    for k in range(LEVELS):
        at = z_ref[0] ^ k
        total = own_ref[at]
        for ref in got_refs:
            total = total + ref[at].astype(F32)
        if k == 0:
            sum_ref[...] = total
        else:
            sent_refs[k - 1][...] = total.astype(BF)


def level_shares(place, columns):
    r, c = columns[0].shape[1:]
    vmem = pl.BlockSpec(memory_space=pltpu.VMEM)
    return pl.pallas_call(
        level_kernel,
        in_specs=[pl.BlockSpec(memory_space=pltpu.SMEM)] + [vmem] * 4,
        out_specs=[vmem] * 4,
        out_shape=[jax.ShapeDtypeStruct((r, c), F32)] + [jax.ShapeDtypeStruct((r, c), BF)] * 3,
        compiler_params=pltpu.CompilerParams(vmem_limit_bytes=VMEM),
        cost_estimate=cost(1),
    )(place.z.reshape(1), *columns)


def level_sums_kernel(*refs):
    for at in range(LEVELS):
        refs[-1][at] = sum(ref[at].astype(F32) for ref in refs[:-1]).astype(BF)


def level_sums(columns):
    shape = columns[0].shape
    return calls(level_sums_kernel, [(shape, BF)], 3)(*columns)[0]


def swap_shares(place, shares):
    slots = [shares[0], None, None, None]
    for k in (3, 2, 1):
        slots[k] = flip(shares[k], "wide", k * place.stride)
    return slots


def product_kernel(step, me_ref, *refs):
    send_ref, keep_ref = refs[-2:]
    left_refs = refs[:-2]
    to_send = pl.program_id(0) < 2

    @pl.when(to_send)
    def _():
        step(left_refs, lambda at, v: send_ref.__setitem__((0, *at), v.astype(BF)))

    @pl.when(jnp.logical_not(to_send))
    def _():
        step(left_refs, lambda at, v: keep_ref.__setitem__((0, *at), v.astype(BF)))


def products(place, step, operands, specs, block):
    def target(j, me):
        return (j % 2) * 2 + jnp.where(j < 2, 1 - me[0] % 2, me[0] % 2)

    wide = place.wide
    grid_spec = pltpu.PrefetchScalarGridSpec(
        num_scalar_prefetch=1,
        grid=(4,),
        in_specs=specs(target),
        out_specs=[
            pl.BlockSpec((1, wide, *block), lambda j, me: (jnp.minimum(j, 1), 0, 0, 0)),
            pl.BlockSpec((1, wide, *block), lambda j, me: (jnp.maximum(j - 2, 0), 0, 0, 0)),
        ],
    )
    return pl.pallas_call(
        functools.partial(product_kernel, step),
        grid_spec=grid_spec,
        out_shape=[
            jax.ShapeDtypeStruct((2, wide, *block), BF),
            jax.ShapeDtypeStruct((2, wide, *block), BF),
        ],
        compiler_params=pltpu.CompilerParams(vmem_limit_bytes=VMEM),
        cost_estimate=cost(8),
    )(place.n.reshape(1), *operands)


def whole(shape):
    return pl.BlockSpec(shape, lambda j, me: (0,) * len(shape))


def grad_blocks(left, right, narrow):
    out = inner_rows(left, right)
    return out.reshape(out.shape[0], narrow, -1)


def products_back_kernel(core_ref, left_ref, right_ref, send_ref, keep_ref, turned_ref):
    @pl.when(pl.program_id(0) == 0)
    def _():
        turned_ref[...] = right_ref[...].T

    value = matmul(turned_ref[...], left_ref[...]).astype(BF)
    cols = send_ref.shape[2]
    first = core_ref[0] == 0
    for x in range(2):
        even = value[2 * x * cols : (2 * x + 1) * cols]
        odd = value[(2 * x + 1) * cols : (2 * x + 2) * cols]
        keep_ref[x, 0] = jnp.where(first, even, odd)
        send_ref[x, 0] = jnp.where(first, odd, even)


def products_back(place, active, grad_ffn):
    t, ff = active.shape
    d = grad_ffn.shape[1]
    cols, rows = d // place.narrow, ff // place.wide
    out = pl.BlockSpec((2, 1, cols, rows), lambda j, core: (0, j, 0, 0))
    return pl.pallas_call(
        products_back_kernel,
        grid_spec=pltpu.PrefetchScalarGridSpec(
            num_scalar_prefetch=1,
            grid=(place.wide,),
            in_specs=[pl.BlockSpec((t, rows), lambda j, core: (0, j)), whole((t, d))],
            out_specs=[out, out],
            scratch_shapes=[pltpu.VMEM((d, t), BF)],
        ),
        out_shape=[jax.ShapeDtypeStruct((2, place.wide, cols, rows), BF)] * 2,
        compiler_params=pltpu.CompilerParams(vmem_limit_bytes=VMEM),
        cost_estimate=cost(7),
    )((place.n % 2).reshape(1), active, grad_ffn)


def finish_back(levels):
    levels = levels.astype(F32)
    return jnp.stack([(levels[1] + levels[2] + levels[3]).T, levels[0].T])


def products_out_in(place, context, blocks, normed, grad_hidden):
    narrow = place.narrow
    t, d = context.shape
    rows = d // place.wide
    cols_out, cols_in = blocks.shape[2], grad_hidden.shape[1] // narrow
    fold = cols_in // cols_out
    low = rows // fold

    def step(refs, store):
        context_ref, branch_ref, normed_ref, hidden_ref = refs
        value = inner_rows(normed_ref[...], hidden_ref[...])
        for w in range(place.wide):
            store((w, slice(0, rows)), value[w * rows : (w + 1) * rows])
        value = inner_rows(context_ref[...], branch_ref[0])
        for w in range(place.wide):
            for g in range(fold):
                store(
                    (w, slice(rows, rows + low), slice(g * cols_out, (g + 1) * cols_out)),
                    value[w * rows + g * low : w * rows + (g + 1) * low],
                )

    return products(
        place,
        step,
        (context, blocks, normed, grad_hidden),
        lambda target: [
            whole((t, d)),
            pl.BlockSpec((1, t, cols_out), lambda j, me: (target(j, me), 0, 0)),
            whole((t, d)),
            pl.BlockSpec((t, cols_in), lambda j, me: (0, target(j, me))),
        ],
        (rows + low, cols_in),
    )


def finish_out_in(place, slots, rows):
    parts = sum_levels(place, slots)
    low, cols = parts[0].shape[0] - rows, parts[0].shape[1]
    fold = rows // low
    grad_in = jnp.stack([part[:rows] for part in parts])
    grad_out = [
        jnp.moveaxis(part[rows:].reshape(low, fold, -1), 1, 0).reshape(rows, -1) for part in parts
    ]
    return jnp.stack(grad_out), grad_in


def products_qkv(place, inputs, blocks):
    t, d = inputs.shape
    rows, cols = d // place.wide, blocks.shape[2]
    half = rows // 2

    def step(refs, store):
        left, right = refs
        value = inner_rows(left[...], right[0])
        for w in range(place.wide):
            for g in range(2):
                store(
                    (w, slice(None), slice(g * cols, (g + 1) * cols)),
                    value[w * rows + g * half : w * rows + (g + 1) * half],
                )

    return products(
        place,
        step,
        (inputs, blocks),
        lambda target: [
            whole((t, d)),
            pl.BlockSpec((1, t, cols), lambda j, me: (target(j, me), 0, 0)),
        ],
        (half, 2 * cols),
    )


def finish_qkv(place, slots):
    parts = sum_levels(place, slots)
    cols = parts[0].shape[1] // 2
    return jnp.stack([jnp.concatenate([p[:, :cols], p[:, cols:]]) for p in parts])


def attend_kernel(x_ref, w_ref, rows_ref, seg_row_ref, seg_col_ref, qkv_ref, ctx_ref, lse_ref):
    x = x_ref[...]
    same = seg_col_ref[...] == seg_row_ref[...]
    qkv_ref[0] = (matmul(x, w_ref[0]) + rows_ref[0:1]).astype(BF)
    qkv_ref[1] = matmul(x, w_ref[1]).astype(BF)
    qkv_ref[2] = (matmul(x, w_ref[2]) + rows_ref[1:2]).astype(BF)
    for h in range(GROUP):
        lanes = slice(h * HEAD_DIM, (h + 1) * HEAD_DIM)
        q, k, v = qkv_ref[0, :, lanes], qkv_ref[1, :, lanes], qkv_ref[2, :, lanes]
        scores = jnp.where(same, inner_cols(k, q) * HEAD_DIM ** (-0.5), MASKED)
        top = jnp.max(scores, axis=0, keepdims=True)
        shifted = jnp.exp(scores - top)
        total = jnp.sum(shifted, axis=0, keepdims=True)
        probs = (shifted * (1.0 / total)).astype(BF)
        ctx_ref[:, lanes] = inner_rows(probs, v).astype(BF)
        lse_ref[0, h : h + 1, :] = top + jnp.log(total)


def attend(x, w_qkv, rows, segment):
    t, d = x.shape
    width = GROUP * HEAD_DIM
    steps = d // width
    return pl.pallas_call(
        attend_kernel,
        grid=(steps,),
        in_specs=[
            pl.BlockSpec((t, d), lambda j: (0, 0)),
            pl.BlockSpec((3, d, width), lambda j: (0, 0, j)),
            pl.BlockSpec((8, width), lambda j: (0, j)),
            pl.BlockSpec((1, t), lambda j: (0, 0)),
            pl.BlockSpec((t, 1), lambda j: (0, 0)),
        ],
        out_specs=[
            pl.BlockSpec((3, t, width), lambda j: (0, 0, j)),
            pl.BlockSpec((t, width), lambda j: (0, j)),
            pl.BlockSpec((1, GROUP, t), lambda j: (j, 0, 0)),
        ],
        out_shape=[
            jax.ShapeDtypeStruct((3, t, d), BF),
            jax.ShapeDtypeStruct((t, d), BF),
            jax.ShapeDtypeStruct((steps, GROUP, t), F32),
        ],
        compiler_params=pltpu.CompilerParams(vmem_limit_bytes=VMEM),
        cost_estimate=cost(0.1),
    )(x, w_qkv, rows, segment.reshape(1, t), segment.reshape(t, 1))


def attend_back_kernel(
    gb_ref, w_ref, qkv_ref, lse_ref, seg_row_ref, seg_col_ref, out_ref, blocks_ref, sums_ref
):
    scale = HEAD_DIM ** (-0.5)
    same = seg_col_ref[...] == seg_row_ref[...]
    grad = inner_cols(gb_ref[...], w_ref[...]).astype(BF)
    for h in range(GROUP):
        lanes = slice(h * HEAD_DIM, (h + 1) * HEAD_DIM)
        q, k, v = qkv_ref[0, :, lanes], qkv_ref[1, :, lanes], qkv_ref[2, :, lanes]
        g = grad[:, lanes]
        scores = jnp.where(same, inner_cols(k, q) * scale, MASKED)
        probs = jnp.exp(scores - lse_ref[0, h : h + 1, :])
        grad_probs = inner_cols(v, g)
        delta = jnp.sum(probs * grad_probs, axis=0, keepdims=True)
        grad_scores = (probs * (grad_probs - delta)).astype(BF)
        out_ref[0, :, lanes] = (inner_rows(grad_scores, k) * scale).astype(BF)
        out_ref[1, :, lanes] = (matmul(grad_scores, q) * scale).astype(BF)
        out_ref[2, :, lanes] = matmul(probs.astype(BF), g).astype(BF)
    sums_ref[0:1] = jnp.sum(out_ref[0].astype(F32), axis=0, keepdims=True)
    sums_ref[1:2] = jnp.sum(out_ref[2].astype(F32), axis=0, keepdims=True)
    per_block = blocks_ref.shape[2] // HEAD_DIM
    heads = blocks_ref.shape[0] * per_block // 3
    for step in range(heads // GROUP):

        @pl.when(pl.program_id(0) == step)
        def _(step=step):
            for part in range(3):
                for h in range(GROUP):
                    block, at = divmod(part * heads + step * GROUP + h, per_block)
                    blocks_ref[block, :, at * HEAD_DIM : (at + 1) * HEAD_DIM] = out_ref[
                        part, :, h * HEAD_DIM : (h + 1) * HEAD_DIM
                    ]


def attend_back(grad_branch, w_out, qkv, lse, segment, narrow):
    t, d = grad_branch.shape
    width = GROUP * HEAD_DIM
    return pl.pallas_call(
        attend_back_kernel,
        grid=(d // width,),
        in_specs=[
            pl.BlockSpec((t, d), lambda j: (0, 0)),
            pl.BlockSpec((width, d), lambda j: (j, 0)),
            pl.BlockSpec((3, t, width), lambda j: (0, 0, j)),
            pl.BlockSpec((1, GROUP, t), lambda j: (j, 0, 0)),
            pl.BlockSpec((1, t), lambda j: (0, 0)),
            pl.BlockSpec((t, 1), lambda j: (0, 0)),
        ],
        out_specs=[
            pl.BlockSpec((3, t, width), lambda j: (0, 0, j)),
            pl.BlockSpec((narrow, t, 3 * d // narrow), lambda j: (0, 0, 0)),
            pl.BlockSpec((2, width), lambda j: (0, j)),
        ],
        out_shape=[
            jax.ShapeDtypeStruct((3, t, d), BF),
            jax.ShapeDtypeStruct((narrow, t, 3 * d // narrow), BF),
            jax.ShapeDtypeStruct((2, d), F32),
        ],
        compiler_params=pltpu.CompilerParams(vmem_limit_bytes=VMEM),
        cost_estimate=cost(20),
    )(grad_branch, w_out, qkv, lse, segment.reshape(1, t), segment.reshape(t, 1))


def hidden_kernel(x_ref, w_ref, bias_ref, active_ref, slope_ref):
    pre = matmul(x_ref[...], w_ref[0]) + bias_ref[...]
    below = 0.5 + 0.5 * lax.erf(pre * 0.5**0.5)
    active_ref[...] = (pre * below).astype(BF)
    density = jnp.exp(-0.5 * pre * pre) * (2.0 * math.pi) ** (-0.5)
    slope_ref[...] = (below + pre * density).astype(BF)


def hidden_layer(x, w_in, in_bias):
    t, d = x.shape
    parts, _, width = w_in.shape
    block = pl.BlockSpec((t, width), lambda j: (0, j))
    shape = jax.ShapeDtypeStruct((t, parts * width), BF)
    return pl.pallas_call(
        hidden_kernel,
        grid=(parts,),
        in_specs=[
            pl.BlockSpec((t, d), lambda j: (0, 0)),
            pl.BlockSpec((1, d, width), lambda j: (j, 0, 0)),
            pl.BlockSpec((1, width), lambda j: (0, j)),
        ],
        out_specs=[block, block],
        out_shape=[shape, shape],
        compiler_params=pltpu.CompilerParams(vmem_limit_bytes=VMEM),
        cost_estimate=cost(8),
    )(x, w_in, in_bias)


def norm_parts(value):
    mean = jnp.mean(value, axis=-1, keepdims=True)
    centered = value - mean
    scale = lax.rsqrt(jnp.mean(centered * centered, axis=-1, keepdims=True) + EPSILON)
    return centered * scale, scale


def norm_back(grad, unit, scale, gain):
    e = grad * gain
    part = jnp.mean(e * unit, axis=-1, keepdims=True)
    return (e - jnp.mean(e, axis=-1, keepdims=True) - unit * part) * scale


def total(value):
    return jnp.sum(jnp.sum(value, axis=0, keepdims=True), axis=1, keepdims=True)


def column_sum(value):
    return jnp.sum(value, axis=0, keepdims=True)


def store_blocks(ref, value):
    count, _, width = ref.shape
    for i in range(count):
        ref[i] = value[:, i * width : (i + 1) * width]


def calls(kernel, outs, us, **kwargs):
    return pl.pallas_call(
        kernel,
        out_shape=[jax.ShapeDtypeStruct(shape, dtype) for shape, dtype in outs],
        compiler_params=pltpu.CompilerParams(vmem_limit_bytes=VMEM),
        cost_estimate=cost(us),
        **kwargs,
    )


def branch_kernel(ctx, w, x, rows, valid, normed, low, unit, scale, stats):
    branch = matmul(ctx[...], w[0]) + rows[2:3]
    residual = x[...].astype(F32) + branch
    unit[...], scale[...] = norm_parts(residual)
    normed[...] = unit[...] * rows[6:7] + rows[3:4]
    low[...] = normed[...].astype(BF)
    for i, value in enumerate((residual, branch)):
        stats[i : i + 1] = jnp.broadcast_to(total(valid[...] * value * value), (1, 128))


def branch_layer(context, w_out, inputs, rows, valid):
    t, d = inputs.shape
    outs = [((t, d), F32), ((t, d), BF), ((t, d), F32), ((t, 1), F32), ((2, 128), F32)]
    return calls(branch_kernel, outs, 5)(context, w_out, inputs, rows, valid)


def output_kernel(plan, level, me_ref, active, normed, rows, valid, hot, *refs):
    pieces = refs[:-8]
    low, unit, scale, pooled, stats, w, acc, sems = refs[-8:]
    step = pl.program_id(0)
    width = active.shape[1]
    block = pieces[0].shape[1]

    @pl.when(step == 0)
    def _():
        copies = []
        if plan is None:
            copies.append(pltpu.make_async_copy(pieces[0], w, sems.at[0]))
        for piece, masks in zip(pieces, plan or []):
            for slot, mask in enumerate(masks):
                at = pl.multiple_of(block_of(me_ref[0], mask, level) * block, block)
                target = w.at[pl.ds(at, block)]
                copies.append(
                    pltpu.make_async_copy(piece.at[slot], target, sems.at[len(copies)])
                )
        for copy in copies:
            copy.start()
        for copy in copies:
            copy.wait()

    product = matmul(active[...], w[pl.ds(pl.multiple_of(step * width, width), width)])

    @pl.when(step == 0)
    def _():
        acc[...] = product

    @pl.when(step > 0)
    def _():
        acc[...] += product

    @pl.when(step == pl.num_programs(0) - 1)
    def _():
        ffn_out = acc[...] + rows[4:5]
        residual = normed[...] + ffn_out
        unit[...], scale[...] = norm_parts(residual)
        low[...] = (unit[...] * rows[7:8] + rows[5:6]).astype(BF)
        pooled[...] = matmul(hot[...].astype(BF), low[...]).astype(BF)
        sums = (valid[...] * residual * residual, valid[...] * ffn_out * ffn_out, valid[...])
        for i, value in enumerate(sums):
            stats[i : i + 1] = jnp.broadcast_to(total(value), (1, 128))


def all_of(shape):
    return pl.BlockSpec(shape, lambda j: (0,) * len(shape))


def output_layer(place, active, pieces, plan, normed, rows, valid, hot):
    t, ff = active.shape
    d = normed.shape[1]
    outs = [((t, d), BF), ((t, d), F32), ((t, 1), F32), ((hot.shape[0], d), BF), ((3, 128), F32)]
    outs.append(((ff, d), BF))
    return calls(
        functools.partial(output_kernel, plan, place.wide * place.narrow // LEVELS),
        outs,
        9,
        grid=(ff // d,),
        in_specs=[pl.BlockSpec(memory_space=pltpu.SMEM), pl.BlockSpec((t, d), lambda j: (0, j))]
        + [all_of(a.shape) for a in (normed, rows, valid, hot)]
        + [pl.BlockSpec(memory_space=pl.ANY)] * len(pieces),
        out_specs=[all_of(shape) for shape, _ in outs],
        scratch_shapes=[
            pltpu.VMEM((t, d), F32),
            pltpu.SemaphoreType.DMA((place.wide * place.narrow,)),
        ],
    )(place.me.reshape(1), active, normed, rows, valid, hot, *pieces)


def output_back_kernel(cot, valid, hot, pool, unit, scale, rows, grad, low, sums):
    grad_out = cot[...].astype(F32) * valid[...] + lax.dot_general(
        hot[...],
        pool[...],
        (((0,), (0,)), ((), ())),
        precision=lax.Precision.HIGHEST,
        preferred_element_type=F32,
    )
    sums[0:1] = column_sum(grad_out * unit[...])
    sums[1:2] = column_sum(grad_out)
    grad[...] = norm_back(grad_out, unit[...], scale[...], rows[7:8])
    low[...] = grad[...].astype(BF)
    sums[2:3] = column_sum(low[...].astype(F32))


def output_back(cot, valid, hot, pool, unit, scale, rows):
    t, d = cot.shape
    outs = [((t, d), F32), ((t, d), BF), ((3, d), F32)]
    return calls(output_back_kernel, outs, 6)(cot, valid, hot, pool, unit, scale, rows)


def hidden_back_kernel(
    low, w_back, slope, w_in, grad, unit, scale, rows, hidden, inb, residual, branch, blocks, sums, acc
):
    step = pl.program_id(0)
    hidden[...] = (inner_cols(low[...], w_back[...]) * slope[...].astype(F32)).astype(BF)
    inb[...] = column_sum(hidden[...].astype(F32))
    product = inner_cols(hidden[...], w_in[0])

    @pl.when(step == 0)
    def _():
        acc[...] = grad[...] + product

    @pl.when(step > 0)
    def _():
        acc[...] += product

    @pl.when(step == pl.num_programs(0) - 1)
    def _():
        value = acc[...]
        sums[0:1] = column_sum(value * unit[...])
        sums[1:2] = column_sum(value)
        residual[...] = norm_back(value, unit[...], scale[...], rows[6:7])
        branch[...] = residual[...].astype(BF)
        sums[2:3] = column_sum(branch[...].astype(F32))
        store_blocks(blocks, branch[...])


def hidden_back(low, w_back, slope, w_in, grad, unit, scale, rows, narrow):
    t, d = low.shape
    ff = slope.shape[1]
    tile = pl.BlockSpec((t, d), lambda j: (0, j))
    outs = [
        ((t, ff), BF),
        ((1, ff), F32),
        ((t, d), F32),
        ((t, d), BF),
        ((narrow, t, d // narrow), BF),
        ((3, d), F32),
    ]
    return calls(
        hidden_back_kernel,
        outs,
        14,
        grid=(ff // d,),
        in_specs=[
            all_of(low.shape),
            pl.BlockSpec((d, d), lambda j: (j, 0)),
            tile,
            pl.BlockSpec((1, d, d), lambda j: (j, 0, 0)),
        ]
        + [all_of(a.shape) for a in (grad, unit, scale, rows)],
        out_specs=[tile, pl.BlockSpec((1, d), lambda j: (0, j))]
        + [all_of(shape) for shape, _ in outs[2:]],
        scratch_shapes=[pltpu.VMEM((t, d), F32)],
    )(low, w_back, slope, w_in, grad, unit, scale, rows)


def input_back_kernel(grad, w, residual, out, acc):
    step = pl.program_id(0)
    product = inner_cols(grad[0], w[0])

    @pl.when(step == 0)
    def _():
        acc[...] = residual[...] + product

    @pl.when(step == 1)
    def _():
        acc[...] += product

    @pl.when(step == 2)
    def _():
        out[...] = (acc[...] + product).astype(BF)


def input_back(grad_qkv, w_qkv, residual):
    _, t, d = grad_qkv.shape
    return calls(
        input_back_kernel,
        [((t, d), BF)],
        6,
        grid=(3,),
        in_specs=[
            pl.BlockSpec((1, t, d), lambda j: (j, 0, 0)),
            pl.BlockSpec((1, d, d), lambda j: (j, 0, 0)),
            all_of((t, d)),
        ],
        out_specs=[all_of((t, d))],
        scratch_shapes=[pltpu.VMEM((t, d), F32)],
    )(grad_qkv, w_qkv, residual)[0]


def spread_masks(count, width):
    total_cols = count * width
    column = lax.broadcasted_iota(jnp.int32, (count, total_cols), 1)
    first = lax.broadcasted_iota(jnp.int32, (count, total_cols), 0) * width
    own = (column >= first) & (column < first + width)
    owner = jnp.sum(jnp.where(own, first, 0), axis=0, keepdims=True)
    within = lax.broadcasted_iota(jnp.int32, (width, total_cols), 1) - owner
    spread = within == lax.broadcasted_iota(jnp.int32, (width, total_cols), 0)
    return own, spread.astype(F32)


def unpack_kernel(small, rows, inb):
    count = small.shape[0]
    value = small[...].astype(F32)

    def unpack(part, masks):
        own, spread = masks
        placed = matmul(part.astype(BF), spread.astype(BF))
        return column_sum(jnp.where(own, placed, 0.0))

    width = rows.shape[1] // count
    masks = spread_masks(count, width)
    for r in range(8):
        rows[r : r + 1] = unpack(value[:, r, :width], masks)
    width = inb.shape[1] // count
    inb[...] = unpack(value[:, 0, 128 : 128 + width], spread_masks(count, width))


def unpack_params(small, d, ff):
    return calls(unpack_kernel, [((8, d), F32), ((1, ff), F32)], 0.1)(small)


def pack_kernel(attn, out, ffn, inb, stats_a, stats_b, packed):
    count = packed.shape[0]
    width = out.shape[1] // count
    vectors = (
        attn[0:1], attn[1:2], out[2:3], out[1:2], ffn[2:3], ffn[1:2], out[0:1], ffn[0:1], inb[...]
    )
    packed[...] = jnp.zeros(packed.shape, F32)
    at = 0
    for i, vector in enumerate(vectors):
        if i in (0, 8):
            width = vector.shape[1] // count
            own, spread = spread_masks(count, width)
        packed[:, at : at + width] = lax.dot_general(
            jnp.where(own, vector, 0.0),
            spread,
            (((1,), (1,)), ((), ())),
            precision=lax.Precision.HIGHEST,
            preferred_element_type=F32,
        )
        at += width
    for i, row in enumerate((stats_a[0:1], stats_a[1:2], stats_b[0:1], stats_b[1:2], stats_b[2:3])):
        packed[:, at + i : at + i + 1] = jnp.broadcast_to(row[:, :1], (count, 1))


def pack_sums(count, attn, out, ffn, inb, stats_a, stats_b):
    return calls(pack_kernel, [((count, 384), F32)], 4)(attn, out, ffn, inb, stats_a, stats_b)[0]


def match_grads(rows, label_rows, label_cols):
    is_query, is_pass = label_rows >= 0, label_cols >= 0
    match = jnp.where(is_pass, inner_cols(rows, rows) / SCORE_DIV, MASKED)
    shifted = jnp.exp(match - jnp.max(match, axis=1, keepdims=True))
    probs = shifted / jnp.sum(shifted, axis=1, keepdims=True)
    hot = (label_rows == label_cols).astype(F32)
    grad = jnp.where(is_query & is_pass, (probs - hot) / SCORE_DIV, 0.0).astype(BF)
    return matmul(grad[:POOL], rows) + inner_rows(grad[:, :POOL], rows)


def match_kernel(rows, label_rows, label_cols, out):
    out[...] = match_grads(rows[...], label_rows[...], label_cols[...])


def row_of(z, y, n, s):
    own = (z * s + y) * 3 + n
    spare = y * 3 + (z - 1)
    return jnp.where(z == 0, n * s + y, jnp.where(n < 3, own, spare))


def body(
    passages,
    queries,
    passage_cot,
    query_cot,
    passage_lengths,
    query_lengths,
    labels,
    w_qkv,
    w_out,
    w_in,
    w_back,
    biases,
    norm_gains,
    in_bias,
):
    place = Place()
    s, narrow, devices = place.stride, place.narrow, place.wide * place.narrow
    model_width = passages.shape[2]
    length = passages.shape[1] * narrow
    segs, qsegs = passage_lengths.shape[1] - 1, query_lengths.shape[1] - 1
    on_query = place.z == 0

    piece = model_width // devices
    whole = jnp.concatenate(
        [passage_lengths.reshape(-1), query_lengths.reshape(-1), labels.reshape(-1)]
    )
    whole = jnp.concatenate([whole // 32, whole % 32]).astype(BF)

    w_rows, in_parts = w_out.shape[1], w_in.shape[2] // w_out.shape[2]
    swapped = swap_in_directly(place, passages, queries)
    if s == 2:
        swapped[0], w_qkv = phase(swapped[0], w_qkv)
        towers = pick_towers(place, w_qkv, biases, norm_gains, in_bias, whole)
        got = {k: flip(towers[k], "wide", k * s) for k in (3, 2, 1)}
        levels_qkv = jnp.stack([towers[0], got[1], got[2], got[3]])
        own = [k * s * narrow for k in range(LEVELS)]
        layout = [(0, part, part * w_rows, 0) for part in range(3)] + [(1, 0, 3 * w_rows, 0)]
        shapes = [(3, w_rows, model_width), (1, 8, model_width)]
    else:
        small = jnp.concatenate(
            [biases.reshape(2, -1), norm_gains.reshape(2, -1), in_bias.reshape(2, -1)], axis=1
        )
        small_count = small.shape[1]
        small = jnp.concatenate([small, jnp.broadcast_to(whole, (2, whole.shape[0]))], axis=1)
        to_query = (jnp.arange(devices) < s * narrow)[:, None]
        small = lax.all_to_all(
            jnp.where(to_query, small[1][None], small[0][None]), BOTH, 0, 0, tiled=True
        )
        levels_qkv, own = gather_levels(place, w_qkv), None
        layout = [(0, part, 0, part * model_width) for part in range(3)]
        shapes = [(3, w_rows, model_width)]
    out_in = jnp.concatenate([w_out, w_in], axis=2)
    levels_qkv, swapped, out_in = phase(levels_qkv, swapped, out_in)

    pieces_qkv, plan = gather_columns(place, levels_qkv, own)
    levels_out_in = gather_levels(place, out_in)
    pieces_qkv, levels_out_in, w_back = phase(pieces_qkv, levels_out_in, w_back)

    cores_qkv, core_plan = gather_cores(pieces_qkv, plan)
    cores_qkv, levels_out_in, swapped = phase(cores_qkv, levels_out_in, swapped)

    pieces_out_in, plan = gather_columns(place, levels_out_in)
    inputs = to_row(place, passages, queries, join_swapped(place, queries, swapped))
    inputs, w_back = phase(inputs, w_back)
    levels_back = gather_levels(place, w_back)
    made = assemble(place, cores_qkv, core_plan, layout, shapes)
    w_qkv_all = made[0]

    n_bias, n_gain = biases.shape[1], norm_gains.shape[1]
    ff = in_bias.shape[1] * devices
    if s == 2:
        small = made[1].reshape(devices, 8, -1)
        rows, inb_row = unpack_params(small, model_width, ff)
        ints = small[:, 0, 256 : 256 + whole.shape[0]].astype(F32)
    else:
        params = small[:, :small_count].astype(F32)
        vectors = params[:, : (n_bias + n_gain) * piece].reshape(devices, n_bias + n_gain, piece)
        rows = vectors.transpose(1, 0, 2).reshape(n_bias + n_gain, -1)
        inb_row = params[:, (n_bias + n_gain) * piece :].reshape(1, -1)
        ints = small[:, small_count : small_count + whole.shape[0]].astype(F32)
    half = ints.shape[1] // 2
    ints = (ints[::narrow, :half] * 32 + ints[::narrow, half:]).astype(jnp.int32)
    n_pass = passage_lengths.size
    n_query = query_lengths.size
    pass_lens = ints[:, :n_pass].reshape(-1, segs + 1)
    query_lens = ints[:, n_pass : n_pass + n_query].reshape(-1, qsegs + 1)
    label_all = ints[:, n_pass + n_query :].reshape(-1, qsegs)
    my_row = row_of(place.z, place.y, place.n, s)
    pass_row = pick(pass_lens, jnp.where(on_query, 0, my_row), 0)
    query_row = pick(query_lens, jnp.where(on_query, my_row, 0), 0)
    ends_p = jnp.cumsum(pass_row)[:-1]
    ends_q = jnp.cumsum(query_row)[:-1]
    starts_p, starts_q = ends_p - pass_row[:-1], ends_q - query_row[:-1]
    ends_p = jnp.concatenate([ends_p, jnp.full((qsegs - segs,), length + 1, jnp.int32)])
    ends = jnp.where(on_query, ends_q, ends_p)
    seg_count = jnp.where(on_query, qsegs, segs)
    position = jnp.arange(length, dtype=jnp.int32)
    segment = jnp.sum((position[:, None] >= ends[None, :]).astype(jnp.int32), axis=1)
    valid = (segment < seg_count).astype(F32)[:, None]
    slot = jnp.arange(POOL)
    starts = jnp.where(on_query, jnp.concatenate([starts_q, jnp.full((qsegs,), -1)]), -1)
    for z in range(1, LEVELS):
        here = (place.z == z) & (slot >= qsegs + segs * (z - 1)) & (slot < qsegs + segs * z)
        starts = jnp.where(here, jnp.tile(starts_p, POOL // segs), starts)
    hot = (starts[:, None] == position[None, :]).astype(F32)
    masks = [0]
    if s == 2:
        masks += [dy * narrow + 2 * dx for dx, dy in OTHERS]
        masks += [m ^ 1 for m in masks]
    else:
        for mask in [b * narrow for b in bits_of(s)] + [b for b in reversed(bits_of(narrow))]:
            masks = masks + [m ^ mask for m in masks]
    there = (place.y * narrow + place.n) ^ jnp.array(masks, jnp.int32)
    their_y, their_n = there // narrow, there % narrow
    label_rows = label_all[row_of(jnp.int32(0), their_y, their_n, s)]
    label_rows = jnp.pad(label_rows, ((0, 0), (0, POOL - qsegs)), constant_values=-1)
    levels = jnp.arange(1, LEVELS)
    pass_rows = row_of(levels[None, :], their_y[:, None], their_n[:, None], s)
    pass_ids = (pass_rows[:, :, None] * segs + jnp.arange(segs)).reshape(len(masks), -1)
    spare = POOL - qsegs - pass_ids.shape[1]
    label_cols = jnp.pad(pass_ids, ((0, 0), (qsegs, spare)), constant_values=-1)
    label_rows, label_cols = label_rows.reshape(-1, 1), label_cols.reshape(1, -1)

    qkv, context, log_sum = attend(inputs, w_qkv_all, rows, segment)
    context, pieces_out_in, levels_back, cots = phase(
        context, pieces_out_in, levels_back, (passage_cot, query_cot)
    )

    cores_out_in, core_plan = gather_cores(pieces_out_in, plan)
    cores_out_in, levels_back, cots = phase(cores_out_in, levels_back, cots)

    pieces_back, plan = gather_columns(place, levels_back)
    swapped = swap_in(place, *cots)
    w_out_all, w_in_all = assemble(
        place,
        cores_out_in,
        core_plan,
        [(0, 0, 0, 0)] + [(1, part, 0, (part + 1) * model_width) for part in range(in_parts)],
        [(1, w_rows, model_width), (in_parts, w_rows, model_width)],
    )
    normed, normed_low, unit_one, scale_one, stats_one = branch_layer(
        context, w_out_all, inputs, rows, valid
    )
    active, slope = hidden_layer(normed_low, w_in_all, inb_row)
    active, pieces_back, swapped = phase(active, pieces_back, swapped)

    cores_back, core_plan = gather_cores(pieces_back, plan)
    cot = to_row(place, passage_cot, query_cot, swapped)
    if s != 2:
        back_shape = [(1, w_back.shape[1], model_width)]
        cores_back = assemble(place, cores_back, core_plan, [(0, 0, 0, 0)], back_shape)
        cores_back, core_plan = [cores_back[0][0]], None
    output_low, unit_two, scale_two, pooled, stats_two, w_back_all = output_layer(
        place, active, cores_back, core_plan, normed, rows, valid, hot
    )
    pooled, cot = phase(pooled, cot)

    column = sum([flip(pooled, "wide", k * s).astype(F32) for k in (3, 2, 1)], pooled.astype(F32))
    seen = column.astype(BF)[None]
    if s == 2:
        seen = jnp.concatenate([seen] + [flip_both(seen, dy, 2 * dx) for dx, dy in OTHERS])
        seen = jnp.concatenate([seen, flip(seen, "narrow", 1)])
    else:
        for axis, step in [("wide", b) for b in bits_of(s)] + [
            ("narrow", b) for b in reversed(bits_of(narrow))
        ]:
            seen = jnp.concatenate([seen, flip(seen, axis, step)])
    seen = seen.reshape(-1, model_width)
    if s == 2:
        (grad_pool,) = calls(match_kernel, [((POOL, model_width), F32)], 3)(
            seen, label_rows, label_cols
        )
    else:
        grad_pool = match_grads(seen, label_rows, label_cols)

    grad_pool, output_low = phase(grad_pool, output_low)
    if s == 2:
        out_four = row_pieces(place, output_low)
    grad_resid_two, grad_ffn, sums_two = output_back(
        cot, valid, hot, grad_pool, unit_two, scale_two, rows
    )
    if s == 2:
        send_c, keep_c = products_back(place, active, grad_ffn)
        send_c, out_four = phase(send_c, out_four)
        got_c = flip(send_c, "narrow", 1)
        shares_c = column_shares(place, keep_c, got_c)
        shares_c, grad_ffn = phase(shares_c, grad_ffn)

        columns_c = send_columns(shares_c)
        swapped = swap_out(place, out_four)
    grad_hidden, inb_sums, grad_residual, grad_branch, blocks_b, sums_one = hidden_back(
        grad_ffn, w_back_all, slope, w_in_all, grad_resid_two, unit_one, scale_one, rows, narrow
    )
    if s == 2:
        send_b, keep_b = products_out_in(place, context, blocks_b, normed_low, grad_hidden)
        send_b, columns_c, swapped = phase(send_b, columns_c, swapped)
        passage_out, query_out = from_row(place, out_four, swapped)

        got_b = flip(send_b, "narrow", 1)
        level_c = level_sums(columns_c)
        shares_b = column_shares(place, keep_b, got_b)
        shares_b, level_c, grad_branch = phase(shares_b, level_c, grad_branch)

        columns_b = send_columns(shares_b)
        levels_c = across_levels(level_c, s)
    grad_qkv, blocks_a, sums_qkv = attend_back(
        grad_branch, w_out_all[0], qkv, log_sum, segment, narrow
    )
    if s == 2:
        send_a, keep_a = products_qkv(place, inputs, blocks_a)
        send_a, grad_qkv, columns_b, levels_c = phase(send_a, grad_qkv, columns_b, levels_c)

        got_a = flip(send_a, "narrow", 1)
    input_grad = input_back(grad_qkv, w_qkv_all, grad_residual)
    if s == 2:
        got_a, input_grad, columns_b = phase(got_a, input_grad, columns_b)

        in_four = row_pieces(place, input_grad)
        levels_b = swap_shares(place, level_shares(place, columns_b))
        shares_a = column_shares(place, keep_a, got_a)
        shares_a, levels_b, in_four, sums_qkv, levels_c = phase(
            shares_a, levels_b, in_four, sums_qkv, levels_c
        )

        columns_a = send_columns(shares_a)
        swapped = swap_out(place, in_four)
        packed = pack_sums(devices, sums_qkv, sums_one, sums_two, inb_sums, stats_one, stats_two)
        grad_w_back = finish_back(levels_c)
        columns_a, swapped, packed = phase(columns_a, swapped, packed)

        packed = lax.all_to_all(packed, BOTH, 0, 0, tiled=True)
        levels_a = swap_shares(place, level_shares(place, columns_a))
        grad_w_out, grad_w_in = finish_out_in(place, levels_b, model_width // place.wide)
        passage_grad, query_grad = from_row(place, in_four, swapped)
        grad_w_qkv = finish_qkv(place, levels_a)
    else:
        packed = pack_sums(devices, sums_qkv, sums_one, sums_two, inb_sums, stats_one, stats_two)
        packed = lax.all_to_all(packed, BOTH, 0, 0, tiled=True)
        grad_w_back = scatter_tower(place, grad_blocks(active, grad_ffn, narrow))
        grad_w_out = scatter_tower(place, grad_blocks(context, grad_branch, narrow))
        grad_w_in = scatter_tower(place, grad_blocks(normed_low, grad_hidden, narrow))
        flat = jnp.moveaxis(grad_qkv, 0, 1).reshape(length, -1)
        grad_w_qkv = scatter_tower(place, grad_blocks(inputs, flat, narrow))
        out_four, in_four = row_pieces(place, output_low), row_pieces(place, input_grad)
        passage_out, query_out = from_row(place, out_four, swap_out(place, out_four))
        passage_grad, query_grad = from_row(place, in_four, swap_out(place, in_four))

    packed = packed.reshape(LEVELS, -1, packed.shape[1]).sum(axis=1)
    packed = jnp.stack([packed[1] + packed[2] + packed[3], packed[0]])
    edges = [n_bias * piece, (n_bias + n_gain) * piece]
    edges.append(edges[1] + in_bias.shape[1])
    grad_biases = packed[:, : edges[0]].reshape(2, n_bias, piece)
    grad_gains = packed[:, edges[0] : edges[1]].reshape(2, n_gain, piece)
    grad_inb = packed[:, edges[1] : edges[2]]
    totals = packed[:, edges[2] : edges[2] + 5]
    rms_stats = jnp.sqrt(totals[:, :4] / (totals[:, 4:] * model_width))
    return (
        passage_out,
        query_out,
        passage_grad,
        query_grad,
        grad_w_qkv,
        grad_w_out,
        grad_w_in,
        grad_w_back,
        grad_biases,
        grad_gains,
        grad_inb,
        rms_stats,
    )


def solution(mesh):
    return jax.shard_map(
        body,
        mesh=mesh,
        in_specs=(
            P("wide", "narrow", None),
            P("wide", "narrow", None),
            P("wide", "narrow", None),
            P("wide", "narrow", None),
            P("wide", None),
            P("wide", None),
            P("wide"),
            P(None, ("wide", "narrow"), None),
            P(None, ("wide", "narrow"), None),
            P(None, ("wide", "narrow"), None),
            P(None, ("wide", "narrow"), None),
            P(None, None, ("wide", "narrow")),
            P(None, None, ("wide", "narrow")),
            P(None, ("wide", "narrow")),
        ),
        out_specs=(
            P("wide", "narrow", None),
            P("wide", "narrow", None),
            P("wide", "narrow", None),
            P("wide", "narrow", None),
            P(None, "wide", "narrow"),
            P(None, "wide", "narrow"),
            P(None, "wide", "narrow"),
            P(None, "wide", "narrow"),
            P(None, None, ("wide", "narrow")),
            P(None, None, ("wide", "narrow")),
            P(None, ("wide", "narrow")),
            P(),
        ),
        check_vma=False,
    )
```

```python
import functools
import math

import jax
import jax.numpy as jnp
from jax import lax
from jax.experimental import pallas as pl
from jax.experimental.pallas import tpu as pltpu
from jax.sharding import PartitionSpec as P

HEAD_DIM = 64
LEVELS = 4
GROUP = 4
POOL = 32
STEP = 128
VMEM = 58 << 20
OTHERS = ((1, 1), (1, 0), (0, 1))


def cost(us):
    return pl.CostEstimate(flops=int(us * 1.15e9), bytes_accessed=1024, transcendentals=0)


EPSILON = 1e-05
SCORE_DIV = 12.0
MASKED = -1e30
BF = jnp.bfloat16
F32 = jnp.float32
BOTH = ("wide", "narrow")


def matmul(left, right):
    return jnp.dot(left, right, preferred_element_type=F32)


def inner_rows(left, right):
    return lax.dot_general(left, right, (((0,), (0,)), ((), ())), preferred_element_type=F32)


def inner_cols(left, right):
    return lax.dot_general(left, right, (((1,), (1,)), ((), ())), preferred_element_type=F32)


def flip(x, axis, mask):
    size = lax.axis_size(axis)
    return lax.ppermute(x, axis, [(i, i ^ mask) for i in range(size)])


def flip_both(x, wide_mask, narrow_mask):
    wide, narrow = lax.axis_size("wide"), lax.axis_size("narrow")
    mask = wide_mask * narrow + narrow_mask
    return lax.ppermute(x, BOTH, [(i, i ^ mask) for i in range(wide * narrow)])


def phase(*values):
    return lax.optimization_barrier(values)


def across_levels(x, stride):
    groups = [[k * stride + i for k in range(LEVELS)] for i in range(stride)]
    return lax.all_to_all(x, "wide", 0, 0, axis_index_groups=groups, tiled=True)


def swap_levels(x, k, stride):
    pairs = []
    for i in range(stride):
        pairs += [(i, k * stride + i), (k * stride + i, i)]
    return lax.ppermute(x, "wide", pairs)


def bits_of(size):
    return [1 << b for b in range(size.bit_length() - 1)]


class Place:
    def __init__(self):
        self.wide = lax.axis_size("wide")
        self.narrow = lax.axis_size("narrow")
        self.stride = self.wide // LEVELS
        self.w = lax.axis_index("wide")
        self.n = lax.axis_index("narrow")
        self.z = self.w // self.stride
        self.y = self.w % self.stride
        self.me = self.w * self.narrow + self.n


def swap_in(place, pass_part, query_part):
    query = jnp.broadcast_to(query_part, (LEVELS, *query_part.shape[1:]))
    first = jnp.concatenate([query_part, pass_part])
    return across_levels(jnp.where(place.z == 0, first, query), place.stride)


def swap_in_directly(place, pass_part, query_part):
    return [
        swap_levels(jnp.where(place.z == 0, pass_part[k - 1], query_part[0]), k, place.stride)
        for k in range(1, LEVELS)
    ]


def join_swapped(place, query_part, got):
    first = jnp.where(place.z == 0, query_part[0], got[0] + got[1] + got[2])
    return jnp.stack([first] + got)


def to_row(place, pass_part, query_part, got):
    four = jnp.where(place.z == 0, got, jnp.concatenate([pass_part, got[:1]]))
    mine = lax.all_to_all(four, "narrow", 0, 0, tiled=True)
    return mine.reshape(-1, mine.shape[-1])


def row_pieces(place, row):
    return lax.all_to_all(
        row.reshape(place.narrow, -1, row.shape[-1]), "narrow", 0, 0, tiled=True
    )


def swap_out(place, four):
    last = jnp.broadcast_to(four[3:], four.shape)
    return across_levels(jnp.where(place.z == 0, four, last), place.stride)


def from_row(place, four, got):
    pass_part = jnp.where(place.z == 0, got[1:], four[:3])
    query_part = jnp.where(place.z == 0, four[:1], got[:1])
    return pass_part, query_part


def toggle(places, mask):
    return [(p[0], p[1] ^ mask) if isinstance(p, tuple) else p ^ mask for p in places]


def block_of(me, place, level):
    if isinstance(place, tuple):
        return ((me & (level - 1)) ^ place[1]) + place[0] * level
    return me ^ place


def assemble_kernel(plan, layout, level, me_ref, *refs):
    pieces, outs, sems = refs[: len(plan)], refs[len(plan) : -1], refs[-1]
    me = me_ref[0]
    copies = []
    for piece, masks in zip(pieces, plan):
        for slot, mask in enumerate(masks):
            for out, part, row, column in layout:
                target = outs[out].at[part, block_of(me, mask, level)]
                rows, columns = outs[out].shape[2:]
                source = piece.at[slot, pl.ds(row, rows), pl.ds(column, columns)]
                copies.append(pltpu.make_async_copy(source, target, sems.at[len(copies)]))
    for copy in copies:
        copy.start()
    for copy in copies:
        copy.wait()


def assemble(place, pieces, plan, layout, outs):
    total = place.wide * place.narrow
    made = pl.pallas_call(
        functools.partial(assemble_kernel, plan, layout, total // LEVELS),
        out_shape=[jax.ShapeDtypeStruct((out[0], total, *out[1:]), BF) for out in outs],
        in_specs=[pl.BlockSpec(memory_space=pltpu.SMEM)]
        + [pl.BlockSpec(memory_space=pl.ANY)] * len(pieces),
        out_specs=[pl.BlockSpec(memory_space=pltpu.VMEM)] * len(outs),
        scratch_shapes=[pltpu.SemaphoreType.DMA((total * len(layout),))],
        cost_estimate=cost(0.1),
        compiler_params=pltpu.CompilerParams(vmem_limit_bytes=VMEM),
    )(place.me.reshape(1), *pieces)
    return [out.reshape(out.shape[0], -1, out.shape[3]) for out in made]


def pick_kernel(z_ref, w_ref, bias_ref, gain_ref, inb_ref, ints_ref, *refs):
    outs, small = refs[:-1], refs[-1]
    rows, width = w_ref.shape[1], small.shape[1]
    n_bias, n_gain = bias_ref.shape[1], gain_ref.shape[1]
    for k, out in enumerate(outs):
        tower = jnp.where(z_ref[0] == k, 1, 0)
        for part in range(3):
            out[part * rows : (part + 1) * rows] = w_ref[tower, :, part * width : (part + 1) * width]
        small[...] = jnp.zeros(small.shape, F32)
        small[:n_bias, : bias_ref.shape[2]] = bias_ref[tower].astype(F32)
        small[n_bias : n_bias + n_gain, : gain_ref.shape[2]] = gain_ref[tower].astype(F32)
        small[:1, 128 : 128 + inb_ref.shape[2]] = inb_ref[tower].astype(F32)
        small[:1, 256 : 256 + ints_ref.shape[1]] = ints_ref[...].astype(F32)
        out[3 * rows :] = small[...].astype(BF)


def pick_towers(place, w_qkv, biases, norm_gains, in_bias, ints):
    width = w_qkv.shape[2] // 3
    vmem = pl.BlockSpec(memory_space=pltpu.VMEM)
    return calls(
        pick_kernel,
        [((3 * w_qkv.shape[1] + 8, width), BF)] * LEVELS,
        2,
        in_specs=[pl.BlockSpec(memory_space=pltpu.SMEM)] + [vmem] * 5,
        scratch_shapes=[pltpu.VMEM((8, width), F32)],
    )(place.z.reshape(1), w_qkv, biases, norm_gains, in_bias[:, None], ints[None])


def gather_levels(place, pair):
    first = lax.broadcasted_iota(jnp.int32, (LEVELS, 1, 1), 0) == 0
    return across_levels(jnp.where(first, pair[1:], pair[:1]), place.stride)


def gather_columns(place, levels, own=None):
    s, narrow = place.stride, place.narrow
    if own is None:
        own = [(level, 0) for level in range(LEVELS)]
    pieces, plan = [levels], [own]
    if s == 2:
        for dx, dy in OTHERS:
            pieces.append(flip_both(levels, dy, 2 * dx))
            plan.append(toggle(own, dy * narrow + 2 * dx))
    else:
        for b in bits_of(s):
            for i in range(len(pieces)):
                pieces.append(flip(pieces[i], "wide", b))
                plan.append(toggle(plan[i], b * narrow))
        for i in range(len(pieces)):
            pieces.append(flip(pieces[i], "narrow", 2))
            plan.append(toggle(plan[i], 2))
    return pieces, plan


def gather_cores(pieces, plan):
    others = [flip(piece, "narrow", 1) for piece in pieces]
    return list(pieces) + others, plan + [toggle(places, 1) for places in plan]


def pick(x, index, dim):
    return lax.dynamic_index_in_dim(x, index, dim, keepdims=False)


def halve(x, place, axis, mask, dim):
    index = place.n if axis == "narrow" else place.w
    bit = jnp.where((index & mask) != 0, 1, 0)
    got = flip(pick(x, 1 - bit, dim).astype(BF), axis, mask)
    return pick(x, bit, dim) + got.astype(F32)


def scatter_tower(place, partial):
    s = place.stride
    rows, narrow, cols = partial.shape
    per = rows // place.wide
    x = partial.reshape(rows, 2, 2, cols)
    x = halve(x, place, "narrow", 1, 2)
    x = x.reshape(LEVELS, s, per, 2, cols)
    first, second = x[:2], x[2:]

    def over_columns(part):
        for b in reversed(bits_of(s)):
            shape = part.shape
            part = part.reshape(shape[0], 2, shape[1] // 2, *shape[2:])
            part = halve(part, place, "wide", b, 1)
        return part[:, 0]

    first = over_columns(halve(first, place, "narrow", 2, 3))
    second = halve(over_columns(second), place, "narrow", 2, 2)
    return jnp.stack(sum_levels(place, send_levels(place, jnp.concatenate([first, second]))))


def send_levels(place, levels):
    slots = [None] * LEVELS
    slots[0] = pick(levels, place.z, 0)
    for k in (3, 2, 1):
        slots[k] = flip(pick(levels, place.z ^ k, 0).astype(BF), "wide", k * place.stride)
    return slots


def sum_levels(place, slots):
    tower0 = sum(jnp.where(place.z == k, 0.0, slots[k].astype(F32)) for k in range(LEVELS))
    tower1 = sum(jnp.where(place.z == k, slots[k].astype(F32), 0.0) for k in range(LEVELS))
    return tower0, tower1


def share_kernel(at_ref, keep_ref, got_ref, own_ref, *sent_refs):
    x, y = at_ref[0], at_ref[1]

    def share(dx, dy):
        at = (x ^ dx, 0, y ^ dy)
        return keep_ref[at].astype(F32) + got_ref[at].astype(F32)

    own_ref[0] = share(0, 0)
    for ref, (dx, dy) in zip(sent_refs, OTHERS):
        ref[0] = share(dx, dy).astype(BF)


def column_shares(place, keep, got):
    r, c = got.shape[2:]
    block = pl.BlockSpec((2, 1, place.stride, r, c), lambda i, at: (0, i, 0, 0, 0))
    out = pl.BlockSpec((1, r, c), lambda i, at: (i, 0, 0))
    shape = (2, LEVELS, place.stride, r, c)
    return pl.pallas_call(
        share_kernel,
        grid_spec=pltpu.PrefetchScalarGridSpec(
            num_scalar_prefetch=1, grid=(LEVELS,), in_specs=[block] * 2, out_specs=[out] * 4
        ),
        out_shape=[jax.ShapeDtypeStruct((LEVELS, r, c), F32)]
        + [jax.ShapeDtypeStruct((LEVELS, r, c), BF)] * 3,
        compiler_params=pltpu.CompilerParams(vmem_limit_bytes=VMEM),
        cost_estimate=cost(1),
    )(jnp.stack([place.n // 2, place.y]), keep.reshape(shape), got.reshape(shape))


def send_columns(shares):
    return [shares[0]] + [
        flip_both(sent, dy, 2 * dx) for sent, (dx, dy) in zip(shares[1:], OTHERS)
    ]


def level_kernel(z_ref, own_ref, *refs):
    got_refs, (sum_ref, *sent_refs) = refs[:3], refs[3:]
    for k in range(LEVELS):
        at = z_ref[0] ^ k
        total = own_ref[at]
        for ref in got_refs:
            total = total + ref[at].astype(F32)
        if k == 0:
            sum_ref[...] = total
        else:
            sent_refs[k - 1][...] = total.astype(BF)


def level_shares(place, columns):
    r, c = columns[0].shape[1:]
    vmem = pl.BlockSpec(memory_space=pltpu.VMEM)
    return pl.pallas_call(
        level_kernel,
        in_specs=[pl.BlockSpec(memory_space=pltpu.SMEM)] + [vmem] * 4,
        out_specs=[vmem] * 4,
        out_shape=[jax.ShapeDtypeStruct((r, c), F32)] + [jax.ShapeDtypeStruct((r, c), BF)] * 3,
        compiler_params=pltpu.CompilerParams(vmem_limit_bytes=VMEM),
        cost_estimate=cost(1),
    )(place.z.reshape(1), *columns)


def level_sums_kernel(*refs):
    for at in range(LEVELS):
        refs[-1][at] = sum(ref[at].astype(F32) for ref in refs[:-1]).astype(BF)


def level_sums(columns):
    shape = columns[0].shape
    return calls(level_sums_kernel, [(shape, BF)], 3)(*columns)[0]


def swap_shares(place, shares):
    slots = [shares[0], None, None, None]
    for k in (3, 2, 1):
        slots[k] = flip(shares[k], "wide", k * place.stride)
    return slots


def product_kernel(step, me_ref, *refs):
    send_ref, keep_ref = refs[-2:]
    left_refs = refs[:-2]
    to_send = pl.program_id(0) < 2

    @pl.when(to_send)
    def _():
        step(left_refs, lambda at, v: send_ref.__setitem__((0, *at), v.astype(BF)))

    @pl.when(jnp.logical_not(to_send))
    def _():
        step(left_refs, lambda at, v: keep_ref.__setitem__((0, *at), v.astype(BF)))


def products(place, step, operands, specs, block):
    def target(j, me):
        return (j % 2) * 2 + jnp.where(j < 2, 1 - me[0] % 2, me[0] % 2)

    wide = place.wide
    grid_spec = pltpu.PrefetchScalarGridSpec(
        num_scalar_prefetch=1,
        grid=(4,),
        in_specs=specs(target),
        out_specs=[
            pl.BlockSpec((1, wide, *block), lambda j, me: (jnp.minimum(j, 1), 0, 0, 0)),
            pl.BlockSpec((1, wide, *block), lambda j, me: (jnp.maximum(j - 2, 0), 0, 0, 0)),
        ],
    )
    return pl.pallas_call(
        functools.partial(product_kernel, step),
        grid_spec=grid_spec,
        out_shape=[
            jax.ShapeDtypeStruct((2, wide, *block), BF),
            jax.ShapeDtypeStruct((2, wide, *block), BF),
        ],
        compiler_params=pltpu.CompilerParams(vmem_limit_bytes=VMEM),
        cost_estimate=cost(8),
    )(place.n.reshape(1), *operands)


def whole(shape):
    return pl.BlockSpec(shape, lambda j, me: (0,) * len(shape))


def grad_blocks(left, right, narrow):
    out = inner_rows(left, right)
    return out.reshape(out.shape[0], narrow, -1)


def products_back_kernel(core_ref, left_ref, right_ref, send_ref, keep_ref, turned_ref):
    @pl.when(pl.program_id(0) == 0)
    def _():
        turned_ref[...] = right_ref[...].T

    value = matmul(turned_ref[...], left_ref[...]).astype(BF)
    cols = send_ref.shape[2]
    first = core_ref[0] == 0
    for x in range(2):
        even = value[2 * x * cols : (2 * x + 1) * cols]
        odd = value[(2 * x + 1) * cols : (2 * x + 2) * cols]
        keep_ref[x, 0] = jnp.where(first, even, odd)
        send_ref[x, 0] = jnp.where(first, odd, even)


def products_back(place, active, grad_ffn):
    t, ff = active.shape
    d = grad_ffn.shape[1]
    cols, rows = d // place.narrow, ff // place.wide
    out = pl.BlockSpec((2, 1, cols, rows), lambda j, core: (0, j, 0, 0))
    return pl.pallas_call(
        products_back_kernel,
        grid_spec=pltpu.PrefetchScalarGridSpec(
            num_scalar_prefetch=1,
            grid=(place.wide,),
            in_specs=[pl.BlockSpec((t, rows), lambda j, core: (0, j)), whole((t, d))],
            out_specs=[out, out],
            scratch_shapes=[pltpu.VMEM((d, t), BF)],
        ),
        out_shape=[jax.ShapeDtypeStruct((2, place.wide, cols, rows), BF)] * 2,
        compiler_params=pltpu.CompilerParams(vmem_limit_bytes=VMEM),
        cost_estimate=cost(7),
    )((place.n % 2).reshape(1), active, grad_ffn)


def finish_back(levels):
    levels = levels.astype(F32)
    return jnp.stack([(levels[1] + levels[2] + levels[3]).T, levels[0].T])


def products_out_in(place, context, blocks, normed, grad_hidden):
    narrow = place.narrow
    t, d = context.shape
    rows = d // place.wide
    cols_out, cols_in = blocks.shape[2], grad_hidden.shape[1] // narrow
    fold = cols_in // cols_out
    low = rows // fold

    def step(refs, store):
        context_ref, branch_ref, normed_ref, hidden_ref = refs
        value = inner_rows(normed_ref[...], hidden_ref[...])
        for w in range(place.wide):
            store((w, slice(0, rows)), value[w * rows : (w + 1) * rows])
        value = inner_rows(context_ref[...], branch_ref[0])
        for w in range(place.wide):
            for g in range(fold):
                store(
                    (w, slice(rows, rows + low), slice(g * cols_out, (g + 1) * cols_out)),
                    value[w * rows + g * low : w * rows + (g + 1) * low],
                )

    return products(
        place,
        step,
        (context, blocks, normed, grad_hidden),
        lambda target: [
            whole((t, d)),
            pl.BlockSpec((1, t, cols_out), lambda j, me: (target(j, me), 0, 0)),
            whole((t, d)),
            pl.BlockSpec((t, cols_in), lambda j, me: (0, target(j, me))),
        ],
        (rows + low, cols_in),
    )


def finish_out_in(place, slots, rows):
    parts = sum_levels(place, slots)
    low, cols = parts[0].shape[0] - rows, parts[0].shape[1]
    fold = rows // low
    grad_in = jnp.stack([part[:rows] for part in parts])
    grad_out = [
        jnp.moveaxis(part[rows:].reshape(low, fold, -1), 1, 0).reshape(rows, -1) for part in parts
    ]
    return jnp.stack(grad_out), grad_in


def products_qkv(place, inputs, blocks):
    t, d = inputs.shape
    rows, cols = d // place.wide, blocks.shape[2]
    half = rows // 2

    def step(refs, store):
        left, right = refs
        value = inner_rows(left[...], right[0])
        for w in range(place.wide):
            for g in range(2):
                store(
                    (w, slice(None), slice(g * cols, (g + 1) * cols)),
                    value[w * rows + g * half : w * rows + (g + 1) * half],
                )

    return products(
        place,
        step,
        (inputs, blocks),
        lambda target: [
            whole((t, d)),
            pl.BlockSpec((1, t, cols), lambda j, me: (target(j, me), 0, 0)),
        ],
        (half, 2 * cols),
    )


def finish_qkv(place, slots):
    parts = sum_levels(place, slots)
    cols = parts[0].shape[1] // 2
    return jnp.stack([jnp.concatenate([p[:, :cols], p[:, cols:]]) for p in parts])


def attend_kernel(x_ref, w_ref, rows_ref, seg_row_ref, seg_col_ref, qkv_ref, ctx_ref, lse_ref):
    x = x_ref[...]
    same = seg_col_ref[...] == seg_row_ref[...]

    def project(part, carry):
        bias = jnp.where(part == 0, rows_ref[0:1], jnp.where(part == 2, rows_ref[1:2], 0.0))
        qkv_ref[part] = (matmul(x, w_ref[part]) + bias).astype(BF)
        return carry

    lax.fori_loop(0, 3, project, 0)

    def pair(p, carry):
        at = pl.ds(pl.multiple_of(p * 2 * HEAD_DIM, 2 * HEAD_DIM), 2 * HEAD_DIM)
        queries, keys, values = qkv_ref[0, :, at], qkv_ref[1, :, at], qkv_ref[2, :, at]
        contexts = []
        for h in range(2):
            lanes = slice(h * HEAD_DIM, (h + 1) * HEAD_DIM)
            q, k, v = queries[:, lanes], keys[:, lanes], values[:, lanes]
            scores = jnp.where(same, inner_cols(k, q) * HEAD_DIM ** (-0.5), MASKED)
            top = jnp.max(scores, axis=0, keepdims=True)
            shifted = jnp.exp(scores - top)
            total = jnp.sum(shifted, axis=0, keepdims=True)
            probs = (shifted * (1.0 / total)).astype(BF)
            contexts.append(inner_rows(probs, v).astype(BF))
            lse_ref[0, pl.ds(2 * p + h, 1), :] = top + jnp.log(total)
        ctx_ref[:, at] = jnp.concatenate(contexts, axis=1)
        return carry

    lax.fori_loop(0, GROUP // 2, pair, 0)


def attend(x, w_qkv, rows, segment):
    t, d = x.shape
    width = GROUP * HEAD_DIM
    steps = d // width
    return pl.pallas_call(
        attend_kernel,
        grid=(steps,),
        in_specs=[
            pl.BlockSpec((t, d), lambda j: (0, 0)),
            pl.BlockSpec((3, d, width), lambda j: (0, 0, j)),
            pl.BlockSpec((8, width), lambda j: (0, j)),
            pl.BlockSpec((1, t), lambda j: (0, 0)),
            pl.BlockSpec((t, 1), lambda j: (0, 0)),
        ],
        out_specs=[
            pl.BlockSpec((3, t, width), lambda j: (0, 0, j)),
            pl.BlockSpec((t, width), lambda j: (0, j)),
            pl.BlockSpec((1, GROUP, t), lambda j: (j, 0, 0)),
        ],
        out_shape=[
            jax.ShapeDtypeStruct((3, t, d), BF),
            jax.ShapeDtypeStruct((t, d), BF),
            jax.ShapeDtypeStruct((steps, GROUP, t), F32),
        ],
        compiler_params=pltpu.CompilerParams(vmem_limit_bytes=VMEM),
        cost_estimate=cost(0.1),
    )(x, w_qkv, rows, segment.reshape(1, t), segment.reshape(t, 1))


def attend_back_kernel(
    gb_ref, w_ref, qkv_ref, lse_ref, seg_row_ref, seg_col_ref, out_ref, blocks_ref, sums_ref, grad_ref
):
    scale = HEAD_DIM ** (-0.5)
    same = seg_col_ref[...] == seg_row_ref[...]
    grad_ref[...] = inner_cols(gb_ref[...], w_ref[...]).astype(BF)

    def pair(p, carry):
        at = pl.ds(pl.multiple_of(p * 2 * HEAD_DIM, 2 * HEAD_DIM), 2 * HEAD_DIM)
        queries, keys, values = qkv_ref[0, :, at], qkv_ref[1, :, at], qkv_ref[2, :, at]
        grads, outs = grad_ref[:, at], []
        for h in range(2):
            lanes = slice(h * HEAD_DIM, (h + 1) * HEAD_DIM)
            q, k, v, g = queries[:, lanes], keys[:, lanes], values[:, lanes], grads[:, lanes]
            scores = jnp.where(same, inner_cols(k, q) * scale, MASKED)
            probs = jnp.exp(scores - lse_ref[0, pl.ds(2 * p + h, 1), :])
            grad_probs = inner_cols(v, g)
            delta = jnp.sum(probs * grad_probs, axis=0, keepdims=True)
            grad_scores = (probs * (grad_probs - delta)).astype(BF)
            outs.append(
                (
                    (inner_rows(grad_scores, k) * scale).astype(BF),
                    (matmul(grad_scores, q) * scale).astype(BF),
                    matmul(probs.astype(BF), g).astype(BF),
                )
            )
        for part in range(3):
            out_ref[part, :, at] = jnp.concatenate([outs[0][part], outs[1][part]], axis=1)
        return carry

    lax.fori_loop(0, GROUP // 2, pair, 0)
    sums_ref[0:1] = jnp.sum(out_ref[0].astype(F32), axis=0, keepdims=True)
    sums_ref[1:2] = jnp.sum(out_ref[2].astype(F32), axis=0, keepdims=True)
    per_block = blocks_ref.shape[2] // HEAD_DIM
    heads = blocks_ref.shape[0] * per_block // 3
    for step in range(heads // GROUP):

        @pl.when(pl.program_id(0) == step)
        def _(step=step):
            for part in range(3):
                for h in range(GROUP):
                    block, at = divmod(part * heads + step * GROUP + h, per_block)
                    blocks_ref[block, :, at * HEAD_DIM : (at + 1) * HEAD_DIM] = out_ref[
                        part, :, h * HEAD_DIM : (h + 1) * HEAD_DIM
                    ]


def attend_back(grad_branch, w_out, qkv, lse, segment, narrow):
    t, d = grad_branch.shape
    width = GROUP * HEAD_DIM
    return pl.pallas_call(
        attend_back_kernel,
        grid=(d // width,),
        in_specs=[
            pl.BlockSpec((t, d), lambda j: (0, 0)),
            pl.BlockSpec((width, d), lambda j: (j, 0)),
            pl.BlockSpec((3, t, width), lambda j: (0, 0, j)),
            pl.BlockSpec((1, GROUP, t), lambda j: (j, 0, 0)),
            pl.BlockSpec((1, t), lambda j: (0, 0)),
            pl.BlockSpec((t, 1), lambda j: (0, 0)),
        ],
        out_specs=[
            pl.BlockSpec((3, t, width), lambda j: (0, 0, j)),
            pl.BlockSpec((narrow, t, 3 * d // narrow), lambda j: (0, 0, 0)),
            pl.BlockSpec((2, width), lambda j: (0, j)),
        ],
        out_shape=[
            jax.ShapeDtypeStruct((3, t, d), BF),
            jax.ShapeDtypeStruct((narrow, t, 3 * d // narrow), BF),
            jax.ShapeDtypeStruct((2, d), F32),
        ],
        scratch_shapes=[pltpu.VMEM((t, width), BF)],
        compiler_params=pltpu.CompilerParams(vmem_limit_bytes=VMEM),
        cost_estimate=cost(20),
    )(grad_branch, w_out, qkv, lse, segment.reshape(1, t), segment.reshape(t, 1))


def hidden_kernel(x_ref, w_ref, bias_ref, active_ref, slope_ref, pre_ref):
    pre_ref[...] = matmul(x_ref[...], w_ref[0]) + bias_ref[...]

    def body(at, carry):
        pre = pre_ref[at]
        below = 0.5 + 0.5 * lax.erf(pre * 0.5**0.5)
        active_ref[at] = (pre * below).astype(BF)
        density = jnp.exp(-0.5 * pre * pre) * (2.0 * math.pi) ** (-0.5)
        slope_ref[at] = (below + pre * density).astype(BF)
        return carry

    by_rows(pre_ref.shape[0], body)


def hidden_layer(x, w_in, in_bias):
    t, d = x.shape
    parts, _, width = w_in.shape
    block = pl.BlockSpec((t, width), lambda j: (0, j))
    shape = jax.ShapeDtypeStruct((t, parts * width), BF)
    return pl.pallas_call(
        hidden_kernel,
        grid=(parts,),
        in_specs=[
            pl.BlockSpec((t, d), lambda j: (0, 0)),
            pl.BlockSpec((1, d, width), lambda j: (j, 0, 0)),
            pl.BlockSpec((1, width), lambda j: (0, j)),
        ],
        out_specs=[block, block],
        out_shape=[shape, shape],
        scratch_shapes=[pltpu.VMEM((t, width), F32)],
        compiler_params=pltpu.CompilerParams(vmem_limit_bytes=VMEM),
        cost_estimate=cost(8),
    )(x, w_in, in_bias)


def norm_parts(value):
    mean = jnp.mean(value, axis=-1, keepdims=True)
    centered = value - mean
    scale = lax.rsqrt(jnp.mean(centered * centered, axis=-1, keepdims=True) + EPSILON)
    return centered * scale, scale


def norm_back(grad, unit, scale, gain):
    e = grad * gain
    part = jnp.mean(e * unit, axis=-1, keepdims=True)
    return (e - jnp.mean(e, axis=-1, keepdims=True) - unit * part) * scale


def total(value):
    return jnp.sum(jnp.sum(value, axis=0, keepdims=True), axis=1, keepdims=True)


def column_sum(value):
    return jnp.sum(value, axis=0, keepdims=True)


def by_rows(count, body, carry=None):
    if carry is None:
        carry = jnp.zeros((1, 128), F32)
    return lax.fori_loop(
        0, count // STEP, lambda i, c: body(pl.ds(pl.multiple_of(i * STEP, STEP), STEP), c), carry
    )


def store_blocks(ref, at, value):
    count, _, width = ref.shape
    for i in range(count):
        ref[i, at] = value[:, i * width : (i + 1) * width]


def calls(kernel, outs, us, **kwargs):
    return pl.pallas_call(
        kernel,
        out_shape=[jax.ShapeDtypeStruct(shape, dtype) for shape, dtype in outs],
        compiler_params=pltpu.CompilerParams(vmem_limit_bytes=VMEM),
        cost_estimate=cost(us),
        **kwargs,
    )


def branch_kernel(ctx, w, x, rows, valid, normed, low, unit, scale, stats, acc):
    acc[...] = matmul(ctx[...], w[0])
    zero = jnp.zeros((1, acc.shape[1]), F32)

    def body(at, sums):
        branch = acc[at] + rows[2:3]
        residual = x[at].astype(F32) + branch
        unit[at], scale[at] = norm_parts(residual)
        normed[at] = unit[at] * rows[6:7] + rows[3:4]
        low[at] = normed[at].astype(BF)
        return tuple(
            s + column_sum(valid[at] * value * value) for s, value in zip(sums, (residual, branch))
        )

    for i, value in enumerate(by_rows(acc.shape[0], body, (zero, zero))):
        stats[i : i + 1] = jnp.broadcast_to(total(value), (1, 128))


def branch_layer(context, w_out, inputs, rows, valid):
    t, d = inputs.shape
    outs = [((t, d), F32), ((t, d), BF), ((t, d), F32), ((t, 1), F32), ((2, 128), F32)]
    scratch = [pltpu.VMEM((t, d), F32)]
    return calls(branch_kernel, outs, 5, scratch_shapes=scratch)(
        context, w_out, inputs, rows, valid
    )


def output_kernel(plan, level, me_ref, active, normed, rows, valid, hot, *refs):
    pieces = refs[:-8]
    low, unit, scale, pooled, stats, w, acc, sems = refs[-8:]
    step = pl.program_id(0)
    width = active.shape[1]
    block = pieces[0].shape[1]

    @pl.when(step == 0)
    def _():
        copies = []
        if plan is None:
            copies.append(pltpu.make_async_copy(pieces[0], w, sems.at[0]))
        for piece, masks in zip(pieces, plan or []):
            for slot, mask in enumerate(masks):
                at = pl.multiple_of(block_of(me_ref[0], mask, level) * block, block)
                target = w.at[pl.ds(at, block)]
                copies.append(
                    pltpu.make_async_copy(piece.at[slot], target, sems.at[len(copies)])
                )
        for copy in copies:
            copy.start()
        for copy in copies:
            copy.wait()

    product = matmul(active[...], w[pl.ds(pl.multiple_of(step * width, width), width)])

    @pl.when(step == 0)
    def _():
        acc[...] = product

    @pl.when(step > 0)
    def _():
        acc[...] += product

    @pl.when(step == pl.num_programs(0) - 1)
    def _():
        zero = jnp.zeros((1, acc.shape[1]), F32)

        def body(at, sums):
            ffn_out = acc[at] + rows[4:5]
            residual = normed[at] + ffn_out
            unit[at], scale[at] = norm_parts(residual)
            low[at] = (unit[at] * rows[7:8] + rows[5:6]).astype(BF)
            values = (valid[at] * residual * residual, valid[at] * ffn_out * ffn_out)
            return tuple(s + column_sum(value) for s, value in zip(sums, values))

        sums = by_rows(acc.shape[0], body, (zero, zero))
        for i, value in enumerate((*sums, valid[...])):
            stats[i : i + 1] = jnp.broadcast_to(total(value), (1, 128))
        pooled[...] = matmul(hot[...].astype(BF), low[...]).astype(BF)


def all_of(shape):
    return pl.BlockSpec(shape, lambda j: (0,) * len(shape))


def output_layer(place, active, pieces, plan, normed, rows, valid, hot):
    t, ff = active.shape
    d = normed.shape[1]
    outs = [((t, d), BF), ((t, d), F32), ((t, 1), F32), ((hot.shape[0], d), BF), ((3, 128), F32)]
    outs.append(((ff, d), BF))
    return calls(
        functools.partial(output_kernel, plan, place.wide * place.narrow // LEVELS),
        outs,
        9,
        grid=(ff // d,),
        in_specs=[pl.BlockSpec(memory_space=pltpu.SMEM), pl.BlockSpec((t, d), lambda j: (0, j))]
        + [all_of(a.shape) for a in (normed, rows, valid, hot)]
        + [pl.BlockSpec(memory_space=pl.ANY)] * len(pieces),
        out_specs=[all_of(shape) for shape, _ in outs],
        scratch_shapes=[
            pltpu.VMEM((t, d), F32),
            pltpu.SemaphoreType.DMA((place.wide * place.narrow,)),
        ],
    )(place.me.reshape(1), active, normed, rows, valid, hot, *pieces)


def output_back_kernel(cot, valid, hot, pool, unit, scale, rows, grad, low, sums):
    zero = jnp.zeros((1, grad.shape[1]), F32)

    def body(at, totals):
        grad_out = cot[at].astype(F32) * valid[at] + lax.dot_general(
            hot[:, at],
            pool[...],
            (((0,), (0,)), ((), ())),
            precision=lax.Precision.HIGHEST,
            preferred_element_type=F32,
        )
        grad[at] = norm_back(grad_out, unit[at], scale[at], rows[7:8])
        low[at] = grad[at].astype(BF)
        values = (grad_out * unit[at], grad_out, low[at].astype(F32))
        return tuple(t + column_sum(value) for t, value in zip(totals, values))

    for i, value in enumerate(by_rows(grad.shape[0], body, (zero,) * 3)):
        sums[i : i + 1] = value


def output_back(cot, valid, hot, pool, unit, scale, rows):
    t, d = cot.shape
    outs = [((t, d), F32), ((t, d), BF), ((3, d), F32)]
    return calls(output_back_kernel, outs, 6)(cot, valid, hot, pool, unit, scale, rows)


def hidden_back_kernel(
    low, w_back, slope, w_in, grad, unit, scale, rows, hidden, inb, residual, branch, blocks, sums, acc
):
    step = pl.program_id(0)
    product = inner_cols(low[...], w_back[...])
    hidden[...] = (product * slope[...].astype(F32)).astype(BF)
    inb[...] = column_sum(hidden[...].astype(F32))
    product = inner_cols(hidden[...], w_in[0])

    @pl.when(step == 0)
    def _():
        acc[...] = grad[...] + product

    @pl.when(step > 0)
    def _():
        acc[...] += product

    @pl.when(step == pl.num_programs(0) - 1)
    def _():
        zero = jnp.zeros((1, acc.shape[1]), F32)

        def body(at, totals):
            value = acc[at]
            residual[at] = norm_back(value, unit[at], scale[at], rows[6:7])
            branch[at] = residual[at].astype(BF)
            store_blocks(blocks, at, branch[at])
            values = (value * unit[at], value, branch[at].astype(F32))
            return tuple(t + column_sum(value) for t, value in zip(totals, values))

        for i, value in enumerate(by_rows(acc.shape[0], body, (zero,) * 3)):
            sums[i : i + 1] = value


def hidden_back(low, w_back, slope, w_in, grad, unit, scale, rows, narrow):
    t, d = low.shape
    ff = slope.shape[1]
    tile = pl.BlockSpec((t, d), lambda j: (0, j))
    outs = [
        ((t, ff), BF),
        ((1, ff), F32),
        ((t, d), F32),
        ((t, d), BF),
        ((narrow, t, d // narrow), BF),
        ((3, d), F32),
    ]
    return calls(
        hidden_back_kernel,
        outs,
        14,
        grid=(ff // d,),
        in_specs=[
            all_of(low.shape),
            pl.BlockSpec((d, d), lambda j: (j, 0)),
            tile,
            pl.BlockSpec((1, d, d), lambda j: (j, 0, 0)),
        ]
        + [all_of(a.shape) for a in (grad, unit, scale, rows)],
        out_specs=[tile, pl.BlockSpec((1, d), lambda j: (0, j))]
        + [all_of(shape) for shape, _ in outs[2:]],
        scratch_shapes=[pltpu.VMEM((t, d), F32)],
    )(low, w_back, slope, w_in, grad, unit, scale, rows)


def input_back_kernel(grad, w, residual, out, acc):
    step = pl.program_id(0)
    product = inner_cols(grad[0], w[0])

    @pl.when(step == 0)
    def _():
        acc[...] = residual[...] + product

    @pl.when(step == 1)
    def _():
        acc[...] += product

    @pl.when(step == 2)
    def _():
        out[...] = (acc[...] + product).astype(BF)


def input_back(grad_qkv, w_qkv, residual):
    _, t, d = grad_qkv.shape
    return calls(
        input_back_kernel,
        [((t, d), BF)],
        6,
        grid=(3,),
        in_specs=[
            pl.BlockSpec((1, t, d), lambda j: (j, 0, 0)),
            pl.BlockSpec((1, d, d), lambda j: (j, 0, 0)),
            all_of((t, d)),
        ],
        out_specs=[all_of((t, d))],
        scratch_shapes=[pltpu.VMEM((t, d), F32)],
    )(grad_qkv, w_qkv, residual)[0]


def spread_masks(count, width):
    total_cols = count * width
    column = lax.broadcasted_iota(jnp.int32, (count, total_cols), 1)
    first = lax.broadcasted_iota(jnp.int32, (count, total_cols), 0) * width
    own = (column >= first) & (column < first + width)
    owner = jnp.sum(jnp.where(own, first, 0), axis=0, keepdims=True)
    within = lax.broadcasted_iota(jnp.int32, (width, total_cols), 1) - owner
    spread = within == lax.broadcasted_iota(jnp.int32, (width, total_cols), 0)
    return own, spread.astype(F32)


def unpack_kernel(small, rows, inb):
    count = small.shape[0]
    value = small[...].astype(F32)

    def unpack(part, masks):
        own, spread = masks
        placed = matmul(part.astype(BF), spread.astype(BF))
        return column_sum(jnp.where(own, placed, 0.0))

    width = rows.shape[1] // count
    masks = spread_masks(count, width)
    for r in range(8):
        rows[r : r + 1] = unpack(value[:, r, :width], masks)
    width = inb.shape[1] // count
    inb[...] = unpack(value[:, 0, 128 : 128 + width], spread_masks(count, width))


def unpack_params(small, d, ff):
    return calls(unpack_kernel, [((8, d), F32), ((1, ff), F32)], 0.1)(small)


def pack_kernel(attn, out, ffn, inb, stats_a, stats_b, packed, rows, parts):
    count = packed.shape[0]
    vectors = (attn[0:1], attn[1:2], out[2:3], out[1:2], ffn[2:3], ffn[1:2], out[0:1], ffn[0:1])

    def pack(vector, own, spread):
        return lax.dot_general(
            jnp.where(own, vector, 0.0),
            spread,
            (((1,), (1,)), ((), ())),
            precision=lax.Precision.HIGHEST,
            preferred_element_type=F32,
        )

    for i, vector in enumerate(vectors):
        rows[i : i + 1] = vector
    packed[...] = jnp.zeros(packed.shape, F32)
    width = rows.shape[1] // count
    masks = spread_masks(count, width)

    def body(i, carry):
        parts[i] = pack(rows[pl.ds(i, 1)], *masks)
        return carry

    lax.fori_loop(0, len(vectors), body, 0)
    for i in range(len(vectors)):
        packed[:, i * width : (i + 1) * width] = parts[i]
    at = len(vectors) * width
    width = inb.shape[1] // count
    packed[:, at : at + width] = pack(inb[...], *spread_masks(count, width))
    at += width
    for i, row in enumerate((stats_a[0:1], stats_a[1:2], stats_b[0:1], stats_b[1:2], stats_b[2:3])):
        packed[:, at + i : at + i + 1] = jnp.broadcast_to(row[:, :1], (count, 1))


def pack_sums(count, attn, out, ffn, inb, stats_a, stats_b):
    width = attn.shape[1]
    scratch = [pltpu.VMEM((8, width), F32), pltpu.VMEM((8, count, width // count), F32)]
    return calls(pack_kernel, [((count, 384), F32)], 4, scratch_shapes=scratch)(
        attn, out, ffn, inb, stats_a, stats_b
    )[0]


def match_grads(rows, label_rows, label_cols):
    is_query, is_pass = label_rows >= 0, label_cols >= 0
    match = jnp.where(is_pass, inner_cols(rows, rows) / SCORE_DIV, MASKED)
    shifted = jnp.exp(match - jnp.max(match, axis=1, keepdims=True))
    probs = shifted / jnp.sum(shifted, axis=1, keepdims=True)
    hot = (label_rows == label_cols).astype(F32)
    grad = jnp.where(is_query & is_pass, (probs - hot) / SCORE_DIV, 0.0).astype(BF)
    return matmul(grad[:POOL], rows) + inner_rows(grad[:, :POOL], rows)


def match_kernel(rows, label_rows, label_cols, out):
    out[...] = match_grads(rows[...], label_rows[...], label_cols[...])


def row_of(z, y, n, s):
    own = (z * s + y) * 3 + n
    spare = y * 3 + (z - 1)
    return jnp.where(z == 0, n * s + y, jnp.where(n < 3, own, spare))


def body(
    passages,
    queries,
    passage_cot,
    query_cot,
    passage_lengths,
    query_lengths,
    labels,
    w_qkv,
    w_out,
    w_in,
    w_back,
    biases,
    norm_gains,
    in_bias,
):
    place = Place()
    s, narrow, devices = place.stride, place.narrow, place.wide * place.narrow
    model_width = passages.shape[2]
    length = passages.shape[1] * narrow
    segs, qsegs = passage_lengths.shape[1] - 1, query_lengths.shape[1] - 1
    on_query = place.z == 0

    piece = model_width // devices
    whole = jnp.concatenate(
        [passage_lengths.reshape(-1), query_lengths.reshape(-1), labels.reshape(-1)]
    )
    whole = jnp.concatenate([whole // 32, whole % 32]).astype(BF)

    w_rows, in_parts = w_out.shape[1], w_in.shape[2] // w_out.shape[2]
    swapped = swap_in_directly(place, passages, queries)
    if s == 2:
        swapped[0], w_qkv = phase(swapped[0], w_qkv)
        towers = pick_towers(place, w_qkv, biases, norm_gains, in_bias, whole)
        got = {k: flip(towers[k], "wide", k * s) for k in (3, 2, 1)}
        levels_qkv = jnp.stack([towers[0], got[1], got[2], got[3]])
        own = [k * s * narrow for k in range(LEVELS)]
        layout = [(0, part, part * w_rows, 0) for part in range(3)] + [(1, 0, 3 * w_rows, 0)]
        shapes = [(3, w_rows, model_width), (1, 8, model_width)]
    else:
        small = jnp.concatenate(
            [biases.reshape(2, -1), norm_gains.reshape(2, -1), in_bias.reshape(2, -1)], axis=1
        )
        small_count = small.shape[1]
        small = jnp.concatenate([small, jnp.broadcast_to(whole, (2, whole.shape[0]))], axis=1)
        to_query = (jnp.arange(devices) < s * narrow)[:, None]
        small = lax.all_to_all(
            jnp.where(to_query, small[1][None], small[0][None]), BOTH, 0, 0, tiled=True
        )
        levels_qkv, own = gather_levels(place, w_qkv), None
        layout = [(0, part, 0, part * model_width) for part in range(3)]
        shapes = [(3, w_rows, model_width)]
    out_in = jnp.concatenate([w_out, w_in], axis=2)
    levels_qkv, swapped, out_in = phase(levels_qkv, swapped, out_in)

    pieces_qkv, plan = gather_columns(place, levels_qkv, own)
    levels_out_in = gather_levels(place, out_in)
    pieces_qkv, levels_out_in, w_back = phase(pieces_qkv, levels_out_in, w_back)

    cores_qkv, core_plan = gather_cores(pieces_qkv, plan)
    cores_qkv, levels_out_in, swapped = phase(cores_qkv, levels_out_in, swapped)

    pieces_out_in, plan = gather_columns(place, levels_out_in)
    inputs = to_row(place, passages, queries, join_swapped(place, queries, swapped))
    inputs, w_back = phase(inputs, w_back)
    levels_back = gather_levels(place, w_back)
    made = assemble(place, cores_qkv, core_plan, layout, shapes)
    w_qkv_all = made[0]

    n_bias, n_gain = biases.shape[1], norm_gains.shape[1]
    ff = in_bias.shape[1] * devices
    if s == 2:
        small = made[1].reshape(devices, 8, -1)
        rows, inb_row = unpack_params(small, model_width, ff)
        ints = small[:, 0, 256 : 256 + whole.shape[0]].astype(F32)
    else:
        params = small[:, :small_count].astype(F32)
        vectors = params[:, : (n_bias + n_gain) * piece].reshape(devices, n_bias + n_gain, piece)
        rows = vectors.transpose(1, 0, 2).reshape(n_bias + n_gain, -1)
        inb_row = params[:, (n_bias + n_gain) * piece :].reshape(1, -1)
        ints = small[:, small_count : small_count + whole.shape[0]].astype(F32)
    half = ints.shape[1] // 2
    ints = (ints[::narrow, :half] * 32 + ints[::narrow, half:]).astype(jnp.int32)
    n_pass = passage_lengths.size
    n_query = query_lengths.size
    pass_lens = ints[:, :n_pass].reshape(-1, segs + 1)
    query_lens = ints[:, n_pass : n_pass + n_query].reshape(-1, qsegs + 1)
    label_all = ints[:, n_pass + n_query :].reshape(-1, qsegs)
    my_row = row_of(place.z, place.y, place.n, s)
    pass_row = pick(pass_lens, jnp.where(on_query, 0, my_row), 0)
    query_row = pick(query_lens, jnp.where(on_query, my_row, 0), 0)
    ends_p = jnp.cumsum(pass_row)[:-1]
    ends_q = jnp.cumsum(query_row)[:-1]
    starts_p, starts_q = ends_p - pass_row[:-1], ends_q - query_row[:-1]
    ends_p = jnp.concatenate([ends_p, jnp.full((qsegs - segs,), length + 1, jnp.int32)])
    ends = jnp.where(on_query, ends_q, ends_p)
    seg_count = jnp.where(on_query, qsegs, segs)
    position = jnp.arange(length, dtype=jnp.int32)
    segment = jnp.sum((position[:, None] >= ends[None, :]).astype(jnp.int32), axis=1)
    valid = (segment < seg_count).astype(F32)[:, None]
    slot = jnp.arange(POOL)
    starts = jnp.where(on_query, jnp.concatenate([starts_q, jnp.full((qsegs,), -1)]), -1)
    for z in range(1, LEVELS):
        here = (place.z == z) & (slot >= qsegs + segs * (z - 1)) & (slot < qsegs + segs * z)
        starts = jnp.where(here, jnp.tile(starts_p, POOL // segs), starts)
    hot = (starts[:, None] == position[None, :]).astype(F32)
    masks = [0]
    if s == 2:
        masks += [dy * narrow + 2 * dx for dx, dy in OTHERS]
        masks += [m ^ 1 for m in masks]
    else:
        for mask in [b * narrow for b in bits_of(s)] + [b for b in reversed(bits_of(narrow))]:
            masks = masks + [m ^ mask for m in masks]
    there = (place.y * narrow + place.n) ^ jnp.array(masks, jnp.int32)
    their_y, their_n = there // narrow, there % narrow
    label_rows = label_all[row_of(jnp.int32(0), their_y, their_n, s)]
    label_rows = jnp.pad(label_rows, ((0, 0), (0, POOL - qsegs)), constant_values=-1)
    levels = jnp.arange(1, LEVELS)
    pass_rows = row_of(levels[None, :], their_y[:, None], their_n[:, None], s)
    pass_ids = (pass_rows[:, :, None] * segs + jnp.arange(segs)).reshape(len(masks), -1)
    spare = POOL - qsegs - pass_ids.shape[1]
    label_cols = jnp.pad(pass_ids, ((0, 0), (qsegs, spare)), constant_values=-1)
    label_rows, label_cols = label_rows.reshape(-1, 1), label_cols.reshape(1, -1)

    qkv, context, log_sum = attend(inputs, w_qkv_all, rows, segment)
    context, pieces_out_in, levels_back, cots = phase(
        context, pieces_out_in, levels_back, (passage_cot, query_cot)
    )

    cores_out_in, core_plan = gather_cores(pieces_out_in, plan)
    cores_out_in, levels_back, cots = phase(cores_out_in, levels_back, cots)

    pieces_back, plan = gather_columns(place, levels_back)
    swapped = swap_in(place, *cots)
    w_out_all, w_in_all = assemble(
        place,
        cores_out_in,
        core_plan,
        [(0, 0, 0, 0)] + [(1, part, 0, (part + 1) * model_width) for part in range(in_parts)],
        [(1, w_rows, model_width), (in_parts, w_rows, model_width)],
    )
    normed, normed_low, unit_one, scale_one, stats_one = branch_layer(
        context, w_out_all, inputs, rows, valid
    )
    active, slope = hidden_layer(normed_low, w_in_all, inb_row)
    active, pieces_back, swapped = phase(active, pieces_back, swapped)

    cores_back, core_plan = gather_cores(pieces_back, plan)
    cot = to_row(place, passage_cot, query_cot, swapped)
    if s != 2:
        back_shape = [(1, w_back.shape[1], model_width)]
        cores_back = assemble(place, cores_back, core_plan, [(0, 0, 0, 0)], back_shape)
        cores_back, core_plan = [cores_back[0][0]], None
    output_low, unit_two, scale_two, pooled, stats_two, w_back_all = output_layer(
        place, active, cores_back, core_plan, normed, rows, valid, hot
    )
    pooled, cot = phase(pooled, cot)

    column = sum([flip(pooled, "wide", k * s).astype(F32) for k in (3, 2, 1)], pooled.astype(F32))
    seen = column.astype(BF)[None]
    if s == 2:
        seen = jnp.concatenate([seen] + [flip_both(seen, dy, 2 * dx) for dx, dy in OTHERS])
        seen = jnp.concatenate([seen, flip(seen, "narrow", 1)])
    else:
        for axis, step in [("wide", b) for b in bits_of(s)] + [
            ("narrow", b) for b in reversed(bits_of(narrow))
        ]:
            seen = jnp.concatenate([seen, flip(seen, axis, step)])
    seen = seen.reshape(-1, model_width)
    if s == 2:
        (grad_pool,) = calls(match_kernel, [((POOL, model_width), F32)], 3)(
            seen, label_rows, label_cols
        )
    else:
        grad_pool = match_grads(seen, label_rows, label_cols)

    grad_pool, output_low = phase(grad_pool, output_low)
    if s == 2:
        out_four = row_pieces(place, output_low)
    grad_resid_two, grad_ffn, sums_two = output_back(
        cot, valid, hot, grad_pool, unit_two, scale_two, rows
    )
    if s == 2:
        send_c, keep_c = products_back(place, active, grad_ffn)
        send_c, out_four = phase(send_c, out_four)
        got_c = flip(send_c, "narrow", 1)
        shares_c = column_shares(place, keep_c, got_c)
        shares_c, grad_ffn = phase(shares_c, grad_ffn)

        columns_c = send_columns(shares_c)
        swapped = swap_out(place, out_four)
    grad_hidden, inb_sums, grad_residual, grad_branch, blocks_b, sums_one = hidden_back(
        grad_ffn, w_back_all, slope, w_in_all, grad_resid_two, unit_one, scale_one, rows, narrow
    )
    if s == 2:
        send_b, keep_b = products_out_in(place, context, blocks_b, normed_low, grad_hidden)
        send_b, columns_c, swapped = phase(send_b, columns_c, swapped)
        passage_out, query_out = from_row(place, out_four, swapped)

        got_b = flip(send_b, "narrow", 1)
        level_c = level_sums(columns_c)
        shares_b = column_shares(place, keep_b, got_b)
        shares_b, level_c, grad_branch = phase(shares_b, level_c, grad_branch)

        columns_b = send_columns(shares_b)
        levels_c = across_levels(level_c, s)
    grad_qkv, blocks_a, sums_qkv = attend_back(
        grad_branch, w_out_all[0], qkv, log_sum, segment, narrow
    )
    if s == 2:
        send_a, keep_a = products_qkv(place, inputs, blocks_a)
        send_a, grad_qkv, columns_b, levels_c = phase(send_a, grad_qkv, columns_b, levels_c)

        got_a = flip(send_a, "narrow", 1)
    input_grad = input_back(grad_qkv, w_qkv_all, grad_residual)
    if s == 2:
        got_a, input_grad, columns_b = phase(got_a, input_grad, columns_b)

        in_four = row_pieces(place, input_grad)
        levels_b = swap_shares(place, level_shares(place, columns_b))
        shares_a = column_shares(place, keep_a, got_a)
        shares_a, levels_b, in_four, sums_qkv, levels_c = phase(
            shares_a, levels_b, in_four, sums_qkv, levels_c
        )

        columns_a = send_columns(shares_a)
        swapped = swap_out(place, in_four)
        packed = pack_sums(devices, sums_qkv, sums_one, sums_two, inb_sums, stats_one, stats_two)
        grad_w_back = finish_back(levels_c)
        columns_a, swapped, packed = phase(columns_a, swapped, packed)

        packed = lax.all_to_all(packed, BOTH, 0, 0, tiled=True)
        levels_a = swap_shares(place, level_shares(place, columns_a))
        grad_w_out, grad_w_in = finish_out_in(place, levels_b, model_width // place.wide)
        passage_grad, query_grad = from_row(place, in_four, swapped)
        grad_w_qkv = finish_qkv(place, levels_a)
    else:
        packed = pack_sums(devices, sums_qkv, sums_one, sums_two, inb_sums, stats_one, stats_two)
        packed = lax.all_to_all(packed, BOTH, 0, 0, tiled=True)
        grad_w_back = scatter_tower(place, grad_blocks(active, grad_ffn, narrow))
        grad_w_out = scatter_tower(place, grad_blocks(context, grad_branch, narrow))
        grad_w_in = scatter_tower(place, grad_blocks(normed_low, grad_hidden, narrow))
        flat = jnp.moveaxis(grad_qkv, 0, 1).reshape(length, -1)
        grad_w_qkv = scatter_tower(place, grad_blocks(inputs, flat, narrow))
        out_four, in_four = row_pieces(place, output_low), row_pieces(place, input_grad)
        passage_out, query_out = from_row(place, out_four, swap_out(place, out_four))
        passage_grad, query_grad = from_row(place, in_four, swap_out(place, in_four))

    packed = packed.reshape(LEVELS, -1, packed.shape[1]).sum(axis=1)
    packed = jnp.stack([packed[1] + packed[2] + packed[3], packed[0]])
    edges = [n_bias * piece, (n_bias + n_gain) * piece]
    edges.append(edges[1] + in_bias.shape[1])
    grad_biases = packed[:, : edges[0]].reshape(2, n_bias, piece)
    grad_gains = packed[:, edges[0] : edges[1]].reshape(2, n_gain, piece)
    grad_inb = packed[:, edges[1] : edges[2]]
    totals = packed[:, edges[2] : edges[2] + 5]
    rms_stats = jnp.sqrt(totals[:, :4] / (totals[:, 4:] * model_width))
    return (
        passage_out,
        query_out,
        passage_grad,
        query_grad,
        grad_w_qkv,
        grad_w_out,
        grad_w_in,
        grad_w_back,
        grad_biases,
        grad_gains,
        grad_inb,
        rms_stats,
    )


def solution(mesh):
    return jax.shard_map(
        body,
        mesh=mesh,
        in_specs=(
            P("wide", "narrow", None),
            P("wide", "narrow", None),
            P("wide", "narrow", None),
            P("wide", "narrow", None),
            P("wide", None),
            P("wide", None),
            P("wide"),
            P(None, ("wide", "narrow"), None),
            P(None, ("wide", "narrow"), None),
            P(None, ("wide", "narrow"), None),
            P(None, ("wide", "narrow"), None),
            P(None, None, ("wide", "narrow")),
            P(None, None, ("wide", "narrow")),
            P(None, ("wide", "narrow")),
        ),
        out_specs=(
            P("wide", "narrow", None),
            P("wide", "narrow", None),
            P("wide", "narrow", None),
            P("wide", "narrow", None),
            P(None, "wide", "narrow"),
            P(None, "wide", "narrow"),
            P(None, "wide", "narrow"),
            P(None, "wide", "narrow"),
            P(None, None, ("wide", "narrow")),
            P(None, None, ("wide", "narrow")),
            P(None, ("wide", "narrow")),
            P(),
        ),
        check_vma=False,
    )
```

```python
import functools
import math

import jax
import jax.numpy as jnp
from jax import lax
from jax.experimental import pallas as pl
from jax.experimental.pallas import tpu as pltpu
from jax.sharding import PartitionSpec as P

HEAD_DIM = 64
LEVELS = 4
GROUP = 4
POOL = 32
STEP = 128
VMEM = 58 << 20
OTHERS = ((1, 1), (1, 0), (0, 1))


def cost(us):
    return pl.CostEstimate(flops=int(us * 1.15e9), bytes_accessed=1024, transcendentals=0)


EPSILON = 1e-05
SCORE_DIV = 12.0
MASKED = -1e30
BF = jnp.bfloat16
F32 = jnp.float32
BOTH = ("wide", "narrow")


def matmul(left, right):
    return jnp.dot(left, right, preferred_element_type=F32)


def inner_rows(left, right):
    return lax.dot_general(left, right, (((0,), (0,)), ((), ())), preferred_element_type=F32)


def inner_cols(left, right):
    return lax.dot_general(left, right, (((1,), (1,)), ((), ())), preferred_element_type=F32)


def flip(x, axis, mask):
    size = lax.axis_size(axis)
    return lax.ppermute(x, axis, [(i, i ^ mask) for i in range(size)])


def flip_both(x, wide_mask, narrow_mask):
    wide, narrow = lax.axis_size("wide"), lax.axis_size("narrow")
    mask = wide_mask * narrow + narrow_mask
    return lax.ppermute(x, BOTH, [(i, i ^ mask) for i in range(wide * narrow)])


def phase(*values):
    return lax.optimization_barrier(values)


def across_levels(x, stride):
    groups = [[k * stride + i for k in range(LEVELS)] for i in range(stride)]
    return lax.all_to_all(x, "wide", 0, 0, axis_index_groups=groups, tiled=True)


def swap_levels(x, k, stride):
    pairs = []
    for i in range(stride):
        pairs += [(i, k * stride + i), (k * stride + i, i)]
    return lax.ppermute(x, "wide", pairs)


def bits_of(size):
    return [1 << b for b in range(size.bit_length() - 1)]


class Place:
    def __init__(self):
        self.wide = lax.axis_size("wide")
        self.narrow = lax.axis_size("narrow")
        self.stride = self.wide // LEVELS
        self.w = lax.axis_index("wide")
        self.n = lax.axis_index("narrow")
        self.z = self.w // self.stride
        self.y = self.w % self.stride
        self.me = self.w * self.narrow + self.n


def swap_in(place, pass_part, query_part):
    query = jnp.broadcast_to(query_part, (LEVELS, *query_part.shape[1:]))
    first = jnp.concatenate([query_part, pass_part])
    return across_levels(jnp.where(place.z == 0, first, query), place.stride)


def swap_in_directly(place, pass_part, query_part):
    return [
        swap_levels(jnp.where(place.z == 0, pass_part[k - 1], query_part[0]), k, place.stride)
        for k in range(1, LEVELS)
    ]


def join_swapped(place, query_part, got):
    first = jnp.where(place.z == 0, query_part[0], got[0] + got[1] + got[2])
    return jnp.stack([first] + got)


def to_row(place, pass_part, query_part, got):
    four = jnp.where(place.z == 0, got, jnp.concatenate([pass_part, got[:1]]))
    mine = lax.all_to_all(four, "narrow", 0, 0, tiled=True)
    return mine.reshape(-1, mine.shape[-1])


def row_pieces(place, row):
    return lax.all_to_all(
        row.reshape(place.narrow, -1, row.shape[-1]), "narrow", 0, 0, tiled=True
    )


def swap_out(place, four):
    last = jnp.broadcast_to(four[3:], four.shape)
    return across_levels(jnp.where(place.z == 0, four, last), place.stride)


def from_row(place, four, got):
    pass_part = jnp.where(place.z == 0, got[1:], four[:3])
    query_part = jnp.where(place.z == 0, four[:1], got[:1])
    return pass_part, query_part


def toggle(places, mask):
    return [(p[0], p[1] ^ mask) if isinstance(p, tuple) else p ^ mask for p in places]


def block_of(me, place, level):
    if isinstance(place, tuple):
        return ((me & (level - 1)) ^ place[1]) + place[0] * level
    return me ^ place


def assemble_kernel(plan, layout, level, me_ref, *refs):
    pieces, outs, sems = refs[: len(plan)], refs[len(plan) : -1], refs[-1]
    me = me_ref[0]
    copies = []
    for piece, masks in zip(pieces, plan):
        for slot, mask in enumerate(masks):
            for out, part, row, column in layout:
                target = outs[out].at[part, block_of(me, mask, level)]
                rows, columns = outs[out].shape[2:]
                source = piece.at[slot, pl.ds(row, rows), pl.ds(column, columns)]
                copies.append(pltpu.make_async_copy(source, target, sems.at[len(copies)]))
    for copy in copies:
        copy.start()
    for copy in copies:
        copy.wait()


def assemble(place, pieces, plan, layout, outs):
    total = place.wide * place.narrow
    made = pl.pallas_call(
        functools.partial(assemble_kernel, plan, layout, total // LEVELS),
        out_shape=[jax.ShapeDtypeStruct((out[0], total, *out[1:]), BF) for out in outs],
        in_specs=[pl.BlockSpec(memory_space=pltpu.SMEM)]
        + [pl.BlockSpec(memory_space=pl.ANY)] * len(pieces),
        out_specs=[pl.BlockSpec(memory_space=pltpu.VMEM)] * len(outs),
        scratch_shapes=[pltpu.SemaphoreType.DMA((total * len(layout),))],
        cost_estimate=cost(0.1),
        compiler_params=pltpu.CompilerParams(vmem_limit_bytes=VMEM),
    )(place.me.reshape(1), *pieces)
    return [out.reshape(out.shape[0], -1, out.shape[3]) for out in made]


def pick_kernel(z_ref, w_ref, bias_ref, gain_ref, inb_ref, ints_ref, *refs):
    outs, small = refs[:-1], refs[-1]
    rows, width = w_ref.shape[1], small.shape[1]
    n_bias, n_gain = bias_ref.shape[1], gain_ref.shape[1]
    for k, out in enumerate(outs):
        tower = jnp.where(z_ref[0] == k, 1, 0)
        for part in range(3):
            out[part * rows : (part + 1) * rows] = w_ref[tower, :, part * width : (part + 1) * width]
        small[...] = jnp.zeros(small.shape, F32)
        small[:n_bias, : bias_ref.shape[2]] = bias_ref[tower].astype(F32)
        small[n_bias : n_bias + n_gain, : gain_ref.shape[2]] = gain_ref[tower].astype(F32)
        small[:1, 128 : 128 + inb_ref.shape[2]] = inb_ref[tower].astype(F32)
        small[:1, 256 : 256 + ints_ref.shape[1]] = ints_ref[...].astype(F32)
        out[3 * rows :] = small[...].astype(BF)


def pick_towers(place, w_qkv, biases, norm_gains, in_bias, ints):
    width = w_qkv.shape[2] // 3
    vmem = pl.BlockSpec(memory_space=pltpu.VMEM)
    return calls(
        pick_kernel,
        [((3 * w_qkv.shape[1] + 8, width), BF)] * LEVELS,
        2,
        in_specs=[pl.BlockSpec(memory_space=pltpu.SMEM)] + [vmem] * 5,
        scratch_shapes=[pltpu.VMEM((8, width), F32)],
    )(place.z.reshape(1), w_qkv, biases, norm_gains, in_bias[:, None], ints[None])


def gather_levels(place, pair):
    first = lax.broadcasted_iota(jnp.int32, (LEVELS, 1, 1), 0) == 0
    return across_levels(jnp.where(first, pair[1:], pair[:1]), place.stride)


def gather_columns(place, levels, own=None):
    s, narrow = place.stride, place.narrow
    if own is None:
        own = [(level, 0) for level in range(LEVELS)]
    pieces, plan = [levels], [own]
    if s == 2:
        for dx, dy in OTHERS:
            pieces.append(flip_both(levels, dy, 2 * dx))
            plan.append(toggle(own, dy * narrow + 2 * dx))
    else:
        for b in bits_of(s):
            for i in range(len(pieces)):
                pieces.append(flip(pieces[i], "wide", b))
                plan.append(toggle(plan[i], b * narrow))
        for i in range(len(pieces)):
            pieces.append(flip(pieces[i], "narrow", 2))
            plan.append(toggle(plan[i], 2))
    return pieces, plan


def gather_cores(pieces, plan):
    others = [flip(piece, "narrow", 1) for piece in pieces]
    return list(pieces) + others, plan + [toggle(places, 1) for places in plan]


def pick(x, index, dim):
    return lax.dynamic_index_in_dim(x, index, dim, keepdims=False)


def halve(x, place, axis, mask, dim):
    index = place.n if axis == "narrow" else place.w
    bit = jnp.where((index & mask) != 0, 1, 0)
    got = flip(pick(x, 1 - bit, dim).astype(BF), axis, mask)
    return pick(x, bit, dim) + got.astype(F32)


def scatter_tower(place, partial):
    s = place.stride
    rows, narrow, cols = partial.shape
    per = rows // place.wide
    x = partial.reshape(rows, 2, 2, cols)
    x = halve(x, place, "narrow", 1, 2)
    x = x.reshape(LEVELS, s, per, 2, cols)
    first, second = x[:2], x[2:]

    def over_columns(part):
        for b in reversed(bits_of(s)):
            shape = part.shape
            part = part.reshape(shape[0], 2, shape[1] // 2, *shape[2:])
            part = halve(part, place, "wide", b, 1)
        return part[:, 0]

    first = over_columns(halve(first, place, "narrow", 2, 3))
    second = halve(over_columns(second), place, "narrow", 2, 2)
    return jnp.stack(sum_levels(place, send_levels(place, jnp.concatenate([first, second]))))


def send_levels(place, levels):
    slots = [None] * LEVELS
    slots[0] = pick(levels, place.z, 0)
    for k in (3, 2, 1):
        slots[k] = flip(pick(levels, place.z ^ k, 0).astype(BF), "wide", k * place.stride)
    return slots


def sum_levels(place, slots):
    tower0 = sum(jnp.where(place.z == k, 0.0, slots[k].astype(F32)) for k in range(LEVELS))
    tower1 = sum(jnp.where(place.z == k, slots[k].astype(F32), 0.0) for k in range(LEVELS))
    return tower0, tower1


def share_kernel(at_ref, keep_ref, got_ref, own_ref, *sent_refs):
    x, y = at_ref[0], at_ref[1]

    def share(dx, dy):
        at = (x ^ dx, 0, y ^ dy)
        return keep_ref[at].astype(F32) + got_ref[at].astype(F32)

    own_ref[0] = share(0, 0)
    for ref, (dx, dy) in zip(sent_refs, OTHERS):
        ref[0] = share(dx, dy).astype(BF)


def column_shares(place, keep, got):
    r, c = got.shape[2:]
    block = pl.BlockSpec((2, 1, place.stride, r, c), lambda i, at: (0, i, 0, 0, 0))
    out = pl.BlockSpec((1, r, c), lambda i, at: (i, 0, 0))
    shape = (2, LEVELS, place.stride, r, c)
    return pl.pallas_call(
        share_kernel,
        grid_spec=pltpu.PrefetchScalarGridSpec(
            num_scalar_prefetch=1, grid=(LEVELS,), in_specs=[block] * 2, out_specs=[out] * 4
        ),
        out_shape=[jax.ShapeDtypeStruct((LEVELS, r, c), F32)]
        + [jax.ShapeDtypeStruct((LEVELS, r, c), BF)] * 3,
        compiler_params=pltpu.CompilerParams(vmem_limit_bytes=VMEM),
        cost_estimate=cost(1),
    )(jnp.stack([place.n // 2, place.y]), keep.reshape(shape), got.reshape(shape))


def send_columns(shares):
    return [shares[0]] + [
        flip_both(sent, dy, 2 * dx) for sent, (dx, dy) in zip(shares[1:], OTHERS)
    ]


def level_kernel(z_ref, own_ref, *refs):
    got_refs, (sum_ref, *sent_refs) = refs[:3], refs[3:]
    for k in range(LEVELS):
        at = z_ref[0] ^ k
        total = own_ref[at]
        for ref in got_refs:
            total = total + ref[at].astype(F32)
        if k == 0:
            sum_ref[...] = total
        else:
            sent_refs[k - 1][...] = total.astype(BF)


def level_shares(place, columns):
    r, c = columns[0].shape[1:]
    vmem = pl.BlockSpec(memory_space=pltpu.VMEM)
    return pl.pallas_call(
        level_kernel,
        in_specs=[pl.BlockSpec(memory_space=pltpu.SMEM)] + [vmem] * 4,
        out_specs=[vmem] * 4,
        out_shape=[jax.ShapeDtypeStruct((r, c), F32)] + [jax.ShapeDtypeStruct((r, c), BF)] * 3,
        compiler_params=pltpu.CompilerParams(vmem_limit_bytes=VMEM),
        cost_estimate=cost(1),
    )(place.z.reshape(1), *columns)


def level_sums_kernel(*refs):
    for at in range(LEVELS):
        refs[-1][at] = sum(ref[at].astype(F32) for ref in refs[:-1]).astype(BF)


def level_sums(columns):
    shape = columns[0].shape
    return calls(level_sums_kernel, [(shape, BF)], 3)(*columns)[0]


def swap_shares(place, shares):
    slots = [shares[0], None, None, None]
    for k in (3, 2, 1):
        slots[k] = flip(shares[k], "wide", k * place.stride)
    return slots


def product_kernel(step, me_ref, *refs):
    send_ref, keep_ref = refs[-2:]
    left_refs = refs[:-2]
    to_send = pl.program_id(0) < 2

    @pl.when(to_send)
    def _():
        step(left_refs, lambda at, v: send_ref.__setitem__((0, *at), v.astype(BF)))

    @pl.when(jnp.logical_not(to_send))
    def _():
        step(left_refs, lambda at, v: keep_ref.__setitem__((0, *at), v.astype(BF)))


def products(place, step, operands, specs, block):
    def target(j, me):
        return (j % 2) * 2 + jnp.where(j < 2, 1 - me[0] % 2, me[0] % 2)

    wide = place.wide
    grid_spec = pltpu.PrefetchScalarGridSpec(
        num_scalar_prefetch=1,
        grid=(4,),
        in_specs=specs(target),
        out_specs=[
            pl.BlockSpec((1, wide, *block), lambda j, me: (jnp.minimum(j, 1), 0, 0, 0)),
            pl.BlockSpec((1, wide, *block), lambda j, me: (jnp.maximum(j - 2, 0), 0, 0, 0)),
        ],
    )
    return pl.pallas_call(
        functools.partial(product_kernel, step),
        grid_spec=grid_spec,
        out_shape=[
            jax.ShapeDtypeStruct((2, wide, *block), BF),
            jax.ShapeDtypeStruct((2, wide, *block), BF),
        ],
        compiler_params=pltpu.CompilerParams(vmem_limit_bytes=VMEM),
        cost_estimate=cost(8),
    )(place.n.reshape(1), *operands)


def whole(shape):
    return pl.BlockSpec(shape, lambda j, me: (0,) * len(shape))


def grad_blocks(left, right, narrow):
    out = inner_rows(left, right)
    return out.reshape(out.shape[0], narrow, -1)


def products_back_kernel(core_ref, left_ref, right_ref, send_ref, keep_ref, turned_ref):
    @pl.when(pl.program_id(0) == 0)
    def _():
        turned_ref[...] = right_ref[...].T

    value = matmul(turned_ref[...], left_ref[...]).astype(BF)
    cols = send_ref.shape[2]
    first = core_ref[0] == 0
    for x in range(2):
        even = value[2 * x * cols : (2 * x + 1) * cols]
        odd = value[(2 * x + 1) * cols : (2 * x + 2) * cols]
        keep_ref[x, 0] = jnp.where(first, even, odd)
        send_ref[x, 0] = jnp.where(first, odd, even)


def products_back(place, active, grad_ffn):
    t, ff = active.shape
    d = grad_ffn.shape[1]
    cols, rows = d // place.narrow, ff // place.wide
    out = pl.BlockSpec((2, 1, cols, rows), lambda j, core: (0, j, 0, 0))
    return pl.pallas_call(
        products_back_kernel,
        grid_spec=pltpu.PrefetchScalarGridSpec(
            num_scalar_prefetch=1,
            grid=(place.wide,),
            in_specs=[pl.BlockSpec((t, rows), lambda j, core: (0, j)), whole((t, d))],
            out_specs=[out, out],
            scratch_shapes=[pltpu.VMEM((d, t), BF)],
        ),
        out_shape=[jax.ShapeDtypeStruct((2, place.wide, cols, rows), BF)] * 2,
        compiler_params=pltpu.CompilerParams(vmem_limit_bytes=VMEM),
        cost_estimate=cost(7),
    )((place.n % 2).reshape(1), active, grad_ffn)


def finish_back(levels):
    levels = levels.astype(F32)
    return jnp.stack([(levels[1] + levels[2] + levels[3]).T, levels[0].T])


def products_out_in(place, context, blocks, normed, grad_hidden):
    narrow = place.narrow
    t, d = context.shape
    rows = d // place.wide
    cols_out, cols_in = blocks.shape[2], grad_hidden.shape[1] // narrow
    fold = cols_in // cols_out
    low = rows // fold

    def step(refs, store):
        context_ref, branch_ref, normed_ref, hidden_ref = refs

        def body(i, carry):
            at = pl.ds(pl.multiple_of(i * 4 * rows, 4 * rows), 4 * rows)
            value = inner_rows(normed_ref[:, at], hidden_ref[...])
            for w in range(4):
                store((4 * i + w, slice(0, rows)), value[w * rows : (w + 1) * rows])
            value = inner_rows(context_ref[:, at], branch_ref[0])
            for w in range(4):
                for g in range(fold):
                    store(
                        (4 * i + w, slice(rows, rows + low), slice(g * cols_out, (g + 1) * cols_out)),
                        value[w * rows + g * low : w * rows + (g + 1) * low],
                    )
            return carry

        lax.fori_loop(0, place.wide // 4, body, 0)

    return products(
        place,
        step,
        (context, blocks, normed, grad_hidden),
        lambda target: [
            whole((t, d)),
            pl.BlockSpec((1, t, cols_out), lambda j, me: (target(j, me), 0, 0)),
            whole((t, d)),
            pl.BlockSpec((t, cols_in), lambda j, me: (0, target(j, me))),
        ],
        (rows + low, cols_in),
    )


def finish_out_in(place, slots, rows):
    parts = sum_levels(place, slots)
    low, cols = parts[0].shape[0] - rows, parts[0].shape[1]
    fold = rows // low
    grad_in = jnp.stack([part[:rows] for part in parts])
    grad_out = [
        jnp.moveaxis(part[rows:].reshape(low, fold, -1), 1, 0).reshape(rows, -1) for part in parts
    ]
    return jnp.stack(grad_out), grad_in


def products_qkv(place, inputs, blocks):
    t, d = inputs.shape
    rows, cols = d // place.wide, blocks.shape[2]
    half = rows // 2

    def step(refs, store):
        left, right = refs

        def body(i, carry):
            at = pl.ds(pl.multiple_of(i * 4 * rows, 4 * rows), 4 * rows)
            value = inner_rows(left[:, at], right[0])
            for w in range(4):
                for g in range(2):
                    store(
                        (4 * i + w, slice(None), slice(g * cols, (g + 1) * cols)),
                        value[w * rows + g * half : w * rows + (g + 1) * half],
                    )
            return carry

        lax.fori_loop(0, place.wide // 4, body, 0)

    return products(
        place,
        step,
        (inputs, blocks),
        lambda target: [
            whole((t, d)),
            pl.BlockSpec((1, t, cols), lambda j, me: (target(j, me), 0, 0)),
        ],
        (half, 2 * cols),
    )


def finish_qkv(place, slots):
    parts = sum_levels(place, slots)
    cols = parts[0].shape[1] // 2
    return jnp.stack([jnp.concatenate([p[:, :cols], p[:, cols:]]) for p in parts])


def attend_kernel(x_ref, w_ref, rows_ref, seg_row_ref, seg_col_ref, qkv_ref, ctx_ref, lse_ref):
    x = x_ref[...]
    same = seg_col_ref[...] == seg_row_ref[...]

    def project(part, carry):
        bias = jnp.where(part == 0, rows_ref[0:1], jnp.where(part == 2, rows_ref[1:2], 0.0))
        qkv_ref[part] = (matmul(x, w_ref[part]) + bias).astype(BF)
        return carry

    lax.fori_loop(0, 3, project, 0)
    for h in range(GROUP):
        lanes = slice(h * HEAD_DIM, (h + 1) * HEAD_DIM)
        q, k, v = qkv_ref[0, :, lanes], qkv_ref[1, :, lanes], qkv_ref[2, :, lanes]
        scores = jnp.where(same, inner_cols(k, q) * HEAD_DIM ** (-0.5), MASKED)
        top = jnp.max(scores, axis=0, keepdims=True)
        shifted = jnp.exp(scores - top)
        total = jnp.sum(shifted, axis=0, keepdims=True)
        probs = (shifted * (1.0 / total)).astype(BF)
        ctx_ref[:, lanes] = inner_rows(probs, v).astype(BF)
        lse_ref[0, h : h + 1, :] = top + jnp.log(total)


def attend(x, w_qkv, rows, segment):
    t, d = x.shape
    width = GROUP * HEAD_DIM
    steps = d // width
    return pl.pallas_call(
        attend_kernel,
        grid=(steps,),
        in_specs=[
            pl.BlockSpec((t, d), lambda j: (0, 0)),
            pl.BlockSpec((3, d, width), lambda j: (0, 0, j)),
            pl.BlockSpec((8, width), lambda j: (0, j)),
            pl.BlockSpec((1, t), lambda j: (0, 0)),
            pl.BlockSpec((t, 1), lambda j: (0, 0)),
        ],
        out_specs=[
            pl.BlockSpec((3, t, width), lambda j: (0, 0, j)),
            pl.BlockSpec((t, width), lambda j: (0, j)),
            pl.BlockSpec((1, GROUP, t), lambda j: (j, 0, 0)),
        ],
        out_shape=[
            jax.ShapeDtypeStruct((3, t, d), BF),
            jax.ShapeDtypeStruct((t, d), BF),
            jax.ShapeDtypeStruct((steps, GROUP, t), F32),
        ],
        compiler_params=pltpu.CompilerParams(vmem_limit_bytes=VMEM),
        cost_estimate=cost(0.1),
    )(x, w_qkv, rows, segment.reshape(1, t), segment.reshape(t, 1))


def attend_back_kernel(
    gb_ref, w_ref, qkv_ref, lse_ref, seg_row_ref, seg_col_ref, out_ref, blocks_ref, sums_ref, grad_ref
):
    scale = HEAD_DIM ** (-0.5)
    same = seg_col_ref[...] == seg_row_ref[...]
    grad_ref[...] = inner_cols(gb_ref[...], w_ref[...]).astype(BF)

    def pair(p, carry):
        at = pl.ds(pl.multiple_of(p * 2 * HEAD_DIM, 2 * HEAD_DIM), 2 * HEAD_DIM)
        queries, keys, values = qkv_ref[0, :, at], qkv_ref[1, :, at], qkv_ref[2, :, at]
        grads, outs = grad_ref[:, at], []
        for h in range(2):
            lanes = slice(h * HEAD_DIM, (h + 1) * HEAD_DIM)
            q, k, v, g = queries[:, lanes], keys[:, lanes], values[:, lanes], grads[:, lanes]
            scores = jnp.where(same, inner_cols(k, q) * scale, MASKED)
            probs = jnp.exp(scores - lse_ref[0, pl.ds(2 * p + h, 1), :])
            grad_probs = inner_cols(v, g)
            delta = jnp.sum(probs * grad_probs, axis=0, keepdims=True)
            grad_scores = (probs * (grad_probs - delta)).astype(BF)
            outs.append(
                (
                    (inner_rows(grad_scores, k) * scale).astype(BF),
                    (matmul(grad_scores, q) * scale).astype(BF),
                    matmul(probs.astype(BF), g).astype(BF),
                )
            )
        for part in range(3):
            out_ref[part, :, at] = jnp.concatenate([outs[0][part], outs[1][part]], axis=1)
        return carry

    lax.fori_loop(0, GROUP // 2, pair, 0)
    sums_ref[0:1] = jnp.sum(out_ref[0].astype(F32), axis=0, keepdims=True)
    sums_ref[1:2] = jnp.sum(out_ref[2].astype(F32), axis=0, keepdims=True)
    per_block = blocks_ref.shape[2] // HEAD_DIM
    heads = blocks_ref.shape[0] * per_block // 3
    for step in range(heads // GROUP):

        @pl.when(pl.program_id(0) == step)
        def _(step=step):
            for part in range(3):
                for h in range(GROUP):
                    block, at = divmod(part * heads + step * GROUP + h, per_block)
                    blocks_ref[block, :, at * HEAD_DIM : (at + 1) * HEAD_DIM] = out_ref[
                        part, :, h * HEAD_DIM : (h + 1) * HEAD_DIM
                    ]


def attend_back(grad_branch, w_out, qkv, lse, segment, narrow):
    t, d = grad_branch.shape
    width = GROUP * HEAD_DIM
    return pl.pallas_call(
        attend_back_kernel,
        grid=(d // width,),
        in_specs=[
            pl.BlockSpec((t, d), lambda j: (0, 0)),
            pl.BlockSpec((width, d), lambda j: (j, 0)),
            pl.BlockSpec((3, t, width), lambda j: (0, 0, j)),
            pl.BlockSpec((1, GROUP, t), lambda j: (j, 0, 0)),
            pl.BlockSpec((1, t), lambda j: (0, 0)),
            pl.BlockSpec((t, 1), lambda j: (0, 0)),
        ],
        out_specs=[
            pl.BlockSpec((3, t, width), lambda j: (0, 0, j)),
            pl.BlockSpec((narrow, t, 3 * d // narrow), lambda j: (0, 0, 0)),
            pl.BlockSpec((2, width), lambda j: (0, j)),
        ],
        out_shape=[
            jax.ShapeDtypeStruct((3, t, d), BF),
            jax.ShapeDtypeStruct((narrow, t, 3 * d // narrow), BF),
            jax.ShapeDtypeStruct((2, d), F32),
        ],
        scratch_shapes=[pltpu.VMEM((t, width), BF)],
        compiler_params=pltpu.CompilerParams(vmem_limit_bytes=VMEM),
        cost_estimate=cost(20),
    )(grad_branch, w_out, qkv, lse, segment.reshape(1, t), segment.reshape(t, 1))


def hidden_kernel(x_ref, w_ref, bias_ref, active_ref, slope_ref, pre_ref):
    pre_ref[...] = matmul(x_ref[...], w_ref[0]) + bias_ref[...]

    def body(at, carry):
        pre = pre_ref[at]
        below = 0.5 + 0.5 * lax.erf(pre * 0.5**0.5)
        active_ref[at] = (pre * below).astype(BF)
        density = jnp.exp(-0.5 * pre * pre) * (2.0 * math.pi) ** (-0.5)
        slope_ref[at] = (below + pre * density).astype(BF)
        return carry

    by_rows(pre_ref.shape[0], body)


def hidden_layer(x, w_in, in_bias):
    t, d = x.shape
    parts, _, width = w_in.shape
    block = pl.BlockSpec((t, width), lambda j: (0, j))
    shape = jax.ShapeDtypeStruct((t, parts * width), BF)
    return pl.pallas_call(
        hidden_kernel,
        grid=(parts,),
        in_specs=[
            pl.BlockSpec((t, d), lambda j: (0, 0)),
            pl.BlockSpec((1, d, width), lambda j: (j, 0, 0)),
            pl.BlockSpec((1, width), lambda j: (0, j)),
        ],
        out_specs=[block, block],
        out_shape=[shape, shape],
        scratch_shapes=[pltpu.VMEM((t, width), F32)],
        compiler_params=pltpu.CompilerParams(vmem_limit_bytes=VMEM),
        cost_estimate=cost(8),
    )(x, w_in, in_bias)


def norm_parts(value):
    mean = jnp.mean(value, axis=-1, keepdims=True)
    centered = value - mean
    scale = lax.rsqrt(jnp.mean(centered * centered, axis=-1, keepdims=True) + EPSILON)
    return centered * scale, scale


def norm_back(grad, unit, scale, gain):
    e = grad * gain
    part = jnp.mean(e * unit, axis=-1, keepdims=True)
    return (e - jnp.mean(e, axis=-1, keepdims=True) - unit * part) * scale


def total(value):
    return jnp.sum(jnp.sum(value, axis=0, keepdims=True), axis=1, keepdims=True)


def column_sum(value):
    return jnp.sum(value, axis=0, keepdims=True)


def by_rows(count, body, carry=None):
    if carry is None:
        carry = jnp.zeros((1, 128), F32)
    return lax.fori_loop(
        0, count // STEP, lambda i, c: body(pl.ds(pl.multiple_of(i * STEP, STEP), STEP), c), carry
    )


def store_blocks(ref, at, value):
    count, _, width = ref.shape
    for i in range(count):
        ref[i, at] = value[:, i * width : (i + 1) * width]


def calls(kernel, outs, us, **kwargs):
    return pl.pallas_call(
        kernel,
        out_shape=[jax.ShapeDtypeStruct(shape, dtype) for shape, dtype in outs],
        compiler_params=pltpu.CompilerParams(vmem_limit_bytes=VMEM),
        cost_estimate=cost(us),
        **kwargs,
    )


def branch_kernel(ctx, w, x, rows, valid, normed, low, unit, scale, stats, acc):
    acc[...] = matmul(ctx[...], w[0])
    zero = jnp.zeros((1, acc.shape[1]), F32)

    def body(at, sums):
        branch = acc[at] + rows[2:3]
        residual = x[at].astype(F32) + branch
        unit[at], scale[at] = norm_parts(residual)
        normed[at] = unit[at] * rows[6:7] + rows[3:4]
        low[at] = normed[at].astype(BF)
        return tuple(
            s + column_sum(valid[at] * value * value) for s, value in zip(sums, (residual, branch))
        )

    for i, value in enumerate(by_rows(acc.shape[0], body, (zero, zero))):
        stats[i : i + 1] = jnp.broadcast_to(total(value), (1, 128))


def branch_layer(context, w_out, inputs, rows, valid):
    t, d = inputs.shape
    outs = [((t, d), F32), ((t, d), BF), ((t, d), F32), ((t, 1), F32), ((2, 128), F32)]
    scratch = [pltpu.VMEM((t, d), F32)]
    return calls(branch_kernel, outs, 5, scratch_shapes=scratch)(
        context, w_out, inputs, rows, valid
    )


def output_kernel(plan, level, me_ref, active, normed, rows, valid, hot, *refs):
    pieces = refs[:-8]
    low, unit, scale, pooled, stats, w, acc, sems = refs[-8:]
    step = pl.program_id(0)
    width = active.shape[1]
    block = pieces[0].shape[1]

    @pl.when(step == 0)
    def _():
        copies = []
        if plan is None:
            copies.append(pltpu.make_async_copy(pieces[0], w, sems.at[0]))
        for piece, masks in zip(pieces, plan or []):
            for slot, mask in enumerate(masks):
                at = pl.multiple_of(block_of(me_ref[0], mask, level) * block, block)
                target = w.at[pl.ds(at, block)]
                copies.append(
                    pltpu.make_async_copy(piece.at[slot], target, sems.at[len(copies)])
                )
        for copy in copies:
            copy.start()
        for copy in copies:
            copy.wait()

    product = matmul(active[...], w[pl.ds(pl.multiple_of(step * width, width), width)])

    @pl.when(step == 0)
    def _():
        acc[...] = product

    @pl.when(step > 0)
    def _():
        acc[...] += product

    @pl.when(step == pl.num_programs(0) - 1)
    def _():
        zero = jnp.zeros((1, acc.shape[1]), F32)

        def body(at, sums):
            ffn_out = acc[at] + rows[4:5]
            residual = normed[at] + ffn_out
            unit[at], scale[at] = norm_parts(residual)
            low[at] = (unit[at] * rows[7:8] + rows[5:6]).astype(BF)
            values = (valid[at] * residual * residual, valid[at] * ffn_out * ffn_out)
            return tuple(s + column_sum(value) for s, value in zip(sums, values))

        sums = by_rows(acc.shape[0], body, (zero, zero))
        for i, value in enumerate((*sums, valid[...])):
            stats[i : i + 1] = jnp.broadcast_to(total(value), (1, 128))
        pooled[...] = matmul(hot[...].astype(BF), low[...]).astype(BF)


def all_of(shape):
    return pl.BlockSpec(shape, lambda j: (0,) * len(shape))


def output_layer(place, active, pieces, plan, normed, rows, valid, hot):
    t, ff = active.shape
    d = normed.shape[1]
    outs = [((t, d), BF), ((t, d), F32), ((t, 1), F32), ((hot.shape[0], d), BF), ((3, 128), F32)]
    outs.append(((ff, d), BF))
    return calls(
        functools.partial(output_kernel, plan, place.wide * place.narrow // LEVELS),
        outs,
        9,
        grid=(ff // d,),
        in_specs=[pl.BlockSpec(memory_space=pltpu.SMEM), pl.BlockSpec((t, d), lambda j: (0, j))]
        + [all_of(a.shape) for a in (normed, rows, valid, hot)]
        + [pl.BlockSpec(memory_space=pl.ANY)] * len(pieces),
        out_specs=[all_of(shape) for shape, _ in outs],
        scratch_shapes=[
            pltpu.VMEM((t, d), F32),
            pltpu.SemaphoreType.DMA((place.wide * place.narrow,)),
        ],
    )(place.me.reshape(1), active, normed, rows, valid, hot, *pieces)


def output_back_kernel(cot, valid, hot, pool, unit, scale, rows, grad, low, sums):
    zero = jnp.zeros((1, grad.shape[1]), F32)

    def body(at, totals):
        grad_out = cot[at].astype(F32) * valid[at] + lax.dot_general(
            hot[:, at],
            pool[...],
            (((0,), (0,)), ((), ())),
            precision=lax.Precision.HIGHEST,
            preferred_element_type=F32,
        )
        grad[at] = norm_back(grad_out, unit[at], scale[at], rows[7:8])
        low[at] = grad[at].astype(BF)
        values = (grad_out * unit[at], grad_out, low[at].astype(F32))
        return tuple(t + column_sum(value) for t, value in zip(totals, values))

    for i, value in enumerate(by_rows(grad.shape[0], body, (zero,) * 3)):
        sums[i : i + 1] = value


def output_back(cot, valid, hot, pool, unit, scale, rows):
    t, d = cot.shape
    outs = [((t, d), F32), ((t, d), BF), ((3, d), F32)]
    return calls(output_back_kernel, outs, 6)(cot, valid, hot, pool, unit, scale, rows)


def hidden_back_kernel(
    low, w_back, slope, w_in, grad, unit, scale, rows, hidden, inb, residual, branch, blocks, sums, acc
):
    step = pl.program_id(0)
    product = inner_cols(low[...], w_back[...])
    hidden[...] = (product * slope[...].astype(F32)).astype(BF)
    inb[...] = column_sum(hidden[...].astype(F32))
    product = inner_cols(hidden[...], w_in[0])

    @pl.when(step == 0)
    def _():
        acc[...] = grad[...] + product

    @pl.when(step > 0)
    def _():
        acc[...] += product

    @pl.when(step == pl.num_programs(0) - 1)
    def _():
        zero = jnp.zeros((1, acc.shape[1]), F32)

        def body(at, totals):
            value = acc[at]
            residual[at] = norm_back(value, unit[at], scale[at], rows[6:7])
            branch[at] = residual[at].astype(BF)
            store_blocks(blocks, at, branch[at])
            values = (value * unit[at], value, branch[at].astype(F32))
            return tuple(t + column_sum(value) for t, value in zip(totals, values))

        for i, value in enumerate(by_rows(acc.shape[0], body, (zero,) * 3)):
            sums[i : i + 1] = value


def hidden_back(low, w_back, slope, w_in, grad, unit, scale, rows, narrow):
    t, d = low.shape
    ff = slope.shape[1]
    tile = pl.BlockSpec((t, d), lambda j: (0, j))
    outs = [
        ((t, ff), BF),
        ((1, ff), F32),
        ((t, d), F32),
        ((t, d), BF),
        ((narrow, t, d // narrow), BF),
        ((3, d), F32),
    ]
    return calls(
        hidden_back_kernel,
        outs,
        14,
        grid=(ff // d,),
        in_specs=[
            all_of(low.shape),
            pl.BlockSpec((d, d), lambda j: (j, 0)),
            tile,
            pl.BlockSpec((1, d, d), lambda j: (j, 0, 0)),
        ]
        + [all_of(a.shape) for a in (grad, unit, scale, rows)],
        out_specs=[tile, pl.BlockSpec((1, d), lambda j: (0, j))]
        + [all_of(shape) for shape, _ in outs[2:]],
        scratch_shapes=[pltpu.VMEM((t, d), F32)],
    )(low, w_back, slope, w_in, grad, unit, scale, rows)


def input_back_kernel(grad, w, residual, out, acc):
    step = pl.program_id(0)
    product = inner_cols(grad[0], w[0])

    @pl.when(step == 0)
    def _():
        acc[...] = residual[...] + product

    @pl.when(step == 1)
    def _():
        acc[...] += product

    @pl.when(step == 2)
    def _():
        out[...] = (acc[...] + product).astype(BF)


def input_back(grad_qkv, w_qkv, residual):
    _, t, d = grad_qkv.shape
    return calls(
        input_back_kernel,
        [((t, d), BF)],
        6,
        grid=(3,),
        in_specs=[
            pl.BlockSpec((1, t, d), lambda j: (j, 0, 0)),
            pl.BlockSpec((1, d, d), lambda j: (j, 0, 0)),
            all_of((t, d)),
        ],
        out_specs=[all_of((t, d))],
        scratch_shapes=[pltpu.VMEM((t, d), F32)],
    )(grad_qkv, w_qkv, residual)[0]


def spread_masks(count, width):
    total_cols = count * width
    column = lax.broadcasted_iota(jnp.int32, (count, total_cols), 1)
    first = lax.broadcasted_iota(jnp.int32, (count, total_cols), 0) * width
    own = (column >= first) & (column < first + width)
    owner = jnp.sum(jnp.where(own, first, 0), axis=0, keepdims=True)
    within = lax.broadcasted_iota(jnp.int32, (width, total_cols), 1) - owner
    spread = within == lax.broadcasted_iota(jnp.int32, (width, total_cols), 0)
    return own, spread.astype(F32)


def unpack_kernel(small, rows, inb):
    count = small.shape[0]
    value = small[...].astype(F32)

    def unpack(part, masks):
        own, spread = masks
        placed = matmul(part.astype(BF), spread.astype(BF))
        return column_sum(jnp.where(own, placed, 0.0))

    width = rows.shape[1] // count
    masks = spread_masks(count, width)
    for r in range(8):
        rows[r : r + 1] = unpack(value[:, r, :width], masks)
    width = inb.shape[1] // count
    inb[...] = unpack(value[:, 0, 128 : 128 + width], spread_masks(count, width))


def unpack_params(small, d, ff):
    return calls(unpack_kernel, [((8, d), F32), ((1, ff), F32)], 0.1)(small)


def pack_kernel(attn, out, ffn, inb, stats_a, stats_b, packed, rows, parts):
    count = packed.shape[0]
    vectors = (attn[0:1], attn[1:2], out[2:3], out[1:2], ffn[2:3], ffn[1:2], out[0:1], ffn[0:1])

    def pack(vector, own, spread):
        return lax.dot_general(
            jnp.where(own, vector, 0.0),
            spread,
            (((1,), (1,)), ((), ())),
            precision=lax.Precision.HIGHEST,
            preferred_element_type=F32,
        )

    for i, vector in enumerate(vectors):
        rows[i : i + 1] = vector
    packed[...] = jnp.zeros(packed.shape, F32)
    width = rows.shape[1] // count
    masks = spread_masks(count, width)

    def body(i, carry):
        parts[i] = pack(rows[pl.ds(i, 1)], *masks)
        return carry

    lax.fori_loop(0, len(vectors), body, 0)
    for i in range(len(vectors)):
        packed[:, i * width : (i + 1) * width] = parts[i]
    at = len(vectors) * width
    width = inb.shape[1] // count
    packed[:, at : at + width] = pack(inb[...], *spread_masks(count, width))
    at += width
    for i, row in enumerate((stats_a[0:1], stats_a[1:2], stats_b[0:1], stats_b[1:2], stats_b[2:3])):
        packed[:, at + i : at + i + 1] = jnp.broadcast_to(row[:, :1], (count, 1))


def pack_sums(count, attn, out, ffn, inb, stats_a, stats_b):
    width = attn.shape[1]
    scratch = [pltpu.VMEM((8, width), F32), pltpu.VMEM((8, count, width // count), F32)]
    return calls(pack_kernel, [((count, 384), F32)], 4, scratch_shapes=scratch)(
        attn, out, ffn, inb, stats_a, stats_b
    )[0]


def match_grads(rows, label_rows, label_cols):
    is_query, is_pass = label_rows >= 0, label_cols >= 0
    match = jnp.where(is_pass, inner_cols(rows, rows) / SCORE_DIV, MASKED)
    shifted = jnp.exp(match - jnp.max(match, axis=1, keepdims=True))
    probs = shifted / jnp.sum(shifted, axis=1, keepdims=True)
    hot = (label_rows == label_cols).astype(F32)
    grad = jnp.where(is_query & is_pass, (probs - hot) / SCORE_DIV, 0.0).astype(BF)
    return matmul(grad[:POOL], rows) + inner_rows(grad[:, :POOL], rows)


def match_kernel(rows, label_rows, label_cols, out):
    out[...] = match_grads(rows[...], label_rows[...], label_cols[...])


def row_of(z, y, n, s):
    own = (z * s + y) * 3 + n
    spare = y * 3 + (z - 1)
    return jnp.where(z == 0, n * s + y, jnp.where(n < 3, own, spare))


def body(
    passages,
    queries,
    passage_cot,
    query_cot,
    passage_lengths,
    query_lengths,
    labels,
    w_qkv,
    w_out,
    w_in,
    w_back,
    biases,
    norm_gains,
    in_bias,
):
    place = Place()
    s, narrow, devices = place.stride, place.narrow, place.wide * place.narrow
    model_width = passages.shape[2]
    length = passages.shape[1] * narrow
    segs, qsegs = passage_lengths.shape[1] - 1, query_lengths.shape[1] - 1
    on_query = place.z == 0

    piece = model_width // devices
    whole = jnp.concatenate(
        [passage_lengths.reshape(-1), query_lengths.reshape(-1), labels.reshape(-1)]
    )
    whole = jnp.concatenate([whole // 32, whole % 32]).astype(BF)

    w_rows, in_parts = w_out.shape[1], w_in.shape[2] // w_out.shape[2]
    if s == 2:
        towers = pick_towers(place, w_qkv, biases, norm_gains, in_bias, whole)
        got = {k: flip(towers[k], "wide", k * s) for k in (3, 2, 1)}
        levels_qkv = jnp.stack([towers[0], got[1], got[2], got[3]])
        own = [k * s * narrow for k in range(LEVELS)]
        layout = [(0, part, part * w_rows, 0) for part in range(3)] + [(1, 0, 3 * w_rows, 0)]
        shapes = [(3, w_rows, model_width), (1, 8, model_width)]
    else:
        small = jnp.concatenate(
            [biases.reshape(2, -1), norm_gains.reshape(2, -1), in_bias.reshape(2, -1)], axis=1
        )
        small_count = small.shape[1]
        small = jnp.concatenate([small, jnp.broadcast_to(whole, (2, whole.shape[0]))], axis=1)
        to_query = (jnp.arange(devices) < s * narrow)[:, None]
        small = lax.all_to_all(
            jnp.where(to_query, small[1][None], small[0][None]), BOTH, 0, 0, tiled=True
        )
        levels_qkv, own = gather_levels(place, w_qkv), None
        layout = [(0, part, 0, part * model_width) for part in range(3)]
        shapes = [(3, w_rows, model_width)]
    out_in = jnp.concatenate([w_out, w_in], axis=2)
    levels_qkv, out_in, parts = phase(levels_qkv, out_in, (passages, queries))

    pieces_qkv, plan = gather_columns(place, levels_qkv, own)
    levels_out_in = gather_levels(place, out_in)
    swapped = swap_in_directly(place, *parts)
    pieces_qkv, levels_out_in, w_back, swapped = phase(
        pieces_qkv, levels_out_in, w_back, swapped
    )

    cores_qkv, core_plan = gather_cores(pieces_qkv, plan)
    cores_qkv, levels_out_in, swapped = phase(cores_qkv, levels_out_in, swapped)

    pieces_out_in, plan = gather_columns(place, levels_out_in)
    inputs = to_row(place, passages, queries, join_swapped(place, queries, swapped))
    inputs, w_back, cores_qkv = phase(inputs, w_back, cores_qkv)
    levels_back = gather_levels(place, w_back)
    made = assemble(place, cores_qkv, core_plan, layout, shapes)
    w_qkv_all = made[0]

    n_bias, n_gain = biases.shape[1], norm_gains.shape[1]
    ff = in_bias.shape[1] * devices
    if s == 2:
        small = made[1].reshape(devices, 8, -1)
        rows, inb_row = unpack_params(small, model_width, ff)
        ints = small[:, 0, 256 : 256 + whole.shape[0]].astype(F32)
    else:
        params = small[:, :small_count].astype(F32)
        vectors = params[:, : (n_bias + n_gain) * piece].reshape(devices, n_bias + n_gain, piece)
        rows = vectors.transpose(1, 0, 2).reshape(n_bias + n_gain, -1)
        inb_row = params[:, (n_bias + n_gain) * piece :].reshape(1, -1)
        ints = small[:, small_count : small_count + whole.shape[0]].astype(F32)
    half = ints.shape[1] // 2
    ints = (ints[::narrow, :half] * 32 + ints[::narrow, half:]).astype(jnp.int32)
    n_pass = passage_lengths.size
    n_query = query_lengths.size
    pass_lens = ints[:, :n_pass].reshape(-1, segs + 1)
    query_lens = ints[:, n_pass : n_pass + n_query].reshape(-1, qsegs + 1)
    label_all = ints[:, n_pass + n_query :].reshape(-1, qsegs)
    my_row = row_of(place.z, place.y, place.n, s)
    pass_row = pick(pass_lens, jnp.where(on_query, 0, my_row), 0)
    query_row = pick(query_lens, jnp.where(on_query, my_row, 0), 0)
    ends_p = jnp.cumsum(pass_row)[:-1]
    ends_q = jnp.cumsum(query_row)[:-1]
    starts_p, starts_q = ends_p - pass_row[:-1], ends_q - query_row[:-1]
    ends_p = jnp.concatenate([ends_p, jnp.full((qsegs - segs,), length + 1, jnp.int32)])
    ends = jnp.where(on_query, ends_q, ends_p)
    seg_count = jnp.where(on_query, qsegs, segs)
    position = jnp.arange(length, dtype=jnp.int32)
    segment = jnp.sum((position[:, None] >= ends[None, :]).astype(jnp.int32), axis=1)
    valid = (segment < seg_count).astype(F32)[:, None]
    slot = jnp.arange(POOL)
    starts = jnp.where(on_query, jnp.concatenate([starts_q, jnp.full((qsegs,), -1)]), -1)
    for z in range(1, LEVELS):
        here = (place.z == z) & (slot >= qsegs + segs * (z - 1)) & (slot < qsegs + segs * z)
        starts = jnp.where(here, jnp.tile(starts_p, POOL // segs), starts)
    hot = (starts[:, None] == position[None, :]).astype(F32)
    masks = [0]
    if s == 2:
        masks += [dy * narrow + 2 * dx for dx, dy in OTHERS]
        masks += [m ^ 1 for m in masks]
    else:
        for mask in [b * narrow for b in bits_of(s)] + [b for b in reversed(bits_of(narrow))]:
            masks = masks + [m ^ mask for m in masks]
    there = (place.y * narrow + place.n) ^ jnp.array(masks, jnp.int32)
    their_y, their_n = there // narrow, there % narrow
    label_rows = label_all[row_of(jnp.int32(0), their_y, their_n, s)]
    label_rows = jnp.pad(label_rows, ((0, 0), (0, POOL - qsegs)), constant_values=-1)
    levels = jnp.arange(1, LEVELS)
    pass_rows = row_of(levels[None, :], their_y[:, None], their_n[:, None], s)
    pass_ids = (pass_rows[:, :, None] * segs + jnp.arange(segs)).reshape(len(masks), -1)
    spare = POOL - qsegs - pass_ids.shape[1]
    label_cols = jnp.pad(pass_ids, ((0, 0), (qsegs, spare)), constant_values=-1)
    label_rows, label_cols = label_rows.reshape(-1, 1), label_cols.reshape(1, -1)

    qkv, context, log_sum = attend(inputs, w_qkv_all, rows, segment)
    context, pieces_out_in, levels_back, cots = phase(
        context, pieces_out_in, levels_back, (passage_cot, query_cot)
    )

    cores_out_in, core_plan = gather_cores(pieces_out_in, plan)
    cores_out_in, levels_back, cots = phase(cores_out_in, levels_back, cots)

    pieces_back, plan = gather_columns(place, levels_back)
    swapped = swap_in(place, *cots)
    w_out_all, w_in_all = assemble(
        place,
        cores_out_in,
        core_plan,
        [(0, 0, 0, 0)] + [(1, part, 0, (part + 1) * model_width) for part in range(in_parts)],
        [(1, w_rows, model_width), (in_parts, w_rows, model_width)],
    )
    normed, normed_low, unit_one, scale_one, stats_one = branch_layer(
        context, w_out_all, inputs, rows, valid
    )
    active, slope = hidden_layer(normed_low, w_in_all, inb_row)
    active, pieces_back, swapped = phase(active, pieces_back, swapped)

    cores_back, core_plan = gather_cores(pieces_back, plan)
    cot = to_row(place, passage_cot, query_cot, swapped)
    if s != 2:
        back_shape = [(1, w_back.shape[1], model_width)]
        cores_back = assemble(place, cores_back, core_plan, [(0, 0, 0, 0)], back_shape)
        cores_back, core_plan = [cores_back[0][0]], None
    output_low, unit_two, scale_two, pooled, stats_two, w_back_all = output_layer(
        place, active, cores_back, core_plan, normed, rows, valid, hot
    )
    pooled, cot = phase(pooled, cot)

    column = sum([flip(pooled, "wide", k * s).astype(F32) for k in (3, 2, 1)], pooled.astype(F32))
    seen = column.astype(BF)[None]
    if s == 2:
        seen = jnp.concatenate([seen] + [flip_both(seen, dy, 2 * dx) for dx, dy in OTHERS])
        seen = jnp.concatenate([seen, flip(seen, "narrow", 1)])
    else:
        for axis, step in [("wide", b) for b in bits_of(s)] + [
            ("narrow", b) for b in reversed(bits_of(narrow))
        ]:
            seen = jnp.concatenate([seen, flip(seen, axis, step)])
    seen = seen.reshape(-1, model_width)
    if s == 2:
        (grad_pool,) = calls(match_kernel, [((POOL, model_width), F32)], 3)(
            seen, label_rows, label_cols
        )
    else:
        grad_pool = match_grads(seen, label_rows, label_cols)

    grad_pool, output_low = phase(grad_pool, output_low)
    if s == 2:
        out_four = row_pieces(place, output_low)
    grad_resid_two, grad_ffn, sums_two = output_back(
        cot, valid, hot, grad_pool, unit_two, scale_two, rows
    )
    if s == 2:
        send_c, keep_c = products_back(place, active, grad_ffn)
        send_c, out_four = phase(send_c, out_four)
        got_c = flip(send_c, "narrow", 1)
        shares_c = column_shares(place, keep_c, got_c)
        shares_c, grad_ffn = phase(shares_c, grad_ffn)

        columns_c = send_columns(shares_c)
        swapped = swap_out(place, out_four)
    grad_hidden, inb_sums, grad_residual, grad_branch, blocks_b, sums_one = hidden_back(
        grad_ffn, w_back_all, slope, w_in_all, grad_resid_two, unit_one, scale_one, rows, narrow
    )
    if s == 2:
        send_b, keep_b = products_out_in(place, context, blocks_b, normed_low, grad_hidden)
        send_b, columns_c, swapped = phase(send_b, columns_c, swapped)
        passage_out, query_out = from_row(place, out_four, swapped)

        got_b = flip(send_b, "narrow", 1)
        level_c = level_sums(columns_c)
        shares_b = column_shares(place, keep_b, got_b)
        shares_b, level_c, grad_branch = phase(shares_b, level_c, grad_branch)

        columns_b = send_columns(shares_b)
        levels_c = across_levels(level_c, s)
    grad_qkv, blocks_a, sums_qkv = attend_back(
        grad_branch, w_out_all[0], qkv, log_sum, segment, narrow
    )
    if s == 2:
        send_a, keep_a = products_qkv(place, inputs, blocks_a)
        send_a, grad_qkv, columns_b, levels_c = phase(send_a, grad_qkv, columns_b, levels_c)

        got_a = flip(send_a, "narrow", 1)
    input_grad = input_back(grad_qkv, w_qkv_all, grad_residual)
    if s == 2:
        got_a, input_grad, columns_b = phase(got_a, input_grad, columns_b)

        in_four = row_pieces(place, input_grad)
        levels_b = swap_shares(place, level_shares(place, columns_b))
        shares_a = column_shares(place, keep_a, got_a)
        shares_a, levels_b, in_four, sums_qkv, levels_c = phase(
            shares_a, levels_b, in_four, sums_qkv, levels_c
        )

        columns_a = send_columns(shares_a)
        swapped = swap_out(place, in_four)
        packed = pack_sums(devices, sums_qkv, sums_one, sums_two, inb_sums, stats_one, stats_two)
        grad_w_back = finish_back(levels_c)
        columns_a, swapped, packed = phase(columns_a, swapped, packed)

        packed = lax.all_to_all(packed, BOTH, 0, 0, tiled=True)
        levels_a = swap_shares(place, level_shares(place, columns_a))
        grad_w_out, grad_w_in = finish_out_in(place, levels_b, model_width // place.wide)
        passage_grad, query_grad = from_row(place, in_four, swapped)
        grad_w_qkv = finish_qkv(place, levels_a)
    else:
        packed = pack_sums(devices, sums_qkv, sums_one, sums_two, inb_sums, stats_one, stats_two)
        packed = lax.all_to_all(packed, BOTH, 0, 0, tiled=True)
        grad_w_back = scatter_tower(place, grad_blocks(active, grad_ffn, narrow))
        grad_w_out = scatter_tower(place, grad_blocks(context, grad_branch, narrow))
        grad_w_in = scatter_tower(place, grad_blocks(normed_low, grad_hidden, narrow))
        flat = jnp.moveaxis(grad_qkv, 0, 1).reshape(length, -1)
        grad_w_qkv = scatter_tower(place, grad_blocks(inputs, flat, narrow))
        out_four, in_four = row_pieces(place, output_low), row_pieces(place, input_grad)
        passage_out, query_out = from_row(place, out_four, swap_out(place, out_four))
        passage_grad, query_grad = from_row(place, in_four, swap_out(place, in_four))

    packed = packed.reshape(LEVELS, -1, packed.shape[1]).sum(axis=1)
    packed = jnp.stack([packed[1] + packed[2] + packed[3], packed[0]])
    edges = [n_bias * piece, (n_bias + n_gain) * piece]
    edges.append(edges[1] + in_bias.shape[1])
    grad_biases = packed[:, : edges[0]].reshape(2, n_bias, piece)
    grad_gains = packed[:, edges[0] : edges[1]].reshape(2, n_gain, piece)
    grad_inb = packed[:, edges[1] : edges[2]]
    totals = packed[:, edges[2] : edges[2] + 5]
    rms_stats = jnp.sqrt(totals[:, :4] / (totals[:, 4:] * model_width))
    return (
        passage_out,
        query_out,
        passage_grad,
        query_grad,
        grad_w_qkv,
        grad_w_out,
        grad_w_in,
        grad_w_back,
        grad_biases,
        grad_gains,
        grad_inb,
        rms_stats,
    )


def solution(mesh):
    return jax.shard_map(
        body,
        mesh=mesh,
        in_specs=(
            P("wide", "narrow", None),
            P("wide", "narrow", None),
            P("wide", "narrow", None),
            P("wide", "narrow", None),
            P("wide", None),
            P("wide", None),
            P("wide"),
            P(None, ("wide", "narrow"), None),
            P(None, ("wide", "narrow"), None),
            P(None, ("wide", "narrow"), None),
            P(None, ("wide", "narrow"), None),
            P(None, None, ("wide", "narrow")),
            P(None, None, ("wide", "narrow")),
            P(None, ("wide", "narrow")),
        ),
        out_specs=(
            P("wide", "narrow", None),
            P("wide", "narrow", None),
            P("wide", "narrow", None),
            P("wide", "narrow", None),
            P(None, "wide", "narrow"),
            P(None, "wide", "narrow"),
            P(None, "wide", "narrow"),
            P(None, "wide", "narrow"),
            P(None, None, ("wide", "narrow")),
            P(None, None, ("wide", "narrow")),
            P(None, ("wide", "narrow")),
            P(),
        ),
        check_vma=False,
    )
```

```python
import functools
import math

import jax
import jax.numpy as jnp
from jax import lax
from jax.experimental import pallas as pl
from jax.experimental.pallas import tpu as pltpu
from jax.sharding import PartitionSpec as P

HEAD_DIM = 64
LEVELS = 4
GROUP = 4
POOL = 32
STEP = 128
VMEM = 58 << 20
OTHERS = ((1, 1), (1, 0), (0, 1))


def cost(us):
    return pl.CostEstimate(flops=int(us * 1.15e9), bytes_accessed=1024, transcendentals=0)


EPSILON = 1e-05
SCORE_DIV = 12.0
MASKED = -1e30
BF = jnp.bfloat16
F32 = jnp.float32
BOTH = ("wide", "narrow")


def matmul(left, right):
    return jnp.dot(left, right, preferred_element_type=F32)


def inner_rows(left, right):
    return lax.dot_general(left, right, (((0,), (0,)), ((), ())), preferred_element_type=F32)


def inner_cols(left, right):
    return lax.dot_general(left, right, (((1,), (1,)), ((), ())), preferred_element_type=F32)


def flip(x, axis, mask):
    size = lax.axis_size(axis)
    return lax.ppermute(x, axis, [(i, i ^ mask) for i in range(size)])


def flip_both(x, wide_mask, narrow_mask):
    wide, narrow = lax.axis_size("wide"), lax.axis_size("narrow")
    mask = wide_mask * narrow + narrow_mask
    return lax.ppermute(x, BOTH, [(i, i ^ mask) for i in range(wide * narrow)])


def phase(*values):
    return lax.optimization_barrier(values)


def across_levels(x, stride):
    groups = [[k * stride + i for k in range(LEVELS)] for i in range(stride)]
    return lax.all_to_all(x, "wide", 0, 0, axis_index_groups=groups, tiled=True)


def swap_levels(x, k, stride):
    pairs = []
    for i in range(stride):
        pairs += [(i, k * stride + i), (k * stride + i, i)]
    return lax.ppermute(x, "wide", pairs)


def bits_of(size):
    return [1 << b for b in range(size.bit_length() - 1)]


class Place:
    def __init__(self):
        self.wide = lax.axis_size("wide")
        self.narrow = lax.axis_size("narrow")
        self.stride = self.wide // LEVELS
        self.w = lax.axis_index("wide")
        self.n = lax.axis_index("narrow")
        self.z = self.w // self.stride
        self.y = self.w % self.stride
        self.me = self.w * self.narrow + self.n


def swap_in(place, pass_part, query_part):
    query = jnp.broadcast_to(query_part, (LEVELS, *query_part.shape[1:]))
    first = jnp.concatenate([query_part, pass_part])
    return across_levels(jnp.where(place.z == 0, first, query), place.stride)


def swap_in_directly(place, pass_part, query_part):
    return [
        swap_levels(jnp.where(place.z == 0, pass_part[k - 1], query_part[0]), k, place.stride)
        for k in range(1, LEVELS)
    ]


def join_swapped(place, query_part, got):
    first = jnp.where(place.z == 0, query_part[0], got[0] + got[1] + got[2])
    return jnp.stack([first] + got)


def to_row(place, pass_part, query_part, got):
    four = jnp.where(place.z == 0, got, jnp.concatenate([pass_part, got[:1]]))
    mine = lax.all_to_all(four, "narrow", 0, 0, tiled=True)
    return mine.reshape(-1, mine.shape[-1])


def row_pieces(place, row):
    return lax.all_to_all(
        row.reshape(place.narrow, -1, row.shape[-1]), "narrow", 0, 0, tiled=True
    )


def swap_out(place, four):
    last = jnp.broadcast_to(four[3:], four.shape)
    return across_levels(jnp.where(place.z == 0, four, last), place.stride)


def from_row(place, four, got):
    pass_part = jnp.where(place.z == 0, got[1:], four[:3])
    query_part = jnp.where(place.z == 0, four[:1], got[:1])
    return pass_part, query_part


def toggle(places, mask):
    return [(p[0], p[1] ^ mask) if isinstance(p, tuple) else p ^ mask for p in places]


def block_of(me, place, level):
    if isinstance(place, tuple):
        return ((me & (level - 1)) ^ place[1]) + place[0] * level
    return me ^ place


def assemble_kernel(plan, layout, level, me_ref, *refs):
    pieces, outs, sems = refs[: len(plan)], refs[len(plan) : -1], refs[-1]
    me = me_ref[0]
    copies = []
    for piece, masks in zip(pieces, plan):
        for slot, mask in enumerate(masks):
            for out, part, row, column in layout:
                target = outs[out].at[part, block_of(me, mask, level)]
                rows, columns = outs[out].shape[2:]
                source = piece.at[slot, pl.ds(row, rows), pl.ds(column, columns)]
                copies.append(pltpu.make_async_copy(source, target, sems.at[len(copies)]))
    for copy in copies:
        copy.start()
    for copy in copies:
        copy.wait()


def assemble(place, pieces, plan, layout, outs):
    total = place.wide * place.narrow
    made = pl.pallas_call(
        functools.partial(assemble_kernel, plan, layout, total // LEVELS),
        out_shape=[jax.ShapeDtypeStruct((out[0], total, *out[1:]), BF) for out in outs],
        in_specs=[pl.BlockSpec(memory_space=pltpu.SMEM)]
        + [pl.BlockSpec(memory_space=pl.ANY)] * len(pieces),
        out_specs=[pl.BlockSpec(memory_space=pltpu.VMEM)] * len(outs),
        scratch_shapes=[pltpu.SemaphoreType.DMA((total * len(layout),))],
        cost_estimate=cost(0.1),
        compiler_params=pltpu.CompilerParams(vmem_limit_bytes=VMEM),
    )(place.me.reshape(1), *pieces)
    return [out.reshape(out.shape[0], -1, out.shape[3]) for out in made]


def pick_kernel(z_ref, w_ref, bias_ref, gain_ref, inb_ref, ints_ref, *refs):
    outs, small = refs[:-1], refs[-1]
    rows, width = w_ref.shape[1], small.shape[1]
    n_bias, n_gain = bias_ref.shape[1], gain_ref.shape[1]
    for k, out in enumerate(outs):
        tower = jnp.where(z_ref[0] == k, 1, 0)
        for part in range(3):
            out[part * rows : (part + 1) * rows] = w_ref[tower, :, part * width : (part + 1) * width]
        small[...] = jnp.zeros(small.shape, F32)
        small[:n_bias, : bias_ref.shape[2]] = bias_ref[tower].astype(F32)
        small[n_bias : n_bias + n_gain, : gain_ref.shape[2]] = gain_ref[tower].astype(F32)
        small[:1, 128 : 128 + inb_ref.shape[2]] = inb_ref[tower].astype(F32)
        small[:1, 256 : 256 + ints_ref.shape[1]] = ints_ref[...].astype(F32)
        out[3 * rows :] = small[...].astype(BF)


def pick_towers(place, w_qkv, biases, norm_gains, in_bias, ints):
    width = w_qkv.shape[2] // 3
    vmem = pl.BlockSpec(memory_space=pltpu.VMEM)
    return calls(
        pick_kernel,
        [((3 * w_qkv.shape[1] + 8, width), BF)] * LEVELS,
        2,
        in_specs=[pl.BlockSpec(memory_space=pltpu.SMEM)] + [vmem] * 5,
        scratch_shapes=[pltpu.VMEM((8, width), F32)],
    )(place.z.reshape(1), w_qkv, biases, norm_gains, in_bias[:, None], ints[None])


def gather_levels(place, pair):
    first = lax.broadcasted_iota(jnp.int32, (LEVELS, 1, 1), 0) == 0
    return across_levels(jnp.where(first, pair[1:], pair[:1]), place.stride)


def gather_columns(place, levels, own=None):
    s, narrow = place.stride, place.narrow
    if own is None:
        own = [(level, 0) for level in range(LEVELS)]
    pieces, plan = [levels], [own]
    if s == 2:
        for dx, dy in OTHERS:
            pieces.append(flip_both(levels, dy, 2 * dx))
            plan.append(toggle(own, dy * narrow + 2 * dx))
    else:
        for b in bits_of(s):
            for i in range(len(pieces)):
                pieces.append(flip(pieces[i], "wide", b))
                plan.append(toggle(plan[i], b * narrow))
        for i in range(len(pieces)):
            pieces.append(flip(pieces[i], "narrow", 2))
            plan.append(toggle(plan[i], 2))
    return pieces, plan


def gather_cores(pieces, plan):
    others = [flip(piece, "narrow", 1) for piece in pieces]
    return list(pieces) + others, plan + [toggle(places, 1) for places in plan]


def pick(x, index, dim):
    return lax.dynamic_index_in_dim(x, index, dim, keepdims=False)


def halve(x, place, axis, mask, dim):
    index = place.n if axis == "narrow" else place.w
    bit = jnp.where((index & mask) != 0, 1, 0)
    got = flip(pick(x, 1 - bit, dim).astype(BF), axis, mask)
    return pick(x, bit, dim) + got.astype(F32)


def scatter_tower(place, partial):
    s = place.stride
    rows, narrow, cols = partial.shape
    per = rows // place.wide
    x = partial.reshape(rows, 2, 2, cols)
    x = halve(x, place, "narrow", 1, 2)
    x = x.reshape(LEVELS, s, per, 2, cols)
    first, second = x[:2], x[2:]

    def over_columns(part):
        for b in reversed(bits_of(s)):
            shape = part.shape
            part = part.reshape(shape[0], 2, shape[1] // 2, *shape[2:])
            part = halve(part, place, "wide", b, 1)
        return part[:, 0]

    first = over_columns(halve(first, place, "narrow", 2, 3))
    second = halve(over_columns(second), place, "narrow", 2, 2)
    return jnp.stack(sum_levels(place, send_levels(place, jnp.concatenate([first, second]))))


def send_levels(place, levels):
    slots = [None] * LEVELS
    slots[0] = pick(levels, place.z, 0)
    for k in (3, 2, 1):
        slots[k] = flip(pick(levels, place.z ^ k, 0).astype(BF), "wide", k * place.stride)
    return slots


def sum_levels(place, slots):
    tower0 = sum(jnp.where(place.z == k, 0.0, slots[k].astype(F32)) for k in range(LEVELS))
    tower1 = sum(jnp.where(place.z == k, slots[k].astype(F32), 0.0) for k in range(LEVELS))
    return tower0, tower1


def share_kernel(at_ref, keep_ref, got_ref, *out_refs):
    x, y = at_ref[0], at_ref[1]

    def body(level, carry):
        for ref, (dx, dy) in zip(out_refs, ((0, 0), *OTHERS)):
            at = (x ^ dx, level, y ^ dy)
            ref[level] = (keep_ref[at].astype(F32) + got_ref[at].astype(F32)).astype(BF)
        return carry

    lax.fori_loop(0, keep_ref.shape[1], body, 0)


def column_shares(place, keep, got):
    r, c = got.shape[2:]
    half = LEVELS // 2
    block = pl.BlockSpec((2, half, place.stride, r, c), lambda i, at: (0, i, 0, 0, 0))
    out = pl.BlockSpec((half, r, c), lambda i, at: (i, 0, 0))
    shape = (2, LEVELS, place.stride, r, c)
    return pl.pallas_call(
        share_kernel,
        grid_spec=pltpu.PrefetchScalarGridSpec(
            num_scalar_prefetch=1, grid=(2,), in_specs=[block] * 2, out_specs=[out] * 4
        ),
        out_shape=[jax.ShapeDtypeStruct((LEVELS, r, c), BF)] * 4,
        compiler_params=pltpu.CompilerParams(vmem_limit_bytes=VMEM),
        cost_estimate=cost(1),
    )(jnp.stack([place.n // 2, place.y]), keep.reshape(shape), got.reshape(shape))


def send_columns(shares):
    return [shares[0]] + [
        flip_both(sent, dy, 2 * dx) for sent, (dx, dy) in zip(shares[1:], OTHERS)
    ]


def level_kernel(z_ref, own_ref, *refs):
    got_refs, out_refs = refs[:3], refs[3:]
    step = 24

    def body(i, carry):
        rows = pl.ds(pl.multiple_of(i * step, step), step)
        for k, out_ref in enumerate(out_refs):
            at = (z_ref[0] ^ k, rows)
            total = own_ref[at].astype(F32)
            for ref in got_refs:
                total = total + ref[at].astype(F32)
            out_ref[rows] = total.astype(out_ref.dtype)
        return carry

    lax.fori_loop(0, own_ref.shape[1] // step, body, 0)


def level_shares(place, columns):
    r, c = columns[0].shape[1:]
    vmem = pl.BlockSpec(memory_space=pltpu.VMEM)
    return pl.pallas_call(
        level_kernel,
        in_specs=[pl.BlockSpec(memory_space=pltpu.SMEM)] + [vmem] * 4,
        out_specs=[vmem] * 4,
        out_shape=[jax.ShapeDtypeStruct((r, c), F32)] + [jax.ShapeDtypeStruct((r, c), BF)] * 3,
        compiler_params=pltpu.CompilerParams(vmem_limit_bytes=VMEM),
        cost_estimate=cost(1),
    )(place.z.reshape(1), *columns)


def level_sums_kernel(*refs):
    def body(at, carry):
        refs[-1][at] = sum(ref[at].astype(F32) for ref in refs[:-1]).astype(BF)
        return carry

    lax.fori_loop(0, LEVELS, body, 0)


def level_sums(columns):
    shape = columns[0].shape
    return calls(level_sums_kernel, [(shape, BF)], 3)(*columns)[0]


def swap_shares(place, shares):
    slots = [shares[0], None, None, None]
    for k in (3, 2, 1):
        slots[k] = flip(shares[k], "wide", k * place.stride)
    return slots


def product_kernel(step, me_ref, *refs):
    send_ref, keep_ref = refs[-2:]
    left_refs = refs[:-2]
    to_send = pl.program_id(0) < 2

    @pl.when(to_send)
    def _():
        step(left_refs, lambda at, v: send_ref.__setitem__((0, *at), v.astype(BF)))

    @pl.when(jnp.logical_not(to_send))
    def _():
        step(left_refs, lambda at, v: keep_ref.__setitem__((0, *at), v.astype(BF)))


def products(place, step, operands, specs, block):
    def target(j, me):
        return (j % 2) * 2 + jnp.where(j < 2, 1 - me[0] % 2, me[0] % 2)

    wide = place.wide
    grid_spec = pltpu.PrefetchScalarGridSpec(
        num_scalar_prefetch=1,
        grid=(4,),
        in_specs=specs(target),
        out_specs=[
            pl.BlockSpec((1, wide, *block), lambda j, me: (jnp.minimum(j, 1), 0, 0, 0)),
            pl.BlockSpec((1, wide, *block), lambda j, me: (jnp.maximum(j - 2, 0), 0, 0, 0)),
        ],
    )
    return pl.pallas_call(
        functools.partial(product_kernel, step),
        grid_spec=grid_spec,
        out_shape=[
            jax.ShapeDtypeStruct((2, wide, *block), BF),
            jax.ShapeDtypeStruct((2, wide, *block), BF),
        ],
        compiler_params=pltpu.CompilerParams(vmem_limit_bytes=VMEM),
        cost_estimate=cost(8),
    )(place.n.reshape(1), *operands)


def whole(shape):
    return pl.BlockSpec(shape, lambda j, me: (0,) * len(shape))


def grad_blocks(left, right, narrow):
    out = inner_rows(left, right)
    return out.reshape(out.shape[0], narrow, -1)


def products_back_kernel(core_ref, left_ref, right_ref, send_ref, keep_ref, turned_ref):
    @pl.when(pl.program_id(0) == 0)
    def _():
        turned_ref[...] = right_ref[...].T

    cols, rows = send_ref.shape[2:]
    first = core_ref[0] == 0

    def body(x, carry):
        at = pl.ds(pl.multiple_of(x * 2 * cols, 2 * cols), 2 * cols)
        value = matmul(turned_ref[at], left_ref[...]).astype(BF)
        for w in range(2):
            columns = slice(w * rows, (w + 1) * rows)
            even, odd = value[:cols, columns], value[cols:, columns]
            keep_ref[x, w] = jnp.where(first, even, odd)
            send_ref[x, w] = jnp.where(first, odd, even)
        return carry

    lax.fori_loop(0, 2, body, 0)


def products_back(place, active, grad_ffn):
    t, ff = active.shape
    d = grad_ffn.shape[1]
    cols, rows = d // place.narrow, ff // place.wide
    out = pl.BlockSpec((2, 2, cols, rows), lambda j, core: (0, j, 0, 0))
    return pl.pallas_call(
        products_back_kernel,
        grid_spec=pltpu.PrefetchScalarGridSpec(
            num_scalar_prefetch=1,
            grid=(place.wide // 2,),
            in_specs=[pl.BlockSpec((t, 2 * rows), lambda j, core: (0, j)), whole((t, d))],
            out_specs=[out, out],
            scratch_shapes=[pltpu.VMEM((d, t), BF)],
        ),
        out_shape=[jax.ShapeDtypeStruct((2, place.wide, cols, rows), BF)] * 2,
        compiler_params=pltpu.CompilerParams(vmem_limit_bytes=VMEM),
        cost_estimate=cost(7),
    )((place.n % 2).reshape(1), active, grad_ffn)


def finish_back(levels):
    levels = levels.astype(F32)
    return jnp.stack([(levels[1] + levels[2] + levels[3]).T, levels[0].T])


def products_out_in(place, context, blocks, normed, grad_hidden):
    narrow = place.narrow
    t, d = context.shape
    rows = d // place.wide
    cols_out, cols_in = blocks.shape[2], grad_hidden.shape[1] // narrow
    fold = cols_in // cols_out
    low = rows // fold

    def step(refs, store):
        context_ref, branch_ref, normed_ref, hidden_ref = refs

        def body(i, carry):
            at = pl.ds(pl.multiple_of(i * 4 * rows, 4 * rows), 4 * rows)
            value = inner_rows(normed_ref[:, at], hidden_ref[...])
            for w in range(4):
                store((4 * i + w, slice(0, rows)), value[w * rows : (w + 1) * rows])
            value = inner_rows(context_ref[:, at], branch_ref[0])
            for w in range(4):
                for g in range(fold):
                    store(
                        (4 * i + w, slice(rows, rows + low), slice(g * cols_out, (g + 1) * cols_out)),
                        value[w * rows + g * low : w * rows + (g + 1) * low],
                    )
            return carry

        lax.fori_loop(0, place.wide // 4, body, 0)

    return products(
        place,
        step,
        (context, blocks, normed, grad_hidden),
        lambda target: [
            whole((t, d)),
            pl.BlockSpec((1, t, cols_out), lambda j, me: (target(j, me), 0, 0)),
            whole((t, d)),
            pl.BlockSpec((t, cols_in), lambda j, me: (0, target(j, me))),
        ],
        (rows + low, cols_in),
    )


def finish_out_in(place, slots, rows):
    parts = sum_levels(place, slots)
    low, cols = parts[0].shape[0] - rows, parts[0].shape[1]
    fold = rows // low
    grad_in = jnp.stack([part[:rows] for part in parts])
    grad_out = [
        jnp.moveaxis(part[rows:].reshape(low, fold, -1), 1, 0).reshape(rows, -1) for part in parts
    ]
    return jnp.stack(grad_out), grad_in


def products_qkv(place, inputs, blocks):
    t, d = inputs.shape
    rows, cols = d // place.wide, blocks.shape[2]
    half = rows // 2

    def step(refs, store):
        left, right = refs
        value = inner_rows(left[...], right[0])
        for w in range(place.wide):
            for g in range(2):
                store(
                    (w, slice(None), slice(g * cols, (g + 1) * cols)),
                    value[w * rows + g * half : w * rows + (g + 1) * half],
                )

    return products(
        place,
        step,
        (inputs, blocks),
        lambda target: [
            whole((t, d)),
            pl.BlockSpec((1, t, cols), lambda j, me: (target(j, me), 0, 0)),
        ],
        (half, 2 * cols),
    )


def finish_qkv(place, slots):
    parts = sum_levels(place, slots)
    cols = parts[0].shape[1] // 2
    return jnp.stack([jnp.concatenate([p[:, :cols], p[:, cols:]]) for p in parts])


def attend_kernel(x_ref, w_ref, rows_ref, seg_row_ref, seg_col_ref, qkv_ref, ctx_ref, lse_ref):
    x = x_ref[...]
    same = seg_col_ref[...] == seg_row_ref[...]

    def project(part, carry):
        bias = jnp.where(part == 0, rows_ref[0:1], jnp.where(part == 2, rows_ref[1:2], 0.0))
        qkv_ref[part] = (matmul(x, w_ref[part]) + bias).astype(BF)
        return carry

    lax.fori_loop(0, 3, project, 0)
    for h in range(GROUP):
        lanes = slice(h * HEAD_DIM, (h + 1) * HEAD_DIM)
        q, k, v = qkv_ref[0, :, lanes], qkv_ref[1, :, lanes], qkv_ref[2, :, lanes]
        scores = jnp.where(same, inner_cols(k, q) * HEAD_DIM ** (-0.5), MASKED)
        top = jnp.max(scores, axis=0, keepdims=True)
        shifted = jnp.exp(scores - top)
        total = jnp.sum(shifted, axis=0, keepdims=True)
        probs = (shifted * (1.0 / total)).astype(BF)
        ctx_ref[:, lanes] = inner_rows(probs, v).astype(BF)
        lse_ref[0, h : h + 1, :] = top + jnp.log(total)


def attend(x, w_qkv, rows, segment):
    t, d = x.shape
    width = GROUP * HEAD_DIM
    steps = d // width
    return pl.pallas_call(
        attend_kernel,
        grid=(steps,),
        in_specs=[
            pl.BlockSpec((t, d), lambda j: (0, 0)),
            pl.BlockSpec((3, d, width), lambda j: (0, 0, j)),
            pl.BlockSpec((8, width), lambda j: (0, j)),
            pl.BlockSpec((1, t), lambda j: (0, 0)),
            pl.BlockSpec((t, 1), lambda j: (0, 0)),
        ],
        out_specs=[
            pl.BlockSpec((3, t, width), lambda j: (0, 0, j)),
            pl.BlockSpec((t, width), lambda j: (0, j)),
            pl.BlockSpec((1, GROUP, t), lambda j: (j, 0, 0)),
        ],
        out_shape=[
            jax.ShapeDtypeStruct((3, t, d), BF),
            jax.ShapeDtypeStruct((t, d), BF),
            jax.ShapeDtypeStruct((steps, GROUP, t), F32),
        ],
        compiler_params=pltpu.CompilerParams(vmem_limit_bytes=VMEM),
        cost_estimate=cost(0.1),
    )(x, w_qkv, rows, segment.reshape(1, t), segment.reshape(t, 1))


def attend_back_kernel(
    gb_ref, w_ref, qkv_ref, lse_ref, seg_row_ref, seg_col_ref, out_ref, blocks_ref, sums_ref, grad_ref
):
    scale = HEAD_DIM ** (-0.5)
    same = seg_col_ref[...] == seg_row_ref[...]
    grad_ref[...] = inner_cols(gb_ref[...], w_ref[...]).astype(BF)

    def pair(p, carry):
        at = pl.ds(pl.multiple_of(p * 2 * HEAD_DIM, 2 * HEAD_DIM), 2 * HEAD_DIM)
        queries, keys, values = qkv_ref[0, :, at], qkv_ref[1, :, at], qkv_ref[2, :, at]
        grads, outs = grad_ref[:, at], []
        for h in range(2):
            lanes = slice(h * HEAD_DIM, (h + 1) * HEAD_DIM)
            q, k, v, g = queries[:, lanes], keys[:, lanes], values[:, lanes], grads[:, lanes]
            scores = jnp.where(same, inner_cols(k, q) * scale, MASKED)
            probs = jnp.exp(scores - lse_ref[0, pl.ds(2 * p + h, 1), :])
            grad_probs = inner_cols(v, g)
            delta = jnp.sum(probs * grad_probs, axis=0, keepdims=True)
            grad_scores = (probs * (grad_probs - delta)).astype(BF)
            outs.append(
                (
                    (inner_rows(grad_scores, k) * scale).astype(BF),
                    (matmul(grad_scores, q) * scale).astype(BF),
                    matmul(probs.astype(BF), g).astype(BF),
                )
            )
        for part in range(3):
            out_ref[part, :, at] = jnp.concatenate([outs[0][part], outs[1][part]], axis=1)
        return carry

    lax.fori_loop(0, GROUP // 2, pair, 0)
    sums_ref[0:1] = jnp.sum(out_ref[0].astype(F32), axis=0, keepdims=True)
    sums_ref[1:2] = jnp.sum(out_ref[2].astype(F32), axis=0, keepdims=True)
    per_block = blocks_ref.shape[2] // HEAD_DIM
    heads = blocks_ref.shape[0] * per_block // 3
    for step in range(heads // GROUP):

        @pl.when(pl.program_id(0) == step)
        def _(step=step):
            for part in range(3):
                for h in range(GROUP):
                    block, at = divmod(part * heads + step * GROUP + h, per_block)
                    blocks_ref[block, :, at * HEAD_DIM : (at + 1) * HEAD_DIM] = out_ref[
                        part, :, h * HEAD_DIM : (h + 1) * HEAD_DIM
                    ]


def attend_back(grad_branch, w_out, qkv, lse, segment, narrow):
    t, d = grad_branch.shape
    width = GROUP * HEAD_DIM
    return pl.pallas_call(
        attend_back_kernel,
        grid=(d // width,),
        in_specs=[
            pl.BlockSpec((t, d), lambda j: (0, 0)),
            pl.BlockSpec((width, d), lambda j: (j, 0)),
            pl.BlockSpec((3, t, width), lambda j: (0, 0, j)),
            pl.BlockSpec((1, GROUP, t), lambda j: (j, 0, 0)),
            pl.BlockSpec((1, t), lambda j: (0, 0)),
            pl.BlockSpec((t, 1), lambda j: (0, 0)),
        ],
        out_specs=[
            pl.BlockSpec((3, t, width), lambda j: (0, 0, j)),
            pl.BlockSpec((narrow, t, 3 * d // narrow), lambda j: (0, 0, 0)),
            pl.BlockSpec((2, width), lambda j: (0, j)),
        ],
        out_shape=[
            jax.ShapeDtypeStruct((3, t, d), BF),
            jax.ShapeDtypeStruct((narrow, t, 3 * d // narrow), BF),
            jax.ShapeDtypeStruct((2, d), F32),
        ],
        scratch_shapes=[pltpu.VMEM((t, width), BF)],
        compiler_params=pltpu.CompilerParams(vmem_limit_bytes=VMEM),
        cost_estimate=cost(20),
    )(grad_branch, w_out, qkv, lse, segment.reshape(1, t), segment.reshape(t, 1))


def hidden_kernel(x_ref, w_ref, bias_ref, active_ref, slope_ref, pre_ref):
    pre_ref[...] = matmul(x_ref[...], w_ref[0]) + bias_ref[...]

    def body(at, carry):
        pre = pre_ref[at]
        below = 0.5 + 0.5 * lax.erf(pre * 0.5**0.5)
        active_ref[at] = (pre * below).astype(BF)
        density = jnp.exp(-0.5 * pre * pre) * (2.0 * math.pi) ** (-0.5)
        slope_ref[at] = (below + pre * density).astype(BF)
        return carry

    by_rows(pre_ref.shape[0], body)


def hidden_layer(x, w_in, in_bias):
    t, d = x.shape
    parts, _, width = w_in.shape
    block = pl.BlockSpec((t, width), lambda j: (0, j))
    shape = jax.ShapeDtypeStruct((t, parts * width), BF)
    return pl.pallas_call(
        hidden_kernel,
        grid=(parts,),
        in_specs=[
            pl.BlockSpec((t, d), lambda j: (0, 0)),
            pl.BlockSpec((1, d, width), lambda j: (j, 0, 0)),
            pl.BlockSpec((1, width), lambda j: (0, j)),
        ],
        out_specs=[block, block],
        out_shape=[shape, shape],
        scratch_shapes=[pltpu.VMEM((t, width), F32)],
        compiler_params=pltpu.CompilerParams(vmem_limit_bytes=VMEM),
        cost_estimate=cost(8),
    )(x, w_in, in_bias)


def norm_parts(value):
    mean = jnp.mean(value, axis=-1, keepdims=True)
    centered = value - mean
    scale = lax.rsqrt(jnp.mean(centered * centered, axis=-1, keepdims=True) + EPSILON)
    return centered * scale, scale


def norm_back(grad, unit, scale, gain):
    e = grad * gain
    part = jnp.mean(e * unit, axis=-1, keepdims=True)
    return (e - jnp.mean(e, axis=-1, keepdims=True) - unit * part) * scale


def total(value):
    return jnp.sum(jnp.sum(value, axis=0, keepdims=True), axis=1, keepdims=True)


def column_sum(value):
    return jnp.sum(value, axis=0, keepdims=True)


def by_rows(count, body, carry=None):
    if carry is None:
        carry = jnp.zeros((1, 128), F32)
    return lax.fori_loop(
        0, count // STEP, lambda i, c: body(pl.ds(pl.multiple_of(i * STEP, STEP), STEP), c), carry
    )


def store_blocks(ref, at, value):
    count, _, width = ref.shape
    for i in range(count):
        ref[i, at] = value[:, i * width : (i + 1) * width]


def calls(kernel, outs, us, **kwargs):
    return pl.pallas_call(
        kernel,
        out_shape=[jax.ShapeDtypeStruct(shape, dtype) for shape, dtype in outs],
        compiler_params=pltpu.CompilerParams(vmem_limit_bytes=VMEM),
        cost_estimate=cost(us),
        **kwargs,
    )


def branch_kernel(ctx, w, x, rows, valid, normed, low, unit, scale, stats, acc):
    acc[...] = matmul(ctx[...], w[0])
    zero = jnp.zeros((1, acc.shape[1]), F32)

    def body(at, sums):
        branch = acc[at] + rows[2:3]
        residual = x[at].astype(F32) + branch
        unit[at], scale[at] = norm_parts(residual)
        normed[at] = unit[at] * rows[6:7] + rows[3:4]
        low[at] = normed[at].astype(BF)
        return tuple(
            s + column_sum(valid[at] * value * value) for s, value in zip(sums, (residual, branch))
        )

    for i, value in enumerate(by_rows(acc.shape[0], body, (zero, zero))):
        stats[i : i + 1] = jnp.broadcast_to(total(value), (1, 128))


def branch_layer(context, w_out, inputs, rows, valid):
    t, d = inputs.shape
    outs = [((t, d), F32), ((t, d), BF), ((t, d), F32), ((t, 1), F32), ((2, 128), F32)]
    scratch = [pltpu.VMEM((t, d), F32)]
    return calls(branch_kernel, outs, 5, scratch_shapes=scratch)(
        context, w_out, inputs, rows, valid
    )


def output_kernel(plan, level, me_ref, active, normed, rows, valid, hot, *refs):
    pieces = refs[:-8]
    low, unit, scale, pooled, stats, w, acc, sems = refs[-8:]
    step = pl.program_id(0)
    width = active.shape[1]
    block = pieces[0].shape[1]

    @pl.when(step == 0)
    def _():
        copies = []
        if plan is None:
            copies.append(pltpu.make_async_copy(pieces[0], w, sems.at[0]))
        for piece, masks in zip(pieces, plan or []):
            for slot, mask in enumerate(masks):
                at = pl.multiple_of(block_of(me_ref[0], mask, level) * block, block)
                target = w.at[pl.ds(at, block)]
                copies.append(
                    pltpu.make_async_copy(piece.at[slot], target, sems.at[len(copies)])
                )
        for copy in copies:
            copy.start()
        for copy in copies:
            copy.wait()

    product = matmul(active[...], w[pl.ds(pl.multiple_of(step * width, width), width)])

    @pl.when(step == 0)
    def _():
        acc[...] = product

    @pl.when(step > 0)
    def _():
        acc[...] += product

    @pl.when(step == pl.num_programs(0) - 1)
    def _():
        zero = jnp.zeros((1, acc.shape[1]), F32)

        def body(at, sums):
            ffn_out = acc[at] + rows[4:5]
            residual = normed[at] + ffn_out
            unit[at], scale[at] = norm_parts(residual)
            low[at] = (unit[at] * rows[7:8] + rows[5:6]).astype(BF)
            values = (valid[at] * residual * residual, valid[at] * ffn_out * ffn_out)
            return tuple(s + column_sum(value) for s, value in zip(sums, values))

        sums = by_rows(acc.shape[0], body, (zero, zero))
        for i, value in enumerate((*sums, valid[...])):
            stats[i : i + 1] = jnp.broadcast_to(total(value), (1, 128))
        pooled[...] = matmul(hot[...].astype(BF), low[...]).astype(BF)


def all_of(shape):
    return pl.BlockSpec(shape, lambda j: (0,) * len(shape))


def output_layer(place, active, pieces, plan, normed, rows, valid, hot):
    t, ff = active.shape
    d = normed.shape[1]
    outs = [((t, d), BF), ((t, d), F32), ((t, 1), F32), ((hot.shape[0], d), BF), ((3, 128), F32)]
    outs.append(((ff, d), BF))
    return calls(
        functools.partial(output_kernel, plan, place.wide * place.narrow // LEVELS),
        outs,
        9,
        grid=(ff // d,),
        in_specs=[pl.BlockSpec(memory_space=pltpu.SMEM), pl.BlockSpec((t, d), lambda j: (0, j))]
        + [all_of(a.shape) for a in (normed, rows, valid, hot)]
        + [pl.BlockSpec(memory_space=pl.ANY)] * len(pieces),
        out_specs=[all_of(shape) for shape, _ in outs],
        scratch_shapes=[
            pltpu.VMEM((t, d), F32),
            pltpu.SemaphoreType.DMA((place.wide * place.narrow,)),
        ],
    )(place.me.reshape(1), active, normed, rows, valid, hot, *pieces)


def output_back_kernel(cot, valid, hot, pool, unit, scale, rows, grad, low, sums):
    zero = jnp.zeros((1, grad.shape[1]), F32)

    def body(at, totals):
        grad_out = cot[at].astype(F32) * valid[at] + lax.dot_general(
            hot[:, at],
            pool[...],
            (((0,), (0,)), ((), ())),
            precision=lax.Precision.HIGHEST,
            preferred_element_type=F32,
        )
        grad[at] = norm_back(grad_out, unit[at], scale[at], rows[7:8])
        low[at] = grad[at].astype(BF)
        values = (grad_out * unit[at], grad_out, low[at].astype(F32))
        return tuple(t + column_sum(value) for t, value in zip(totals, values))

    for i, value in enumerate(by_rows(grad.shape[0], body, (zero,) * 3)):
        sums[i : i + 1] = value


def output_back(cot, valid, hot, pool, unit, scale, rows):
    t, d = cot.shape
    outs = [((t, d), F32), ((t, d), BF), ((3, d), F32)]
    return calls(output_back_kernel, outs, 6)(cot, valid, hot, pool, unit, scale, rows)


def hidden_back_kernel(
    low, w_back, slope, w_in, grad, unit, scale, rows, hidden, inb, branch, blocks, sums, acc
):
    step = pl.program_id(0)
    product = inner_cols(low[...], w_back[...])
    hidden[...] = (product * slope[...].astype(F32)).astype(BF)
    inb[...] = column_sum(hidden[...].astype(F32))
    product = inner_cols(hidden[...], w_in[0])

    @pl.when(step == 0)
    def _():
        acc[...] = grad[...] + product

    @pl.when(step > 0)
    def _():
        acc[...] += product

    @pl.when(step == pl.num_programs(0) - 1)
    def _():
        zero = jnp.zeros((1, acc.shape[1]), F32)

        def body(at, totals):
            value = acc[at]
            branch[at] = norm_back(value, unit[at], scale[at], rows[6:7]).astype(BF)
            store_blocks(blocks, at, branch[at])
            values = (value * unit[at], value, branch[at].astype(F32))
            return tuple(t + column_sum(value) for t, value in zip(totals, values))

        for i, value in enumerate(by_rows(acc.shape[0], body, (zero,) * 3)):
            sums[i : i + 1] = value


def hidden_back(low, w_back, slope, w_in, grad, unit, scale, rows, narrow):
    t, d = low.shape
    ff = slope.shape[1]
    tile = pl.BlockSpec((t, d), lambda j: (0, j))
    outs = [
        ((t, ff), BF),
        ((1, ff), F32),
        ((t, d), BF),
        ((narrow, t, d // narrow), BF),
        ((3, d), F32),
    ]
    return calls(
        hidden_back_kernel,
        outs,
        14,
        grid=(ff // d,),
        in_specs=[
            all_of(low.shape),
            pl.BlockSpec((d, d), lambda j: (j, 0)),
            tile,
            pl.BlockSpec((1, d, d), lambda j: (j, 0, 0)),
        ]
        + [all_of(a.shape) for a in (grad, unit, scale, rows)],
        out_specs=[tile, pl.BlockSpec((1, d), lambda j: (0, j))]
        + [all_of(shape) for shape, _ in outs[2:]],
        scratch_shapes=[pltpu.VMEM((t, d), F32)],
    )(low, w_back, slope, w_in, grad, unit, scale, rows)


def input_back_kernel(grad, w, residual, out, acc):
    step = pl.program_id(0)
    product = inner_cols(grad[0], w[0])

    @pl.when(step == 0)
    def _():
        acc[...] = residual[...].astype(F32) + product

    @pl.when(step == 1)
    def _():
        acc[...] += product

    @pl.when(step == 2)
    def _():
        out[...] = (acc[...] + product).astype(BF)


def input_back(grad_qkv, w_qkv, residual):
    _, t, d = grad_qkv.shape
    return calls(
        input_back_kernel,
        [((t, d), BF)],
        6,
        grid=(3,),
        in_specs=[
            pl.BlockSpec((1, t, d), lambda j: (j, 0, 0)),
            pl.BlockSpec((1, d, d), lambda j: (j, 0, 0)),
            all_of((t, d)),
        ],
        out_specs=[all_of((t, d))],
        scratch_shapes=[pltpu.VMEM((t, d), F32)],
    )(grad_qkv, w_qkv, residual)[0]


def spread_masks(count, width):
    total_cols = count * width
    column = lax.broadcasted_iota(jnp.int32, (count, total_cols), 1)
    first = lax.broadcasted_iota(jnp.int32, (count, total_cols), 0) * width
    own = (column >= first) & (column < first + width)
    owner = jnp.sum(jnp.where(own, first, 0), axis=0, keepdims=True)
    within = lax.broadcasted_iota(jnp.int32, (width, total_cols), 1) - owner
    spread = within == lax.broadcasted_iota(jnp.int32, (width, total_cols), 0)
    return own, spread.astype(F32)


def unpack_kernel(small, rows, inb):
    count = small.shape[0]
    value = small[...].astype(F32)

    def unpack(part, masks):
        own, spread = masks
        placed = matmul(part.astype(BF), spread.astype(BF))
        return column_sum(jnp.where(own, placed, 0.0))

    width = rows.shape[1] // count
    masks = spread_masks(count, width)
    for r in range(8):
        rows[r : r + 1] = unpack(value[:, r, :width], masks)
    width = inb.shape[1] // count
    inb[...] = unpack(value[:, 0, 128 : 128 + width], spread_masks(count, width))


def unpack_params(small, d, ff):
    return calls(unpack_kernel, [((8, d), F32), ((1, ff), F32)], 0.1)(small)


def pack_kernel(attn, out, ffn, inb, stats_a, stats_b, packed, rows, parts):
    count = packed.shape[0]
    vectors = (attn[0:1], attn[1:2], out[2:3], out[1:2], ffn[2:3], ffn[1:2], out[0:1], ffn[0:1])

    def pack(vector, own, spread):
        return lax.dot_general(
            jnp.where(own, vector, 0.0),
            spread,
            (((1,), (1,)), ((), ())),
            precision=lax.Precision.HIGHEST,
            preferred_element_type=F32,
        )

    for i, vector in enumerate(vectors):
        rows[i : i + 1] = vector
    packed[...] = jnp.zeros(packed.shape, F32)
    width = rows.shape[1] // count
    masks = spread_masks(count, width)

    def body(i, carry):
        parts[i] = pack(rows[pl.ds(i, 1)], *masks)
        return carry

    lax.fori_loop(0, len(vectors), body, 0)
    for i in range(len(vectors)):
        packed[:, i * width : (i + 1) * width] = parts[i]
    at = len(vectors) * width
    width = inb.shape[1] // count
    packed[:, at : at + width] = pack(inb[...], *spread_masks(count, width))
    at += width
    for i, row in enumerate((stats_a[0:1], stats_a[1:2], stats_b[0:1], stats_b[1:2], stats_b[2:3])):
        packed[:, at + i : at + i + 1] = jnp.broadcast_to(row[:, :1], (count, 1))


def pack_sums(count, attn, out, ffn, inb, stats_a, stats_b):
    width = attn.shape[1]
    scratch = [pltpu.VMEM((8, width), F32), pltpu.VMEM((8, count, width // count), F32)]
    return calls(pack_kernel, [((count, 384), F32)], 4, scratch_shapes=scratch)(
        attn, out, ffn, inb, stats_a, stats_b
    )[0]


def match_grads(rows, label_rows, label_cols):
    is_query, is_pass = label_rows >= 0, label_cols >= 0
    match = jnp.where(is_pass, inner_cols(rows, rows) / SCORE_DIV, MASKED)
    shifted = jnp.exp(match - jnp.max(match, axis=1, keepdims=True))
    probs = shifted / jnp.sum(shifted, axis=1, keepdims=True)
    hot = (label_rows == label_cols).astype(F32)
    grad = jnp.where(is_query & is_pass, (probs - hot) / SCORE_DIV, 0.0).astype(BF)
    return matmul(grad[:POOL], rows) + inner_rows(grad[:, :POOL], rows)


def match_kernel(rows, label_rows, label_cols, out):
    out[...] = match_grads(rows[...], label_rows[...], label_cols[...])


def row_of(z, y, n, s):
    own = (z * s + y) * 3 + n
    spare = y * 3 + (z - 1)
    return jnp.where(z == 0, n * s + y, jnp.where(n < 3, own, spare))


def body(
    passages,
    queries,
    passage_cot,
    query_cot,
    passage_lengths,
    query_lengths,
    labels,
    w_qkv,
    w_out,
    w_in,
    w_back,
    biases,
    norm_gains,
    in_bias,
):
    place = Place()
    s, narrow, devices = place.stride, place.narrow, place.wide * place.narrow
    model_width = passages.shape[2]
    length = passages.shape[1] * narrow
    segs, qsegs = passage_lengths.shape[1] - 1, query_lengths.shape[1] - 1
    on_query = place.z == 0

    piece = model_width // devices
    whole = jnp.concatenate(
        [passage_lengths.reshape(-1), query_lengths.reshape(-1), labels.reshape(-1)]
    )
    whole = jnp.concatenate([whole // 32, whole % 32]).astype(BF)

    w_rows, in_parts = w_out.shape[1], w_in.shape[2] // w_out.shape[2]
    if s == 2:
        towers = pick_towers(place, w_qkv, biases, norm_gains, in_bias, whole)
        got = {k: flip(towers[k], "wide", k * s) for k in (3, 2, 1)}
        levels_qkv = jnp.stack([towers[0], got[1], got[2], got[3]])
        own = [k * s * narrow for k in range(LEVELS)]
        layout = [(0, part, part * w_rows, 0) for part in range(3)] + [(1, 0, 3 * w_rows, 0)]
        shapes = [(3, w_rows, model_width), (1, 8, model_width)]
    else:
        small = jnp.concatenate(
            [biases.reshape(2, -1), norm_gains.reshape(2, -1), in_bias.reshape(2, -1)], axis=1
        )
        small_count = small.shape[1]
        small = jnp.concatenate([small, jnp.broadcast_to(whole, (2, whole.shape[0]))], axis=1)
        to_query = (jnp.arange(devices) < s * narrow)[:, None]
        small = lax.all_to_all(
            jnp.where(to_query, small[1][None], small[0][None]), BOTH, 0, 0, tiled=True
        )
        levels_qkv, own = gather_levels(place, w_qkv), None
        layout = [(0, part, 0, part * model_width) for part in range(3)]
        shapes = [(3, w_rows, model_width)]
    out_in = jnp.concatenate([w_out, w_in], axis=2)
    levels_qkv, out_in, parts = phase(levels_qkv, out_in, (passages, queries))

    pieces_qkv, plan = gather_columns(place, levels_qkv, own)
    levels_out_in = gather_levels(place, out_in)
    swapped = swap_in_directly(place, *parts)
    pieces_qkv, levels_out_in, w_back, swapped = phase(
        pieces_qkv, levels_out_in, w_back, swapped
    )

    cores_qkv, core_plan = gather_cores(pieces_qkv, plan)
    cores_qkv, levels_out_in, swapped = phase(cores_qkv, levels_out_in, swapped)

    pieces_out_in, plan = gather_columns(place, levels_out_in)
    inputs = to_row(place, passages, queries, join_swapped(place, queries, swapped))
    inputs, w_back, cores_qkv = phase(inputs, w_back, cores_qkv)
    levels_back = gather_levels(place, w_back)
    made = assemble(place, cores_qkv, core_plan, layout, shapes)
    w_qkv_all = made[0]

    n_bias, n_gain = biases.shape[1], norm_gains.shape[1]
    ff = in_bias.shape[1] * devices
    if s == 2:
        small = made[1].reshape(devices, 8, -1)
        rows, inb_row = unpack_params(small, model_width, ff)
        ints = small[:, 0, 256 : 256 + whole.shape[0]].astype(F32)
    else:
        params = small[:, :small_count].astype(F32)
        vectors = params[:, : (n_bias + n_gain) * piece].reshape(devices, n_bias + n_gain, piece)
        rows = vectors.transpose(1, 0, 2).reshape(n_bias + n_gain, -1)
        inb_row = params[:, (n_bias + n_gain) * piece :].reshape(1, -1)
        ints = small[:, small_count : small_count + whole.shape[0]].astype(F32)
    half = ints.shape[1] // 2
    ints = (ints[::narrow, :half] * 32 + ints[::narrow, half:]).astype(jnp.int32)
    n_pass = passage_lengths.size
    n_query = query_lengths.size
    pass_lens = ints[:, :n_pass].reshape(-1, segs + 1)
    query_lens = ints[:, n_pass : n_pass + n_query].reshape(-1, qsegs + 1)
    label_all = ints[:, n_pass + n_query :].reshape(-1, qsegs)
    my_row = row_of(place.z, place.y, place.n, s)
    pass_row = pick(pass_lens, jnp.where(on_query, 0, my_row), 0)
    query_row = pick(query_lens, jnp.where(on_query, my_row, 0), 0)
    ends_p = jnp.cumsum(pass_row)[:-1]
    ends_q = jnp.cumsum(query_row)[:-1]
    starts_p, starts_q = ends_p - pass_row[:-1], ends_q - query_row[:-1]
    ends_p = jnp.concatenate([ends_p, jnp.full((qsegs - segs,), length + 1, jnp.int32)])
    ends = jnp.where(on_query, ends_q, ends_p)
    seg_count = jnp.where(on_query, qsegs, segs)
    position = jnp.arange(length, dtype=jnp.int32)
    segment = jnp.sum((position[:, None] >= ends[None, :]).astype(jnp.int32), axis=1)
    valid = (segment < seg_count).astype(F32)[:, None]
    slot = jnp.arange(POOL)
    starts = jnp.where(on_query, jnp.concatenate([starts_q, jnp.full((qsegs,), -1)]), -1)
    for z in range(1, LEVELS):
        here = (place.z == z) & (slot >= qsegs + segs * (z - 1)) & (slot < qsegs + segs * z)
        starts = jnp.where(here, jnp.tile(starts_p, POOL // segs), starts)
    hot = (starts[:, None] == position[None, :]).astype(F32)
    masks = [0]
    if s == 2:
        masks += [dy * narrow + 2 * dx for dx, dy in OTHERS]
        masks += [m ^ 1 for m in masks]
    else:
        for mask in [b * narrow for b in bits_of(s)] + [b for b in reversed(bits_of(narrow))]:
            masks = masks + [m ^ mask for m in masks]
    there = (place.y * narrow + place.n) ^ jnp.array(masks, jnp.int32)
    their_y, their_n = there // narrow, there % narrow
    label_rows = label_all[row_of(jnp.int32(0), their_y, their_n, s)]
    label_rows = jnp.pad(label_rows, ((0, 0), (0, POOL - qsegs)), constant_values=-1)
    levels = jnp.arange(1, LEVELS)
    pass_rows = row_of(levels[None, :], their_y[:, None], their_n[:, None], s)
    pass_ids = (pass_rows[:, :, None] * segs + jnp.arange(segs)).reshape(len(masks), -1)
    spare = POOL - qsegs - pass_ids.shape[1]
    label_cols = jnp.pad(pass_ids, ((0, 0), (qsegs, spare)), constant_values=-1)
    label_rows, label_cols = label_rows.reshape(-1, 1), label_cols.reshape(1, -1)

    qkv, context, log_sum = attend(inputs, w_qkv_all, rows, segment)
    context, pieces_out_in, levels_back, cots = phase(
        context, pieces_out_in, levels_back, (passage_cot, query_cot)
    )

    cores_out_in, core_plan = gather_cores(pieces_out_in, plan)
    cores_out_in, levels_back, cots = phase(cores_out_in, levels_back, cots)

    pieces_back, plan = gather_columns(place, levels_back)
    swapped = swap_in(place, *cots)
    w_out_all, w_in_all = assemble(
        place,
        cores_out_in,
        core_plan,
        [(0, 0, 0, 0)] + [(1, part, 0, (part + 1) * model_width) for part in range(in_parts)],
        [(1, w_rows, model_width), (in_parts, w_rows, model_width)],
    )
    normed, normed_low, unit_one, scale_one, stats_one = branch_layer(
        context, w_out_all, inputs, rows, valid
    )
    active, slope = hidden_layer(normed_low, w_in_all, inb_row)
    active, pieces_back, swapped = phase(active, pieces_back, swapped)

    cores_back, core_plan = gather_cores(pieces_back, plan)
    cot = to_row(place, passage_cot, query_cot, swapped)
    if s != 2:
        back_shape = [(1, w_back.shape[1], model_width)]
        cores_back = assemble(place, cores_back, core_plan, [(0, 0, 0, 0)], back_shape)
        cores_back, core_plan = [cores_back[0][0]], None
    output_low, unit_two, scale_two, pooled, stats_two, w_back_all = output_layer(
        place, active, cores_back, core_plan, normed, rows, valid, hot
    )
    pooled, cot = phase(pooled, cot)

    column = sum([flip(pooled, "wide", k * s).astype(F32) for k in (3, 2, 1)], pooled.astype(F32))
    seen = column.astype(BF)[None]
    if s == 2:
        seen = jnp.concatenate([seen] + [flip_both(seen, dy, 2 * dx) for dx, dy in OTHERS])
        seen = jnp.concatenate([seen, flip(seen, "narrow", 1)])
    else:
        for axis, step in [("wide", b) for b in bits_of(s)] + [
            ("narrow", b) for b in reversed(bits_of(narrow))
        ]:
            seen = jnp.concatenate([seen, flip(seen, axis, step)])
    seen = seen.reshape(-1, model_width)
    if s == 2:
        (grad_pool,) = calls(match_kernel, [((POOL, model_width), F32)], 3)(
            seen, label_rows, label_cols
        )
    else:
        grad_pool = match_grads(seen, label_rows, label_cols)

    grad_pool, output_low = phase(grad_pool, output_low)
    if s == 2:
        out_four = row_pieces(place, output_low)
    grad_resid_two, grad_ffn, sums_two = output_back(
        cot, valid, hot, grad_pool, unit_two, scale_two, rows
    )
    if s == 2:
        send_c, keep_c = products_back(place, active, grad_ffn)
        send_c, out_four = phase(send_c, out_four)
        got_c = flip(send_c, "narrow", 1)
        shares_c = column_shares(place, keep_c, got_c)
        shares_c, grad_ffn = phase(shares_c, grad_ffn)

        columns_c = send_columns(shares_c)
        swapped = swap_out(place, out_four)
    grad_hidden, inb_sums, grad_branch, blocks_b, sums_one = hidden_back(
        grad_ffn, w_back_all, slope, w_in_all, grad_resid_two, unit_one, scale_one, rows, narrow
    )
    if s == 2:
        send_b, keep_b = products_out_in(place, context, blocks_b, normed_low, grad_hidden)
        send_b, columns_c, swapped = phase(send_b, columns_c, swapped)
        passage_out, query_out = from_row(place, out_four, swapped)

        got_b = flip(send_b, "narrow", 1)
        level_c = level_sums(columns_c)
        shares_b = column_shares(place, keep_b, got_b)
        shares_b, level_c, grad_branch = phase(shares_b, level_c, grad_branch)

        columns_b = send_columns(shares_b)
        levels_c = across_levels(level_c, s)
    grad_qkv, blocks_a, sums_qkv = attend_back(
        grad_branch, w_out_all[0], qkv, log_sum, segment, narrow
    )
    if s == 2:
        send_a, keep_a = products_qkv(place, inputs, blocks_a)
        send_a, grad_qkv, columns_b, levels_c = phase(send_a, grad_qkv, columns_b, levels_c)

        got_a = flip(send_a, "narrow", 1)
    input_grad = input_back(grad_qkv, w_qkv_all, grad_branch)
    if s == 2:
        got_a, input_grad, columns_b = phase(got_a, input_grad, columns_b)

        in_four = row_pieces(place, input_grad)
        levels_b = swap_shares(place, level_shares(place, columns_b))
        shares_a = column_shares(place, keep_a, got_a)
        late = levels_b.pop(3)
        shares_a, levels_b, in_four, sums_qkv, levels_c = phase(
            shares_a, levels_b, in_four, sums_qkv, levels_c
        )
        levels_b.insert(3, late)

        columns_a = send_columns(shares_a)
        swapped = swap_out(place, in_four)
        packed = pack_sums(devices, sums_qkv, sums_one, sums_two, inb_sums, stats_one, stats_two)
        grad_w_back = finish_back(levels_c)
        columns_a, swapped, packed, levels_b = phase(columns_a, swapped, packed, levels_b)

        packed = lax.all_to_all(packed, BOTH, 0, 0, tiled=True)
        levels_a = swap_shares(place, level_shares(place, columns_a))
        grad_w_out, grad_w_in = finish_out_in(place, levels_b, model_width // place.wide)
        passage_grad, query_grad = from_row(place, in_four, swapped)
        grad_w_qkv = finish_qkv(place, levels_a)
    else:
        packed = pack_sums(devices, sums_qkv, sums_one, sums_two, inb_sums, stats_one, stats_two)
        packed = lax.all_to_all(packed, BOTH, 0, 0, tiled=True)
        grad_w_back = scatter_tower(place, grad_blocks(active, grad_ffn, narrow))
        grad_w_out = scatter_tower(place, grad_blocks(context, grad_branch, narrow))
        grad_w_in = scatter_tower(place, grad_blocks(normed_low, grad_hidden, narrow))
        flat = jnp.moveaxis(grad_qkv, 0, 1).reshape(length, -1)
        grad_w_qkv = scatter_tower(place, grad_blocks(inputs, flat, narrow))
        out_four, in_four = row_pieces(place, output_low), row_pieces(place, input_grad)
        passage_out, query_out = from_row(place, out_four, swap_out(place, out_four))
        passage_grad, query_grad = from_row(place, in_four, swap_out(place, in_four))

    packed = packed.reshape(LEVELS, -1, packed.shape[1]).sum(axis=1)
    packed = jnp.stack([packed[1] + packed[2] + packed[3], packed[0]])
    edges = [n_bias * piece, (n_bias + n_gain) * piece]
    edges.append(edges[1] + in_bias.shape[1])
    grad_biases = packed[:, : edges[0]].reshape(2, n_bias, piece)
    grad_gains = packed[:, edges[0] : edges[1]].reshape(2, n_gain, piece)
    grad_inb = packed[:, edges[1] : edges[2]]
    totals = packed[:, edges[2] : edges[2] + 5]
    rms_stats = jnp.sqrt(totals[:, :4] / (totals[:, 4:] * model_width))
    return (
        passage_out,
        query_out,
        passage_grad,
        query_grad,
        grad_w_qkv,
        grad_w_out,
        grad_w_in,
        grad_w_back,
        grad_biases,
        grad_gains,
        grad_inb,
        rms_stats,
    )


def solution(mesh):
    return jax.shard_map(
        body,
        mesh=mesh,
        in_specs=(
            P("wide", "narrow", None),
            P("wide", "narrow", None),
            P("wide", "narrow", None),
            P("wide", "narrow", None),
            P("wide", None),
            P("wide", None),
            P("wide"),
            P(None, ("wide", "narrow"), None),
            P(None, ("wide", "narrow"), None),
            P(None, ("wide", "narrow"), None),
            P(None, ("wide", "narrow"), None),
            P(None, None, ("wide", "narrow")),
            P(None, None, ("wide", "narrow")),
            P(None, ("wide", "narrow")),
        ),
        out_specs=(
            P("wide", "narrow", None),
            P("wide", "narrow", None),
            P("wide", "narrow", None),
            P("wide", "narrow", None),
            P(None, "wide", "narrow"),
            P(None, "wide", "narrow"),
            P(None, "wide", "narrow"),
            P(None, "wide", "narrow"),
            P(None, None, ("wide", "narrow")),
            P(None, None, ("wide", "narrow")),
            P(None, ("wide", "narrow")),
            P(),
        ),
        check_vma=False,
    )
```

```python
import functools
import math

import jax
import jax.numpy as jnp
from jax import lax
from jax.experimental import pallas as pl
from jax.experimental.pallas import tpu as pltpu
from jax.sharding import PartitionSpec as P

HEAD_DIM = 64
LEVELS = 4
GROUP = 4
POOL = 32
STEP = 128
VMEM = 58 << 20
OTHERS = ((1, 1), (1, 0), (0, 1))


def cost(us):
    return pl.CostEstimate(flops=int(us * 1.15e9), bytes_accessed=1024, transcendentals=0)


EPSILON = 1e-05
SCORE_DIV = 12.0
MASKED = -1e30
BF = jnp.bfloat16
F32 = jnp.float32
BOTH = ("wide", "narrow")


def matmul(left, right):
    return jnp.dot(left, right, preferred_element_type=F32)


def inner_rows(left, right):
    return lax.dot_general(left, right, (((0,), (0,)), ((), ())), preferred_element_type=F32)


def inner_cols(left, right):
    return lax.dot_general(left, right, (((1,), (1,)), ((), ())), preferred_element_type=F32)


def flip(x, axis, mask):
    size = lax.axis_size(axis)
    return lax.ppermute(x, axis, [(i, i ^ mask) for i in range(size)])


def flip_both(x, wide_mask, narrow_mask):
    wide, narrow = lax.axis_size("wide"), lax.axis_size("narrow")
    mask = wide_mask * narrow + narrow_mask
    return lax.ppermute(x, BOTH, [(i, i ^ mask) for i in range(wide * narrow)])


def phase(*values):
    return lax.optimization_barrier(values)


def across_levels(x, stride):
    groups = [[k * stride + i for k in range(LEVELS)] for i in range(stride)]
    return lax.all_to_all(x, "wide", 0, 0, axis_index_groups=groups, tiled=True)


def swap_levels(x, k, stride):
    pairs = []
    for i in range(stride):
        pairs += [(i, k * stride + i), (k * stride + i, i)]
    return lax.ppermute(x, "wide", pairs)


def bits_of(size):
    return [1 << b for b in range(size.bit_length() - 1)]


class Place:
    def __init__(self):
        self.wide = lax.axis_size("wide")
        self.narrow = lax.axis_size("narrow")
        self.stride = self.wide // LEVELS
        self.w = lax.axis_index("wide")
        self.n = lax.axis_index("narrow")
        self.z = self.w // self.stride
        self.y = self.w % self.stride
        self.me = self.w * self.narrow + self.n


def swap_in(place, pass_part, query_part):
    query = jnp.broadcast_to(query_part, (LEVELS, *query_part.shape[1:]))
    first = jnp.concatenate([query_part, pass_part])
    return across_levels(jnp.where(place.z == 0, first, query), place.stride)


def swap_in_directly(place, pass_part, query_part):
    return [
        swap_levels(jnp.where(place.z == 0, pass_part[k - 1], query_part[0]), k, place.stride)
        for k in range(1, LEVELS)
    ]


def join_swapped(place, query_part, got):
    first = jnp.where(place.z == 0, query_part[0], got[0] + got[1] + got[2])
    return jnp.stack([first] + got)


def to_row(place, pass_part, query_part, got):
    four = jnp.where(place.z == 0, got, jnp.concatenate([pass_part, got[:1]]))
    mine = lax.all_to_all(four, "narrow", 0, 0, tiled=True)
    return mine.reshape(-1, mine.shape[-1])


def row_pieces(place, row):
    return lax.all_to_all(
        row.reshape(place.narrow, -1, row.shape[-1]), "narrow", 0, 0, tiled=True
    )


def swap_out(place, four):
    last = jnp.broadcast_to(four[3:], four.shape)
    return across_levels(jnp.where(place.z == 0, four, last), place.stride)


def from_row(place, four, got):
    pass_part = jnp.where(place.z == 0, got[1:], four[:3])
    query_part = jnp.where(place.z == 0, four[:1], got[:1])
    return pass_part, query_part


def toggle(places, mask):
    return [(p[0], p[1] ^ mask) if isinstance(p, tuple) else p ^ mask for p in places]


def block_of(me, place, level):
    if isinstance(place, tuple):
        return ((me & (level - 1)) ^ place[1]) + place[0] * level
    return me ^ place


def assemble_kernel(plan, layout, level, me_ref, *refs):
    pieces, outs, sems = refs[: len(plan)], refs[len(plan) : -1], refs[-1]
    me = me_ref[0]
    copies = []
    for piece, masks in zip(pieces, plan):
        for slot, mask in enumerate(masks):
            for out, part, row, column in layout:
                target = outs[out].at[part, block_of(me, mask, level)]
                rows, columns = outs[out].shape[2:]
                source = piece.at[slot, pl.ds(row, rows), pl.ds(column, columns)]
                copies.append(pltpu.make_async_copy(source, target, sems.at[len(copies)]))
    for copy in copies:
        copy.start()
    for copy in copies:
        copy.wait()


def assemble(place, pieces, plan, layout, outs):
    total = place.wide * place.narrow
    made = pl.pallas_call(
        functools.partial(assemble_kernel, plan, layout, total // LEVELS),
        out_shape=[jax.ShapeDtypeStruct((out[0], total, *out[1:]), BF) for out in outs],
        in_specs=[pl.BlockSpec(memory_space=pltpu.SMEM)]
        + [pl.BlockSpec(memory_space=pl.ANY)] * len(pieces),
        out_specs=[pl.BlockSpec(memory_space=pltpu.VMEM)] * len(outs),
        scratch_shapes=[pltpu.SemaphoreType.DMA((total * len(layout),))],
        cost_estimate=cost(0.1),
        compiler_params=pltpu.CompilerParams(vmem_limit_bytes=VMEM),
    )(place.me.reshape(1), *pieces)
    return [out.reshape(out.shape[0], -1, out.shape[3]) for out in made]


def pick_kernel(z_ref, w_ref, bias_ref, gain_ref, inb_ref, ints_ref, *refs):
    outs, small = refs[:-1], refs[-1]
    rows, width = w_ref.shape[1], small.shape[1]
    n_bias, n_gain = bias_ref.shape[1], gain_ref.shape[1]
    for k, out in enumerate(outs):
        tower = jnp.where(z_ref[0] == k, 1, 0)
        for part in range(3):
            out[part * rows : (part + 1) * rows] = w_ref[tower, :, part * width : (part + 1) * width]
        small[...] = jnp.zeros(small.shape, F32)
        small[:n_bias, : bias_ref.shape[2]] = bias_ref[tower].astype(F32)
        small[n_bias : n_bias + n_gain, : gain_ref.shape[2]] = gain_ref[tower].astype(F32)
        small[:1, 128 : 128 + inb_ref.shape[2]] = inb_ref[tower].astype(F32)
        small[:1, 256 : 256 + ints_ref.shape[1]] = ints_ref[...].astype(F32)
        out[3 * rows :] = small[...].astype(BF)


def pick_towers(place, w_qkv, biases, norm_gains, in_bias, ints):
    width = w_qkv.shape[2] // 3
    vmem = pl.BlockSpec(memory_space=pltpu.VMEM)
    return calls(
        pick_kernel,
        [((3 * w_qkv.shape[1] + 8, width), BF)] * LEVELS,
        2,
        in_specs=[pl.BlockSpec(memory_space=pltpu.SMEM)] + [vmem] * 5,
        scratch_shapes=[pltpu.VMEM((8, width), F32)],
    )(place.z.reshape(1), w_qkv, biases, norm_gains, in_bias[:, None], ints[None])


def gather_levels(place, pair):
    first = lax.broadcasted_iota(jnp.int32, (LEVELS, 1, 1), 0) == 0
    return across_levels(jnp.where(first, pair[1:], pair[:1]), place.stride)


def gather_columns(place, levels, own=None):
    s, narrow = place.stride, place.narrow
    if own is None:
        own = [(level, 0) for level in range(LEVELS)]
    pieces, plan = [levels], [own]
    if s == 2:
        for dx, dy in OTHERS:
            pieces.append(flip_both(levels, dy, 2 * dx))
            plan.append(toggle(own, dy * narrow + 2 * dx))
    else:
        for b in bits_of(s):
            for i in range(len(pieces)):
                pieces.append(flip(pieces[i], "wide", b))
                plan.append(toggle(plan[i], b * narrow))
        for i in range(len(pieces)):
            pieces.append(flip(pieces[i], "narrow", 2))
            plan.append(toggle(plan[i], 2))
    return pieces, plan


def gather_cores(pieces, plan):
    others = [flip(piece, "narrow", 1) for piece in pieces]
    return list(pieces) + others, plan + [toggle(places, 1) for places in plan]


def pick(x, index, dim):
    return lax.dynamic_index_in_dim(x, index, dim, keepdims=False)


def halve(x, place, axis, mask, dim):
    index = place.n if axis == "narrow" else place.w
    bit = jnp.where((index & mask) != 0, 1, 0)
    got = flip(pick(x, 1 - bit, dim).astype(BF), axis, mask)
    return pick(x, bit, dim) + got.astype(F32)


def scatter_tower(place, partial):
    s = place.stride
    rows, narrow, cols = partial.shape
    per = rows // place.wide
    x = partial.reshape(rows, 2, 2, cols)
    x = halve(x, place, "narrow", 1, 2)
    x = x.reshape(LEVELS, s, per, 2, cols)
    first, second = x[:2], x[2:]

    def over_columns(part):
        for b in reversed(bits_of(s)):
            shape = part.shape
            part = part.reshape(shape[0], 2, shape[1] // 2, *shape[2:])
            part = halve(part, place, "wide", b, 1)
        return part[:, 0]

    first = over_columns(halve(first, place, "narrow", 2, 3))
    second = halve(over_columns(second), place, "narrow", 2, 2)
    return jnp.stack(sum_levels(place, send_levels(place, jnp.concatenate([first, second]))))


def send_levels(place, levels):
    slots = [None] * LEVELS
    slots[0] = pick(levels, place.z, 0)
    for k in (3, 2, 1):
        slots[k] = flip(pick(levels, place.z ^ k, 0).astype(BF), "wide", k * place.stride)
    return slots


def sum_levels(place, slots):
    tower0 = sum(jnp.where(place.z == k, 0.0, slots[k].astype(F32)) for k in range(LEVELS))
    tower1 = sum(jnp.where(place.z == k, slots[k].astype(F32), 0.0) for k in range(LEVELS))
    return tower0, tower1


def share_kernel(at_ref, keep_ref, got_ref, *out_refs):
    x, y = at_ref[0], at_ref[1]

    def body(level, carry):
        for ref, (dx, dy) in zip(out_refs, ((0, 0), *OTHERS)):
            at = (x ^ dx, level, y ^ dy)
            ref[level] = (keep_ref[at].astype(F32) + got_ref[at].astype(F32)).astype(BF)
        return carry

    lax.fori_loop(0, keep_ref.shape[1], body, 0)


def column_shares(place, keep, got):
    r, c = got.shape[2:]
    half = LEVELS // 2
    block = pl.BlockSpec((2, half, place.stride, r, c), lambda i, at: (0, i, 0, 0, 0))
    out = pl.BlockSpec((half, r, c), lambda i, at: (i, 0, 0))
    shape = (2, LEVELS, place.stride, r, c)
    return pl.pallas_call(
        share_kernel,
        grid_spec=pltpu.PrefetchScalarGridSpec(
            num_scalar_prefetch=1, grid=(2,), in_specs=[block] * 2, out_specs=[out] * 4
        ),
        out_shape=[jax.ShapeDtypeStruct((LEVELS, r, c), BF)] * 4,
        compiler_params=pltpu.CompilerParams(vmem_limit_bytes=VMEM),
        cost_estimate=cost(1),
    )(jnp.stack([place.n // 2, place.y]), keep.reshape(shape), got.reshape(shape))


def send_columns(shares):
    return [shares[0]] + [
        flip_both(sent, dy, 2 * dx) for sent, (dx, dy) in zip(shares[1:], OTHERS)
    ]


def level_kernel(z_ref, own_ref, *refs):
    got_refs, out_refs = refs[:3], refs[3:]
    step = 24

    def body(i, carry):
        rows = pl.ds(pl.multiple_of(i * step, step), step)
        for k, out_ref in enumerate(out_refs):
            at = (z_ref[0] ^ k, rows)
            total = own_ref[at].astype(F32)
            for ref in got_refs:
                total = total + ref[at].astype(F32)
            out_ref[rows] = total.astype(out_ref.dtype)
        return carry

    lax.fori_loop(0, own_ref.shape[1] // step, body, 0)


def level_shares(place, columns):
    r, c = columns[0].shape[1:]
    vmem = pl.BlockSpec(memory_space=pltpu.VMEM)
    return pl.pallas_call(
        level_kernel,
        in_specs=[pl.BlockSpec(memory_space=pltpu.SMEM)] + [vmem] * 4,
        out_specs=[vmem] * 4,
        out_shape=[jax.ShapeDtypeStruct((r, c), F32)] + [jax.ShapeDtypeStruct((r, c), BF)] * 3,
        compiler_params=pltpu.CompilerParams(vmem_limit_bytes=VMEM),
        cost_estimate=cost(1),
    )(place.z.reshape(1), *columns)


def level_sums_kernel(*refs):
    def body(at, carry):
        refs[-1][at] = sum(ref[at].astype(F32) for ref in refs[:-1]).astype(BF)
        return carry

    lax.fori_loop(0, LEVELS, body, 0)


def level_sums(columns):
    shape = columns[0].shape
    return calls(level_sums_kernel, [(shape, BF)], 3)(*columns)[0]


def swap_shares(place, shares):
    slots = [shares[0], None, None, None]
    for k in (3, 2, 1):
        slots[k] = flip(shares[k], "wide", k * place.stride)
    return slots


def product_kernel(step, me_ref, *refs):
    send_ref, keep_ref = refs[-2:]
    left_refs = refs[:-2]
    to_send = pl.program_id(0) < 2

    @pl.when(to_send)
    def _():
        step(left_refs, lambda at, v: send_ref.__setitem__((0, *at), v.astype(BF)))

    @pl.when(jnp.logical_not(to_send))
    def _():
        step(left_refs, lambda at, v: keep_ref.__setitem__((0, *at), v.astype(BF)))


def products(place, step, operands, specs, block):
    def target(j, me):
        return (j % 2) * 2 + jnp.where(j < 2, 1 - me[0] % 2, me[0] % 2)

    wide = place.wide
    grid_spec = pltpu.PrefetchScalarGridSpec(
        num_scalar_prefetch=1,
        grid=(4,),
        in_specs=specs(target),
        out_specs=[
            pl.BlockSpec((1, wide, *block), lambda j, me: (jnp.minimum(j, 1), 0, 0, 0)),
            pl.BlockSpec((1, wide, *block), lambda j, me: (jnp.maximum(j - 2, 0), 0, 0, 0)),
        ],
    )
    return pl.pallas_call(
        functools.partial(product_kernel, step),
        grid_spec=grid_spec,
        out_shape=[
            jax.ShapeDtypeStruct((2, wide, *block), BF),
            jax.ShapeDtypeStruct((2, wide, *block), BF),
        ],
        compiler_params=pltpu.CompilerParams(vmem_limit_bytes=VMEM),
        cost_estimate=cost(8),
    )(place.n.reshape(1), *operands)


def whole(shape):
    return pl.BlockSpec(shape, lambda j, me: (0,) * len(shape))


def grad_blocks(left, right, narrow):
    out = inner_rows(left, right)
    return out.reshape(out.shape[0], narrow, -1)


def products_back_kernel(core_ref, left_ref, right_ref, send_ref, keep_ref, turned_ref):
    @pl.when(pl.program_id(0) == 0)
    def _():
        turned_ref[...] = right_ref[...].T

    cols, rows = send_ref.shape[2:]
    first = core_ref[0] == 0

    def body(x, carry):
        at = pl.ds(pl.multiple_of(x * 2 * cols, 2 * cols), 2 * cols)
        value = matmul(turned_ref[at], left_ref[...]).astype(BF)
        for w in range(2):
            columns = slice(w * rows, (w + 1) * rows)
            even, odd = value[:cols, columns], value[cols:, columns]
            keep_ref[x, w] = jnp.where(first, even, odd)
            send_ref[x, w] = jnp.where(first, odd, even)
        return carry

    lax.fori_loop(0, 2, body, 0)


def products_back(place, active, grad_ffn):
    t, ff = active.shape
    d = grad_ffn.shape[1]
    cols, rows = d // place.narrow, ff // place.wide
    out = pl.BlockSpec((2, 2, cols, rows), lambda j, core: (0, j, 0, 0))
    return pl.pallas_call(
        products_back_kernel,
        grid_spec=pltpu.PrefetchScalarGridSpec(
            num_scalar_prefetch=1,
            grid=(place.wide // 2,),
            in_specs=[pl.BlockSpec((t, 2 * rows), lambda j, core: (0, j)), whole((t, d))],
            out_specs=[out, out],
            scratch_shapes=[pltpu.VMEM((d, t), BF)],
        ),
        out_shape=[jax.ShapeDtypeStruct((2, place.wide, cols, rows), BF)] * 2,
        compiler_params=pltpu.CompilerParams(vmem_limit_bytes=VMEM),
        cost_estimate=cost(7),
    )((place.n % 2).reshape(1), active, grad_ffn)


def finish_back(levels):
    levels = levels.astype(F32)
    return jnp.stack([(levels[1] + levels[2] + levels[3]).T, levels[0].T])


def products_out_in(place, context, blocks, normed, grad_hidden):
    narrow = place.narrow
    t, d = context.shape
    rows = d // place.wide
    cols_out, cols_in = blocks.shape[2], grad_hidden.shape[1] // narrow
    fold = cols_in // cols_out
    low = rows // fold

    def step(refs, store):
        context_ref, branch_ref, normed_ref, hidden_ref = refs

        def body(i, carry):
            at = pl.ds(pl.multiple_of(i * 4 * rows, 4 * rows), 4 * rows)
            value = inner_rows(normed_ref[:, at], hidden_ref[...])
            for w in range(4):
                store((4 * i + w, slice(0, rows)), value[w * rows : (w + 1) * rows])
            value = inner_rows(context_ref[:, at], branch_ref[0])
            for w in range(4):
                for g in range(fold):
                    store(
                        (4 * i + w, slice(rows, rows + low), slice(g * cols_out, (g + 1) * cols_out)),
                        value[w * rows + g * low : w * rows + (g + 1) * low],
                    )
            return carry

        lax.fori_loop(0, place.wide // 4, body, 0)

    return products(
        place,
        step,
        (context, blocks, normed, grad_hidden),
        lambda target: [
            whole((t, d)),
            pl.BlockSpec((1, t, cols_out), lambda j, me: (target(j, me), 0, 0)),
            whole((t, d)),
            pl.BlockSpec((t, cols_in), lambda j, me: (0, target(j, me))),
        ],
        (rows + low, cols_in),
    )


def finish_out_in(place, slots, rows):
    parts = sum_levels(place, slots)
    low, cols = parts[0].shape[0] - rows, parts[0].shape[1]
    fold = rows // low
    grad_in = jnp.stack([part[:rows] for part in parts])
    grad_out = [
        jnp.moveaxis(part[rows:].reshape(low, fold, -1), 1, 0).reshape(rows, -1) for part in parts
    ]
    return jnp.stack(grad_out), grad_in


def products_qkv(place, inputs, blocks):
    t, d = inputs.shape
    rows, cols = d // place.wide, blocks.shape[2]
    half = rows // 2

    def step(refs, store):
        left, right = refs
        value = inner_rows(left[...], right[0])
        for w in range(place.wide):
            for g in range(2):
                store(
                    (w, slice(None), slice(g * cols, (g + 1) * cols)),
                    value[w * rows + g * half : w * rows + (g + 1) * half],
                )

    return products(
        place,
        step,
        (inputs, blocks),
        lambda target: [
            whole((t, d)),
            pl.BlockSpec((1, t, cols), lambda j, me: (target(j, me), 0, 0)),
        ],
        (half, 2 * cols),
    )


def finish_qkv(place, slots):
    parts = sum_levels(place, slots)
    cols = parts[0].shape[1] // 2
    return jnp.stack([jnp.concatenate([p[:, :cols], p[:, cols:]]) for p in parts])


def attend_kernel(x_ref, w_ref, rows_ref, seg_row_ref, seg_col_ref, qkv_ref, ctx_ref, lse_ref):
    x = x_ref[...]
    same = seg_col_ref[...] == seg_row_ref[...]

    def project(part, carry):
        bias = jnp.where(part == 0, rows_ref[0:1], jnp.where(part == 2, rows_ref[1:2], 0.0))
        qkv_ref[part] = (matmul(x, w_ref[part]) + bias).astype(BF)
        return carry

    lax.fori_loop(0, 3, project, 0)
    for h in range(GROUP):
        lanes = slice(h * HEAD_DIM, (h + 1) * HEAD_DIM)
        q, k, v = qkv_ref[0, :, lanes], qkv_ref[1, :, lanes], qkv_ref[2, :, lanes]
        scores = jnp.where(same, inner_cols(k, q) * HEAD_DIM ** (-0.5), MASKED)
        top = jnp.max(scores, axis=0, keepdims=True)
        shifted = jnp.exp(scores - top)
        total = jnp.sum(shifted, axis=0, keepdims=True)
        probs = (shifted * (1.0 / total)).astype(BF)
        ctx_ref[:, lanes] = inner_rows(probs, v).astype(BF)
        lse_ref[0, h : h + 1, :] = top + jnp.log(total)


def attend(x, w_qkv, rows, segment):
    t, d = x.shape
    width = GROUP * HEAD_DIM
    steps = d // width
    return pl.pallas_call(
        attend_kernel,
        grid=(steps,),
        in_specs=[
            pl.BlockSpec((t, d), lambda j: (0, 0)),
            pl.BlockSpec((3, d, width), lambda j: (0, 0, j)),
            pl.BlockSpec((8, width), lambda j: (0, j)),
            pl.BlockSpec((1, t), lambda j: (0, 0)),
            pl.BlockSpec((t, 1), lambda j: (0, 0)),
        ],
        out_specs=[
            pl.BlockSpec((3, t, width), lambda j: (0, 0, j)),
            pl.BlockSpec((t, width), lambda j: (0, j)),
            pl.BlockSpec((1, GROUP, t), lambda j: (j, 0, 0)),
        ],
        out_shape=[
            jax.ShapeDtypeStruct((3, t, d), BF),
            jax.ShapeDtypeStruct((t, d), BF),
            jax.ShapeDtypeStruct((steps, GROUP, t), F32),
        ],
        compiler_params=pltpu.CompilerParams(vmem_limit_bytes=VMEM),
        cost_estimate=cost(0.1),
    )(x, w_qkv, rows, segment.reshape(1, t), segment.reshape(t, 1))


def attend_back_kernel(
    gb_ref, w_ref, qkv_ref, lse_ref, seg_row_ref, seg_col_ref, out_ref, blocks_ref, sums_ref, grad_ref
):
    scale = HEAD_DIM ** (-0.5)
    same = seg_col_ref[...] == seg_row_ref[...]
    grad_ref[...] = inner_cols(gb_ref[...], w_ref[...]).astype(BF)

    def pair(p, carry):
        at = pl.ds(pl.multiple_of(p * 2 * HEAD_DIM, 2 * HEAD_DIM), 2 * HEAD_DIM)
        queries, keys, values = qkv_ref[0, :, at], qkv_ref[1, :, at], qkv_ref[2, :, at]
        grads, outs = grad_ref[:, at], []
        for h in range(2):
            lanes = slice(h * HEAD_DIM, (h + 1) * HEAD_DIM)
            q, k, v, g = queries[:, lanes], keys[:, lanes], values[:, lanes], grads[:, lanes]
            scores = jnp.where(same, inner_cols(k, q) * scale, MASKED)
            probs = jnp.exp(scores - lse_ref[0, pl.ds(2 * p + h, 1), :])
            grad_probs = inner_cols(v, g)
            delta = jnp.sum(probs * grad_probs, axis=0, keepdims=True)
            grad_scores = (probs * (grad_probs - delta)).astype(BF)
            outs.append(
                (
                    (inner_rows(grad_scores, k) * scale).astype(BF),
                    (matmul(grad_scores, q) * scale).astype(BF),
                    matmul(probs.astype(BF), g).astype(BF),
                )
            )
        for part in range(3):
            out_ref[part, :, at] = jnp.concatenate([outs[0][part], outs[1][part]], axis=1)
        return carry

    lax.fori_loop(0, GROUP // 2, pair, 0)
    sums_ref[0:1] = jnp.sum(out_ref[0].astype(F32), axis=0, keepdims=True)
    sums_ref[1:2] = jnp.sum(out_ref[2].astype(F32), axis=0, keepdims=True)
    per_block = blocks_ref.shape[2] // HEAD_DIM
    heads = blocks_ref.shape[0] * per_block // 3
    for step in range(heads // GROUP):

        @pl.when(pl.program_id(0) == step)
        def _(step=step):
            for part in range(3):
                for h in range(GROUP):
                    block, at = divmod(part * heads + step * GROUP + h, per_block)
                    blocks_ref[block, :, at * HEAD_DIM : (at + 1) * HEAD_DIM] = out_ref[
                        part, :, h * HEAD_DIM : (h + 1) * HEAD_DIM
                    ]


def attend_back(grad_branch, w_out, qkv, lse, segment, narrow):
    t, d = grad_branch.shape
    width = GROUP * HEAD_DIM
    return pl.pallas_call(
        attend_back_kernel,
        grid=(d // width,),
        in_specs=[
            pl.BlockSpec((t, d), lambda j: (0, 0)),
            pl.BlockSpec((width, d), lambda j: (j, 0)),
            pl.BlockSpec((3, t, width), lambda j: (0, 0, j)),
            pl.BlockSpec((1, GROUP, t), lambda j: (j, 0, 0)),
            pl.BlockSpec((1, t), lambda j: (0, 0)),
            pl.BlockSpec((t, 1), lambda j: (0, 0)),
        ],
        out_specs=[
            pl.BlockSpec((3, t, width), lambda j: (0, 0, j)),
            pl.BlockSpec((narrow, t, 3 * d // narrow), lambda j: (0, 0, 0)),
            pl.BlockSpec((2, width), lambda j: (0, j)),
        ],
        out_shape=[
            jax.ShapeDtypeStruct((3, t, d), BF),
            jax.ShapeDtypeStruct((narrow, t, 3 * d // narrow), BF),
            jax.ShapeDtypeStruct((2, d), F32),
        ],
        scratch_shapes=[pltpu.VMEM((t, width), BF)],
        compiler_params=pltpu.CompilerParams(vmem_limit_bytes=VMEM),
        cost_estimate=cost(20),
    )(grad_branch, w_out, qkv, lse, segment.reshape(1, t), segment.reshape(t, 1))


def hidden_kernel(x_ref, w_ref, bias_ref, active_ref, slope_ref, pre_ref):
    pre_ref[...] = matmul(x_ref[...], w_ref[0]) + bias_ref[...]

    def body(at, carry):
        pre = pre_ref[at]
        below = 0.5 + 0.5 * lax.erf(pre * 0.5**0.5)
        active_ref[at] = (pre * below).astype(BF)
        density = jnp.exp(-0.5 * pre * pre) * (2.0 * math.pi) ** (-0.5)
        slope_ref[at] = (below + pre * density).astype(BF)
        return carry

    by_rows(pre_ref.shape[0], body)


def hidden_layer(x, w_in, in_bias):
    t, d = x.shape
    parts, _, width = w_in.shape
    block = pl.BlockSpec((t, width), lambda j: (0, j))
    shape = jax.ShapeDtypeStruct((t, parts * width), BF)
    return pl.pallas_call(
        hidden_kernel,
        grid=(parts,),
        in_specs=[
            pl.BlockSpec((t, d), lambda j: (0, 0)),
            pl.BlockSpec((1, d, width), lambda j: (j, 0, 0)),
            pl.BlockSpec((1, width), lambda j: (0, j)),
        ],
        out_specs=[block, block],
        out_shape=[shape, shape],
        scratch_shapes=[pltpu.VMEM((t, width), F32)],
        compiler_params=pltpu.CompilerParams(vmem_limit_bytes=VMEM),
        cost_estimate=cost(8),
    )(x, w_in, in_bias)


def norm_parts(value):
    mean = jnp.mean(value, axis=-1, keepdims=True)
    centered = value - mean
    scale = lax.rsqrt(jnp.mean(centered * centered, axis=-1, keepdims=True) + EPSILON)
    return centered * scale, scale


def norm_back(grad, unit, scale, gain):
    unit = unit.astype(F32)
    e = grad * gain
    part = jnp.mean(e * unit, axis=-1, keepdims=True)
    return (e - jnp.mean(e, axis=-1, keepdims=True) - unit * part) * scale


def total(value):
    return jnp.sum(jnp.sum(value, axis=0, keepdims=True), axis=1, keepdims=True)


def column_sum(value):
    return jnp.sum(value, axis=0, keepdims=True)


def by_rows(count, body, carry=None):
    if carry is None:
        carry = jnp.zeros((1, 128), F32)
    return lax.fori_loop(
        0, count // STEP, lambda i, c: body(pl.ds(pl.multiple_of(i * STEP, STEP), STEP), c), carry
    )


def store_blocks(ref, at, value):
    count, _, width = ref.shape
    for i in range(count):
        ref[i, at] = value[:, i * width : (i + 1) * width]


def calls(kernel, outs, us, **kwargs):
    return pl.pallas_call(
        kernel,
        out_shape=[jax.ShapeDtypeStruct(shape, dtype) for shape, dtype in outs],
        compiler_params=pltpu.CompilerParams(vmem_limit_bytes=VMEM),
        cost_estimate=cost(us),
        **kwargs,
    )


def branch_kernel(ctx, w, x, rows, valid, normed, low, unit, scale, stats, acc):
    acc[...] = matmul(ctx[...], w[0])
    zero = jnp.zeros((1, acc.shape[1]), F32)

    def body(at, sums):
        branch = acc[at] + rows[2:3]
        residual = x[at].astype(F32) + branch
        value, scale[at] = norm_parts(residual)
        unit[at] = value.astype(BF)
        normed[at] = value * rows[6:7] + rows[3:4]
        low[at] = normed[at].astype(BF)
        return tuple(
            s + column_sum(valid[at] * value * value) for s, value in zip(sums, (residual, branch))
        )

    for i, value in enumerate(by_rows(acc.shape[0], body, (zero, zero))):
        stats[i : i + 1] = jnp.broadcast_to(total(value), (1, 128))


def branch_layer(context, w_out, inputs, rows, valid):
    t, d = inputs.shape
    outs = [((t, d), F32), ((t, d), BF), ((t, d), BF), ((t, 1), F32), ((2, 128), F32)]
    scratch = [pltpu.VMEM((t, d), F32)]
    return calls(branch_kernel, outs, 5, scratch_shapes=scratch)(
        context, w_out, inputs, rows, valid
    )


def output_kernel(plan, level, me_ref, active, normed, rows, valid, hot, *refs):
    pieces = refs[:-8]
    low, unit, scale, pooled, stats, w, acc, sems = refs[-8:]
    step = pl.program_id(0)
    width = active.shape[1]
    block = pieces[0].shape[1]

    @pl.when(step == 0)
    def _():
        copies = []
        if plan is None:
            copies.append(pltpu.make_async_copy(pieces[0], w, sems.at[0]))
        for piece, masks in zip(pieces, plan or []):
            for slot, mask in enumerate(masks):
                at = pl.multiple_of(block_of(me_ref[0], mask, level) * block, block)
                target = w.at[pl.ds(at, block)]
                copies.append(
                    pltpu.make_async_copy(piece.at[slot], target, sems.at[len(copies)])
                )
        for copy in copies:
            copy.start()
        for copy in copies:
            copy.wait()

    product = matmul(active[...], w[pl.ds(pl.multiple_of(step * width, width), width)])

    @pl.when(step == 0)
    def _():
        acc[...] = product

    @pl.when(step > 0)
    def _():
        acc[...] += product

    @pl.when(step == pl.num_programs(0) - 1)
    def _():
        zero = jnp.zeros((1, acc.shape[1]), F32)

        def body(at, sums):
            ffn_out = acc[at] + rows[4:5]
            residual = normed[at] + ffn_out
            value, scale[at] = norm_parts(residual)
            unit[at] = value.astype(BF)
            low[at] = (value * rows[7:8] + rows[5:6]).astype(BF)
            values = (valid[at] * residual * residual, valid[at] * ffn_out * ffn_out)
            return tuple(s + column_sum(value) for s, value in zip(sums, values))

        sums = by_rows(acc.shape[0], body, (zero, zero))
        for i, value in enumerate((*sums, valid[...])):
            stats[i : i + 1] = jnp.broadcast_to(total(value), (1, 128))
        pooled[...] = matmul(hot[...].astype(BF), low[...]).astype(BF)


def all_of(shape):
    return pl.BlockSpec(shape, lambda j: (0,) * len(shape))


def output_layer(place, active, pieces, plan, normed, rows, valid, hot):
    t, ff = active.shape
    d = normed.shape[1]
    outs = [((t, d), BF), ((t, d), BF), ((t, 1), F32), ((hot.shape[0], d), BF), ((3, 128), F32)]
    outs.append(((ff, d), BF))
    return calls(
        functools.partial(output_kernel, plan, place.wide * place.narrow // LEVELS),
        outs,
        9,
        grid=(ff // d,),
        in_specs=[pl.BlockSpec(memory_space=pltpu.SMEM), pl.BlockSpec((t, d), lambda j: (0, j))]
        + [all_of(a.shape) for a in (normed, rows, valid, hot)]
        + [pl.BlockSpec(memory_space=pl.ANY)] * len(pieces),
        out_specs=[all_of(shape) for shape, _ in outs],
        scratch_shapes=[
            pltpu.VMEM((t, d), F32),
            pltpu.SemaphoreType.DMA((place.wide * place.narrow,)),
        ],
    )(place.me.reshape(1), active, normed, rows, valid, hot, *pieces)


def output_back_kernel(cot, valid, hot, pool, unit, scale, rows, grad, low, sums):
    zero = jnp.zeros((1, grad.shape[1]), F32)

    def body(at, totals):
        grad_out = cot[at].astype(F32) * valid[at] + lax.dot_general(
            hot[:, at],
            pool[...],
            (((0,), (0,)), ((), ())),
            precision=lax.Precision.HIGHEST,
            preferred_element_type=F32,
        )
        grad[at] = norm_back(grad_out, unit[at], scale[at], rows[7:8])
        low[at] = grad[at].astype(BF)
        values = (grad_out * unit[at].astype(F32), grad_out, low[at].astype(F32))
        return tuple(t + column_sum(value) for t, value in zip(totals, values))

    for i, value in enumerate(by_rows(grad.shape[0], body, (zero,) * 3)):
        sums[i : i + 1] = value


def output_back(cot, valid, hot, pool, unit, scale, rows):
    t, d = cot.shape
    outs = [((t, d), F32), ((t, d), BF), ((3, d), F32)]
    return calls(output_back_kernel, outs, 6)(cot, valid, hot, pool, unit, scale, rows)


def hidden_back_kernel(
    low, w_back, slope, w_in, grad, unit, scale, rows, hidden, inb, branch, blocks, sums, acc
):
    step = pl.program_id(0)
    product = inner_cols(low[...], w_back[...])
    hidden[...] = (product * slope[...].astype(F32)).astype(BF)
    inb[...] = column_sum(hidden[...].astype(F32))
    product = inner_cols(hidden[...], w_in[0])

    @pl.when(step == 0)
    def _():
        acc[...] = grad[...] + product

    @pl.when(step > 0)
    def _():
        acc[...] += product

    @pl.when(step == pl.num_programs(0) - 1)
    def _():
        zero = jnp.zeros((1, acc.shape[1]), F32)

        def body(at, totals):
            value = acc[at]
            branch[at] = norm_back(value, unit[at], scale[at], rows[6:7]).astype(BF)
            store_blocks(blocks, at, branch[at])
            values = (value * unit[at].astype(F32), value, branch[at].astype(F32))
            return tuple(t + column_sum(value) for t, value in zip(totals, values))

        for i, value in enumerate(by_rows(acc.shape[0], body, (zero,) * 3)):
            sums[i : i + 1] = value


def hidden_back(low, w_back, slope, w_in, grad, unit, scale, rows, narrow):
    t, d = low.shape
    ff = slope.shape[1]
    tile = pl.BlockSpec((t, d), lambda j: (0, j))
    outs = [
        ((t, ff), BF),
        ((1, ff), F32),
        ((t, d), BF),
        ((narrow, t, d // narrow), BF),
        ((3, d), F32),
    ]
    return calls(
        hidden_back_kernel,
        outs,
        14,
        grid=(ff // d,),
        in_specs=[
            all_of(low.shape),
            pl.BlockSpec((d, d), lambda j: (j, 0)),
            tile,
            pl.BlockSpec((1, d, d), lambda j: (j, 0, 0)),
        ]
        + [all_of(a.shape) for a in (grad, unit, scale, rows)],
        out_specs=[tile, pl.BlockSpec((1, d), lambda j: (0, j))]
        + [all_of(shape) for shape, _ in outs[2:]],
        scratch_shapes=[pltpu.VMEM((t, d), F32)],
    )(low, w_back, slope, w_in, grad, unit, scale, rows)


def input_back_kernel(grad, w, residual, out, acc):
    step = pl.program_id(0)
    product = inner_cols(grad[0], w[0])

    @pl.when(step == 0)
    def _():
        acc[...] = residual[...].astype(F32) + product

    @pl.when(step == 1)
    def _():
        acc[...] += product

    @pl.when(step == 2)
    def _():
        out[...] = (acc[...] + product).astype(BF)


def input_back(grad_qkv, w_qkv, residual):
    _, t, d = grad_qkv.shape
    return calls(
        input_back_kernel,
        [((t, d), BF)],
        6,
        grid=(3,),
        in_specs=[
            pl.BlockSpec((1, t, d), lambda j: (j, 0, 0)),
            pl.BlockSpec((1, d, d), lambda j: (j, 0, 0)),
            all_of((t, d)),
        ],
        out_specs=[all_of((t, d))],
        scratch_shapes=[pltpu.VMEM((t, d), F32)],
    )(grad_qkv, w_qkv, residual)[0]


def spread_masks(count, width):
    total_cols = count * width
    column = lax.broadcasted_iota(jnp.int32, (count, total_cols), 1)
    first = lax.broadcasted_iota(jnp.int32, (count, total_cols), 0) * width
    own = (column >= first) & (column < first + width)
    owner = jnp.sum(jnp.where(own, first, 0), axis=0, keepdims=True)
    within = lax.broadcasted_iota(jnp.int32, (width, total_cols), 1) - owner
    spread = within == lax.broadcasted_iota(jnp.int32, (width, total_cols), 0)
    return own, spread.astype(F32)


def unpack_kernel(small, rows, inb):
    count = small.shape[0]
    value = small[...].astype(F32)

    def unpack(part, masks):
        own, spread = masks
        placed = matmul(part.astype(BF), spread.astype(BF))
        return column_sum(jnp.where(own, placed, 0.0))

    width = rows.shape[1] // count
    masks = spread_masks(count, width)
    for r in range(8):
        rows[r : r + 1] = unpack(value[:, r, :width], masks)
    width = inb.shape[1] // count
    inb[...] = unpack(value[:, 0, 128 : 128 + width], spread_masks(count, width))


def unpack_params(small, d, ff):
    return calls(unpack_kernel, [((8, d), F32), ((1, ff), F32)], 0.1)(small)


def pack_kernel(attn, out, ffn, inb, stats_a, stats_b, packed, rows, parts):
    count = packed.shape[0]
    vectors = (attn[0:1], attn[1:2], out[2:3], out[1:2], ffn[2:3], ffn[1:2], out[0:1], ffn[0:1])

    def pack(vector, own, spread):
        return lax.dot_general(
            jnp.where(own, vector, 0.0),
            spread,
            (((1,), (1,)), ((), ())),
            precision=lax.Precision.HIGHEST,
            preferred_element_type=F32,
        )

    for i, vector in enumerate(vectors):
        rows[i : i + 1] = vector
    packed[...] = jnp.zeros(packed.shape, F32)
    width = rows.shape[1] // count
    masks = spread_masks(count, width)

    def body(i, carry):
        parts[i] = pack(rows[pl.ds(i, 1)], *masks)
        return carry

    lax.fori_loop(0, len(vectors), body, 0)
    for i in range(len(vectors)):
        packed[:, i * width : (i + 1) * width] = parts[i]
    at = len(vectors) * width
    width = inb.shape[1] // count
    packed[:, at : at + width] = pack(inb[...], *spread_masks(count, width))
    at += width
    for i, row in enumerate((stats_a[0:1], stats_a[1:2], stats_b[0:1], stats_b[1:2], stats_b[2:3])):
        packed[:, at + i : at + i + 1] = jnp.broadcast_to(row[:, :1], (count, 1))


def pack_sums(count, attn, out, ffn, inb, stats_a, stats_b):
    width = attn.shape[1]
    scratch = [pltpu.VMEM((8, width), F32), pltpu.VMEM((8, count, width // count), F32)]
    return calls(pack_kernel, [((count, 384), F32)], 4, scratch_shapes=scratch)(
        attn, out, ffn, inb, stats_a, stats_b
    )[0]


def match_grads(rows, label_rows, label_cols):
    is_query, is_pass = label_rows >= 0, label_cols >= 0
    match = jnp.where(is_pass, inner_cols(rows, rows) / SCORE_DIV, MASKED)
    shifted = jnp.exp(match - jnp.max(match, axis=1, keepdims=True))
    probs = shifted / jnp.sum(shifted, axis=1, keepdims=True)
    hot = (label_rows == label_cols).astype(F32)
    grad = jnp.where(is_query & is_pass, (probs - hot) / SCORE_DIV, 0.0).astype(BF)
    return matmul(grad[:POOL], rows) + inner_rows(grad[:, :POOL], rows)


def match_kernel(rows, label_rows, label_cols, out):
    out[...] = match_grads(rows[...], label_rows[...], label_cols[...])


def row_of(z, y, n, s):
    own = (z * s + y) * 3 + n
    spare = y * 3 + (z - 1)
    return jnp.where(z == 0, n * s + y, jnp.where(n < 3, own, spare))


def body(
    passages,
    queries,
    passage_cot,
    query_cot,
    passage_lengths,
    query_lengths,
    labels,
    w_qkv,
    w_out,
    w_in,
    w_back,
    biases,
    norm_gains,
    in_bias,
):
    place = Place()
    s, narrow, devices = place.stride, place.narrow, place.wide * place.narrow
    model_width = passages.shape[2]
    length = passages.shape[1] * narrow
    segs, qsegs = passage_lengths.shape[1] - 1, query_lengths.shape[1] - 1
    on_query = place.z == 0

    piece = model_width // devices
    whole = jnp.concatenate(
        [passage_lengths.reshape(-1), query_lengths.reshape(-1), labels.reshape(-1)]
    )
    whole = jnp.concatenate([whole // 32, whole % 32]).astype(BF)

    w_rows, in_parts = w_out.shape[1], w_in.shape[2] // w_out.shape[2]
    if s == 2:
        towers = pick_towers(place, w_qkv, biases, norm_gains, in_bias, whole)
        got = {k: flip(towers[k], "wide", k * s) for k in (3, 2, 1)}
        levels_qkv = jnp.stack([towers[0], got[1], got[2], got[3]])
        own = [k * s * narrow for k in range(LEVELS)]
        layout = [(0, part, part * w_rows, 0) for part in range(3)] + [(1, 0, 3 * w_rows, 0)]
        shapes = [(3, w_rows, model_width), (1, 8, model_width)]
    else:
        small = jnp.concatenate(
            [biases.reshape(2, -1), norm_gains.reshape(2, -1), in_bias.reshape(2, -1)], axis=1
        )
        small_count = small.shape[1]
        small = jnp.concatenate([small, jnp.broadcast_to(whole, (2, whole.shape[0]))], axis=1)
        to_query = (jnp.arange(devices) < s * narrow)[:, None]
        small = lax.all_to_all(
            jnp.where(to_query, small[1][None], small[0][None]), BOTH, 0, 0, tiled=True
        )
        levels_qkv, own = gather_levels(place, w_qkv), None
        layout = [(0, part, 0, part * model_width) for part in range(3)]
        shapes = [(3, w_rows, model_width)]
    out_in = jnp.concatenate([w_out, w_in], axis=2)
    levels_qkv, out_in, parts = phase(levels_qkv, out_in, (passages, queries))

    pieces_qkv, plan = gather_columns(place, levels_qkv, own)
    levels_out_in = gather_levels(place, out_in)
    swapped = swap_in_directly(place, *parts)
    pieces_qkv, levels_out_in, w_back, swapped = phase(
        pieces_qkv, levels_out_in, w_back, swapped
    )

    cores_qkv, core_plan = gather_cores(pieces_qkv, plan)
    cores_qkv, levels_out_in, swapped = phase(cores_qkv, levels_out_in, swapped)

    pieces_out_in, plan = gather_columns(place, levels_out_in)
    inputs = to_row(place, passages, queries, join_swapped(place, queries, swapped))
    inputs, w_back, cores_qkv = phase(inputs, w_back, cores_qkv)
    levels_back = gather_levels(place, w_back)
    made = assemble(place, cores_qkv, core_plan, layout, shapes)
    w_qkv_all = made[0]

    n_bias, n_gain = biases.shape[1], norm_gains.shape[1]
    ff = in_bias.shape[1] * devices
    if s == 2:
        small = made[1].reshape(devices, 8, -1)
        rows, inb_row = unpack_params(small, model_width, ff)
        ints = small[:, 0, 256 : 256 + whole.shape[0]].astype(F32)
    else:
        params = small[:, :small_count].astype(F32)
        vectors = params[:, : (n_bias + n_gain) * piece].reshape(devices, n_bias + n_gain, piece)
        rows = vectors.transpose(1, 0, 2).reshape(n_bias + n_gain, -1)
        inb_row = params[:, (n_bias + n_gain) * piece :].reshape(1, -1)
        ints = small[:, small_count : small_count + whole.shape[0]].astype(F32)
    half = ints.shape[1] // 2
    ints = (ints[::narrow, :half] * 32 + ints[::narrow, half:]).astype(jnp.int32)
    n_pass = passage_lengths.size
    n_query = query_lengths.size
    pass_lens = ints[:, :n_pass].reshape(-1, segs + 1)
    query_lens = ints[:, n_pass : n_pass + n_query].reshape(-1, qsegs + 1)
    label_all = ints[:, n_pass + n_query :].reshape(-1, qsegs)
    my_row = row_of(place.z, place.y, place.n, s)
    pass_row = pick(pass_lens, jnp.where(on_query, 0, my_row), 0)
    query_row = pick(query_lens, jnp.where(on_query, my_row, 0), 0)
    ends_p = jnp.cumsum(pass_row)[:-1]
    ends_q = jnp.cumsum(query_row)[:-1]
    starts_p, starts_q = ends_p - pass_row[:-1], ends_q - query_row[:-1]
    ends_p = jnp.concatenate([ends_p, jnp.full((qsegs - segs,), length + 1, jnp.int32)])
    ends = jnp.where(on_query, ends_q, ends_p)
    seg_count = jnp.where(on_query, qsegs, segs)
    position = jnp.arange(length, dtype=jnp.int32)
    segment = jnp.sum((position[:, None] >= ends[None, :]).astype(jnp.int32), axis=1)
    valid = (segment < seg_count).astype(F32)[:, None]
    slot = jnp.arange(POOL)
    starts = jnp.where(on_query, jnp.concatenate([starts_q, jnp.full((qsegs,), -1)]), -1)
    for z in range(1, LEVELS):
        here = (place.z == z) & (slot >= qsegs + segs * (z - 1)) & (slot < qsegs + segs * z)
        starts = jnp.where(here, jnp.tile(starts_p, POOL // segs), starts)
    hot = (starts[:, None] == position[None, :]).astype(F32)
    masks = [0]
    if s == 2:
        masks += [dy * narrow + 2 * dx for dx, dy in OTHERS]
        masks += [m ^ 1 for m in masks]
    else:
        for mask in [b * narrow for b in bits_of(s)] + [b for b in reversed(bits_of(narrow))]:
            masks = masks + [m ^ mask for m in masks]
    there = (place.y * narrow + place.n) ^ jnp.array(masks, jnp.int32)
    their_y, their_n = there // narrow, there % narrow
    label_rows = label_all[row_of(jnp.int32(0), their_y, their_n, s)]
    label_rows = jnp.pad(label_rows, ((0, 0), (0, POOL - qsegs)), constant_values=-1)
    levels = jnp.arange(1, LEVELS)
    pass_rows = row_of(levels[None, :], their_y[:, None], their_n[:, None], s)
    pass_ids = (pass_rows[:, :, None] * segs + jnp.arange(segs)).reshape(len(masks), -1)
    spare = POOL - qsegs - pass_ids.shape[1]
    label_cols = jnp.pad(pass_ids, ((0, 0), (qsegs, spare)), constant_values=-1)
    label_rows, label_cols = label_rows.reshape(-1, 1), label_cols.reshape(1, -1)

    qkv, context, log_sum = attend(inputs, w_qkv_all, rows, segment)
    context, pieces_out_in, levels_back, cots = phase(
        context, pieces_out_in, levels_back, (passage_cot, query_cot)
    )

    cores_out_in, core_plan = gather_cores(pieces_out_in, plan)
    cores_out_in, levels_back, cots = phase(cores_out_in, levels_back, cots)

    pieces_back, plan = gather_columns(place, levels_back)
    swapped = swap_in(place, *cots)
    w_out_all, w_in_all = assemble(
        place,
        cores_out_in,
        core_plan,
        [(0, 0, 0, 0)] + [(1, part, 0, (part + 1) * model_width) for part in range(in_parts)],
        [(1, w_rows, model_width), (in_parts, w_rows, model_width)],
    )
    normed, normed_low, unit_one, scale_one, stats_one = branch_layer(
        context, w_out_all, inputs, rows, valid
    )
    active, slope = hidden_layer(normed_low, w_in_all, inb_row)
    active, pieces_back, swapped = phase(active, pieces_back, swapped)

    cores_back, core_plan = gather_cores(pieces_back, plan)
    cot = to_row(place, passage_cot, query_cot, swapped)
    if s != 2:
        back_shape = [(1, w_back.shape[1], model_width)]
        cores_back = assemble(place, cores_back, core_plan, [(0, 0, 0, 0)], back_shape)
        cores_back, core_plan = [cores_back[0][0]], None
    output_low, unit_two, scale_two, pooled, stats_two, w_back_all = output_layer(
        place, active, cores_back, core_plan, normed, rows, valid, hot
    )
    pooled, cot = phase(pooled, cot)

    column = sum([flip(pooled, "wide", k * s).astype(F32) for k in (3, 2, 1)], pooled.astype(F32))
    seen = column.astype(BF)[None]
    if s == 2:
        seen = jnp.concatenate([seen] + [flip_both(seen, dy, 2 * dx) for dx, dy in OTHERS])
        seen = jnp.concatenate([seen, flip(seen, "narrow", 1)])
    else:
        for axis, step in [("wide", b) for b in bits_of(s)] + [
            ("narrow", b) for b in reversed(bits_of(narrow))
        ]:
            seen = jnp.concatenate([seen, flip(seen, axis, step)])
    seen = seen.reshape(-1, model_width)
    if s == 2:
        (grad_pool,) = calls(match_kernel, [((POOL, model_width), F32)], 3)(
            seen, label_rows, label_cols
        )
    else:
        grad_pool = match_grads(seen, label_rows, label_cols)

    grad_pool, output_low = phase(grad_pool, output_low)
    if s == 2:
        out_four = row_pieces(place, output_low)
    grad_resid_two, grad_ffn, sums_two = output_back(
        cot, valid, hot, grad_pool, unit_two, scale_two, rows
    )
    if s == 2:
        send_c, keep_c = products_back(place, active, grad_ffn)
        send_c, out_four = phase(send_c, out_four)
        got_c = flip(send_c, "narrow", 1)
        shares_c = column_shares(place, keep_c, got_c)
        shares_c, grad_ffn = phase(shares_c, grad_ffn)

        columns_c = send_columns(shares_c)
        swapped = swap_out(place, out_four)
    grad_hidden, inb_sums, grad_branch, blocks_b, sums_one = hidden_back(
        grad_ffn, w_back_all, slope, w_in_all, grad_resid_two, unit_one, scale_one, rows, narrow
    )
    if s == 2:
        send_b, keep_b = products_out_in(place, context, blocks_b, normed_low, grad_hidden)
        send_b, columns_c, swapped = phase(send_b, columns_c, swapped)
        passage_out, query_out = from_row(place, out_four, swapped)

        got_b = flip(send_b, "narrow", 1)
        level_c = level_sums(columns_c)
        shares_b = column_shares(place, keep_b, got_b)
        shares_b, level_c, grad_branch = phase(shares_b, level_c, grad_branch)

        columns_b = send_columns(shares_b)
        levels_c = across_levels(level_c, s)
    grad_qkv, blocks_a, sums_qkv = attend_back(
        grad_branch, w_out_all[0], qkv, log_sum, segment, narrow
    )
    if s == 2:
        send_a, keep_a = products_qkv(place, inputs, blocks_a)
        send_a, grad_qkv, columns_b, levels_c = phase(send_a, grad_qkv, columns_b, levels_c)

        got_a = flip(send_a, "narrow", 1)
    input_grad = input_back(grad_qkv, w_qkv_all, grad_branch)
    if s == 2:
        got_a, input_grad, columns_b = phase(got_a, input_grad, columns_b)

        in_four = row_pieces(place, input_grad)
        levels_b = swap_shares(place, level_shares(place, columns_b))
        shares_a = column_shares(place, keep_a, got_a)
        late = levels_b.pop(3)
        shares_a, levels_b, in_four, sums_qkv, levels_c = phase(
            shares_a, levels_b, in_four, sums_qkv, levels_c
        )
        levels_b.insert(3, late)

        columns_a = send_columns(shares_a)
        swapped = swap_out(place, in_four)
        packed = pack_sums(devices, sums_qkv, sums_one, sums_two, inb_sums, stats_one, stats_two)
        grad_w_back = finish_back(levels_c)
        columns_a, swapped, packed = phase(columns_a, swapped, packed)

        packed = lax.all_to_all(packed, BOTH, 0, 0, tiled=True)
        levels_a = swap_shares(place, level_shares(place, columns_a))
        grad_w_out, grad_w_in = finish_out_in(place, levels_b, model_width // place.wide)
        passage_grad, query_grad = from_row(place, in_four, swapped)
        grad_w_qkv = finish_qkv(place, levels_a)
    else:
        packed = pack_sums(devices, sums_qkv, sums_one, sums_two, inb_sums, stats_one, stats_two)
        packed = lax.all_to_all(packed, BOTH, 0, 0, tiled=True)
        grad_w_back = scatter_tower(place, grad_blocks(active, grad_ffn, narrow))
        grad_w_out = scatter_tower(place, grad_blocks(context, grad_branch, narrow))
        grad_w_in = scatter_tower(place, grad_blocks(normed_low, grad_hidden, narrow))
        flat = jnp.moveaxis(grad_qkv, 0, 1).reshape(length, -1)
        grad_w_qkv = scatter_tower(place, grad_blocks(inputs, flat, narrow))
        out_four, in_four = row_pieces(place, output_low), row_pieces(place, input_grad)
        passage_out, query_out = from_row(place, out_four, swap_out(place, out_four))
        passage_grad, query_grad = from_row(place, in_four, swap_out(place, in_four))

    packed = packed.reshape(LEVELS, -1, packed.shape[1]).sum(axis=1)
    packed = jnp.stack([packed[1] + packed[2] + packed[3], packed[0]])
    edges = [n_bias * piece, (n_bias + n_gain) * piece]
    edges.append(edges[1] + in_bias.shape[1])
    grad_biases = packed[:, : edges[0]].reshape(2, n_bias, piece)
    grad_gains = packed[:, edges[0] : edges[1]].reshape(2, n_gain, piece)
    grad_inb = packed[:, edges[1] : edges[2]]
    totals = packed[:, edges[2] : edges[2] + 5]
    rms_stats = jnp.sqrt(totals[:, :4] / (totals[:, 4:] * model_width))
    return (
        passage_out,
        query_out,
        passage_grad,
        query_grad,
        grad_w_qkv,
        grad_w_out,
        grad_w_in,
        grad_w_back,
        grad_biases,
        grad_gains,
        grad_inb,
        rms_stats,
    )


def solution(mesh):
    return jax.shard_map(
        body,
        mesh=mesh,
        in_specs=(
            P("wide", "narrow", None),
            P("wide", "narrow", None),
            P("wide", "narrow", None),
            P("wide", "narrow", None),
            P("wide", None),
            P("wide", None),
            P("wide"),
            P(None, ("wide", "narrow"), None),
            P(None, ("wide", "narrow"), None),
            P(None, ("wide", "narrow"), None),
            P(None, ("wide", "narrow"), None),
            P(None, None, ("wide", "narrow")),
            P(None, None, ("wide", "narrow")),
            P(None, ("wide", "narrow")),
        ),
        out_specs=(
            P("wide", "narrow", None),
            P("wide", "narrow", None),
            P("wide", "narrow", None),
            P("wide", "narrow", None),
            P(None, "wide", "narrow"),
            P(None, "wide", "narrow"),
            P(None, "wide", "narrow"),
            P(None, "wide", "narrow"),
            P(None, None, ("wide", "narrow")),
            P(None, None, ("wide", "narrow")),
            P(None, ("wide", "narrow")),
            P(),
        ),
        check_vma=False,
    )
```

```python
import functools
import math

import jax
import jax.numpy as jnp
from jax import lax
from jax.experimental import pallas as pl
from jax.experimental.pallas import tpu as pltpu
from jax.sharding import PartitionSpec as P

HEAD_DIM = 64
LEVELS = 4
GROUP = 4
POOL = 32
STEP = 128
VMEM = 58 << 20
OTHERS = ((1, 1), (1, 0), (0, 1))


def cost(us):
    return pl.CostEstimate(flops=int(us * 1.15e9), bytes_accessed=1024, transcendentals=0)


EPSILON = 1e-05
SCORE_DIV = 12.0
MASKED = -1e30
BF = jnp.bfloat16
F32 = jnp.float32
BOTH = ("wide", "narrow")


def matmul(left, right):
    return jnp.dot(left, right, preferred_element_type=F32)


def inner_rows(left, right):
    return lax.dot_general(left, right, (((0,), (0,)), ((), ())), preferred_element_type=F32)


def inner_cols(left, right):
    return lax.dot_general(left, right, (((1,), (1,)), ((), ())), preferred_element_type=F32)


def flip(x, axis, mask):
    size = lax.axis_size(axis)
    return lax.ppermute(x, axis, [(i, i ^ mask) for i in range(size)])


def flip_both(x, wide_mask, narrow_mask):
    wide, narrow = lax.axis_size("wide"), lax.axis_size("narrow")
    mask = wide_mask * narrow + narrow_mask
    return lax.ppermute(x, BOTH, [(i, i ^ mask) for i in range(wide * narrow)])


def phase(*values):
    return lax.optimization_barrier(values)


def across_levels(x, stride):
    groups = [[k * stride + i for k in range(LEVELS)] for i in range(stride)]
    return lax.all_to_all(x, "wide", 0, 0, axis_index_groups=groups, tiled=True)


def swap_levels(x, k, stride):
    pairs = []
    for i in range(stride):
        pairs += [(i, k * stride + i), (k * stride + i, i)]
    return lax.ppermute(x, "wide", pairs)


def bits_of(size):
    return [1 << b for b in range(size.bit_length() - 1)]


class Place:
    def __init__(self):
        self.wide = lax.axis_size("wide")
        self.narrow = lax.axis_size("narrow")
        self.stride = self.wide // LEVELS
        self.w = lax.axis_index("wide")
        self.n = lax.axis_index("narrow")
        self.z = self.w // self.stride
        self.y = self.w % self.stride
        self.me = self.w * self.narrow + self.n


def swap_in(place, pass_part, query_part):
    query = jnp.broadcast_to(query_part, (LEVELS, *query_part.shape[1:]))
    first = jnp.concatenate([query_part, pass_part])
    return across_levels(jnp.where(place.z == 0, first, query), place.stride)


def swap_in_directly(place, pass_part, query_part):
    return [
        swap_levels(jnp.where(place.z == 0, pass_part[k - 1], query_part[0]), k, place.stride)
        for k in range(1, LEVELS)
    ]


def join_swapped(place, query_part, got):
    first = jnp.where(place.z == 0, query_part[0], got[0] + got[1] + got[2])
    return jnp.stack([first] + got)


def to_row(place, pass_part, query_part, got):
    four = jnp.where(place.z == 0, got, jnp.concatenate([pass_part, got[:1]]))
    mine = lax.all_to_all(four, "narrow", 0, 0, tiled=True)
    return mine.reshape(-1, mine.shape[-1])


def row_pieces(place, row):
    return lax.all_to_all(
        row.reshape(place.narrow, -1, row.shape[-1]), "narrow", 0, 0, tiled=True
    )


def swap_out(place, four):
    last = jnp.broadcast_to(four[3:], four.shape)
    return across_levels(jnp.where(place.z == 0, four, last), place.stride)


def from_row(place, four, got):
    pass_part = jnp.where(place.z == 0, got[1:], four[:3])
    query_part = jnp.where(place.z == 0, four[:1], got[:1])
    return pass_part, query_part


def toggle(places, mask):
    return [(p[0], p[1] ^ mask) if isinstance(p, tuple) else p ^ mask for p in places]


def block_of(me, place, level):
    if isinstance(place, tuple):
        return ((me & (level - 1)) ^ place[1]) + place[0] * level
    return me ^ place


def assemble_kernel(plan, layout, level, me_ref, *refs):
    pieces, outs, sems = refs[: len(plan)], refs[len(plan) : -1], refs[-1]
    me = me_ref[0]
    copies = []
    for piece, masks in zip(pieces, plan):
        for slot, mask in enumerate(masks):
            for out, part, row, column in layout:
                target = outs[out].at[part, block_of(me, mask, level)]
                rows, columns = outs[out].shape[2:]
                source = piece.at[slot, pl.ds(row, rows), pl.ds(column, columns)]
                copies.append(pltpu.make_async_copy(source, target, sems.at[len(copies)]))
    for copy in copies:
        copy.start()
    for copy in copies:
        copy.wait()


def assemble(place, pieces, plan, layout, outs):
    total = place.wide * place.narrow
    made = pl.pallas_call(
        functools.partial(assemble_kernel, plan, layout, total // LEVELS),
        out_shape=[jax.ShapeDtypeStruct((out[0], total, *out[1:]), BF) for out in outs],
        in_specs=[pl.BlockSpec(memory_space=pltpu.SMEM)]
        + [pl.BlockSpec(memory_space=pl.ANY)] * len(pieces),
        out_specs=[pl.BlockSpec(memory_space=pltpu.VMEM)] * len(outs),
        scratch_shapes=[pltpu.SemaphoreType.DMA((total * len(layout),))],
        cost_estimate=cost(0.1),
        compiler_params=pltpu.CompilerParams(vmem_limit_bytes=VMEM),
    )(place.me.reshape(1), *pieces)
    return [out.reshape(out.shape[0], -1, out.shape[3]) for out in made]


def pick_kernel(z_ref, w_ref, bias_ref, gain_ref, inb_ref, ints_ref, *refs):
    outs, small = refs[:-1], refs[-1]
    rows, width = w_ref.shape[1], small.shape[1]
    n_bias, n_gain = bias_ref.shape[1], gain_ref.shape[1]
    for k, out in enumerate(outs):
        tower = jnp.where(z_ref[0] == k, 1, 0)
        for part in range(3):
            out[part * rows : (part + 1) * rows] = w_ref[tower, :, part * width : (part + 1) * width]
        small[...] = jnp.zeros(small.shape, F32)
        small[:n_bias, : bias_ref.shape[2]] = bias_ref[tower].astype(F32)
        small[n_bias : n_bias + n_gain, : gain_ref.shape[2]] = gain_ref[tower].astype(F32)
        small[:1, 128 : 128 + inb_ref.shape[2]] = inb_ref[tower].astype(F32)
        small[:1, 256 : 256 + ints_ref.shape[1]] = ints_ref[...].astype(F32)
        out[3 * rows :] = small[...].astype(BF)


def pick_towers(place, w_qkv, biases, norm_gains, in_bias, ints):
    width = w_qkv.shape[2] // 3
    vmem = pl.BlockSpec(memory_space=pltpu.VMEM)
    return calls(
        pick_kernel,
        [((3 * w_qkv.shape[1] + 8, width), BF)] * LEVELS,
        2,
        in_specs=[pl.BlockSpec(memory_space=pltpu.SMEM)] + [vmem] * 5,
        scratch_shapes=[pltpu.VMEM((8, width), F32)],
    )(place.z.reshape(1), w_qkv, biases, norm_gains, in_bias[:, None], ints[None])


def gather_levels(place, pair):
    first = lax.broadcasted_iota(jnp.int32, (LEVELS, 1, 1), 0) == 0
    return across_levels(jnp.where(first, pair[1:], pair[:1]), place.stride)


def gather_columns(place, levels, own=None):
    s, narrow = place.stride, place.narrow
    if own is None:
        own = [(level, 0) for level in range(LEVELS)]
    pieces, plan = [levels], [own]
    if s == 2:
        for dx, dy in OTHERS:
            pieces.append(flip_both(levels, dy, 2 * dx))
            plan.append(toggle(own, dy * narrow + 2 * dx))
    else:
        for b in bits_of(s):
            for i in range(len(pieces)):
                pieces.append(flip(pieces[i], "wide", b))
                plan.append(toggle(plan[i], b * narrow))
        for i in range(len(pieces)):
            pieces.append(flip(pieces[i], "narrow", 2))
            plan.append(toggle(plan[i], 2))
    return pieces, plan


def gather_cores(pieces, plan):
    others = [flip(piece, "narrow", 1) for piece in pieces]
    return list(pieces) + others, plan + [toggle(places, 1) for places in plan]


def pick(x, index, dim):
    return lax.dynamic_index_in_dim(x, index, dim, keepdims=False)


def halve(x, place, axis, mask, dim):
    index = place.n if axis == "narrow" else place.w
    bit = jnp.where((index & mask) != 0, 1, 0)
    got = flip(pick(x, 1 - bit, dim).astype(BF), axis, mask)
    return pick(x, bit, dim) + got.astype(F32)


def scatter_tower(place, partial):
    s = place.stride
    rows, narrow, cols = partial.shape
    per = rows // place.wide
    x = partial.reshape(rows, 2, 2, cols)
    x = halve(x, place, "narrow", 1, 2)
    x = x.reshape(LEVELS, s, per, 2, cols)
    first, second = x[:2], x[2:]

    def over_columns(part):
        for b in reversed(bits_of(s)):
            shape = part.shape
            part = part.reshape(shape[0], 2, shape[1] // 2, *shape[2:])
            part = halve(part, place, "wide", b, 1)
        return part[:, 0]

    first = over_columns(halve(first, place, "narrow", 2, 3))
    second = halve(over_columns(second), place, "narrow", 2, 2)
    return jnp.stack(sum_levels(place, send_levels(place, jnp.concatenate([first, second]))))


def send_levels(place, levels):
    slots = [None] * LEVELS
    slots[0] = pick(levels, place.z, 0)
    for k in (3, 2, 1):
        slots[k] = flip(pick(levels, place.z ^ k, 0).astype(BF), "wide", k * place.stride)
    return slots


def sum_levels(place, slots):
    tower0 = sum(jnp.where(place.z == k, 0.0, slots[k].astype(F32)) for k in range(LEVELS))
    tower1 = sum(jnp.where(place.z == k, slots[k].astype(F32), 0.0) for k in range(LEVELS))
    return tower0, tower1


def share_kernel(at_ref, keep_ref, got_ref, *out_refs):
    x, y = at_ref[0], at_ref[1]

    def body(level, carry):
        for ref, (dx, dy) in zip(out_refs, ((0, 0), *OTHERS)):
            at = (x ^ dx, level, y ^ dy)
            ref[level] = (keep_ref[at].astype(F32) + got_ref[at].astype(F32)).astype(BF)
        return carry

    lax.fori_loop(0, keep_ref.shape[1], body, 0)


def column_shares(place, keep, got):
    r, c = got.shape[2:]
    half = LEVELS // 2
    block = pl.BlockSpec((2, half, place.stride, r, c), lambda i, at: (0, i, 0, 0, 0))
    out = pl.BlockSpec((half, r, c), lambda i, at: (i, 0, 0))
    shape = (2, LEVELS, place.stride, r, c)
    return pl.pallas_call(
        share_kernel,
        grid_spec=pltpu.PrefetchScalarGridSpec(
            num_scalar_prefetch=1, grid=(2,), in_specs=[block] * 2, out_specs=[out] * 4
        ),
        out_shape=[jax.ShapeDtypeStruct((LEVELS, r, c), BF)] * 4,
        compiler_params=pltpu.CompilerParams(vmem_limit_bytes=VMEM),
        cost_estimate=cost(1),
    )(jnp.stack([place.n // 2, place.y]), keep.reshape(shape), got.reshape(shape))


def send_columns(shares):
    return [shares[0]] + [
        flip_both(sent, dy, 2 * dx) for sent, (dx, dy) in zip(shares[1:], OTHERS)
    ]


def level_kernel(z_ref, own_ref, *refs):
    got_refs, out_refs = refs[:3], refs[3:]
    step = 24

    def body(i, carry):
        rows = pl.ds(pl.multiple_of(i * step, step), step)
        for k, out_ref in enumerate(out_refs):
            at = (z_ref[0] ^ k, rows)
            total = own_ref[at].astype(F32)
            for ref in got_refs:
                total = total + ref[at].astype(F32)
            out_ref[rows] = total.astype(out_ref.dtype)
        return carry

    lax.fori_loop(0, own_ref.shape[1] // step, body, 0)


def level_shares(place, columns):
    r, c = columns[0].shape[1:]
    vmem = pl.BlockSpec(memory_space=pltpu.VMEM)
    return pl.pallas_call(
        level_kernel,
        in_specs=[pl.BlockSpec(memory_space=pltpu.SMEM)] + [vmem] * 4,
        out_specs=[vmem] * 4,
        out_shape=[jax.ShapeDtypeStruct((r, c), F32)] + [jax.ShapeDtypeStruct((r, c), BF)] * 3,
        compiler_params=pltpu.CompilerParams(vmem_limit_bytes=VMEM),
        cost_estimate=cost(1),
    )(place.z.reshape(1), *columns)


def level_sums_kernel(*refs):
    def body(at, carry):
        refs[-1][at] = sum(ref[at].astype(F32) for ref in refs[:-1]).astype(BF)
        return carry

    lax.fori_loop(0, LEVELS, body, 0)


def level_sums(columns):
    shape = columns[0].shape
    return calls(level_sums_kernel, [(shape, BF)], 3)(*columns)[0]


def swap_shares(place, shares):
    slots = [shares[0], None, None, None]
    for k in (3, 2, 1):
        slots[k] = flip(shares[k], "wide", k * place.stride)
    return slots


def product_kernel(step, me_ref, *refs):
    send_ref, keep_ref = refs[-2:]
    left_refs = refs[:-2]
    to_send = pl.program_id(0) < 2

    @pl.when(to_send)
    def _():
        step(left_refs, lambda at, v: send_ref.__setitem__((0, *at), v.astype(BF)))

    @pl.when(jnp.logical_not(to_send))
    def _():
        step(left_refs, lambda at, v: keep_ref.__setitem__((0, *at), v.astype(BF)))


def products(place, step, operands, specs, block):
    def target(j, me):
        return (j % 2) * 2 + jnp.where(j < 2, 1 - me[0] % 2, me[0] % 2)

    wide = place.wide
    grid_spec = pltpu.PrefetchScalarGridSpec(
        num_scalar_prefetch=1,
        grid=(4,),
        in_specs=specs(target),
        out_specs=[
            pl.BlockSpec((1, wide, *block), lambda j, me: (jnp.minimum(j, 1), 0, 0, 0)),
            pl.BlockSpec((1, wide, *block), lambda j, me: (jnp.maximum(j - 2, 0), 0, 0, 0)),
        ],
    )
    return pl.pallas_call(
        functools.partial(product_kernel, step),
        grid_spec=grid_spec,
        out_shape=[
            jax.ShapeDtypeStruct((2, wide, *block), BF),
            jax.ShapeDtypeStruct((2, wide, *block), BF),
        ],
        compiler_params=pltpu.CompilerParams(vmem_limit_bytes=VMEM),
        cost_estimate=cost(8),
    )(place.n.reshape(1), *operands)


def whole(shape):
    return pl.BlockSpec(shape, lambda j, me: (0,) * len(shape))


def grad_blocks(left, right, narrow):
    out = inner_rows(left, right)
    return out.reshape(out.shape[0], narrow, -1)


def products_back_kernel(core_ref, left_ref, right_ref, send_ref, keep_ref, turned_ref):
    @pl.when(pl.program_id(0) == 0)
    def _():
        turned_ref[...] = right_ref[...].T

    cols, rows = send_ref.shape[2:]
    first = core_ref[0] == 0

    def body(x, carry):
        at = pl.ds(pl.multiple_of(x * 2 * cols, 2 * cols), 2 * cols)
        value = matmul(turned_ref[at], left_ref[...]).astype(BF)
        for w in range(2):
            columns = slice(w * rows, (w + 1) * rows)
            even, odd = value[:cols, columns], value[cols:, columns]
            keep_ref[x, w] = jnp.where(first, even, odd)
            send_ref[x, w] = jnp.where(first, odd, even)
        return carry

    lax.fori_loop(0, 2, body, 0)


def products_back(place, active, grad_ffn):
    t, ff = active.shape
    d = grad_ffn.shape[1]
    cols, rows = d // place.narrow, ff // place.wide
    out = pl.BlockSpec((2, 2, cols, rows), lambda j, core: (0, j, 0, 0))
    return pl.pallas_call(
        products_back_kernel,
        grid_spec=pltpu.PrefetchScalarGridSpec(
            num_scalar_prefetch=1,
            grid=(place.wide // 2,),
            in_specs=[pl.BlockSpec((t, 2 * rows), lambda j, core: (0, j)), whole((t, d))],
            out_specs=[out, out],
            scratch_shapes=[pltpu.VMEM((d, t), BF)],
        ),
        out_shape=[jax.ShapeDtypeStruct((2, place.wide, cols, rows), BF)] * 2,
        compiler_params=pltpu.CompilerParams(vmem_limit_bytes=VMEM),
        cost_estimate=cost(7),
    )((place.n % 2).reshape(1), active, grad_ffn)


def finish_back(levels):
    levels = levels.astype(F32)
    return jnp.stack([(levels[1] + levels[2] + levels[3]).T, levels[0].T])


def products_out_in(place, context, blocks, normed, grad_hidden):
    narrow = place.narrow
    t, d = context.shape
    rows = d // place.wide
    cols_out, cols_in = blocks.shape[2], grad_hidden.shape[1] // narrow
    fold = cols_in // cols_out
    low = rows // fold

    def step(refs, store):
        context_ref, branch_ref, normed_ref, hidden_ref = refs

        def body(i, carry):
            at = pl.ds(pl.multiple_of(i * 4 * rows, 4 * rows), 4 * rows)
            value = inner_rows(normed_ref[:, at], hidden_ref[...])
            for w in range(4):
                store((4 * i + w, slice(0, rows)), value[w * rows : (w + 1) * rows])
            value = inner_rows(context_ref[:, at], branch_ref[0])
            for w in range(4):
                for g in range(fold):
                    store(
                        (4 * i + w, slice(rows, rows + low), slice(g * cols_out, (g + 1) * cols_out)),
                        value[w * rows + g * low : w * rows + (g + 1) * low],
                    )
            return carry

        lax.fori_loop(0, place.wide // 4, body, 0)

    return products(
        place,
        step,
        (context, blocks, normed, grad_hidden),
        lambda target: [
            whole((t, d)),
            pl.BlockSpec((1, t, cols_out), lambda j, me: (target(j, me), 0, 0)),
            whole((t, d)),
            pl.BlockSpec((t, cols_in), lambda j, me: (0, target(j, me))),
        ],
        (rows + low, cols_in),
    )


def finish_out_in(place, slots, rows):
    parts = sum_levels(place, slots)
    low, cols = parts[0].shape[0] - rows, parts[0].shape[1]
    fold = rows // low
    grad_in = jnp.stack([part[:rows] for part in parts])
    grad_out = [
        jnp.moveaxis(part[rows:].reshape(low, fold, -1), 1, 0).reshape(rows, -1) for part in parts
    ]
    return jnp.stack(grad_out), grad_in


def products_qkv(place, inputs, blocks):
    t, d = inputs.shape
    rows, cols = d // place.wide, blocks.shape[2]
    half = rows // 2

    def step(refs, store):
        left, right = refs
        value = inner_rows(left[...], right[0])
        for w in range(place.wide):
            for g in range(2):
                store(
                    (w, slice(None), slice(g * cols, (g + 1) * cols)),
                    value[w * rows + g * half : w * rows + (g + 1) * half],
                )

    return products(
        place,
        step,
        (inputs, blocks),
        lambda target: [
            whole((t, d)),
            pl.BlockSpec((1, t, cols), lambda j, me: (target(j, me), 0, 0)),
        ],
        (half, 2 * cols),
    )


def finish_qkv(place, slots):
    parts = sum_levels(place, slots)
    cols = parts[0].shape[1] // 2
    return jnp.stack([jnp.concatenate([p[:, :cols], p[:, cols:]]) for p in parts])


def attend_kernel(x_ref, w_ref, rows_ref, seg_row_ref, seg_col_ref, qkv_ref, ctx_ref, lse_ref):
    x = x_ref[...]
    same = seg_col_ref[...] == seg_row_ref[...]
    qkv_ref[0] = (matmul(x, w_ref[0]) + rows_ref[0:1]).astype(BF)
    qkv_ref[1] = matmul(x, w_ref[1]).astype(BF)
    qkv_ref[2] = (matmul(x, w_ref[2]) + rows_ref[1:2]).astype(BF)
    for h in range(GROUP):
        lanes = slice(h * HEAD_DIM, (h + 1) * HEAD_DIM)
        q, k, v = qkv_ref[0, :, lanes], qkv_ref[1, :, lanes], qkv_ref[2, :, lanes]
        scores = jnp.where(same, inner_cols(k, q) * HEAD_DIM ** (-0.5), MASKED)
        top = jnp.max(scores, axis=0, keepdims=True)
        shifted = jnp.exp(scores - top)
        total = jnp.sum(shifted, axis=0, keepdims=True)
        probs = (shifted * (1.0 / total)).astype(BF)
        ctx_ref[:, lanes] = inner_rows(probs, v).astype(BF)
        lse_ref[0, h : h + 1, :] = top + jnp.log(total)


def attend(x, w_qkv, rows, segment):
    t, d = x.shape
    width = GROUP * HEAD_DIM
    steps = d // width
    return pl.pallas_call(
        attend_kernel,
        grid=(steps,),
        in_specs=[
            pl.BlockSpec((t, d), lambda j: (0, 0)),
            pl.BlockSpec((3, d, width), lambda j: (0, 0, j)),
            pl.BlockSpec((8, width), lambda j: (0, j)),
            pl.BlockSpec((1, t), lambda j: (0, 0)),
            pl.BlockSpec((t, 1), lambda j: (0, 0)),
        ],
        out_specs=[
            pl.BlockSpec((3, t, width), lambda j: (0, 0, j)),
            pl.BlockSpec((t, width), lambda j: (0, j)),
            pl.BlockSpec((1, GROUP, t), lambda j: (j, 0, 0)),
        ],
        out_shape=[
            jax.ShapeDtypeStruct((3, t, d), BF),
            jax.ShapeDtypeStruct((t, d), BF),
            jax.ShapeDtypeStruct((steps, GROUP, t), F32),
        ],
        compiler_params=pltpu.CompilerParams(vmem_limit_bytes=VMEM),
        cost_estimate=cost(0.1),
    )(x, w_qkv, rows, segment.reshape(1, t), segment.reshape(t, 1))


def attend_back_kernel(
    gb_ref, w_ref, qkv_ref, lse_ref, seg_row_ref, seg_col_ref, out_ref, blocks_ref, sums_ref, grad_ref
):
    scale = HEAD_DIM ** (-0.5)
    same = seg_col_ref[...] == seg_row_ref[...]
    grad_ref[...] = inner_cols(gb_ref[...], w_ref[...]).astype(BF)

    def pair(p, carry):
        at = pl.ds(pl.multiple_of(p * 2 * HEAD_DIM, 2 * HEAD_DIM), 2 * HEAD_DIM)
        queries, keys, values = qkv_ref[0, :, at], qkv_ref[1, :, at], qkv_ref[2, :, at]
        grads, outs = grad_ref[:, at], []
        for h in range(2):
            lanes = slice(h * HEAD_DIM, (h + 1) * HEAD_DIM)
            q, k, v, g = queries[:, lanes], keys[:, lanes], values[:, lanes], grads[:, lanes]
            scores = jnp.where(same, inner_cols(k, q) * scale, MASKED)
            probs = jnp.exp(scores - lse_ref[0, pl.ds(2 * p + h, 1), :])
            grad_probs = inner_cols(v, g)
            delta = jnp.sum(probs * grad_probs, axis=0, keepdims=True)
            grad_scores = (probs * (grad_probs - delta)).astype(BF)
            outs.append(
                (
                    (inner_rows(grad_scores, k) * scale).astype(BF),
                    (matmul(grad_scores, q) * scale).astype(BF),
                    matmul(probs.astype(BF), g).astype(BF),
                )
            )
        for part in range(3):
            out_ref[part, :, at] = jnp.concatenate([outs[0][part], outs[1][part]], axis=1)
        return carry

    lax.fori_loop(0, GROUP // 2, pair, 0)
    sums_ref[0:1] = jnp.sum(out_ref[0].astype(F32), axis=0, keepdims=True)
    sums_ref[1:2] = jnp.sum(out_ref[2].astype(F32), axis=0, keepdims=True)
    per_block = blocks_ref.shape[2] // HEAD_DIM
    heads = blocks_ref.shape[0] * per_block // 3
    for step in range(heads // GROUP):

        @pl.when(pl.program_id(0) == step)
        def _(step=step):
            for part in range(3):
                for h in range(GROUP):
                    block, at = divmod(part * heads + step * GROUP + h, per_block)
                    blocks_ref[block, :, at * HEAD_DIM : (at + 1) * HEAD_DIM] = out_ref[
                        part, :, h * HEAD_DIM : (h + 1) * HEAD_DIM
                    ]


def attend_back(grad_branch, w_out, qkv, lse, segment, narrow):
    t, d = grad_branch.shape
    width = GROUP * HEAD_DIM
    return pl.pallas_call(
        attend_back_kernel,
        grid=(d // width,),
        in_specs=[
            pl.BlockSpec((t, d), lambda j: (0, 0)),
            pl.BlockSpec((width, d), lambda j: (j, 0)),
            pl.BlockSpec((3, t, width), lambda j: (0, 0, j)),
            pl.BlockSpec((1, GROUP, t), lambda j: (j, 0, 0)),
            pl.BlockSpec((1, t), lambda j: (0, 0)),
            pl.BlockSpec((t, 1), lambda j: (0, 0)),
        ],
        out_specs=[
            pl.BlockSpec((3, t, width), lambda j: (0, 0, j)),
            pl.BlockSpec((narrow, t, 3 * d // narrow), lambda j: (0, 0, 0)),
            pl.BlockSpec((2, width), lambda j: (0, j)),
        ],
        out_shape=[
            jax.ShapeDtypeStruct((3, t, d), BF),
            jax.ShapeDtypeStruct((narrow, t, 3 * d // narrow), BF),
            jax.ShapeDtypeStruct((2, d), F32),
        ],
        scratch_shapes=[pltpu.VMEM((t, width), BF)],
        compiler_params=pltpu.CompilerParams(vmem_limit_bytes=VMEM),
        cost_estimate=cost(20),
    )(grad_branch, w_out, qkv, lse, segment.reshape(1, t), segment.reshape(t, 1))


def hidden_kernel(x_ref, w_ref, bias_ref, active_ref, slope_ref):
    pre = matmul(x_ref[...], w_ref[0]) + bias_ref[...]
    below = 0.5 + 0.5 * lax.erf(pre * 0.5**0.5)
    active_ref[...] = (pre * below).astype(BF)
    density = jnp.exp(-0.5 * pre * pre) * (2.0 * math.pi) ** (-0.5)
    slope_ref[...] = (below + pre * density).astype(BF)


def hidden_layer(x, w_in, in_bias):
    t, d = x.shape
    parts, _, width = w_in.shape
    block = pl.BlockSpec((t, width), lambda j: (0, j))
    shape = jax.ShapeDtypeStruct((t, parts * width), BF)
    return pl.pallas_call(
        hidden_kernel,
        grid=(parts,),
        in_specs=[
            pl.BlockSpec((t, d), lambda j: (0, 0)),
            pl.BlockSpec((1, d, width), lambda j: (j, 0, 0)),
            pl.BlockSpec((1, width), lambda j: (0, j)),
        ],
        out_specs=[block, block],
        out_shape=[shape, shape],
        compiler_params=pltpu.CompilerParams(vmem_limit_bytes=VMEM),
        cost_estimate=cost(8),
    )(x, w_in, in_bias)


def norm_parts(value):
    mean = jnp.mean(value, axis=-1, keepdims=True)
    centered = value - mean
    scale = lax.rsqrt(jnp.mean(centered * centered, axis=-1, keepdims=True) + EPSILON)
    return centered * scale, scale


def norm_back(grad, unit, scale, gain):
    unit = unit.astype(F32)
    e = grad * gain
    part = jnp.mean(e * unit, axis=-1, keepdims=True)
    return (e - jnp.mean(e, axis=-1, keepdims=True) - unit * part) * scale


def total(value):
    return jnp.sum(jnp.sum(value, axis=0, keepdims=True), axis=1, keepdims=True)


def column_sum(value):
    return jnp.sum(value, axis=0, keepdims=True)


def by_rows(count, body, carry=None):
    if carry is None:
        carry = jnp.zeros((1, 128), F32)
    return lax.fori_loop(
        0, count // STEP, lambda i, c: body(pl.ds(pl.multiple_of(i * STEP, STEP), STEP), c), carry
    )


def store_blocks(ref, at, value):
    count, _, width = ref.shape
    for i in range(count):
        ref[i, at] = value[:, i * width : (i + 1) * width]


def calls(kernel, outs, us, **kwargs):
    return pl.pallas_call(
        kernel,
        out_shape=[jax.ShapeDtypeStruct(shape, dtype) for shape, dtype in outs],
        compiler_params=pltpu.CompilerParams(vmem_limit_bytes=VMEM),
        cost_estimate=cost(us),
        **kwargs,
    )


def branch_kernel(ctx, w, x, rows, valid, normed, low, unit, scale, stats, acc):
    acc[...] = matmul(ctx[...], w[0])
    zero = jnp.zeros((1, acc.shape[1]), F32)

    def body(at, sums):
        branch = acc[at] + rows[2:3]
        residual = x[at].astype(F32) + branch
        value, scale[at] = norm_parts(residual)
        unit[at] = value.astype(BF)
        normed[at] = value * rows[6:7] + rows[3:4]
        low[at] = normed[at].astype(BF)
        return tuple(
            s + column_sum(valid[at] * value * value) for s, value in zip(sums, (residual, branch))
        )

    for i, value in enumerate(by_rows(acc.shape[0], body, (zero, zero))):
        stats[i : i + 1] = jnp.broadcast_to(total(value), (1, 128))


def branch_layer(context, w_out, inputs, rows, valid):
    t, d = inputs.shape
    outs = [((t, d), F32), ((t, d), BF), ((t, d), BF), ((t, 1), F32), ((2, 128), F32)]
    scratch = [pltpu.VMEM((t, d), F32)]
    return calls(branch_kernel, outs, 5, scratch_shapes=scratch)(
        context, w_out, inputs, rows, valid
    )


def output_kernel(plan, level, me_ref, active, normed, rows, valid, hot, *refs):
    pieces = refs[:-8]
    low, unit, scale, pooled, stats, w, acc, sems = refs[-8:]
    step = pl.program_id(0)
    width = active.shape[1]
    block = pieces[0].shape[1]

    @pl.when(step == 0)
    def _():
        copies = []
        if plan is None:
            copies.append(pltpu.make_async_copy(pieces[0], w, sems.at[0]))
        for piece, masks in zip(pieces, plan or []):
            for slot, mask in enumerate(masks):
                at = pl.multiple_of(block_of(me_ref[0], mask, level) * block, block)
                target = w.at[pl.ds(at, block)]
                copies.append(
                    pltpu.make_async_copy(piece.at[slot], target, sems.at[len(copies)])
                )
        for copy in copies:
            copy.start()
        for copy in copies:
            copy.wait()

    product = matmul(active[...], w[pl.ds(pl.multiple_of(step * width, width), width)])

    @pl.when(step == 0)
    def _():
        acc[...] = product

    @pl.when(step > 0)
    def _():
        acc[...] += product

    @pl.when(step == pl.num_programs(0) - 1)
    def _():
        zero = jnp.zeros((1, acc.shape[1]), F32)

        def body(at, sums):
            ffn_out = acc[at] + rows[4:5]
            residual = normed[at] + ffn_out
            value, scale[at] = norm_parts(residual)
            unit[at] = value.astype(BF)
            low[at] = (value * rows[7:8] + rows[5:6]).astype(BF)
            values = (valid[at] * residual * residual, valid[at] * ffn_out * ffn_out)
            return tuple(s + column_sum(value) for s, value in zip(sums, values))

        sums = by_rows(acc.shape[0], body, (zero, zero))
        for i, value in enumerate((*sums, valid[...])):
            stats[i : i + 1] = jnp.broadcast_to(total(value), (1, 128))
        pooled[...] = matmul(hot[...].astype(BF), low[...]).astype(BF)


def all_of(shape):
    return pl.BlockSpec(shape, lambda j: (0,) * len(shape))


def output_layer(place, active, pieces, plan, normed, rows, valid, hot):
    t, ff = active.shape
    d = normed.shape[1]
    outs = [((t, d), BF), ((t, d), BF), ((t, 1), F32), ((hot.shape[0], d), BF), ((3, 128), F32)]
    outs.append(((ff, d), BF))
    return calls(
        functools.partial(output_kernel, plan, place.wide * place.narrow // LEVELS),
        outs,
        9,
        grid=(ff // d,),
        in_specs=[pl.BlockSpec(memory_space=pltpu.SMEM), pl.BlockSpec((t, d), lambda j: (0, j))]
        + [all_of(a.shape) for a in (normed, rows, valid, hot)]
        + [pl.BlockSpec(memory_space=pl.ANY)] * len(pieces),
        out_specs=[all_of(shape) for shape, _ in outs],
        scratch_shapes=[
            pltpu.VMEM((t, d), F32),
            pltpu.SemaphoreType.DMA((place.wide * place.narrow,)),
        ],
    )(place.me.reshape(1), active, normed, rows, valid, hot, *pieces)


def output_back_kernel(cot, valid, hot, pool, unit, scale, rows, grad, low, sums):
    zero = jnp.zeros((1, grad.shape[1]), F32)

    def body(at, totals):
        grad_out = cot[at].astype(F32) * valid[at] + lax.dot_general(
            hot[:, at],
            pool[...],
            (((0,), (0,)), ((), ())),
            precision=lax.Precision.HIGHEST,
            preferred_element_type=F32,
        )
        grad[at] = norm_back(grad_out, unit[at], scale[at], rows[7:8])
        low[at] = grad[at].astype(BF)
        values = (grad_out * unit[at].astype(F32), grad_out, low[at].astype(F32))
        return tuple(t + column_sum(value) for t, value in zip(totals, values))

    for i, value in enumerate(by_rows(grad.shape[0], body, (zero,) * 3)):
        sums[i : i + 1] = value


def output_back(cot, valid, hot, pool, unit, scale, rows):
    t, d = cot.shape
    outs = [((t, d), F32), ((t, d), BF), ((3, d), F32)]
    return calls(output_back_kernel, outs, 6)(cot, valid, hot, pool, unit, scale, rows)


def hidden_back_kernel(
    low, w_back, slope, w_in, grad, unit, scale, rows, hidden, inb, branch, blocks, sums, acc
):
    step = pl.program_id(0)
    product = inner_cols(low[...], w_back[...])
    hidden[...] = (product * slope[...].astype(F32)).astype(BF)
    inb[...] = column_sum(hidden[...].astype(F32))
    product = inner_cols(hidden[...], w_in[0])

    @pl.when(step == 0)
    def _():
        acc[...] = grad[...] + product

    @pl.when(step > 0)
    def _():
        acc[...] += product

    @pl.when(step == pl.num_programs(0) - 1)
    def _():
        zero = jnp.zeros((1, acc.shape[1]), F32)

        def body(at, totals):
            value = acc[at]
            branch[at] = norm_back(value, unit[at], scale[at], rows[6:7]).astype(BF)
            store_blocks(blocks, at, branch[at])
            values = (value * unit[at].astype(F32), value, branch[at].astype(F32))
            return tuple(t + column_sum(value) for t, value in zip(totals, values))

        for i, value in enumerate(by_rows(acc.shape[0], body, (zero,) * 3)):
            sums[i : i + 1] = value


def hidden_back(low, w_back, slope, w_in, grad, unit, scale, rows, narrow):
    t, d = low.shape
    ff = slope.shape[1]
    tile = pl.BlockSpec((t, d), lambda j: (0, j))
    outs = [
        ((t, ff), BF),
        ((1, ff), F32),
        ((t, d), BF),
        ((narrow, t, d // narrow), BF),
        ((3, d), F32),
    ]
    return calls(
        hidden_back_kernel,
        outs,
        14,
        grid=(ff // d,),
        in_specs=[
            all_of(low.shape),
            pl.BlockSpec((d, d), lambda j: (j, 0)),
            tile,
            pl.BlockSpec((1, d, d), lambda j: (j, 0, 0)),
        ]
        + [all_of(a.shape) for a in (grad, unit, scale, rows)],
        out_specs=[tile, pl.BlockSpec((1, d), lambda j: (0, j))]
        + [all_of(shape) for shape, _ in outs[2:]],
        scratch_shapes=[pltpu.VMEM((t, d), F32)],
    )(low, w_back, slope, w_in, grad, unit, scale, rows)


def input_back_kernel(grad, w, residual, out, acc):
    step = pl.program_id(0)
    product = inner_cols(grad[0], w[0])

    @pl.when(step == 0)
    def _():
        acc[...] = residual[...].astype(F32) + product

    @pl.when(step == 1)
    def _():
        acc[...] += product

    @pl.when(step == 2)
    def _():
        out[...] = (acc[...] + product).astype(BF)


def input_back(grad_qkv, w_qkv, residual):
    _, t, d = grad_qkv.shape
    return calls(
        input_back_kernel,
        [((t, d), BF)],
        6,
        grid=(3,),
        in_specs=[
            pl.BlockSpec((1, t, d), lambda j: (j, 0, 0)),
            pl.BlockSpec((1, d, d), lambda j: (j, 0, 0)),
            all_of((t, d)),
        ],
        out_specs=[all_of((t, d))],
        scratch_shapes=[pltpu.VMEM((t, d), F32)],
    )(grad_qkv, w_qkv, residual)[0]


def spread_masks(count, width):
    total_cols = count * width
    column = lax.broadcasted_iota(jnp.int32, (count, total_cols), 1)
    first = lax.broadcasted_iota(jnp.int32, (count, total_cols), 0) * width
    own = (column >= first) & (column < first + width)
    owner = jnp.sum(jnp.where(own, first, 0), axis=0, keepdims=True)
    within = lax.broadcasted_iota(jnp.int32, (width, total_cols), 1) - owner
    spread = within == lax.broadcasted_iota(jnp.int32, (width, total_cols), 0)
    return own, spread.astype(F32)


def unpack_kernel(small, rows, inb):
    count = small.shape[0]
    value = small[...].astype(F32)

    def unpack(part, masks):
        own, spread = masks
        placed = matmul(part.astype(BF), spread.astype(BF))
        return column_sum(jnp.where(own, placed, 0.0))

    width = rows.shape[1] // count
    masks = spread_masks(count, width)
    for r in range(8):
        rows[r : r + 1] = unpack(value[:, r, :width], masks)
    width = inb.shape[1] // count
    inb[...] = unpack(value[:, 0, 128 : 128 + width], spread_masks(count, width))


def unpack_params(small, d, ff):
    return calls(unpack_kernel, [((8, d), F32), ((1, ff), F32)], 0.1)(small)


def pack_kernel(attn, out, ffn, inb, stats_a, stats_b, packed, rows, parts):
    count = packed.shape[0]
    vectors = (attn[0:1], attn[1:2], out[2:3], out[1:2], ffn[2:3], ffn[1:2], out[0:1], ffn[0:1])

    def pack(vector, own, spread):
        return lax.dot_general(
            jnp.where(own, vector, 0.0),
            spread,
            (((1,), (1,)), ((), ())),
            precision=lax.Precision.HIGHEST,
            preferred_element_type=F32,
        )

    for i, vector in enumerate(vectors):
        rows[i : i + 1] = vector
    packed[...] = jnp.zeros(packed.shape, F32)
    width = rows.shape[1] // count
    masks = spread_masks(count, width)

    def body(i, carry):
        parts[i] = pack(rows[pl.ds(i, 1)], *masks)
        return carry

    lax.fori_loop(0, len(vectors), body, 0)
    for i in range(len(vectors)):
        packed[:, i * width : (i + 1) * width] = parts[i]
    at = len(vectors) * width
    width = inb.shape[1] // count
    packed[:, at : at + width] = pack(inb[...], *spread_masks(count, width))
    at += width
    for i, row in enumerate((stats_a[0:1], stats_a[1:2], stats_b[0:1], stats_b[1:2], stats_b[2:3])):
        packed[:, at + i : at + i + 1] = jnp.broadcast_to(row[:, :1], (count, 1))


def pack_sums(count, attn, out, ffn, inb, stats_a, stats_b):
    width = attn.shape[1]
    scratch = [pltpu.VMEM((8, width), F32), pltpu.VMEM((8, count, width // count), F32)]
    return calls(pack_kernel, [((count, 384), F32)], 4, scratch_shapes=scratch)(
        attn, out, ffn, inb, stats_a, stats_b
    )[0]


def match_grads(rows, label_rows, label_cols):
    is_query, is_pass = label_rows >= 0, label_cols >= 0
    match = jnp.where(is_pass, inner_cols(rows, rows) / SCORE_DIV, MASKED)
    shifted = jnp.exp(match - jnp.max(match, axis=1, keepdims=True))
    probs = shifted / jnp.sum(shifted, axis=1, keepdims=True)
    hot = (label_rows == label_cols).astype(F32)
    grad = jnp.where(is_query & is_pass, (probs - hot) / SCORE_DIV, 0.0).astype(BF)
    return matmul(grad[:POOL], rows) + inner_rows(grad[:, :POOL], rows)


def match_kernel(rows, label_rows, label_cols, out):
    out[...] = match_grads(rows[...], label_rows[...], label_cols[...])


def row_of(z, y, n, s):
    own = (z * s + y) * 3 + n
    spare = y * 3 + (z - 1)
    return jnp.where(z == 0, n * s + y, jnp.where(n < 3, own, spare))


def body(
    passages,
    queries,
    passage_cot,
    query_cot,
    passage_lengths,
    query_lengths,
    labels,
    w_qkv,
    w_out,
    w_in,
    w_back,
    biases,
    norm_gains,
    in_bias,
):
    place = Place()
    s, narrow, devices = place.stride, place.narrow, place.wide * place.narrow
    model_width = passages.shape[2]
    length = passages.shape[1] * narrow
    segs, qsegs = passage_lengths.shape[1] - 1, query_lengths.shape[1] - 1
    on_query = place.z == 0

    piece = model_width // devices
    whole = jnp.concatenate(
        [passage_lengths.reshape(-1), query_lengths.reshape(-1), labels.reshape(-1)]
    )
    whole = jnp.concatenate([whole // 32, whole % 32]).astype(BF)

    w_rows, in_parts = w_out.shape[1], w_in.shape[2] // w_out.shape[2]
    if s == 2:
        towers = pick_towers(place, w_qkv, biases, norm_gains, in_bias, whole)
        got = {k: flip(towers[k], "wide", k * s) for k in (3, 2, 1)}
        levels_qkv = jnp.stack([towers[0], got[1], got[2], got[3]])
        own = [k * s * narrow for k in range(LEVELS)]
        layout = [(0, part, part * w_rows, 0) for part in range(3)] + [(1, 0, 3 * w_rows, 0)]
        shapes = [(3, w_rows, model_width), (1, 8, model_width)]
    else:
        small = jnp.concatenate(
            [biases.reshape(2, -1), norm_gains.reshape(2, -1), in_bias.reshape(2, -1)], axis=1
        )
        small_count = small.shape[1]
        small = jnp.concatenate([small, jnp.broadcast_to(whole, (2, whole.shape[0]))], axis=1)
        to_query = (jnp.arange(devices) < s * narrow)[:, None]
        small = lax.all_to_all(
            jnp.where(to_query, small[1][None], small[0][None]), BOTH, 0, 0, tiled=True
        )
        levels_qkv, own = gather_levels(place, w_qkv), None
        layout = [(0, part, 0, part * model_width) for part in range(3)]
        shapes = [(3, w_rows, model_width)]
    out_in = jnp.concatenate([w_out, w_in], axis=2)
    levels_qkv, out_in, parts = phase(levels_qkv, out_in, (passages, queries))

    pieces_qkv, plan = gather_columns(place, levels_qkv, own)
    levels_out_in = gather_levels(place, out_in)
    swapped = swap_in_directly(place, *parts)
    pieces_qkv, levels_out_in, w_back, swapped = phase(
        pieces_qkv, levels_out_in, w_back, swapped
    )

    cores_qkv, core_plan = gather_cores(pieces_qkv, plan)
    cores_qkv, levels_out_in, swapped = phase(cores_qkv, levels_out_in, swapped)

    pieces_out_in, plan = gather_columns(place, levels_out_in)
    inputs = to_row(place, passages, queries, join_swapped(place, queries, swapped))
    inputs, w_back, cores_qkv = phase(inputs, w_back, cores_qkv)
    levels_back = gather_levels(place, w_back)
    made = assemble(place, cores_qkv, core_plan, layout, shapes)
    w_qkv_all = made[0]

    n_bias, n_gain = biases.shape[1], norm_gains.shape[1]
    ff = in_bias.shape[1] * devices
    if s == 2:
        small = made[1].reshape(devices, 8, -1)
        rows, inb_row = unpack_params(small, model_width, ff)
        ints = small[:, 0, 256 : 256 + whole.shape[0]].astype(F32)
    else:
        params = small[:, :small_count].astype(F32)
        vectors = params[:, : (n_bias + n_gain) * piece].reshape(devices, n_bias + n_gain, piece)
        rows = vectors.transpose(1, 0, 2).reshape(n_bias + n_gain, -1)
        inb_row = params[:, (n_bias + n_gain) * piece :].reshape(1, -1)
        ints = small[:, small_count : small_count + whole.shape[0]].astype(F32)
    half = ints.shape[1] // 2
    ints = (ints[::narrow, :half] * 32 + ints[::narrow, half:]).astype(jnp.int32)
    n_pass = passage_lengths.size
    n_query = query_lengths.size
    pass_lens = ints[:, :n_pass].reshape(-1, segs + 1)
    query_lens = ints[:, n_pass : n_pass + n_query].reshape(-1, qsegs + 1)
    label_all = ints[:, n_pass + n_query :].reshape(-1, qsegs)
    my_row = row_of(place.z, place.y, place.n, s)
    pass_row = pick(pass_lens, jnp.where(on_query, 0, my_row), 0)
    query_row = pick(query_lens, jnp.where(on_query, my_row, 0), 0)
    ends_p = jnp.cumsum(pass_row)[:-1]
    ends_q = jnp.cumsum(query_row)[:-1]
    starts_p, starts_q = ends_p - pass_row[:-1], ends_q - query_row[:-1]
    ends_p = jnp.concatenate([ends_p, jnp.full((qsegs - segs,), length + 1, jnp.int32)])
    ends = jnp.where(on_query, ends_q, ends_p)
    seg_count = jnp.where(on_query, qsegs, segs)
    position = jnp.arange(length, dtype=jnp.int32)
    segment = jnp.sum((position[:, None] >= ends[None, :]).astype(jnp.int32), axis=1)
    valid = (segment < seg_count).astype(F32)[:, None]
    slot = jnp.arange(POOL)
    starts = jnp.where(on_query, jnp.concatenate([starts_q, jnp.full((qsegs,), -1)]), -1)
    for z in range(1, LEVELS):
        here = (place.z == z) & (slot >= qsegs + segs * (z - 1)) & (slot < qsegs + segs * z)
        starts = jnp.where(here, jnp.tile(starts_p, POOL // segs), starts)
    hot = (starts[:, None] == position[None, :]).astype(F32)
    masks = [0]
    if s == 2:
        masks += [dy * narrow + 2 * dx for dx, dy in OTHERS]
        masks += [m ^ 1 for m in masks]
    else:
        for mask in [b * narrow for b in bits_of(s)] + [b for b in reversed(bits_of(narrow))]:
            masks = masks + [m ^ mask for m in masks]
    there = (place.y * narrow + place.n) ^ jnp.array(masks, jnp.int32)
    their_y, their_n = there // narrow, there % narrow
    label_rows = label_all[row_of(jnp.int32(0), their_y, their_n, s)]
    label_rows = jnp.pad(label_rows, ((0, 0), (0, POOL - qsegs)), constant_values=-1)
    levels = jnp.arange(1, LEVELS)
    pass_rows = row_of(levels[None, :], their_y[:, None], their_n[:, None], s)
    pass_ids = (pass_rows[:, :, None] * segs + jnp.arange(segs)).reshape(len(masks), -1)
    spare = POOL - qsegs - pass_ids.shape[1]
    label_cols = jnp.pad(pass_ids, ((0, 0), (qsegs, spare)), constant_values=-1)
    label_rows, label_cols = label_rows.reshape(-1, 1), label_cols.reshape(1, -1)

    qkv, context, log_sum = attend(inputs, w_qkv_all, rows, segment)
    context, pieces_out_in, levels_back, cots = phase(
        context, pieces_out_in, levels_back, (passage_cot, query_cot)
    )

    cores_out_in, core_plan = gather_cores(pieces_out_in, plan)
    cores_out_in, levels_back, cots = phase(cores_out_in, levels_back, cots)

    pieces_back, plan = gather_columns(place, levels_back)
    swapped = swap_in(place, *cots)
    w_out_all, w_in_all = assemble(
        place,
        cores_out_in,
        core_plan,
        [(0, 0, 0, 0)] + [(1, part, 0, (part + 1) * model_width) for part in range(in_parts)],
        [(1, w_rows, model_width), (in_parts, w_rows, model_width)],
    )
    normed, normed_low, unit_one, scale_one, stats_one = branch_layer(
        context, w_out_all, inputs, rows, valid
    )
    active, slope = hidden_layer(normed_low, w_in_all, inb_row)
    active, pieces_back, swapped = phase(active, pieces_back, swapped)

    cores_back, core_plan = gather_cores(pieces_back, plan)
    cot = to_row(place, passage_cot, query_cot, swapped)
    if s != 2:
        back_shape = [(1, w_back.shape[1], model_width)]
        cores_back = assemble(place, cores_back, core_plan, [(0, 0, 0, 0)], back_shape)
        cores_back, core_plan = [cores_back[0][0]], None
    output_low, unit_two, scale_two, pooled, stats_two, w_back_all = output_layer(
        place, active, cores_back, core_plan, normed, rows, valid, hot
    )
    pooled, cot = phase(pooled, cot)

    column = sum([flip(pooled, "wide", k * s).astype(F32) for k in (3, 2, 1)], pooled.astype(F32))
    seen = column.astype(BF)[None]
    if s == 2:
        seen = jnp.concatenate([seen] + [flip_both(seen, dy, 2 * dx) for dx, dy in OTHERS])
        seen = jnp.concatenate([seen, flip(seen, "narrow", 1)])
    else:
        for axis, step in [("wide", b) for b in bits_of(s)] + [
            ("narrow", b) for b in reversed(bits_of(narrow))
        ]:
            seen = jnp.concatenate([seen, flip(seen, axis, step)])
    seen = seen.reshape(-1, model_width)
    if s == 2:
        (grad_pool,) = calls(match_kernel, [((POOL, model_width), F32)], 3)(
            seen, label_rows, label_cols
        )
    else:
        grad_pool = match_grads(seen, label_rows, label_cols)

    grad_pool, output_low = phase(grad_pool, output_low)
    if s == 2:
        out_four = row_pieces(place, output_low)
    grad_resid_two, grad_ffn, sums_two = output_back(
        cot, valid, hot, grad_pool, unit_two, scale_two, rows
    )
    if s == 2:
        send_c, keep_c = products_back(place, active, grad_ffn)
        send_c, out_four = phase(send_c, out_four)
        got_c = flip(send_c, "narrow", 1)
        shares_c = column_shares(place, keep_c, got_c)
        shares_c, grad_ffn = phase(shares_c, grad_ffn)

        columns_c = send_columns(shares_c)
        swapped = swap_out(place, out_four)
    grad_hidden, inb_sums, grad_branch, blocks_b, sums_one = hidden_back(
        grad_ffn, w_back_all, slope, w_in_all, grad_resid_two, unit_one, scale_one, rows, narrow
    )
    if s == 2:
        send_b, keep_b = products_out_in(place, context, blocks_b, normed_low, grad_hidden)
        send_b, columns_c, swapped = phase(send_b, columns_c, swapped)
        passage_out, query_out = from_row(place, out_four, swapped)

        got_b = flip(send_b, "narrow", 1)
        level_c = level_sums(columns_c)
        shares_b = column_shares(place, keep_b, got_b)
        shares_b, level_c, grad_branch = phase(shares_b, level_c, grad_branch)

        columns_b = send_columns(shares_b)
        levels_c = across_levels(level_c, s)
    grad_qkv, blocks_a, sums_qkv = attend_back(
        grad_branch, w_out_all[0], qkv, log_sum, segment, narrow
    )
    if s == 2:
        send_a, keep_a = products_qkv(place, inputs, blocks_a)
        send_a, grad_qkv, columns_b, levels_c = phase(send_a, grad_qkv, columns_b, levels_c)

        got_a = flip(send_a, "narrow", 1)
    input_grad = input_back(grad_qkv, w_qkv_all, grad_branch)
    if s == 2:
        got_a, input_grad, columns_b = phase(got_a, input_grad, columns_b)

        in_four = row_pieces(place, input_grad)
        levels_b = swap_shares(place, level_shares(place, columns_b))
        shares_a = column_shares(place, keep_a, got_a)
        late = levels_b.pop(3)
        shares_a, levels_b, in_four, sums_qkv, levels_c = phase(
            shares_a, levels_b, in_four, sums_qkv, levels_c
        )
        levels_b.insert(3, late)

        columns_a = send_columns(shares_a)
        swapped = swap_out(place, in_four)
        packed = pack_sums(devices, sums_qkv, sums_one, sums_two, inb_sums, stats_one, stats_two)
        grad_w_back = finish_back(levels_c)
        columns_a, swapped, packed = phase(columns_a, swapped, packed)

        level_a = level_shares(place, columns_a)
        level_a, packed = phase(level_a, packed)
        levels_a = swap_shares(place, level_a)
        packed = lax.all_to_all(packed, BOTH, 0, 0, tiled=True)
        grad_w_out, grad_w_in = finish_out_in(place, levels_b, model_width // place.wide)
        passage_grad, query_grad = from_row(place, in_four, swapped)
        grad_w_qkv = finish_qkv(place, levels_a)
    else:
        packed = pack_sums(devices, sums_qkv, sums_one, sums_two, inb_sums, stats_one, stats_two)
        packed = lax.all_to_all(packed, BOTH, 0, 0, tiled=True)
        grad_w_back = scatter_tower(place, grad_blocks(active, grad_ffn, narrow))
        grad_w_out = scatter_tower(place, grad_blocks(context, grad_branch, narrow))
        grad_w_in = scatter_tower(place, grad_blocks(normed_low, grad_hidden, narrow))
        flat = jnp.moveaxis(grad_qkv, 0, 1).reshape(length, -1)
        grad_w_qkv = scatter_tower(place, grad_blocks(inputs, flat, narrow))
        out_four, in_four = row_pieces(place, output_low), row_pieces(place, input_grad)
        passage_out, query_out = from_row(place, out_four, swap_out(place, out_four))
        passage_grad, query_grad = from_row(place, in_four, swap_out(place, in_four))

    packed = packed.reshape(LEVELS, -1, packed.shape[1]).sum(axis=1)
    packed = jnp.stack([packed[1] + packed[2] + packed[3], packed[0]])
    edges = [n_bias * piece, (n_bias + n_gain) * piece]
    edges.append(edges[1] + in_bias.shape[1])
    grad_biases = packed[:, : edges[0]].reshape(2, n_bias, piece)
    grad_gains = packed[:, edges[0] : edges[1]].reshape(2, n_gain, piece)
    grad_inb = packed[:, edges[1] : edges[2]]
    totals = packed[:, edges[2] : edges[2] + 5]
    rms_stats = jnp.sqrt(totals[:, :4] / (totals[:, 4:] * model_width))
    return (
        passage_out,
        query_out,
        passage_grad,
        query_grad,
        grad_w_qkv,
        grad_w_out,
        grad_w_in,
        grad_w_back,
        grad_biases,
        grad_gains,
        grad_inb,
        rms_stats,
    )


def solution(mesh):
    return jax.shard_map(
        body,
        mesh=mesh,
        in_specs=(
            P("wide", "narrow", None),
            P("wide", "narrow", None),
            P("wide", "narrow", None),
            P("wide", "narrow", None),
            P("wide", None),
            P("wide", None),
            P("wide"),
            P(None, ("wide", "narrow"), None),
            P(None, ("wide", "narrow"), None),
            P(None, ("wide", "narrow"), None),
            P(None, ("wide", "narrow"), None),
            P(None, None, ("wide", "narrow")),
            P(None, None, ("wide", "narrow")),
            P(None, ("wide", "narrow")),
        ),
        out_specs=(
            P("wide", "narrow", None),
            P("wide", "narrow", None),
            P("wide", "narrow", None),
            P("wide", "narrow", None),
            P(None, "wide", "narrow"),
            P(None, "wide", "narrow"),
            P(None, "wide", "narrow"),
            P(None, "wide", "narrow"),
            P(None, None, ("wide", "narrow")),
            P(None, None, ("wide", "narrow")),
            P(None, ("wide", "narrow")),
            P(),
        ),
        check_vma=False,
    )
```
